32 devices in a mesh: dp: 8 (over y, x, core), seq: 4 (over z).
Axes of the slice: x: 2, y: 2, z: 4, core: 2. Of those that a mesh axis runs over, the one named last changes fastest.
Arguments:
- tokens: bfloat16 [8, 2048, 768], P('dp', 'seq'), may hold values from -6 to 6
- cotangent: bfloat16 [8, 2048, 768], P('dp', 'seq'), may hold values from -6 to 6
- segment_ids: int32 [8, 2048], P('dp', 'seq'), may hold values from 0 to 7, as said below
- doc_starts: int32 [8, 2048], P('dp', 'seq'), may hold values from 0 to 1, as said below
- valid_mask: int32 [8, 2048], P('dp', 'seq'), may hold values from 0 to 1
- step_number: int32 [1], replicated, may hold values from 1 to 64
- learn_rate: float32 [1], replicated, may hold values from 0.001 to 0.004
- norm_gain: float32 [768], replicated, may hold values from 0.5 to 1.5
- in_weight: bfloat16 [768, 3352], replicated, may hold values from -0.21875 to 0.21875
- conv_weight: float32 [4, 1792], replicated, may hold values from -3 to 3
- conv_bias: float32 [1792], replicated, may hold values from -1.75 to 1.75
- dt_bias: float32 [24], replicated, may hold values from -6 to -2
- a_log: float32 [24], replicated, may hold values from -1 to 2.5
- skip_d: float32 [24], replicated, may hold values from 0.5 to 1.5
- gate_gain: float32 [1536], replicated, may hold values from 0.5 to 1.5
- out_weight: bfloat16 [1536, 768], replicated, may hold values from -0.15625 to 0.15625
- in_momentum: float32 [768, 3352], P('seq'), may hold values from -6 to 6
- out_momentum: float32 [1536, 768], P(None, 'seq'), may hold values from -448 to 448
Outputs:
- output: bfloat16 [8, 2048, 768], P('dp', 'seq')
- input_grad: bfloat16 [8, 2048, 768], P('dp', 'seq')
- new_in_weight: bfloat16 [768, 3352], replicated
- new_out_weight: bfloat16 [1536, 768], replicated
- new_in_momentum: float32 [768, 3352], P('seq')
- new_out_momentum: float32 [1536, 768], P(None, 'seq')
- norm_gain_grad: float32 [768], replicated
- conv_weight_grad: float32 [4, 1792], replicated
- conv_bias_grad: float32 [1792], replicated
- dt_bias_grad: float32 [24], replicated
- a_log_grad: float32 [24], replicated
- skip_grad: float32 [24], replicated
- gate_gain_grad: float32 [1536], replicated
- output_rms: float32 [1], replicated
- mixer_rms: float32 [1], replicated
The draws below stay inside these ranges and needn't reach their ends.
Inputs may be any that keep to these rules, and one draw needn't show every extreme that they name: Within each sequence segment_ids never fall, are 0 at the first position and rise by one exactly where doc_starts is 1; every sequence holds exactly 8 documents. `doc_starts`: 1 at the first position of every sequence; exactly 8 ones in every sequence.
All inputs are finite; a program needn't handle non-finite values.
Results may differ from the reference program's by a relative error of at most 0.0066.
The reference program's roundings to bfloat16 on the way (of `normed_in`, `gate_normed` and `out_grad`) count: a program that leaves them out, or rounds other values in their place, can miss the bound.
Values may be sent and summed in bfloat16 or wider, within the bound.
A program may use at most 192 MiB of HBM per device.

```python
import math
import jax
import jax.numpy as jnp
from jax import lax

D_MODEL = 768
HEADS = 24
HEAD_DIM = 64
D_STATE = 128
CONV_K = 4
LENGTH = 2048
DOCS = 8
D_INNER = 1536
CONV_CH = 1792
PROJ = 3352
BATCH = 8


def draw_documents(key):
    row_keys = jax.random.split(jax.random.fold_in(key, 11), BATCH)

    def one_row(row_key):
        order = jax.random.permutation(row_key, LENGTH - 1) + 1
        chosen = order[:DOCS - 1]
        flags = jnp.zeros((LENGTH,), jnp.int32).at[chosen].set(1)
        return flags.at[0].set(1)
    return jax.vmap(one_row)(row_keys)


def draw_segment_ids(key, part):
    return (jnp.cumsum(draw_documents(key), axis=1) - 1).astype(jnp.int32)


def draw_doc_starts(key, part):
    return draw_documents(key)


def draw_valid_mask(key, part):
    levels = jax.random.randint(jax.random.fold_in(key, 23), (BATCH, LENGTH), 0, 4 * LENGTH)
    thresholds = LENGTH + 3 * jnp.arange(LENGTH)
    return (levels < thresholds[None, :]).astype(jnp.int32)


def block_scale(own_key, shape, cuts, least, largest):
    def one(axis_at, blocks):
        draws = jax.random.uniform(jax.random.fold_in(jax.random.fold_in(own_key, 6), axis_at), (blocks,), jnp.float32, least / len(cuts), largest / len(cuts))
        return jnp.repeat(jnp.exp(draws), shape[axis_at] // blocks).reshape((-1,) + (1,) * (len(shape) - axis_at - 1))

    level = one(*cuts[0])
    for cut in cuts[1:]:
        level = level * one(*cut)
    return level


def centred(own_key, shape, scale, most, pieces=(), held_as=jnp.bfloat16):
    drawn = jax.random.normal(own_key, shape, jnp.float32) * scale
    if len(pieces) > 0:
        drawn = block_scale(own_key, shape, pieces, -0.22, 0.18) * drawn
    return jnp.clip(drawn, min=-most, max=most).astype(held_as)


def setup_inputs(seed: int = 0) -> dict:
    seeds = jax.random.split(jax.random.key(seed), 19)
    tokens = centred(seeds[0], (BATCH, LENGTH, D_MODEL), 1.0, 6.0, ((0, 8), (1, 4)))
    cotangent = centred(seeds[1], (BATCH, LENGTH, D_MODEL), 1.0, 6.0, ((0, 8), (1, 4)))
    segment_ids = draw_segment_ids(jax.random.fold_in(seeds[18], 71), 0)
    doc_starts = draw_doc_starts(jax.random.fold_in(seeds[18], 71), 0)
    valid_mask = draw_valid_mask(jax.random.fold_in(seeds[18], 71), 0)
    step_number = jax.random.randint(seeds[5], (1,), 1, 65).astype(jnp.int32)
    learn_rate = jnp.clip(jnp.exp(jax.random.uniform(seeds[6], (1,), jnp.float32, math.log(0.001), math.log(0.004))), 0.001, 0.004)
    norm_gain = jnp.clip(1.0 + 0.1 * jax.random.normal(seeds[7], (D_MODEL,), jnp.float32), 0.5, 1.5)
    in_weight = centred(seeds[8], (D_MODEL, PROJ), D_MODEL ** -0.5, 0.21875)
    conv_weight = centred(seeds[9], (CONV_K, CONV_CH), CONV_K ** -0.5, 3.0, (), jnp.float32)
    conv_bias = centred(seeds[10], (CONV_CH,), 0.3, 1.75, (), jnp.float32)
    dt_bias = jnp.clip(jax.random.uniform(seeds[11], (HEADS,), jnp.float32, -6.0, -2.0), -6.0, -2.0)
    a_log = jnp.clip(jax.random.uniform(seeds[12], (HEADS,), jnp.float32, -1.0, 2.5), -1.0, 2.5)
    skip_d = jnp.clip(jax.random.uniform(seeds[13], (HEADS,), jnp.float32, 0.5, 1.5), 0.5, 1.5)
    gate_gain = jnp.clip(1.0 + 0.1 * jax.random.normal(seeds[14], (D_INNER,), jnp.float32), 0.5, 1.5)
    out_weight = centred(seeds[15], (D_INNER, D_MODEL), D_INNER ** -0.5, 0.15625)
    in_momentum = centred(seeds[16], (D_MODEL, PROJ), 1.0, 6.0, ((0, 4),), jnp.float32)
    out_momentum = centred(seeds[17], (D_INNER, D_MODEL), (0.6 * (BATCH * LENGTH) ** 0.5), 448.0, ((1, 4),), jnp.float32)
    return dict(tokens=tokens, cotangent=cotangent, segment_ids=segment_ids, doc_starts=doc_starts, valid_mask=valid_mask, step_number=step_number, learn_rate=learn_rate, norm_gain=norm_gain, in_weight=in_weight, conv_weight=conv_weight, conv_bias=conv_bias, dt_bias=dt_bias, a_log=a_log, skip_d=skip_d, gate_gain=gate_gain, out_weight=out_weight, in_momentum=in_momentum, out_momentum=out_momentum)


epsilon = 1e-05
highest = lax.Precision.HIGHEST

@jax.custom_vjp
def low(v):
    return lax.optimization_barrier(v.astype(jnp.bfloat16)).astype(jnp.float32)

@jax.custom_vjp
def low_back(v):
    return v

def low_keep(v):
    return (low(v), None)

def low_pass(kept, grad):
    return (grad,)

def back_keep(v):
    return (v, None)

def back_low(kept, grad):
    return (low(grad),)
low.defvjp(low_keep, low_pass)
low_back.defvjp(back_keep, back_low)

def block_scan(carried_state, inputs):
    signal, writer, reader, step_size, log_decay, start_flags = inputs
    cumulative = jnp.cumsum(log_decay, axis=0)
    counter = jnp.cumsum(start_flags)
    block_size = signal.shape[0]
    causal = jnp.arange(block_size)[:, None] >= jnp.arange(block_size)[None, :]
    same_doc = (counter[:, None] == counter[None, :]) & causal
    by_head = cumulative.T
    gaps = by_head[:, :, None] - by_head[:, None, :]
    decays = jnp.exp(jnp.where(same_doc[None], gaps, -1e+30))
    scores = jnp.einsum('tn,sn->ts', reader, writer, precision=highest)
    weighted = scores[None] * decays
    inner_part = jnp.einsum('hts,shp->thp', weighted, signal * step_size[:, :, None], precision=highest)
    entries = jnp.where((counter == 0)[:, None], jnp.exp(cumulative), 0.0)
    carried = jnp.einsum('tn,hpn->thp', reader, carried_state, precision=highest) * entries[:, :, None]
    final_log = cumulative[-1]
    keeping = jnp.where(counter[-1] == 0, jnp.exp(final_log), 0.0)
    tails = jnp.where((counter == counter[-1])[:, None], jnp.exp(final_log[None, :] - cumulative), 0.0)
    fresh_state = jnp.einsum('th,thp,tn->hpn', tails * step_size, signal, writer, precision=highest)
    return (keeping[:, None, None] * carried_state + fresh_state, inner_part + carried)

def mamba_layer(params, inputs, segments, start_flags):
    norm_gain, in_weight, conv_weight, conv_bias, dt_bias, a_log, skip_d, gate_gain, out_weight = params
    length = inputs.shape[0]
    normed_in = inputs * lax.rsqrt(lax.optimization_barrier(jnp.mean(inputs * inputs, axis=-1, keepdims=True)) + epsilon) * norm_gain
    projected = low_back(jnp.dot(low(normed_in), in_weight, precision=highest, preferred_element_type=jnp.float32))
    gate_in = projected[:, :D_INNER]
    conv_in = projected[:, D_INNER:D_INNER + CONV_CH]
    dt_raw = projected[:, D_INNER + CONV_CH:]
    padded = jnp.concatenate([jnp.zeros((CONV_K - 1, CONV_CH), jnp.float32), conv_in], axis=0)
    seg_pad = jnp.concatenate([jnp.full((CONV_K - 1,), -1, jnp.int32), segments.astype(jnp.int32)])
    summed = conv_bias + jnp.zeros((length, CONV_CH), jnp.float32)
    for k in range(CONV_K):
        matches = (seg_pad[k:k + length] == segments)[:, None]
        summed = summed + jnp.where(matches, padded[k:k + length], 0.0) * conv_weight[k]
    activated = jax.nn.silu(summed)
    signal = activated[:, :D_INNER].reshape(length, HEADS, HEAD_DIM)
    writer = activated[:, D_INNER:D_INNER + D_STATE]
    reader = activated[:, D_INNER + D_STATE:]
    step_size = jax.nn.softplus(dt_raw + dt_bias)
    log_decay = -jnp.exp(a_log) * step_size
    block_size = min(256, length)
    block_count = length // block_size

    def blocks_of(values):
        return values.reshape((block_count, block_size) + values.shape[1:])
    start_state = jnp.zeros((HEADS, HEAD_DIM, D_STATE), jnp.float32)
    _, block_out = lax.scan(jax.checkpoint(block_scan), start_state, (blocks_of(signal), blocks_of(writer), blocks_of(reader), blocks_of(step_size), blocks_of(log_decay), blocks_of(start_flags)))
    ssm_out = block_out.reshape(length, HEADS, HEAD_DIM) + skip_d[:, None] * signal
    gated_out = ssm_out.reshape(length, D_INNER) * jax.nn.silu(gate_in)
    gate_normed = gated_out * lax.rsqrt(lax.optimization_barrier(jnp.mean(gated_out * gated_out, axis=-1, keepdims=True)) + epsilon) * gate_gain
    mixed = jnp.dot(low(gate_normed), out_weight, precision=highest, preferred_element_type=jnp.float32)
    return (inputs + mixed, mixed)

def reference(tokens, cotangent, segment_ids, doc_starts, valid_mask, step_number, learn_rate, norm_gain, in_weight, conv_weight, conv_bias, dt_bias, a_log, skip_d, gate_gain, out_weight, in_momentum, out_momentum):
    params = tuple((p.astype(jnp.float32) for p in (norm_gain, in_weight, conv_weight, conv_bias, dt_bias, a_log, skip_d, gate_gain, out_weight)))

    def one_sequence(carried_sums, record):
        gradients, totals = carried_sums
        token_row, cot_row, seg_row, start_row, valid_row = record
        inputs = token_row.astype(jnp.float32)
        valid_float = valid_row.astype(jnp.float32)
        (block_out, mixed), backward = jax.vjp(lambda p, v: mamba_layer(p, v, seg_row, start_row), params, inputs)
        out_grad = cot_row.astype(jnp.float32) * valid_float[:, None]
        param_grads, in_grad = backward((out_grad, jnp.zeros_like(mixed)))
        gradients = jax.tree.map(lambda a, b: a + b, gradients, param_grads)
        totals = totals + jnp.stack([jnp.sum(valid_float * lax.optimization_barrier(jnp.sum(block_out * block_out, axis=-1))), jnp.sum(valid_float * lax.optimization_barrier(jnp.sum(mixed * mixed, axis=-1))), jnp.sum(valid_float)])
        return ((gradients, totals), (block_out.astype(jnp.bfloat16), in_grad.astype(jnp.bfloat16)))
    start_sums = (jax.tree.map(jnp.zeros_like, params), jnp.zeros((3,), jnp.float32))
    (gradients, totals), (output, input_grad) = lax.scan(one_sequence, start_sums, (tokens, cotangent, segment_ids, doc_starts, valid_mask))
    step_float = step_number[0].astype(jnp.float32)
    rate_now = learn_rate[0] * step_float / (step_float + 16.0)
    new_in_momentum = 0.5 * in_momentum + gradients[1]
    new_out_momentum = 0.5 * out_momentum + gradients[8]
    new_in_weight = (in_weight.astype(jnp.float32) - rate_now * new_in_momentum).astype(jnp.bfloat16)
    new_out_weight = (out_weight.astype(jnp.float32) - rate_now * new_out_momentum).astype(jnp.bfloat16)
    valid_count = jnp.maximum(totals[2], 1.0) * D_MODEL
    output_rms = jnp.sqrt(totals[0] / valid_count).reshape(1)
    mixer_rms = jnp.sqrt(totals[1] / valid_count).reshape(1)
    return (output, input_grad, new_in_weight, new_out_weight, new_in_momentum, new_out_momentum, gradients[0], gradients[2], gradients[3], gradients[4], gradients[5], gradients[6], gradients[7], output_rms, mixer_rms)
```

```python
import functools

import jax
import jax.numpy as jnp
from jax import lax
from jax.experimental import pallas as pl
from jax.experimental.pallas import tpu as pltpu
from jax.sharding import PartitionSpec as P

epsilon = 1e-05
highest = lax.Precision.HIGHEST


def shifted(block, axis, distance):
    devices = range(lax.axis_size(axis))
    route = [(i - distance, i) for i in devices if i - distance in devices]
    return lax.ppermute(block, axis, route)


def entering(value, axis, join, neutral):
    place = lax.axis_index(axis)
    gathered = jax.tree.map(
        lambda a, kind: lax.all_gather(a.astype(kind), axis), value, (jnp.bfloat16, jnp.bfloat16)
    )
    state = jax.tree.map(lambda a, e: jnp.zeros_like(a) + jnp.asarray(e, a.dtype), value, neutral)

    def one(step, state):
        return join(
            state,
            jax.tree.map(
                lambda a, own: lax.dynamic_index_in_dim(a, step, 0, False).astype(own.dtype),
                gathered,
                value,
            ),
        )

    return lax.fori_loop(0, place, one, state)


def carried_in(value, axis, combine, identity):
    length, mine = (lax.axis_size(axis), lax.axis_index(axis))
    everything = jax.tree.map(lambda part: lax.all_gather(part, axis), value)
    start = jax.tree.map(
        lambda part, zero: jnp.broadcast_to(jnp.asarray(zero, part.dtype), part.shape),
        value,
        identity,
    )

    def step(k, before):
        at = length - 1 - k
        reached = at > mine
        new = combine(before, jax.tree.map(lambda part: part[at], everything))
        return jax.tree.map(lambda a, b: jnp.where(reached, a, b), new, before)

    return lax.fori_loop(0, length, step, start)


def pre_norm(values, gain_values):
    return (
        values
        * lax.rsqrt(jnp.mean(values * values, axis=-1, keepdims=True) + epsilon)
        * gain_values
    )


def compose(earlier, later):
    return (earlier[0] * later[0], later[0][:, :, None, None] * earlier[1] + later[1])


LANES = 128


def exchange_kernel(
    bits,
    pieces,
    flows,
    rate_ref,
    grad_ref,
    weight_ref,
    momentum_ref,
    small_ref,
    gathered_ref,
    small_out_ref,
    *scratch,
):
    halves = scratch[:bits]
    (piece_parts, small_acc, small_in, small_parts) = scratch[bits : bits + 4]
    (rs_send, rs_recv, zs_send, zs_recv, zg_send, zg_recv, ag_send, ag_recv) = scratch[
        bits + 4 : bits + 12
    ]
    (sm_send, sm_recv, sz_send, sz_recv) = scratch[bits + 12 :]
    place = lax.axis_index("dp")
    turn = lax.axis_index("seq")
    own = [(place // (1 << b)) % 2 for b in range(bits)]
    partner = [{"dp": place + (1 - 2 * own[b]) * (1 << b)} for b in range(bits)]
    others = [{"seq": (turn + j) % pieces} for j in range(pieces)]

    def order_of(f):
        rest = list(range(1, bits))
        shift = f % max(len(rest), 1)
        return ([0] if bits else []) + rest[shift:] + rest[:shift]

    def index_of(fixed):
        return tuple(fixed.get(b, slice(None)) for b in range(bits - 1, -1, -1))

    barrier = pltpu.get_barrier_semaphore()
    for target in partner + others[1:]:
        pl.semaphore_signal(
            barrier, inc=1, device_id=target, device_id_type=pl.DeviceIdType.MESH
        )
    pl.semaphore_wait(barrier, bits + pieces - 1)

    def remote(src, dst, send, recv, target):
        return pltpu.make_async_remote_copy(
            src_ref=src,
            dst_ref=dst,
            send_sem=send,
            recv_sem=recv,
            device_id=target,
            device_id_type=pl.DeviceIdType.MESH,
        )

    def held(f, k, other):
        order = order_of(f)
        bit = order[k]
        value = 1 - own[bit] if other else own[bit]
        if k == 0:
            return grad_ref.at[(f,) + index_of({bit: value})]
        free = [b for b in range(bits - 1, -1, -1) if b not in order[:k]]
        return halves[k - 1].at[
            (f,) + tuple(value if b == bit else slice(None) for b in free)
        ]

    def rs_copy(f, k):
        return remote(
            held(f, k, True),
            halves[k].at[f],
            rs_send.at[f, k],
            rs_recv.at[f, k],
            partner[order_of(f)[k]],
        )

    def rs_add(f, k):
        kept = held(f, k, False)
        into = halves[k].at[f]
        left = bits - k - 1
        for count in range(1 << left):
            spot = tuple((count >> (left - 1 - i)) & 1 for i in range(left))

            def body(p, carry):
                into[spot + (p,)] = (
                    kept[spot + (p,)].astype(jnp.float32)
                    + into[spot + (p,)].astype(jnp.float32)
                ).astype(jnp.bfloat16)
                return carry

            lax.fori_loop(0, pieces, body, 0)

    mine = index_of({b: own[b] for b in range(bits)})

    def zs_copy(f, j):
        return remote(
            halves[bits - 1].at[f, lax.rem(turn + j, pieces)],
            piece_parts.at[f, j],
            zs_send.at[f, j],
            zs_recv.at[f, j],
            others[j],
        )

    def zg_copy(f, j):
        spot = gathered_ref.at[(f,) + mine + (turn,)]
        return remote(spot, spot, zg_send.at[f, j], zg_recv.at[f, j], others[j])

    def ag_copy(f, k):
        order = order_of(f)
        fixed = {order[i]: own[order[i]] for i in range(k + 1)}
        spot = gathered_ref.at[(f,) + index_of(fixed)]
        return remote(spot, spot, ag_send.at[f, k], ag_recv.at[f, k], partner[order[k]])

    def sm_copy(k):
        return remote(small_acc.at[k], small_in.at[k], sm_send.at[k], sm_recv.at[k], partner[k])

    def sz_copy(j):
        return remote(
            small_acc.at[bits], small_parts.at[turn], sz_send.at[j], sz_recv.at[j], others[j]
        )

    def begin(f, k):
        if k < bits:
            rs_copy(f, k).start()
        else:
            for j in range(1, pieces):
                zs_copy(f, j).start()

    def begin_back(f, k):
        if k >= 0:
            ag_copy(f, k).start()

    small_acc[0] = small_ref[...]
    if bits:
        sm_copy(0).start()
    for f in range(flows):
        begin(f, 0)
    for k in range(bits):
        sm_copy(k).wait_recv()
        small_acc[k + 1] = small_acc[k] + small_in[k]
        if k + 1 < bits:
            sm_copy(k + 1).start()
        else:
            for j in range(1, pieces):
                sz_copy(j).start()
        for f in range(flows):
            rs_copy(f, k).wait_recv()
            rs_add(f, k)
            begin(f, k + 1)
    small_parts[turn] = small_acc[bits]
    rate = rate_ref[0]
    for f in range(flows):
        for j in range(1, pieces):
            zs_copy(f, j).wait_recv()
        total = halves[bits - 1][f, turn].astype(jnp.float32)
        for j in range(1, pieces):
            total = total + piece_parts[f, j].astype(jnp.float32)
        summed = total.astype(jnp.bfloat16)
        gathered_ref[(f,) + mine + (pieces,)] = summed
        moved = 0.5 * momentum_ref[f] + summed.astype(jnp.float32)
        gathered_ref[(f,) + mine + (turn,)] = (
            weight_ref[f].astype(jnp.float32) - rate * moved
        ).astype(jnp.bfloat16)
        for j in range(1, pieces):
            zg_copy(f, j).start()
    for j in range(1, pieces):
        sz_copy(j).wait_recv()
    whole = small_parts[0]
    for j in range(1, pieces):
        whole = whole + small_parts[j]
    small_out_ref[...] = whole
    for f in range(flows):
        for j in range(1, pieces):
            zg_copy(f, j).wait_recv()
        begin_back(f, bits - 1)
    for k in range(bits - 1, -1, -1):
        for f in range(flows):
            ag_copy(f, k).wait_recv()
            begin_back(f, k - 1)
    for k in range(bits):
        sm_copy(k).wait_send()
        for f in range(flows):
            rs_copy(f, k).wait_send()
            ag_copy(f, k).wait_send()
    for j in range(1, pieces):
        sz_copy(j).wait_send()
        for f in range(flows):
            zs_copy(f, j).wait_send()
            zg_copy(f, j).wait_send()


def exchange(rate, grads, weights, momenta, small):
    flows, places, pieces, rows, _ = grads.shape
    bits = places.bit_length() - 1
    assert places == 1 << bits and bits >= 1 and pieces >= 2
    twos = (2,) * bits
    grads = grads.reshape((flows,) + twos + (pieces, rows, LANES))
    small_rows = small.shape[0]
    vmem = pl.BlockSpec(memory_space=pltpu.VMEM)
    dma = pltpu.SemaphoreType.DMA
    gathered, small_out = pl.pallas_call(
        functools.partial(exchange_kernel, bits, pieces, flows),
        out_shape=(
            jax.ShapeDtypeStruct((flows,) + twos + (pieces + 1, rows, LANES), jnp.bfloat16),
            jax.ShapeDtypeStruct((small_rows, LANES), jnp.float32),
        ),
        in_specs=[pl.BlockSpec(memory_space=pltpu.SMEM)] + [vmem] * 4,
        out_specs=(vmem, vmem),
        scratch_shapes=[
            pltpu.VMEM((flows,) + twos[k + 1 :] + (pieces, rows, LANES), jnp.bfloat16)
            for k in range(bits)
        ]
        + [
            pltpu.VMEM((flows, pieces, rows, LANES), jnp.bfloat16),
            pltpu.VMEM((bits + 1, small_rows, LANES), jnp.float32),
            pltpu.VMEM((bits, small_rows, LANES), jnp.float32),
            pltpu.VMEM((pieces, small_rows, LANES), jnp.float32),
        ]
        + [dma((flows, bits))] * 2
        + [dma((flows, pieces))] * 4
        + [dma((flows, bits))] * 2
        + [dma((bits,))] * 2
        + [dma((pieces,))] * 2,
        compiler_params=pltpu.CompilerParams(
            collective_id=0, has_side_effects=True, vmem_limit_bytes=56 * 1024 * 1024
        ),
        name="exchange",
    )(rate, grads, weights, momenta, small)
    return gathered.reshape(flows, places, pieces + 1, rows, LANES), small_out


def local(
    tokens,
    cotangent,
    segment_ids,
    doc_starts,
    valid_mask,
    step_number,
    learn_rate,
    norm_gain,
    in_weight,
    conv_weight,
    conv_bias,
    dt_bias,
    a_log,
    skip_d,
    gate_gain,
    out_weight,
    in_momentum,
    out_momentum,
):
    seq_count, piece_size, model_width = tokens.shape
    head_count = dt_bias.shape[0]
    tap_count, channels = conv_weight.shape
    inner_width = gate_gain.shape[0]
    state_width = (channels - inner_width) // 2
    head_width = inner_width // head_count
    proj_width = in_weight.shape[1]
    row_count = seq_count * piece_size
    inputs = tokens.astype(jnp.float32)
    normed_in, back_pre = jax.vjp(pre_norm, inputs, norm_gain)
    normed_low = normed_in.astype(jnp.bfloat16).reshape(row_count, model_width)
    projected = jnp.dot(normed_low, in_weight, preferred_element_type=jnp.float32).reshape(
        seq_count, piece_size, proj_width
    )
    gate_in = projected[:, :, :inner_width]
    conv_in = projected[:, :, inner_width : inner_width + channels]
    dt_raw = projected[:, :, inner_width + channels :]
    seg_float = segment_ids.astype(jnp.float32)
    prev_rows, prev_seg = shifted(
        (conv_in[:, piece_size - tap_count + 1 :], seg_float[:, piece_size - tap_count + 1 :]),
        "seq",
        1,
    )
    padded = jnp.concatenate([prev_rows, conv_in], axis=1)
    seg_pad = jnp.concatenate([prev_seg, seg_float], axis=1)
    masks = [
        (seg_pad[:, k : k + piece_size] == seg_float).astype(jnp.float32)[:, :, None]
        for k in range(tap_count)
    ]

    def conv_part(padded_in, taps_in, bias_in, raw_in, dt_bias_in, a_log_in):
        summed = bias_in + jnp.zeros((seq_count, piece_size, channels), jnp.float32)
        for k in range(tap_count):
            summed = summed + padded_in[:, k : k + piece_size] * masks[k] * taps_in[k]
        activated = jax.nn.silu(summed)
        signal = activated[:, :, :inner_width].reshape(
            seq_count, piece_size, head_count, head_width
        )
        writer = activated[:, :, inner_width : inner_width + state_width]
        reader = activated[:, :, inner_width + state_width :]
        step_size = jax.nn.softplus(raw_in + dt_bias_in)
        return (signal, writer, reader, step_size, -jnp.exp(a_log_in) * step_size)

    (signal, writer, reader, step_size, log_decay), back_conv = jax.vjp(
        conv_part, padded, conv_weight, conv_bias, dt_raw, dt_bias, a_log
    )
    counter = jnp.cumsum(doc_starts, axis=1)
    positions = jnp.arange(piece_size)
    causal = positions[:, None] >= positions[None, :]
    same_doc = (counter[:, :, None] == counter[:, None, :]) & causal[None]
    first_doc = (counter == 0)[:, :, None]
    last_doc = (counter == counter[:, -1:])[:, :, None]
    untouched = (counter[:, -1] == 0)[:, None]

    def end_state(signal_in, writer_in, step_in, decay_in):
        cumulative = jnp.cumsum(decay_in, axis=1)
        final_log = cumulative[:, -1]
        keeping = jnp.where(untouched, jnp.exp(final_log), 0.0)
        tails = jnp.where(last_doc, jnp.exp(final_log[:, None] - cumulative), 0.0) * step_in
        fresh_state = jnp.einsum(
            "slh,slhp,sln->shpn", tails, signal_in, writer_in, precision=highest
        )
        return (keeping, fresh_state)

    def piece_out(signal_in, writer_in, reader_in, step_in, decay_in, incoming_in):
        cumulative = jnp.cumsum(decay_in, axis=1)
        by_head = jnp.transpose(cumulative, (0, 2, 1))
        gaps = by_head[:, :, :, None] - by_head[:, :, None, :]
        decays = jnp.exp(jnp.where(same_doc[:, None], gaps, -1e30))
        scores = jnp.einsum("stn,sun->stu", reader_in, writer_in, precision=highest)
        weighted = scores[:, None] * decays
        inner_part = jnp.einsum(
            "shtu,suhp->sthp", weighted, signal_in * step_in[..., None], precision=highest
        )
        entries = jnp.where(first_doc, jnp.exp(cumulative), 0.0)
        carried = (
            jnp.einsum("stn,shpn->sthp", reader_in, incoming_in, precision=highest)
            * entries[..., None]
        )
        return inner_part + carried

    (keeping, fresh_state), back_end = jax.vjp(end_state, signal, writer, step_size, log_decay)
    identity = (jnp.ones_like(keeping), jnp.zeros_like(fresh_state))
    _, incoming = entering((keeping, fresh_state), "seq", compose, identity)
    ssm_out, back_out = jax.vjp(piece_out, signal, writer, reader, step_size, log_decay, incoming)

    def gate_norm(ssm_in, signal_in, skip_in, gate_values, gain_values):
        mixer_in = (ssm_in + skip_in[:, None] * signal_in).reshape(
            seq_count, piece_size, inner_width
        )
        gated_out = mixer_in * jax.nn.silu(gate_values)
        return (
            gated_out
            * lax.rsqrt(jnp.mean(gated_out * gated_out, axis=-1, keepdims=True) + epsilon)
            * gain_values
        )

    gate_normed, back_gate = jax.vjp(gate_norm, ssm_out, signal, skip_d, gate_in, gate_gain)
    gate_low = gate_normed.astype(jnp.bfloat16).reshape(row_count, inner_width)
    mixed = jnp.dot(gate_low, out_weight, preferred_element_type=jnp.float32).reshape(
        seq_count, piece_size, model_width
    )
    block_out = inputs + mixed
    valid_float = valid_mask.astype(jnp.float32)
    out_square = jnp.sum(valid_float * jnp.sum(block_out * block_out, axis=-1))
    mix_square = jnp.sum(valid_float * jnp.sum(mixed * mixed, axis=-1))
    valid_count = jnp.sum(valid_float)
    out_grad = cotangent.astype(jnp.float32) * valid_float[:, :, None]
    out_low = out_grad.astype(jnp.bfloat16).reshape(row_count, model_width)
    gate_grad = lax.dot_general(
        out_low, out_weight, (((1,), (1,)), ((), ())), preferred_element_type=jnp.float32
    ).reshape(seq_count, piece_size, inner_width)
    ssm_grad, signal_grad_gate, skip_grad, gate_in_grad, gate_gain_grad = back_gate(gate_grad)
    signal_grad_out, writer_grad_out, reader_grad, step_grad_out, decay_grad_out, state_grad = (
        back_out(ssm_grad)
    )
    _, later_grad = carried_in((keeping, state_grad), "seq", compose, identity)
    keeping_grad = jnp.sum(later_grad * incoming, axis=(2, 3))
    signal_grad_end, writer_grad_end, step_grad_end, decay_grad_end = back_end(
        (keeping_grad, later_grad)
    )
    padded_grad, conv_weight_grad, conv_bias_grad, dt_raw_grad, dt_bias_grad, a_log_grad = (
        back_conv(
            (
                signal_grad_gate + signal_grad_out + signal_grad_end,
                writer_grad_out + writer_grad_end,
                reader_grad,
                step_grad_out + step_grad_end,
                decay_grad_out + decay_grad_end,
            )
        )
    )
    rim_grad = shifted(padded_grad[:, : tap_count - 1].astype(jnp.bfloat16), "seq", -1).astype(
        jnp.float32
    )
    conv_in_grad = padded_grad[:, tap_count - 1 :] + jnp.pad(
        rim_grad, ((0, 0), (piece_size - tap_count + 1, 0), (0, 0))
    )
    proj_grad = (
        jnp.concatenate([gate_in_grad, conv_in_grad, dt_raw_grad], axis=2)
        .astype(jnp.bfloat16)
        .reshape(row_count, proj_width)
    )
    normed_grad = lax.dot_general(
        proj_grad, in_weight, (((1,), (1,)), ((), ())), preferred_element_type=jnp.float32
    ).reshape(seq_count, piece_size, model_width)
    input_grad_pre, norm_gain_grad = back_pre(normed_grad)
    input_grad = (out_grad + input_grad_pre).astype(jnp.bfloat16)
    share_rows = model_width // lax.axis_size("seq")
    in_part = lax.dot_general(
        normed_low, proj_grad, (((0,), (0,)), ((), ())), preferred_element_type=jnp.float32
    )
    out_part = lax.dot_general(
        out_low, gate_low, (((0,), (0,)), ((), ())), preferred_element_type=jnp.float32
    )
    places, pieces = lax.axis_size("dp"), lax.axis_size("seq")
    width = inner_width + proj_width
    flows = -(-width // (LANES * places))
    full = flows * places * LANES

    def tiled(block):
        spread = jnp.pad(block, ((0, 0), (0, full - width)))
        return spread.reshape(-1, flows * places, LANES)

    whole_grad = jnp.concatenate([out_part, in_part], axis=1).astype(jnp.bfloat16)
    grads = (
        tiled(whole_grad)
        .reshape(pieces, share_rows, flows, places, LANES)
        .transpose(2, 3, 0, 1, 4)
    )
    step_float = step_number[0].astype(jnp.float32)
    rate_now = learn_rate[0] * step_float / (step_float + 16.0)
    first_row = lax.axis_index("seq") * share_rows
    own_in = lax.dynamic_slice_in_dim(in_weight, first_row, share_rows, 0)
    own_out = lax.dynamic_slice_in_dim(out_weight, first_row, share_rows, 1)
    place = lax.axis_index("dp")

    def own_piece(out_rows, in_rows):
        block = tiled(jnp.concatenate([jnp.transpose(out_rows), in_rows], axis=1))
        block = block.reshape(share_rows, flows, places, LANES)
        return jnp.transpose(lax.dynamic_index_in_dim(block, place, 2, False), (1, 0, 2))

    parts = (
        norm_gain_grad,
        conv_weight_grad,
        conv_bias_grad,
        dt_bias_grad,
        a_log_grad,
        skip_grad,
        gate_gain_grad,
        out_square,
        mix_square,
        valid_count,
    )
    flat = jnp.concatenate([p.reshape(-1) for p in parts])
    small_rows = -(-flat.shape[0] // (8 * LANES)) * 8
    small = jnp.pad(flat, (0, small_rows * LANES - flat.shape[0])).reshape(small_rows, LANES)
    gathered, small_total = exchange(
        rate_now.reshape(1), grads, own_piece(own_out, own_in), own_piece(out_momentum, in_momentum), small
    )

    def untiled(block):
        return block.reshape(-1, full)[:, :width]

    summed = untiled(
        gathered[:, :, pieces].reshape(flows * places, share_rows, LANES).transpose(1, 0, 2)
    ).astype(jnp.float32)
    new_in_momentum = 0.5 * in_momentum + summed[:, inner_width:]
    new_out_momentum = 0.5 * out_momentum + jnp.transpose(summed[:, :inner_width])
    new_weights = untiled(
        gathered[:, :, :pieces]
        .reshape(flows * places, pieces, share_rows, LANES)
        .transpose(1, 2, 0, 3)
    )
    new_in_weight = new_weights[:, inner_width:]
    new_out_weight = jnp.transpose(new_weights[:, :inner_width])
    flat_total = small_total.reshape(-1)
    totals = []
    at = 0
    for p in parts:
        totals.append(flat_total[at : at + p.size].reshape(p.shape))
        at += p.size
    (
        norm_gain_total,
        conv_weight_total,
        conv_bias_total,
        dt_bias_total,
        a_log_total,
        skip_total,
        gate_gain_total,
        out_square_total,
        mix_square_total,
        valid_total,
    ) = totals
    denominator = jnp.maximum(valid_total, 1.0) * model_width
    output_rms = jnp.sqrt(out_square_total / denominator).reshape(1)
    mixer_rms = jnp.sqrt(mix_square_total / denominator).reshape(1)
    return (
        block_out.astype(jnp.bfloat16),
        input_grad,
        new_in_weight,
        new_out_weight,
        new_in_momentum,
        new_out_momentum,
        norm_gain_total,
        conv_weight_total,
        conv_bias_total,
        dt_bias_total,
        a_log_total,
        skip_total,
        gate_gain_total,
        output_rms,
        mixer_rms,
    )


def solution(mesh):
    placed = (
        P("dp", "seq", None),
        P("dp", "seq", None),
        P("dp", "seq"),
        P("dp", "seq"),
        P("dp", "seq"),
        P(),
        P(),
        P(),
        P(),
        P(),
        P(),
        P(),
        P(),
        P(),
        P(),
        P(),
        P("seq", None),
        P(None, "seq"),
    )
    return jax.shard_map(
        local,
        mesh=mesh,
        in_specs=placed,
        out_specs=(
            P("dp", "seq", None),
            P("dp", "seq", None),
            P(),
            P(),
            P("seq", None),
            P(None, "seq"),
            P(),
            P(),
            P(),
            P(),
            P(),
            P(),
            P(),
            P(),
            P(),
        ),
        check_vma=False,
    )
```

```python
import functools

import jax
import jax.numpy as jnp
from jax import lax
from jax.experimental import pallas as pl
from jax.experimental.pallas import tpu as pltpu
from jax.sharding import PartitionSpec as P

LANES = 128


def exchange_kernel(
    bits,
    pieces,
    flows,
    rate_ref,
    grad_ref,
    weight_ref,
    momentum_ref,
    small_ref,
    gathered_ref,
    small_out_ref,
    *scratch,
):
    halves = scratch[:bits]
    (piece_parts, small_acc, small_in, small_parts) = scratch[bits : bits + 4]
    (rs_send, rs_recv, zs_send, zs_recv, zg_send, zg_recv, ag_send, ag_recv) = scratch[
        bits + 4 : bits + 12
    ]
    (sm_send, sm_recv, sz_send, sz_recv) = scratch[bits + 12 :]
    place = lax.axis_index("dp")
    turn = lax.axis_index("seq")
    own = [(place // (1 << b)) % 2 for b in range(bits)]
    partner = [{"dp": place + (1 - 2 * own[b]) * (1 << b)} for b in range(bits)]
    others = [{"seq": (turn + j) % pieces} for j in range(pieces)]

    def order_of(f):
        rest = list(range(1, bits))
        shift = f % max(len(rest), 1)
        return ([0] if bits else []) + rest[shift:] + rest[:shift]

    def index_of(fixed):
        return tuple(fixed.get(b, slice(None)) for b in range(bits - 1, -1, -1))

    barrier = pltpu.get_barrier_semaphore()
    for target in partner + others[1:]:
        pl.semaphore_signal(
            barrier, inc=1, device_id=target, device_id_type=pl.DeviceIdType.MESH
        )
    pl.semaphore_wait(barrier, bits + pieces - 1)

    def remote(src, dst, send, recv, target):
        return pltpu.make_async_remote_copy(
            src_ref=src,
            dst_ref=dst,
            send_sem=send,
            recv_sem=recv,
            device_id=target,
            device_id_type=pl.DeviceIdType.MESH,
        )

    def held(f, k, other):
        order = order_of(f)
        bit = order[k]
        value = 1 - own[bit] if other else own[bit]
        if k == 0:
            return grad_ref.at[(f,) + index_of({bit: value})]
        free = [b for b in range(bits - 1, -1, -1) if b not in order[:k]]
        return halves[k - 1].at[
            (f,) + tuple(value if b == bit else slice(None) for b in free)
        ]

    def rs_copy(f, k):
        return remote(
            held(f, k, True),
            halves[k].at[f],
            rs_send.at[f, k],
            rs_recv.at[f, k],
            partner[order_of(f)[k]],
        )

    def rs_add(f, k):
        kept = held(f, k, False)
        into = halves[k].at[f]
        left = bits - k - 1
        for count in range(1 << left):
            spot = tuple((count >> (left - 1 - i)) & 1 for i in range(left))

            def body(p, carry):
                into[spot + (p,)] = (
                    kept[spot + (p,)].astype(jnp.float32)
                    + into[spot + (p,)].astype(jnp.float32)
                ).astype(jnp.bfloat16)
                return carry

            lax.fori_loop(0, pieces, body, 0)

    mine = index_of({b: own[b] for b in range(bits)})

    def zs_copy(f, j):
        return remote(
            halves[bits - 1].at[f, lax.rem(turn + j, pieces)],
            piece_parts.at[f, j],
            zs_send.at[f, j],
            zs_recv.at[f, j],
            others[j],
        )

    def zg_copy(f, j):
        spot = gathered_ref.at[(f,) + mine + (turn,)]
        return remote(spot, spot, zg_send.at[f, j], zg_recv.at[f, j], others[j])

    def ag_copy(f, k):
        order = order_of(f)
        fixed = {order[i]: own[order[i]] for i in range(k + 1)}
        spot = gathered_ref.at[(f,) + index_of(fixed)]
        return remote(spot, spot, ag_send.at[f, k], ag_recv.at[f, k], partner[order[k]])

    def sm_copy(k):
        return remote(small_acc.at[k], small_in.at[k], sm_send.at[k], sm_recv.at[k], partner[k])

    def sz_copy(j):
        return remote(
            small_acc.at[bits], small_parts.at[turn], sz_send.at[j], sz_recv.at[j], others[j]
        )

    def begin(f, k):
        if k < bits:
            rs_copy(f, k).start()
        else:
            for j in range(1, pieces):
                zs_copy(f, j).start()

    def begin_back(f, k):
        if k >= 0:
            ag_copy(f, k).start()

    small_acc[0] = small_ref[...]
    if bits:
        sm_copy(0).start()
    for f in range(flows):
        begin(f, 0)
    for k in range(bits):
        sm_copy(k).wait_recv()
        small_acc[k + 1] = small_acc[k] + small_in[k]
        if k + 1 < bits:
            sm_copy(k + 1).start()
        else:
            for j in range(1, pieces):
                sz_copy(j).start()
        for f in range(flows):
            rs_copy(f, k).wait_recv()
            rs_add(f, k)
            begin(f, k + 1)
    small_parts[turn] = small_acc[bits]
    rate = rate_ref[0]
    for f in range(flows):
        for j in range(1, pieces):
            zs_copy(f, j).wait_recv()
        total = halves[bits - 1][f, turn].astype(jnp.float32)
        for j in range(1, pieces):
            total = total + piece_parts[f, j].astype(jnp.float32)
        summed = total.astype(jnp.bfloat16)
        gathered_ref[(f,) + mine + (pieces,)] = summed
        moved = 0.5 * momentum_ref[f] + summed.astype(jnp.float32)
        gathered_ref[(f,) + mine + (turn,)] = (
            weight_ref[f].astype(jnp.float32) - rate * moved
        ).astype(jnp.bfloat16)
        for j in range(1, pieces):
            zg_copy(f, j).start()
    for j in range(1, pieces):
        sz_copy(j).wait_recv()
    whole = small_parts[0]
    for j in range(1, pieces):
        whole = whole + small_parts[j]
    small_out_ref[...] = whole
    for f in range(flows):
        for j in range(1, pieces):
            zg_copy(f, j).wait_recv()
        begin_back(f, bits - 1)
    for k in range(bits - 1, -1, -1):
        for f in range(flows):
            ag_copy(f, k).wait_recv()
            begin_back(f, k - 1)
    for k in range(bits):
        sm_copy(k).wait_send()
        for f in range(flows):
            rs_copy(f, k).wait_send()
            ag_copy(f, k).wait_send()
    for j in range(1, pieces):
        sz_copy(j).wait_send()
        for f in range(flows):
            zs_copy(f, j).wait_send()
            zg_copy(f, j).wait_send()


def exchange(rate, grads, weights, momenta, small):
    flows, places, pieces, rows, _ = grads.shape
    bits = places.bit_length() - 1
    assert places == 1 << bits and bits >= 1 and pieces >= 2
    twos = (2,) * bits
    grads = grads.reshape((flows,) + twos + (pieces, rows, LANES))
    small_rows = small.shape[0]
    vmem = pl.BlockSpec(memory_space=pltpu.VMEM)
    dma = pltpu.SemaphoreType.DMA
    gathered, small_out = pl.pallas_call(
        functools.partial(exchange_kernel, bits, pieces, flows),
        out_shape=(
            jax.ShapeDtypeStruct((flows,) + twos + (pieces + 1, rows, LANES), jnp.bfloat16),
            jax.ShapeDtypeStruct((small_rows, LANES), jnp.float32),
        ),
        in_specs=[pl.BlockSpec(memory_space=pltpu.SMEM)] + [vmem] * 4,
        out_specs=(vmem, vmem),
        scratch_shapes=[
            pltpu.VMEM((flows,) + twos[k + 1 :] + (pieces, rows, LANES), jnp.bfloat16)
            for k in range(bits)
        ]
        + [
            pltpu.VMEM((flows, pieces, rows, LANES), jnp.bfloat16),
            pltpu.VMEM((bits + 1, small_rows, LANES), jnp.float32),
            pltpu.VMEM((bits, small_rows, LANES), jnp.float32),
            pltpu.VMEM((pieces, small_rows, LANES), jnp.float32),
        ]
        + [dma((flows, bits))] * 2
        + [dma((flows, pieces))] * 4
        + [dma((flows, bits))] * 2
        + [dma((bits,))] * 2
        + [dma((pieces,))] * 2,
        compiler_params=pltpu.CompilerParams(
            collective_id=0, has_side_effects=True, vmem_limit_bytes=56 * 1024 * 1024
        ),
        name="exchange",
    )(rate, grads, weights, momenta, small)
    return gathered.reshape(flows, places, pieces + 1, rows, LANES), small_out


CHUNK = 128
HALO = 16
GATE_BLOCK = 256
EPS = 1e-05
NEGATIVE = -1e30
F32, BF16 = jnp.float32, jnp.bfloat16


def mm(a, b):
    return jnp.dot(a, b, preferred_element_type=F32)


def mm_nt(a, b):
    return lax.dot_general(a, b, (((1,), (1,)), ((), ())), preferred_element_type=F32)


def mm_tn(a, b):
    return lax.dot_general(a, b, (((0,), (0,)), ((), ())), preferred_element_type=F32)


def split(a):
    high = a.astype(BF16)
    return high, (a - high.astype(F32)).astype(BF16)


def exact_mm(a, b):
    return jnp.dot(a, b, preferred_element_type=F32, precision=lax.Precision.HIGHEST)


def spread(a, heads_ref):
    high, low = split(a)
    return mm(high, heads_ref[...]) + mm(low, heads_ref[...])


def gather_heads(a, heads_ref):
    high, low = split(a)
    return mm_nt(high, heads_ref[...]) + mm_nt(low, heads_ref[...])


def sigmoid(v):
    return 1.0 / (1.0 + jnp.exp(-v))


def softplus(v):
    return jnp.maximum(v, 0.0) + jnp.log1p(jnp.exp(-jnp.abs(v)))


def triangle(size, upper):
    row = lax.broadcasted_iota(jnp.int32, (size, size), 0)
    column = lax.broadcasted_iota(jnp.int32, (size, size), 1)
    return ((row <= column) if upper else (row >= column)).astype(F32)


def front_kernel(
    sizes,
    tokens_ref,
    halo_ref,
    gain_ref,
    weight_ref,
    taps_ref,
    bias_ref,
    masks_ref,
    dt_bias_ref,
    a_log_ref,
    heads_ref,
    normed_ref,
    gate_ref,
    conv_ref,
    halo_out_ref,
    summed_ref,
    raw_ref,
    cum_ref,
    state_ref,
    keep_ref,
    padded,
    product,
    active,
):
    seqs, piece, inner, channels, heads = sizes
    gate_blocks, conv_blocks = inner // GATE_BLOCK, channels // GATE_BLOCK
    step = pl.program_id(0)
    stride = piece + HALO

    @pl.when(step == 0)
    def _():
        gain = gain_ref[...]
        for n in range(seqs):
            for source, start, to, count in (
                (halo_ref, n * HALO, n * stride, HALO),
                (tokens_ref, n * piece, n * stride + HALO, piece),
            ):

                def body(i, carry):
                    values = source[pl.ds(pl.multiple_of(start + i * 16, 16), 16)].astype(F32)
                    scale = lax.rsqrt(jnp.mean(values * values, axis=-1, keepdims=True) + EPS)
                    low = (values * scale * gain).astype(BF16)
                    padded[pl.ds(pl.multiple_of(to + i * 16, 16), 16)] = low
                    return carry

                lax.fori_loop(0, count // 16, body, 0)
            normed_ref[pl.ds(n * piece, piece)] = padded[pl.ds(n * stride + HALO, piece)]

    product[...] = mm(padded[...], weight_ref[...])

    @pl.when(step < gate_blocks)
    def _():
        for n in range(seqs):
            gate_ref[pl.ds(n * piece, piece)] = product[pl.ds(n * stride + HALO, piece)]

    @pl.when((step >= gate_blocks) & (step < gate_blocks + conv_blocks))
    def _():
        at = pl.multiple_of((step - gate_blocks) * GATE_BLOCK, GATE_BLOCK)
        for n in range(seqs):
            conv_ref[pl.ds(n * piece, piece)] = product[pl.ds(n * stride + HALO, piece)]
            halo_out_ref[pl.ds(n * HALO, HALO)] = product[pl.ds(n * stride, HALO)]
            for i in range(piece // 64):
                rows = pl.ds(n * piece + i * 64, 64)
                total = jnp.broadcast_to(bias_ref[...], (64, GATE_BLOCK))
                for k in range(4):
                    source = product[pl.ds(n * stride + HALO - 3 + k + i * 64, 64)]
                    total = total + source * masks_ref[rows, k : k + 1] * taps_ref[k : k + 1]
                summed_ref[rows] = total
                active[rows, pl.ds(at, GATE_BLOCK)] = (total * sigmoid(total)).astype(BF16)

    @pl.when(step == gate_blocks + conv_blocks)
    def _():
        lane = lax.broadcasted_iota(jnp.int32, (piece, 128), 1)
        lower = triangle(CHUNK, False)
        for n in range(seqs):
            rows = pl.ds(n * piece, piece)
            raw = jnp.where(lane < heads, product[pl.ds(n * stride + HALO, piece), :128], 0.0)
            raw = raw + dt_bias_ref[...]
            raw_ref[rows] = raw
            steps = jnp.where(lane < heads, softplus(raw), 0.0)
            decay = -jnp.exp(a_log_ref[...]) * steps
            total = jnp.zeros((1, 128), F32)
            pieces = []
            for c in range(piece // CHUNK):
                cumulative = exact_mm(lower, decay[c * CHUNK : (c + 1) * CHUNK])
                cum_ref[pl.ds(n * piece + c * CHUNK, CHUNK)] = cumulative
                pieces.append(cumulative + total)
                total = total + cumulative[CHUNK - 1 :]
            whole = jnp.concatenate(pieces, axis=0) if len(pieces) > 1 else pieces[0]
            tails = jnp.exp(total - whole) * steps * masks_ref[rows, 7:8]
            weighted = (spread(tails, heads_ref) * active[rows, :inner].astype(F32)).astype(BF16)
            state_ref[n] = mm_tn(active[rows, inner : inner + 128], weighted)
            last = masks_ref[n * piece + piece - 1 : n * piece + piece, 6:7]
            keep = jnp.exp(total) * last
            keep_ref[n] = spread(jnp.broadcast_to(keep, (8, 128)), heads_ref)


def front(tokens, halo, gain, weight, taps, bias, masks, dt_bias, a_log, heads_map, sizes):
    seqs, piece, inner, channels, heads = sizes
    total, model = tokens.shape
    stride = seqs * (piece + HALO)
    gate_blocks, conv_blocks = inner // GATE_BLOCK, channels // GATE_BLOCK
    full = lambda *shape: pl.BlockSpec(shape, lambda j: (0,) * len(shape))

    def conv_at(j):
        return (0, jnp.clip(j - gate_blocks, 0, conv_blocks - 1))

    return pl.pallas_call(
        functools.partial(front_kernel, sizes),
        grid=(gate_blocks + conv_blocks + 1,),
        in_specs=[
            full(total, model),
            full(seqs * HALO, model),
            full(1, model),
            pl.BlockSpec((model, GATE_BLOCK), lambda j: (0, j)),
            pl.BlockSpec((4, GATE_BLOCK), conv_at),
            pl.BlockSpec((1, GATE_BLOCK), conv_at),
            full(total, 16),
            full(1, 128),
            full(1, 128),
            full(128, inner),
        ],
        out_specs=(
            full(total, model),
            pl.BlockSpec((total, GATE_BLOCK), lambda j: (0, jnp.minimum(j, gate_blocks - 1))),
            pl.BlockSpec((total, GATE_BLOCK), conv_at),
            pl.BlockSpec((seqs * HALO, GATE_BLOCK), conv_at),
            pl.BlockSpec((total, GATE_BLOCK), conv_at),
            full(total, 128),
            full(total, 128),
            full(seqs, 128, inner),
            full(seqs, 8, inner),
        ),
        out_shape=(
            jax.ShapeDtypeStruct((total, model), BF16),
            jax.ShapeDtypeStruct((total, inner), F32),
            jax.ShapeDtypeStruct((total, channels), F32),
            jax.ShapeDtypeStruct((seqs * HALO, channels), F32),
            jax.ShapeDtypeStruct((total, channels), F32),
            jax.ShapeDtypeStruct((total, 128), F32),
            jax.ShapeDtypeStruct((total, 128), F32),
            jax.ShapeDtypeStruct((seqs, 128, inner), F32),
            jax.ShapeDtypeStruct((seqs, 8, inner), F32),
        ),
        scratch_shapes=[
            pltpu.VMEM((stride, model), BF16),
            pltpu.VMEM((stride, GATE_BLOCK), F32),
            pltpu.VMEM((total, channels), BF16),
        ],
        compiler_params=pltpu.CompilerParams(vmem_limit_bytes=48 * 1024 * 1024),
        name="front",
    )(tokens, halo, gain, weight, taps, bias, masks, dt_bias, a_log, heads_map)


def chain_kernel(ways, blocks, own_ref, keep_ref, out_ref, sent, taken, send, recv):
    size = lax.axis_size("seq")
    turn = lax.axis_index("seq")
    first = turn == (0 if ways > 0 else size - 1)
    final = turn == (size - 1 if ways > 0 else 0)
    ahead = {"seq": lax.rem(turn + ways + size, size)}
    behind = {"seq": lax.rem(turn - ways + size, size)}
    barrier = pltpu.get_barrier_semaphore()

    @pl.when(jnp.logical_not(first))
    def _():
        pl.semaphore_signal(
            barrier, inc=1, device_id=behind, device_id_type=pl.DeviceIdType.MESH
        )

    @pl.when(jnp.logical_not(final))
    def _():
        pl.semaphore_wait(barrier, 1)

    width = own_ref.shape[2] // blocks

    def copy(c):
        return pltpu.make_async_remote_copy(
            src_ref=sent.at[c],
            dst_ref=taken.at[c],
            send_sem=send.at[c],
            recv_sem=recv.at[c],
            device_id=ahead,
            device_id_type=pl.DeviceIdType.MESH,
        )

    @pl.when(first)
    def _():
        out_ref[...] = jnp.zeros_like(out_ref)
        for c in range(blocks):
            at = slice(c * width, (c + 1) * width)
            sent[c] = own_ref[:, :, at].astype(BF16)
            copy(c).start()

    @pl.when(jnp.logical_not(first))
    def _():
        for c in range(blocks):
            at = slice(c * width, (c + 1) * width)
            copy(c).wait_recv()

            @pl.when(jnp.logical_not(final))
            def _():
                sent[c] = (
                    own_ref[:, :, at] + keep_ref[:, 0:1, at] * taken[c].astype(F32)
                ).astype(BF16)
                copy(c).start()

            out_ref[:, :, at] = taken[c].astype(F32)

    @pl.when(jnp.logical_not(final))
    def _():
        for c in range(blocks):
            copy(c).wait_send()


def chain(own, keep, ways, blocks=6):
    seqs, depth, inner = own.shape
    vmem = pl.BlockSpec(memory_space=pltpu.VMEM)
    part = (blocks, seqs, depth, inner // blocks)
    return pl.pallas_call(
        functools.partial(chain_kernel, ways, blocks),
        out_shape=jax.ShapeDtypeStruct(own.shape, F32),
        in_specs=[vmem, vmem],
        out_specs=vmem,
        scratch_shapes=[pltpu.VMEM(part, BF16)] * 2 + [pltpu.SemaphoreType.DMA((blocks,))] * 2,
        compiler_params=pltpu.CompilerParams(
            collective_id=1 if ways > 0 else 2,
            has_side_effects=True,
            vmem_limit_bytes=32 * 1024 * 1024,
        ),
        name="chain",
    )(own, keep)


def decays_of(cum, cum_t, bias, h):
    return jnp.exp(cum[:, h : h + 1] - cum_t[h : h + 1, :] + bias)


def mask_bias(seg_col, seg_row):
    row = lax.broadcasted_iota(jnp.int32, (CHUNK, CHUNK), 0)
    column = lax.broadcasted_iota(jnp.int32, (CHUNK, CHUNK), 1)
    return jnp.where((row >= column) & (seg_col == seg_row), 0.0, NEGATIVE)


def scores_of(reader, writer):
    rh, rl = split(reader)
    wh, wl = split(writer)
    return mm_nt(rh, wh) + (mm_nt(rh, wl) + mm_nt(rl, wh))


def forward_kernel(
    sizes,
    chunks,
    summed_ref,
    gate_ref,
    raw_ref,
    cum_ref,
    masks_ref,
    seg_row_ref,
    incoming_ref,
    tokens_ref,
    cot_ref,
    weight_ref,
    gain_ref,
    skip_ref,
    heads_ref,
    output_ref,
    low_ref,
    out_low_ref,
    gate_grad_ref,
    ssm_grad_ref,
    starts_ref,
    dot_ref,
    sums_ref,
    wide_ref,
    state_grad_ref,
    state,
    prefix,
    active,
    mixed_in,
    factors,
    grads,
    inv,
):
    seqs, piece, inner, channels, heads = sizes
    c = pl.program_id(1)

    @pl.when((c == 0) & (pl.program_id(0) == 0))
    def _():
        sums_ref[...] = jnp.zeros_like(sums_ref)
        wide_ref[...] = jnp.zeros_like(wide_ref)

    @pl.when(c == 0)
    def _():
        state[...] = incoming_ref[0]
        prefix[...] = jnp.zeros_like(prefix)
        state_grad_ref[...] = jnp.zeros_like(state_grad_ref)

    def activate(i, carry):
        rows = pl.ds(pl.multiple_of(i * 16, 16), 16)
        values = summed_ref[rows]
        active[rows] = values * sigmoid(values)
        return carry

    lax.fori_loop(0, CHUNK // 16, activate, 0)
    lane = lax.broadcasted_iota(jnp.int32, (CHUNK, 128), 1)
    steps = jnp.where(lane < heads, softplus(raw_ref[...]), 0.0)
    cum = cum_ref[...]
    cum_t = jnp.transpose(cum)
    final = cum[CHUNK - 1 :]
    enter = jnp.exp(cum) * masks_ref[:, 4:5]
    tails = jnp.exp(final - cum) * steps * masks_ref[:, 5:6]
    from_start = jnp.exp(cum + prefix[0:1]) * masks_ref[:, 6:7]
    prefix[...] = prefix[...] + final
    for i, block in enumerate((steps, enter, tails, from_start)):
        factors[i] = spread(block, heads_ref)
    writer = active[:, inner : inner + 128]
    reader = active[:, inner + 128 : inner + 256]
    scores = scores_of(reader, writer)
    bias = mask_bias(masks_ref[:, 8:9], seg_row_ref[0:1])
    half = lax.broadcasted_iota(jnp.int32, (CHUNK, 128), 1) < 64
    state_low = state[...].astype(BF16)
    starts_ref[0] = state_low
    reader_low = reader.astype(BF16)
    for pair in range(heads // 2):
        at = slice(pair * 128, (pair + 1) * 128)
        moved = (active[:, at] * factors[0, :, at]).astype(BF16)
        zero = jnp.zeros_like(moved)
        one = (scores * decays_of(cum, cum_t, bias, 2 * pair)).astype(BF16)
        two = (scores * decays_of(cum, cum_t, bias, 2 * pair + 1)).astype(BF16)
        both = jnp.concatenate([one, two], axis=1)
        stacked = jnp.concatenate(
            [jnp.where(half, moved, zero), jnp.where(half, zero, moved)], axis=0
        )
        carried = mm(reader_low, state_low[:, at]) * factors[1, :, at]
        mixed_in[:, at] = mm(both, stacked) + carried
    weighted = (active[:, :inner] * factors[2]).astype(BF16)
    kept = jnp.exp(final) * masks_ref[CHUNK - 1 :, 4:5]
    kept = spread(jnp.broadcast_to(kept, (8, 128)), heads_ref)[0:1]
    state[...] = state[...] * kept + mm_tn(writer.astype(BF16), weighted)

    gain = gain_ref[...]
    skip = skip_ref[...]

    def gating(i, carry):
        rows = pl.ds(pl.multiple_of(i * 16, 16), 16)
        gate = gate_ref[rows]
        mixer = mixed_in[rows] + skip * active[rows, :inner]
        gated = mixer * gate * sigmoid(gate)
        scale = lax.rsqrt(jnp.mean(gated * gated, axis=-1, keepdims=True) + EPS)
        inv[rows] = jnp.broadcast_to(scale, (16, 128))
        low_ref[rows] = (gated * scale * gain).astype(BF16)
        return carry

    lax.fori_loop(0, CHUNK // 16, gating, 0)
    mixed = mm(low_ref[...], weight_ref[...])
    block_out = tokens_ref[...].astype(F32) + mixed
    output_ref[...] = block_out.astype(BF16)
    valid = masks_ref[:, 9:10]
    sums_ref[0:1] += jnp.sum(valid * block_out * block_out, axis=0, keepdims=True)
    sums_ref[1:2] += jnp.sum(valid * mixed * mixed, axis=0, keepdims=True)
    out_low = (cot_ref[...].astype(F32) * valid).astype(BF16)
    out_low_ref[...] = out_low
    grads[...] = mm_nt(out_low, weight_ref[...])

    def backing(i, carry):
        gain_sum, skip_sum = carry
        rows = pl.ds(pl.multiple_of(i * 16, 16), 16)
        gate = gate_ref[rows]
        turned = sigmoid(gate)
        silu = gate * turned
        signal = active[rows, :inner]
        mixer = mixed_in[rows] + skip * signal
        gated = mixer * silu
        scale = inv[rows, 0:1]
        grad = grads[rows]
        gain_sum = gain_sum + grad * gated * scale
        grad = grad * gain
        inside = jnp.mean(grad * gated, axis=-1, keepdims=True)
        gated_grad = scale * grad - gated * (scale * scale * scale * inside)
        ssm_grad = gated_grad * silu
        ssm_grad_ref[rows] = ssm_grad
        grads[rows] = ssm_grad
        skip_sum = skip_sum + ssm_grad * signal
        gate_grad_ref[rows] = (gated_grad * mixer * turned * (1.0 + gate * (1.0 - turned))).astype(
            BF16
        )
        return gain_sum, skip_sum

    start = jnp.zeros((16, inner), F32)
    gain_sum, skip_sum = lax.fori_loop(0, CHUNK // 16, backing, (start, start))
    wide_ref[0:1] += jnp.sum(gain_sum, axis=0, keepdims=True)
    wide_ref[1:2] += jnp.sum(skip_sum, axis=0, keepdims=True)
    reader_t = jnp.transpose(reader_low)
    for pair in range(heads // 2):
        at = slice(pair * 128, (pair + 1) * 128)
        state_grad_ref[0, :, at] += mm(
            reader_t, (grads[:, at] * factors[3, :, at]).astype(BF16)
        )
        mixed_in[:, at] = mixed_in[:, at] * grads[:, at].astype(BF16).astype(F32)
    dot_ref[...] = gather_heads(mixed_in[...], heads_ref)


def forward(
    summed, gate, raw, cum, masks, seg_row, incoming, tokens, cot, weight, gain, skip, heads_map, sizes
):
    seqs, piece, inner, channels, heads = sizes
    total, model = tokens.shape
    chunks = piece // CHUNK
    full = lambda *shape: pl.BlockSpec(shape, lambda n, c: (0,) * len(shape))
    rows = lambda width: pl.BlockSpec((CHUNK, width), lambda n, c: (n * chunks + c, 0))
    each = lambda depth: pl.BlockSpec((1, depth, inner), lambda n, c: (n, 0, 0))
    shape = jax.ShapeDtypeStruct
    return pl.pallas_call(
        functools.partial(forward_kernel, sizes, chunks),
        grid=(seqs, chunks),
        in_specs=[
            rows(channels),
            rows(inner),
            rows(128),
            rows(128),
            rows(16),
            pl.BlockSpec((1, CHUNK), lambda n, c: (0, n * chunks + c)),
            each(128),
            rows(model),
            rows(model),
            full(inner, model),
            full(1, inner),
            full(1, inner),
            full(128, inner),
        ],
        out_specs=(
            rows(model),
            rows(inner),
            rows(model),
            rows(inner),
            rows(inner),
            pl.BlockSpec((1, 128, inner), lambda n, c: (n * chunks + c, 0, 0)),
            rows(128),
            full(8, model),
            full(8, inner),
            each(128),
        ),
        out_shape=(
            shape((total, model), BF16),
            shape((total, inner), BF16),
            shape((total, model), BF16),
            shape((total, inner), BF16),
            shape((total, inner), F32),
            shape((seqs * chunks, 128, inner), BF16),
            shape((total, 128), F32),
            shape((8, model), F32),
            shape((8, inner), F32),
            shape((seqs, 128, inner), F32),
        ),
        scratch_shapes=[
            pltpu.VMEM((128, inner), F32),
            pltpu.VMEM((8, 128), F32),
            pltpu.VMEM((CHUNK, channels), F32),
            pltpu.VMEM((CHUNK, inner), F32),
            pltpu.VMEM((4, CHUNK, inner), F32),
            pltpu.VMEM((CHUNK, inner), F32),
            pltpu.VMEM((CHUNK, 128), F32),
        ],
        compiler_params=pltpu.CompilerParams(vmem_limit_bytes=48 * 1024 * 1024),
        name="forward",
    )(summed, gate, raw, cum, masks, seg_row, incoming, tokens, cot, weight, gain, skip, heads_map)


def backward_kernel(
    sizes,
    chunks,
    summed_ref,
    conv_ref,
    halo_ref,
    raw_ref,
    cum_ref,
    masks_ref,
    seg_row_ref,
    later_ref,
    ssm_grad_ref,
    starts_ref,
    dot_ref,
    taps_ref,
    a_log_ref,
    skip_ref,
    heads_ref,
    proj_grad_ref,
    tail_ref,
    rim_ref,
    conv_sums_ref,
    head_sums_ref,
    state_grad,
    after,
    active,
    factors,
    moved_grad,
    shifted_rows,
    all_grad,
):
    seqs, piece, inner, channels, heads = sizes
    c = pl.program_id(1)

    @pl.when((c == 0) & (pl.program_id(0) == 0))
    def _():
        conv_sums_ref[...] = jnp.zeros_like(conv_sums_ref)
        head_sums_ref[...] = jnp.zeros_like(head_sums_ref)

    @pl.when(c == 0)
    def _():
        state_grad[...] = later_ref[0]
        after[...] = jnp.zeros_like(after)

    def activate(i, carry):
        rows = pl.ds(pl.multiple_of(i * 16, 16), 16)
        values = summed_ref[rows]
        active[rows] = values * sigmoid(values)
        return carry

    lax.fori_loop(0, CHUNK // 16, activate, 0)
    lane = lax.broadcasted_iota(jnp.int32, (CHUNK, 128), 1)
    raw = raw_ref[...]
    steps = jnp.where(lane < heads, softplus(raw), 0.0)
    cum = cum_ref[...]
    cum_t = jnp.transpose(cum)
    final = cum[CHUNK - 1 :]
    enter = jnp.exp(cum) * masks_ref[:, 4:5]
    tails = jnp.exp(final - cum) * masks_ref[:, 5:6]
    for i, block in enumerate((steps, enter, tails)):
        factors[i] = spread(block, heads_ref)
    writer = active[:, inner : inner + 128]
    reader = active[:, inner + 128 : inner + 256]
    scores = scores_of(reader, writer)
    bias = mask_bias(masks_ref[:, 8:9], seg_row_ref[0:1])
    half = lax.broadcasted_iota(jnp.int32, (CHUNK, 128), 1) < 64
    writer_low, reader_low = writer.astype(BF16), reader.astype(BF16)
    reader_t = jnp.transpose(reader_low)
    later = state_grad[...].astype(BF16)
    kept = jnp.exp(final) * masks_ref[CHUNK - 1 :, 4:5]
    kept = spread(jnp.broadcast_to(kept, (8, 128)), heads_ref)[0:1]
    scores_grad = jnp.zeros((CHUNK, CHUNK), F32)
    reader_grad = jnp.zeros((CHUNK, 128), F32)
    writer_grad = jnp.zeros((CHUNK, 128), F32)
    skip = skip_ref[...]
    for pair in range(heads // 2):
        at = slice(pair * 128, (pair + 1) * 128)
        signal = active[:, at]
        step_x = factors[0, :, at]
        moved = (signal * step_x).astype(BF16)
        grad = ssm_grad_ref[:, at]
        grad_low = grad.astype(BF16)
        zero = jnp.zeros_like(grad_low)
        stacked = jnp.concatenate(
            [jnp.where(half, grad_low, zero), jnp.where(half, zero, grad_low)], axis=0
        )
        both_grad = mm_nt(stacked, moved)
        one = decays_of(cum, cum_t, bias, 2 * pair)
        two = decays_of(cum, cum_t, bias, 2 * pair + 1)
        scores_grad = scores_grad + both_grad[:CHUNK] * one + both_grad[CHUNK:] * two
        both = jnp.concatenate([(scores * one).astype(BF16), (scores * two).astype(BF16)], axis=0)
        tail_x = factors[2, :, at]
        from_later = mm(writer_low, later[:, at])
        total = mm_tn(both, stacked) + from_later * tail_x
        weighted = (signal * step_x * tail_x).astype(BF16)
        entered = (grad * factors[1, :, at]).astype(BF16)
        start = starts_ref[0, :, at]
        reader_grad = reader_grad + mm_nt(entered, start)
        writer_grad = writer_grad + mm_nt(weighted, later[:, at])
        passed = jnp.sum(start.astype(F32) * later[:, at].astype(F32), axis=0, keepdims=True)
        factors[1, 0:1, at] = kept[:, at] * passed + jnp.sum(
            moved.astype(F32) * (from_later * tail_x), axis=0, keepdims=True
        )
        state_grad[:, at] = state_grad[:, at] * kept[:, at] + mm(reader_t, entered)
        moved_grad[:, at] = total * signal
        factors[2, :, at] = total * moved.astype(F32)
        all_grad[:, at] = total * step_x + skip[:, at] * grad
    sh, sl = split(scores_grad)
    reader_grad = reader_grad + mm(sh, writer_low) + mm(sl, writer_low)
    writer_grad = writer_grad + mm_tn(sh, reader_low) + mm_tn(sl, reader_low)
    all_grad[:, inner : inner + 128] = writer_grad
    all_grad[:, inner + 128 : inner + 256] = reader_grad
    step_grad = gather_heads(moved_grad[...], heads_ref)
    change = dot_ref[...] - gather_heads(factors[2], heads_ref)
    at_end = gather_heads(
        jnp.broadcast_to(factors[1, 0:1], (8, inner)), heads_ref
    )[0:1]
    row = lax.broadcasted_iota(jnp.int32, (CHUNK, 128), 0)
    change = change + jnp.where(row == CHUNK - 1, at_end, 0.0)
    decay_grad = exact_mm(triangle(CHUNK, True), change)
    rate = -jnp.exp(a_log_ref[...])
    raw_grad = jnp.where(lane < heads, (step_grad + decay_grad * rate) * sigmoid(raw), 0.0)
    head_sums_ref[0:1] += jnp.sum(raw_grad, axis=0, keepdims=True)
    head_sums_ref[1:2] += jnp.sum(decay_grad * steps * rate, axis=0, keepdims=True)
    proj_grad_ref[:, channels : channels + 128] = raw_grad.astype(BF16)
    proj_grad_ref[:, channels + 128 :] = jnp.zeros((CHUNK, 128), BF16)

    for block in range(channels // GATE_BLOCK):
        at = slice(block * GATE_BLOCK, (block + 1) * GATE_BLOCK)
        values = summed_ref[:, at]
        turned = sigmoid(values)
        grad = all_grad[:, at] * turned * (1.0 + values * (1.0 - turned))
        conv_sums_ref[4:5, at] += jnp.sum(grad, axis=0, keepdims=True)
        conv = conv_ref[:, at]
        result = grad * taps_ref[3:4, at]
        conv_sums_ref[3:4, at] += jnp.sum(grad * conv, axis=0, keepdims=True)
        rim = jnp.zeros((8, GATE_BLOCK), F32)
        shifted_rows[0:8] = jnp.zeros((8, GATE_BLOCK), F32)
        for k in range(3):
            shifted_rows[8 : 8 + CHUNK] = grad * masks_ref[:, k : k + 1]
            shifted_rows[8 + CHUNK :] = after[k, :, at]
            after[k, :, at] = shifted_rows[8:16]
            here = shifted_rows[11 - k : 11 - k + CHUNK]
            result = result + here * taps_ref[k : k + 1, at]
            conv_sums_ref[k : k + 1, at] += jnp.sum(here * conv, axis=0, keepdims=True)
            early = shifted_rows[3 - k : 11 - k]
            rim = rim + early * taps_ref[k : k + 1, at]

            @pl.when(c == chunks - 1)
            def _():
                conv_sums_ref[k : k + 1, at] += jnp.sum(
                    early * halo_ref[HALO - 8 :, at], axis=0, keepdims=True
                )

        proj_grad_ref[:, at] = result.astype(BF16)

        @pl.when(c == 0)
        def _():
            tail_ref[0, :, at] = result[CHUNK - 8 :]

        @pl.when(c == chunks - 1)
        def _():
            rim_ref[0, :, at] = rim.astype(BF16)


def backward(
    summed,
    conv,
    halo,
    raw,
    cum,
    masks,
    seg_row,
    later,
    ssm_grad,
    starts,
    dots,
    taps,
    a_log,
    skip,
    heads_map,
    sizes,
):
    seqs, piece, inner, channels, heads = sizes
    total = summed.shape[0]
    chunks = piece // CHUNK
    full = lambda *shape: pl.BlockSpec(shape, lambda n, c: (0,) * len(shape))
    spot = lambda n, c: n * chunks + chunks - 1 - c
    rows = lambda width: pl.BlockSpec((CHUNK, width), lambda n, c: (spot(n, c), 0))
    each = lambda depth, width: pl.BlockSpec((1, depth, width), lambda n, c: (n, 0, 0))
    shape = jax.ShapeDtypeStruct
    return pl.pallas_call(
        functools.partial(backward_kernel, sizes, chunks),
        grid=(seqs, chunks),
        in_specs=[
            rows(channels),
            rows(channels),
            pl.BlockSpec((HALO, channels), lambda n, c: (n, 0)),
            rows(128),
            rows(128),
            rows(16),
            pl.BlockSpec((1, CHUNK), lambda n, c: (0, spot(n, c))),
            each(128, inner),
            rows(inner),
            pl.BlockSpec((1, 128, inner), lambda n, c: (spot(n, c), 0, 0)),
            rows(128),
            full(4, channels),
            full(1, 128),
            full(1, inner),
            full(128, inner),
        ],
        out_specs=(
            rows(channels + 256),
            each(8, channels),
            each(8, channels),
            full(8, channels),
            full(8, 128),
        ),
        out_shape=(
            shape((total, channels + 256), BF16),
            shape((seqs, 8, channels), F32),
            shape((seqs, 8, channels), BF16),
            shape((8, channels), F32),
            shape((8, 128), F32),
        ),
        scratch_shapes=[
            pltpu.VMEM((128, inner), F32),
            pltpu.VMEM((3, 8, channels), F32),
            pltpu.VMEM((CHUNK, channels), F32),
            pltpu.VMEM((3, CHUNK, inner), F32),
            pltpu.VMEM((CHUNK, inner), F32),
            pltpu.VMEM((CHUNK + 16, GATE_BLOCK), F32),
            pltpu.VMEM((CHUNK, channels), F32),
        ],
        compiler_params=pltpu.CompilerParams(vmem_limit_bytes=48 * 1024 * 1024),
        name="backward",
    )(
        summed,
        conv,
        halo,
        raw,
        cum,
        masks,
        seg_row,
        later,
        ssm_grad,
        starts,
        dots,
        taps,
        a_log,
        skip,
        heads_map,
    )


def input_kernel(
    tokens_ref, out_low_ref, gate_grad_ref, proj_grad_ref, weight_ref, gain_ref, grad_ref, sums_ref
):
    inner = gate_grad_ref.shape[1]
    rest = weight_ref.shape[1] - inner

    @pl.when(pl.program_id(0) == 0)
    def _():
        sums_ref[...] = jnp.zeros_like(sums_ref)

    normed_grad = mm_nt(gate_grad_ref[...], weight_ref[:, :inner]) + mm_nt(
        proj_grad_ref[:, :rest], weight_ref[:, inner:]
    )
    values = tokens_ref[...].astype(F32)
    scale = lax.rsqrt(jnp.mean(values * values, axis=-1, keepdims=True) + EPS)
    sums_ref[0:1] += jnp.sum(normed_grad * values * scale, axis=0, keepdims=True)
    pushed = normed_grad * gain_ref[...]
    inside = jnp.mean(pushed * values, axis=-1, keepdims=True)
    grad_ref[...] = (
        out_low_ref[...].astype(F32)
        + scale * pushed
        - values * (scale * scale * scale * inside)
    ).astype(BF16)


def input_gradient(tokens, out_low, gate_grad, proj_grad, weight, gain):
    total, model = tokens.shape
    block = 128
    rows = lambda width: pl.BlockSpec((block, width), lambda i: (i, 0))
    full = lambda *shape: pl.BlockSpec(shape, lambda i: (0,) * len(shape))
    return pl.pallas_call(
        input_kernel,
        grid=(total // block,),
        in_specs=[
            rows(model),
            rows(model),
            rows(gate_grad.shape[1]),
            rows(proj_grad.shape[1]),
            full(*weight.shape),
            full(1, model),
        ],
        out_specs=(rows(model), full(8, model)),
        out_shape=(
            jax.ShapeDtypeStruct((total, model), BF16),
            jax.ShapeDtypeStruct((8, model), F32),
        ),
        compiler_params=pltpu.CompilerParams(vmem_limit_bytes=48 * 1024 * 1024),
        name="input_gradient",
    )(tokens, out_low, gate_grad, proj_grad, weight, gain)


def weight_kernel(counts, out_low_ref, normed_ref, low_ref, gate_grad_ref, proj_grad_ref, grad_ref, turned):
    low_count, gate_count = counts
    step = pl.program_id(0)

    @pl.when(step == 0)
    def _():
        turned[0] = jnp.transpose(out_low_ref[...])
        turned[1] = jnp.transpose(normed_ref[...])

    def put(result):
        grad_ref[0] = result[:, :LANES].astype(BF16)
        grad_ref[1] = result[:, LANES:].astype(BF16)

    @pl.when(step < low_count)
    def _():
        put(mm(turned[0], low_ref[...]))

    @pl.when((step >= low_count) & (step < low_count + gate_count))
    def _():
        put(mm(turned[1], gate_grad_ref[...]))

    @pl.when(step >= low_count + gate_count)
    def _():
        put(mm(turned[1], proj_grad_ref[...]))


def weight_gradient(out_low, normed, low, gate_grad, proj_grad):
    total, model = normed.shape
    wide = 2 * LANES
    low_count, gate_count, proj_count = (a.shape[1] // wide for a in (low, gate_grad, proj_grad))
    full = lambda *shape: pl.BlockSpec(shape, lambda j: (0,) * len(shape))

    def columns(before, count):
        return pl.BlockSpec((total, wide), lambda j: (0, jnp.clip(j - before, 0, count - 1)))

    return pl.pallas_call(
        functools.partial(weight_kernel, (low_count, gate_count)),
        grid=(low_count + gate_count + proj_count,),
        in_specs=[
            full(total, model),
            full(total, model),
            columns(0, low_count),
            columns(low_count, gate_count),
            columns(low_count + gate_count, proj_count),
        ],
        out_specs=pl.BlockSpec((2, model, LANES), lambda j: (j, 0, 0)),
        out_shape=jax.ShapeDtypeStruct(
            (2 * (low_count + gate_count + proj_count), model, LANES), BF16
        ),
        scratch_shapes=[pltpu.VMEM((2, model, total), BF16)],
        compiler_params=pltpu.CompilerParams(vmem_limit_bytes=48 * 1024 * 1024),
        name="weight_gradient",
    )(out_low, normed, low, gate_grad, proj_grad)


def local(
    tokens,
    cotangent,
    segment_ids,
    doc_starts,
    valid_mask,
    step_number,
    learn_rate,
    norm_gain,
    in_weight,
    conv_weight,
    conv_bias,
    dt_bias,
    a_log,
    skip_d,
    gate_gain,
    out_weight,
    in_momentum,
    out_momentum,
):
    seqs, piece, model_width = tokens.shape
    heads = dt_bias.shape[0]
    tap_count, channels = conv_weight.shape
    inner_width = gate_gain.shape[0]
    proj_width = in_weight.shape[1]
    total = seqs * piece
    sizes = (seqs, piece, inner_width, channels, heads)
    places, pieces = lax.axis_size("dp"), lax.axis_size("seq")
    turn = lax.axis_index("seq")
    seg = segment_ids.astype(F32)
    sent = jnp.concatenate(
        [
            tokens[:, piece - HALO :],
            jnp.broadcast_to(seg[:, piece - HALO :, None], (seqs, HALO, LANES)).astype(BF16),
        ],
        axis=2,
    )
    route = [(i, i + 1) for i in range(pieces - 1)]
    arrived = lax.ppermute(sent, "seq", route)
    halo = arrived[:, :, :model_width].reshape(seqs * HALO, model_width)
    early_seg = jnp.where(turn == 0, -1.0, arrived[:, :, model_width].astype(F32))
    seg_pad = jnp.concatenate([early_seg, seg], axis=1)

    def same(other):
        return (other == seg).astype(F32)

    by_chunk = seg.reshape(seqs, piece // CHUNK, CHUNK)
    before = seg_pad[:, HALO - 1 : HALO - 1 + piece].reshape(by_chunk.shape)[:, :, :1]
    chunk_first = jnp.broadcast_to(before, by_chunk.shape).reshape(seqs, piece)
    chunk_last = jnp.broadcast_to(by_chunk[:, :, -1:], by_chunk.shape).reshape(seqs, piece)
    valid_float = valid_mask.astype(F32)
    columns = [same(seg_pad[:, HALO - 3 + k : HALO - 3 + k + piece]) for k in range(4)] + [
        same(chunk_first),
        same(chunk_last),
        same(early_seg[:, -1:]),
        same(seg[:, -1:]),
        seg,
        valid_float,
    ]
    columns = columns + [jnp.zeros_like(seg)] * (16 - len(columns))
    masks = jnp.stack(columns, axis=2).reshape(total, 16)
    seg_row = seg.reshape(1, total)
    heads_map = (
        lax.broadcasted_iota(jnp.int32, (LANES, inner_width), 0)
        == lax.broadcasted_iota(jnp.int32, (LANES, inner_width), 1) // (inner_width // heads)
    ).astype(BF16)

    def lanes(values):
        return jnp.pad(values, (0, LANES - heads)).reshape(1, LANES)

    flat_tokens = tokens.reshape(total, model_width)
    flat_cot = cotangent.reshape(total, model_width)
    bias_row, decay_row = lanes(dt_bias), lanes(a_log)
    skip_row = jnp.repeat(skip_d, inner_width // heads).reshape(1, inner_width)
    gain_row = gate_gain.reshape(1, inner_width)
    normed, gate, conv, conv_halo, summed, raw, cum, fresh, keep = front(
        flat_tokens,
        halo,
        norm_gain.reshape(1, model_width),
        in_weight,
        conv_weight,
        conv_bias.reshape(1, channels),
        masks,
        bias_row,
        decay_row,
        heads_map,
        sizes,
    )
    incoming = chain(fresh, keep, 1)
    output, low, out_low, gate_grad, ssm_grad, starts, dots, squares, wide, state_grad = forward(
        summed,
        gate,
        raw,
        cum,
        masks,
        seg_row,
        incoming,
        flat_tokens,
        flat_cot,
        out_weight,
        gain_row,
        skip_row,
        heads_map,
        sizes,
    )
    later = chain(state_grad, keep, -1)
    proj_grad, tail, rim, conv_sums, head_sums = backward(
        summed,
        conv,
        conv_halo,
        raw,
        cum,
        masks,
        seg_row,
        later,
        ssm_grad,
        starts,
        dots,
        conv_weight,
        decay_row,
        skip_row,
        heads_map,
        sizes,
    )
    rim_in = lax.ppermute(rim, "seq", [(b, a) for a, b in route])
    fixed = (tail + rim_in.astype(F32)).astype(BF16)
    proj_grad = (
        proj_grad.reshape(seqs, piece, -1)
        .at[:, piece - 8 :, :channels]
        .set(fixed)
        .reshape(total, -1)
    )
    input_grad, gain_sums = input_gradient(
        flat_tokens, out_low, gate_grad, proj_grad, in_weight, norm_gain.reshape(1, model_width)
    )
    grad_tiles = weight_gradient(out_low, normed, low, gate_grad, proj_grad)
    share_rows = model_width // pieces
    width = inner_width + proj_width
    flows = -(-grad_tiles.shape[0] // places)
    full = flows * places * LANES
    grad_tiles = jnp.pad(
        grad_tiles, ((0, flows * places - grad_tiles.shape[0]), (0, 0), (0, 0))
    )
    grads = grad_tiles.reshape(flows, places, pieces, share_rows, LANES)

    def tiled(block):
        spread_out = jnp.pad(block, ((0, 0), (0, full - width)))
        return spread_out.reshape(-1, flows * places, LANES)

    norm_gain_grad = gain_sums[0]
    conv_weight_grad = conv_sums[:tap_count]
    conv_bias_grad = conv_sums[tap_count]
    dt_bias_grad = head_sums[0, :heads]
    a_log_grad = head_sums[1, :heads]
    gate_gain_grad = wide[0]
    skip_grad = wide[1].reshape(heads, -1).sum(axis=1)
    out_square = squares[0].sum()
    mix_square = squares[1].sum()
    valid_count = valid_float.sum()
    step_float = step_number[0].astype(jnp.float32)
    rate_now = learn_rate[0] * step_float / (step_float + 16.0)
    first_row = lax.axis_index("seq") * share_rows
    own_in = lax.dynamic_slice_in_dim(in_weight, first_row, share_rows, 0)
    own_out = lax.dynamic_slice_in_dim(out_weight, first_row, share_rows, 1)
    place = lax.axis_index("dp")

    def own_piece(out_rows, in_rows):
        block = tiled(jnp.concatenate([jnp.transpose(out_rows), in_rows], axis=1))
        block = block.reshape(share_rows, flows, places, LANES)
        return jnp.transpose(lax.dynamic_index_in_dim(block, place, 2, False), (1, 0, 2))

    parts = (
        norm_gain_grad,
        conv_weight_grad,
        conv_bias_grad,
        dt_bias_grad,
        a_log_grad,
        skip_grad,
        gate_gain_grad,
        out_square,
        mix_square,
        valid_count,
    )
    flat = jnp.concatenate([p.reshape(-1) for p in parts])
    small_rows = -(-flat.shape[0] // (8 * LANES)) * 8
    small = jnp.pad(flat, (0, small_rows * LANES - flat.shape[0])).reshape(small_rows, LANES)
    gathered, small_total = exchange(
        rate_now.reshape(1), grads, own_piece(own_out, own_in), own_piece(out_momentum, in_momentum), small
    )

    def untiled(block):
        return block.reshape(-1, full)[:, :width]

    summed = untiled(
        gathered[:, :, pieces].reshape(flows * places, share_rows, LANES).transpose(1, 0, 2)
    ).astype(jnp.float32)
    new_in_momentum = 0.5 * in_momentum + summed[:, inner_width:]
    new_out_momentum = 0.5 * out_momentum + jnp.transpose(summed[:, :inner_width])
    new_weights = untiled(
        gathered[:, :, :pieces]
        .reshape(flows * places, pieces, share_rows, LANES)
        .transpose(1, 2, 0, 3)
    )
    new_in_weight = new_weights[:, inner_width:]
    new_out_weight = jnp.transpose(new_weights[:, :inner_width])
    flat_total = small_total.reshape(-1)
    totals = []
    at = 0
    for p in parts:
        totals.append(flat_total[at : at + p.size].reshape(p.shape))
        at += p.size
    (
        norm_gain_total,
        conv_weight_total,
        conv_bias_total,
        dt_bias_total,
        a_log_total,
        skip_total,
        gate_gain_total,
        out_square_total,
        mix_square_total,
        valid_total,
    ) = totals
    denominator = jnp.maximum(valid_total, 1.0) * model_width
    output_rms = jnp.sqrt(out_square_total / denominator).reshape(1)
    mixer_rms = jnp.sqrt(mix_square_total / denominator).reshape(1)
    return (
        output.reshape(tokens.shape),
        input_grad.reshape(tokens.shape),
        new_in_weight,
        new_out_weight,
        new_in_momentum,
        new_out_momentum,
        norm_gain_total,
        conv_weight_total,
        conv_bias_total,
        dt_bias_total,
        a_log_total,
        skip_total,
        gate_gain_total,
        output_rms,
        mixer_rms,
    )


def solution(mesh):
    placed = (
        P("dp", "seq", None),
        P("dp", "seq", None),
        P("dp", "seq"),
        P("dp", "seq"),
        P("dp", "seq"),
        P(),
        P(),
        P(),
        P(),
        P(),
        P(),
        P(),
        P(),
        P(),
        P(),
        P(),
        P("seq", None),
        P(None, "seq"),
    )
    return jax.shard_map(
        local,
        mesh=mesh,
        in_specs=placed,
        out_specs=(
            P("dp", "seq", None),
            P("dp", "seq", None),
            P(),
            P(),
            P("seq", None),
            P(None, "seq"),
            P(),
            P(),
            P(),
            P(),
            P(),
            P(),
            P(),
            P(),
            P(),
        ),
        check_vma=False,
    )
```

```python
import functools

import jax
import jax.numpy as jnp
from jax import lax
from jax.experimental import pallas as pl
from jax.experimental.pallas import tpu as pltpu
from jax.sharding import PartitionSpec as P

LANES = 128


def exchange_kernel(
    bits,
    pieces,
    flows,
    rate_ref,
    grad_ref,
    weight_ref,
    momentum_ref,
    conv_sums_ref,
    wide_ref,
    head_sums_ref,
    gain_sums_ref,
    squares_ref,
    gathered_ref,
    small_out_ref,
    *scratch,
):
    halves = scratch[:bits]
    (piece_parts, small_acc, small_in, small_parts) = scratch[bits : bits + 4]
    (rs_send, rs_recv, zs_send, zs_recv, zg_send, zg_recv, ag_send, ag_recv) = scratch[
        bits + 4 : bits + 12
    ]
    (sm_send, sm_recv, sz_send, sz_recv) = scratch[bits + 12 :]
    place = lax.axis_index("dp")
    turn = lax.axis_index("seq")
    own = [(place // (1 << b)) % 2 for b in range(bits)]
    partner = [{"dp": place + (1 - 2 * own[b]) * (1 << b)} for b in range(bits)]
    others = [{"seq": (turn + j) % pieces} for j in range(pieces)]

    def order_of(f):
        rest = list(range(1, bits))
        shift = f % max(len(rest), 1)
        return ([0] if bits else []) + rest[shift:] + rest[:shift]

    def index_of(fixed):
        return tuple(fixed.get(b, slice(None)) for b in range(bits - 1, -1, -1))

    barrier = pltpu.get_barrier_semaphore()
    for target in partner + others[1:]:
        pl.semaphore_signal(
            barrier, inc=1, device_id=target, device_id_type=pl.DeviceIdType.MESH
        )
    pl.semaphore_wait(barrier, bits + pieces - 1)

    def remote(src, dst, send, recv, target):
        return pltpu.make_async_remote_copy(
            src_ref=src,
            dst_ref=dst,
            send_sem=send,
            recv_sem=recv,
            device_id=target,
            device_id_type=pl.DeviceIdType.MESH,
        )

    def held(f, k, other):
        order = order_of(f)
        bit = order[k]
        value = 1 - own[bit] if other else own[bit]
        if k == 0:
            return grad_ref.at[(f,) + index_of({bit: value})]
        free = [b for b in range(bits - 1, -1, -1) if b not in order[:k]]
        return halves[k - 1].at[
            (f,) + tuple(value if b == bit else slice(None) for b in free)
        ]

    def rs_copy(f, k):
        return remote(
            held(f, k, True),
            halves[k].at[f],
            rs_send.at[f, k],
            rs_recv.at[f, k],
            partner[order_of(f)[k]],
        )

    def rs_add(f, k):
        kept = held(f, k, False)
        into = halves[k].at[f]
        left = bits - k - 1
        for count in range(1 << left):
            spot = tuple((count >> (left - 1 - i)) & 1 for i in range(left))

            def body(p, carry):
                into[spot + (p,)] = (
                    kept[spot + (p,)].astype(jnp.float32)
                    + into[spot + (p,)].astype(jnp.float32)
                ).astype(jnp.bfloat16)
                return carry

            lax.fori_loop(0, pieces, body, 0)

    mine = index_of({b: own[b] for b in range(bits)})

    def zs_copy(f, j):
        return remote(
            halves[bits - 1].at[f, lax.rem(turn + j, pieces)],
            piece_parts.at[f, j],
            zs_send.at[f, j],
            zs_recv.at[f, j],
            others[j],
        )

    def zg_copy(f, j):
        spot = gathered_ref.at[(f,) + mine + (turn,)]
        return remote(spot, spot, zg_send.at[f, j], zg_recv.at[f, j], others[j])

    def ag_copy(f, k):
        order = order_of(f)
        fixed = {order[i]: own[order[i]] for i in range(k + 1)}
        spot = gathered_ref.at[(f,) + index_of(fixed)]
        return remote(spot, spot, ag_send.at[f, k], ag_recv.at[f, k], partner[order[k]])

    def sm_copy(k):
        return remote(small_acc.at[k], small_in.at[k], sm_send.at[k], sm_recv.at[k], partner[k])

    def sz_copy(j):
        return remote(
            small_acc.at[bits], small_parts.at[turn], sz_send.at[j], sz_recv.at[j], others[j]
        )

    def begin(f, k):
        if k < bits:
            rs_copy(f, k).start()
        else:
            for j in range(1, pieces):
                zs_copy(f, j).start()

    def begin_back(f, k):
        if k >= 0:
            ag_copy(f, k).start()

    inner, model = wide_ref.shape[1], gain_sums_ref.shape[1]
    small_acc[0, 0:5] = conv_sums_ref[0:5]
    small_acc[0, 5:7, :inner] = wide_ref[0:2]
    small_acc[0, 5:7, inner : inner + 128] = head_sums_ref[0:2]
    small_acc[0, 5:8, inner + 128 :] = squares_ref[0:3]
    small_acc[0, 7:8, :model] = gain_sums_ref[0:1]
    small_acc[0, 7:8, model : inner + 128] = jnp.zeros((1, inner + 128 - model), jnp.float32)
    if bits:
        sm_copy(0).start()
    for f in range(flows):
        begin(f, 0)
    for k in range(bits):
        sm_copy(k).wait_recv()
        small_acc[k + 1] = small_acc[k] + small_in[k]
        if k + 1 < bits:
            sm_copy(k + 1).start()
        else:
            for j in range(1, pieces):
                sz_copy(j).start()
        for f in range(flows):
            rs_copy(f, k).wait_recv()
            rs_add(f, k)
            begin(f, k + 1)
    small_parts[turn] = small_acc[bits]
    rate = rate_ref[0]
    for f in range(flows):
        for j in range(1, pieces):
            zs_copy(f, j).wait_recv()
        total = halves[bits - 1][f, turn].astype(jnp.float32)
        for j in range(1, pieces):
            total = total + piece_parts[f, j].astype(jnp.float32)
        summed = total.astype(jnp.bfloat16)
        gathered_ref[(f,) + mine + (pieces,)] = summed
        moved = 0.5 * momentum_ref[f] + summed.astype(jnp.float32)
        gathered_ref[(f,) + mine + (turn,)] = (
            weight_ref[f].astype(jnp.float32) - rate * moved
        ).astype(jnp.bfloat16)
        for j in range(1, pieces):
            zg_copy(f, j).start()
    for j in range(1, pieces):
        sz_copy(j).wait_recv()
    whole = small_parts[0]
    for j in range(1, pieces):
        whole = whole + small_parts[j]
    small_out_ref[...] = whole
    for f in range(flows):
        for j in range(1, pieces):
            zg_copy(f, j).wait_recv()
        begin_back(f, bits - 1)
    for k in range(bits - 1, -1, -1):
        for f in range(flows):
            ag_copy(f, k).wait_recv()
            begin_back(f, k - 1)
    for k in range(bits):
        sm_copy(k).wait_send()
        for f in range(flows):
            rs_copy(f, k).wait_send()
            ag_copy(f, k).wait_send()
    for j in range(1, pieces):
        sz_copy(j).wait_send()
        for f in range(flows):
            zs_copy(f, j).wait_send()
            zg_copy(f, j).wait_send()


def exchange(rate, grads, weights, momenta, sums):
    flows, places, pieces, rows, _ = grads.shape
    bits = places.bit_length() - 1
    assert places == 1 << bits and bits >= 1 and pieces >= 2
    twos = (2,) * bits
    grads = grads.reshape((flows,) + twos + (pieces, rows, LANES))
    small = sums[0].shape
    vmem = pl.BlockSpec(memory_space=pltpu.VMEM)
    dma = pltpu.SemaphoreType.DMA
    gathered, small_out = pl.pallas_call(
        functools.partial(exchange_kernel, bits, pieces, flows),
        out_shape=(
            jax.ShapeDtypeStruct((flows,) + twos + (pieces + 1, rows, LANES), jnp.bfloat16),
            jax.ShapeDtypeStruct(small, jnp.float32),
        ),
        in_specs=[pl.BlockSpec(memory_space=pltpu.SMEM)] + [vmem] * 8,
        out_specs=(vmem, vmem),
        scratch_shapes=[
            pltpu.VMEM((flows,) + twos[k + 1 :] + (pieces, rows, LANES), jnp.bfloat16)
            for k in range(bits)
        ]
        + [
            pltpu.VMEM((flows, pieces, rows, LANES), jnp.bfloat16),
            pltpu.VMEM((bits + 1,) + small, jnp.float32),
            pltpu.VMEM((bits,) + small, jnp.float32),
            pltpu.VMEM((pieces,) + small, jnp.float32),
        ]
        + [dma((flows, bits))] * 2
        + [dma((flows, pieces))] * 4
        + [dma((flows, bits))] * 2
        + [dma((bits,))] * 2
        + [dma((pieces,))] * 2,
        compiler_params=pltpu.CompilerParams(
            collective_id=0, has_side_effects=True, vmem_limit_bytes=56 * 1024 * 1024
        ),
        name="exchange",
    )(rate, grads, weights, momenta, *sums)
    return gathered.reshape(flows, places, pieces + 1, rows, LANES), small_out


CHUNK = 128
HALO = 16
GATE_BLOCK = 256
EPS = 1e-05
NEGATIVE = -1e30
F32, BF16 = jnp.float32, jnp.bfloat16


def mm(a, b):
    return jnp.dot(a, b, preferred_element_type=F32)


def mm_nt(a, b):
    return lax.dot_general(a, b, (((1,), (1,)), ((), ())), preferred_element_type=F32)


def mm_tn(a, b):
    return lax.dot_general(a, b, (((0,), (0,)), ((), ())), preferred_element_type=F32)


def split(a):
    high = a.astype(BF16)
    return high, (a - high.astype(F32)).astype(BF16)


def exact_mm(a, b):
    return jnp.dot(a, b, preferred_element_type=F32, precision=lax.Precision.HIGHEST)


def spread(a, heads_ref):
    high, low = split(a)
    return mm(high, heads_ref[...]) + mm(low, heads_ref[...])


def gather_heads(a, heads_ref):
    high, low = split(a)
    return mm_nt(high, heads_ref[...]) + mm_nt(low, heads_ref[...])


def sigmoid(v):
    return 1.0 / (1.0 + jnp.exp(-v))


def softplus(v):
    return jnp.maximum(v, 0.0) + jnp.log1p(jnp.exp(-jnp.abs(v)))


def triangle(size, upper):
    row = lax.broadcasted_iota(jnp.int32, (size, size), 0)
    column = lax.broadcasted_iota(jnp.int32, (size, size), 1)
    return ((row <= column) if upper else (row >= column)).astype(F32)


def front_kernel(
    sizes,
    tokens_ref,
    halo_ref,
    gain_ref,
    weight_ref,
    taps_ref,
    bias_ref,
    seg_ref,
    valid_ref,
    dt_bias_ref,
    a_log_ref,
    heads_ref,
    normed_ref,
    masks_ref,
    gate_ref,
    conv_ref,
    halo_out_ref,
    summed_ref,
    raw_ref,
    cum_ref,
    state_ref,
    keep_ref,
    padded,
    product,
    active,
):
    seqs, piece, inner, channels, heads = sizes
    gate_blocks, conv_blocks = inner // GATE_BLOCK, channels // GATE_BLOCK
    step = pl.program_id(0)
    stride = piece + HALO

    @pl.when(step == 0)
    def _():
        gain = gain_ref[...]
        for n in range(seqs):
            padded_seg = seg_ref[n : n + 1]
            seg = padded_seg[:, HALO:]

            def over_chunks(at):
                return jnp.concatenate(
                    [
                        jnp.broadcast_to(
                            padded_seg[:, c * CHUNK + at : c * CHUNK + at + 1], (1, CHUNK)
                        )
                        for c in range(piece // CHUNK)
                    ],
                    axis=1,
                )

            others = [padded_seg[:, HALO - 3 + k : HALO - 3 + k + piece] for k in range(4)] + [
                over_chunks(HALO - 1),
                over_chunks(HALO + CHUNK - 1),
                jnp.broadcast_to(padded_seg[:, HALO - 1 : HALO], (1, piece)),
                jnp.broadcast_to(padded_seg[:, HALO + piece - 1 :], (1, piece)),
            ]
            lines = [(other == seg).astype(F32) for other in others] + [
                seg,
                valid_ref[n : n + 1].astype(F32),
            ]
            lines = lines + [jnp.zeros_like(seg)] * (16 - len(lines))
            masks_ref[pl.ds(n * piece, piece)] = jnp.transpose(jnp.concatenate(lines, axis=0))
            for source, start, to, count in (
                (halo_ref, n * HALO, n * stride, HALO),
                (tokens_ref, n * piece, n * stride + HALO, piece),
            ):

                def body(i, carry):
                    values = source[pl.ds(pl.multiple_of(start + i * 16, 16), 16)].astype(F32)
                    scale = lax.rsqrt(jnp.mean(values * values, axis=-1, keepdims=True) + EPS)
                    low = (values * scale * gain).astype(BF16)
                    padded[pl.ds(pl.multiple_of(to + i * 16, 16), 16)] = low
                    return carry

                lax.fori_loop(0, count // 16, body, 0)
            normed_ref[pl.ds(n * piece, piece)] = padded[pl.ds(n * stride + HALO, piece)]

    product[...] = mm_nt(padded[...], weight_ref[...])

    @pl.when(step < gate_blocks)
    def _():
        for n in range(seqs):
            gate_ref[pl.ds(n * piece, piece)] = product[pl.ds(n * stride + HALO, piece)]

    @pl.when((step >= gate_blocks) & (step < gate_blocks + conv_blocks))
    def _():
        at = pl.multiple_of((step - gate_blocks) * GATE_BLOCK, GATE_BLOCK)
        for n in range(seqs):
            conv_ref[pl.ds(n * piece, piece)] = product[pl.ds(n * stride + HALO, piece)]
            halo_out_ref[pl.ds(n * HALO, HALO)] = product[pl.ds(n * stride, HALO)]
            for i in range(piece // 64):
                rows = pl.ds(n * piece + i * 64, 64)
                total = jnp.broadcast_to(bias_ref[...], (64, GATE_BLOCK))
                for k in range(4):
                    source = product[pl.ds(n * stride + HALO - 3 + k + i * 64, 64)]
                    total = total + source * masks_ref[rows, k : k + 1] * taps_ref[k : k + 1]
                summed_ref[rows] = total
                active[rows, pl.ds(at, GATE_BLOCK)] = (total * sigmoid(total)).astype(BF16)

    @pl.when(step == gate_blocks + conv_blocks)
    def _():
        lane = lax.broadcasted_iota(jnp.int32, (piece, 128), 1)
        lower = triangle(CHUNK, False)
        for n in range(seqs):
            rows = pl.ds(n * piece, piece)
            raw = jnp.where(lane < heads, product[pl.ds(n * stride + HALO, piece), :128], 0.0)
            raw = raw + dt_bias_ref[...]
            raw_ref[rows] = raw
            steps = jnp.where(lane < heads, softplus(raw), 0.0)
            decay = -jnp.exp(a_log_ref[...]) * steps
            total = jnp.zeros((1, 128), F32)
            pieces = []
            for c in range(piece // CHUNK):
                cumulative = exact_mm(lower, decay[c * CHUNK : (c + 1) * CHUNK])
                cum_ref[pl.ds(n * piece + c * CHUNK, CHUNK)] = cumulative
                pieces.append(cumulative + total)
                total = total + cumulative[CHUNK - 1 :]
            whole = jnp.concatenate(pieces, axis=0) if len(pieces) > 1 else pieces[0]
            tails = jnp.exp(total - whole) * steps * masks_ref[rows, 7:8]
            weighted = (spread(tails, heads_ref) * active[rows, :inner].astype(F32)).astype(BF16)
            state_ref[n] = mm_tn(active[rows, inner : inner + 128], weighted)
            last = masks_ref[n * piece + piece - 1 : n * piece + piece, 6:7]
            keep = jnp.exp(total) * last
            keep_ref[n] = spread(jnp.broadcast_to(keep, (8, 128)), heads_ref)


def front(tokens, halo, gain, weight, taps, bias, segs, valid, dt_bias, a_log, heads_map, sizes):
    seqs, piece, inner, channels, heads = sizes
    total, model = tokens.shape
    stride = seqs * (piece + HALO)
    gate_blocks, conv_blocks = inner // GATE_BLOCK, channels // GATE_BLOCK
    full = lambda *shape: pl.BlockSpec(shape, lambda j: (0,) * len(shape))

    def conv_at(j):
        return (0, jnp.clip(j - gate_blocks, 0, conv_blocks - 1))

    return pl.pallas_call(
        functools.partial(front_kernel, sizes),
        grid=(gate_blocks + conv_blocks + 1,),
        in_specs=[
            full(total, model),
            full(seqs * HALO, model),
            full(1, model),
            pl.BlockSpec((GATE_BLOCK, model), lambda j: (j, 0)),
            pl.BlockSpec((4, GATE_BLOCK), conv_at),
            pl.BlockSpec((1, GATE_BLOCK), conv_at),
            full(*segs.shape),
            full(*valid.shape),
            full(1, 128),
            full(1, 128),
            full(128, inner),
        ],
        out_specs=(
            full(total, model),
            full(total, 16),
            pl.BlockSpec((total, GATE_BLOCK), lambda j: (0, jnp.minimum(j, gate_blocks - 1))),
            pl.BlockSpec((total, GATE_BLOCK), conv_at),
            pl.BlockSpec((seqs * HALO, GATE_BLOCK), conv_at),
            pl.BlockSpec((total, GATE_BLOCK), conv_at),
            full(total, 128),
            full(total, 128),
            full(seqs, 128, inner),
            full(seqs, 8, inner),
        ),
        out_shape=(
            jax.ShapeDtypeStruct((total, model), BF16),
            jax.ShapeDtypeStruct((total, 16), F32),
            jax.ShapeDtypeStruct((total, inner), F32),
            jax.ShapeDtypeStruct((total, channels), F32),
            jax.ShapeDtypeStruct((seqs * HALO, channels), F32),
            jax.ShapeDtypeStruct((total, channels), F32),
            jax.ShapeDtypeStruct((total, 128), F32),
            jax.ShapeDtypeStruct((total, 128), F32),
            jax.ShapeDtypeStruct((seqs, 128, inner), F32),
            jax.ShapeDtypeStruct((seqs, 8, inner), F32),
        ),
        scratch_shapes=[
            pltpu.VMEM((stride, model), BF16),
            pltpu.VMEM((stride, GATE_BLOCK), F32),
            pltpu.VMEM((total, channels), BF16),
        ],
        compiler_params=pltpu.CompilerParams(vmem_limit_bytes=48 * 1024 * 1024),
        name="front",
    )(tokens, halo, gain, weight, taps, bias, segs, valid, dt_bias, a_log, heads_map)


def chain_kernel(ways, blocks, own_ref, keep_ref, out_ref, sent, taken, send, recv):
    size = lax.axis_size("seq")
    turn = lax.axis_index("seq")
    first = turn == (0 if ways > 0 else size - 1)
    final = turn == (size - 1 if ways > 0 else 0)
    ahead = {"seq": lax.rem(turn + ways + size, size)}
    behind = {"seq": lax.rem(turn - ways + size, size)}
    barrier = pltpu.get_barrier_semaphore()

    @pl.when(jnp.logical_not(first))
    def _():
        pl.semaphore_signal(
            barrier, inc=1, device_id=behind, device_id_type=pl.DeviceIdType.MESH
        )

    @pl.when(jnp.logical_not(final))
    def _():
        pl.semaphore_wait(barrier, 1)

    width = own_ref.shape[2] // blocks

    def copy(c):
        return pltpu.make_async_remote_copy(
            src_ref=sent.at[c],
            dst_ref=taken.at[c],
            send_sem=send.at[c],
            recv_sem=recv.at[c],
            device_id=ahead,
            device_id_type=pl.DeviceIdType.MESH,
        )

    @pl.when(first)
    def _():
        out_ref[...] = jnp.zeros_like(out_ref)
        for c in range(blocks):
            at = slice(c * width, (c + 1) * width)
            sent[c] = own_ref[:, :, at].astype(BF16)
            copy(c).start()

    @pl.when(jnp.logical_not(first))
    def _():
        for c in range(blocks):
            at = slice(c * width, (c + 1) * width)
            copy(c).wait_recv()

            @pl.when(jnp.logical_not(final))
            def _():
                sent[c] = (
                    own_ref[:, :, at] + keep_ref[:, 0:1, at] * taken[c].astype(F32)
                ).astype(BF16)
                copy(c).start()

            out_ref[:, :, at] = taken[c].astype(F32)

    @pl.when(jnp.logical_not(final))
    def _():
        for c in range(blocks):
            copy(c).wait_send()


def chain(own, keep, ways, blocks=6):
    seqs, depth, inner = own.shape
    vmem = pl.BlockSpec(memory_space=pltpu.VMEM)
    part = (blocks, seqs, depth, inner // blocks)
    return pl.pallas_call(
        functools.partial(chain_kernel, ways, blocks),
        out_shape=jax.ShapeDtypeStruct(own.shape, F32),
        in_specs=[vmem, vmem],
        out_specs=vmem,
        scratch_shapes=[pltpu.VMEM(part, BF16)] * 2 + [pltpu.SemaphoreType.DMA((blocks,))] * 2,
        compiler_params=pltpu.CompilerParams(
            collective_id=1 if ways > 0 else 2,
            has_side_effects=True,
            vmem_limit_bytes=32 * 1024 * 1024,
        ),
        name="chain",
    )(own, keep)


def decays_of(cum, cum_t, bias, h):
    return jnp.exp(cum[:, h : h + 1] - cum_t[h : h + 1, :] + bias)


def mask_bias(seg_col, seg_row):
    row = lax.broadcasted_iota(jnp.int32, (CHUNK, CHUNK), 0)
    column = lax.broadcasted_iota(jnp.int32, (CHUNK, CHUNK), 1)
    return jnp.where((row >= column) & (seg_col == seg_row), 0.0, NEGATIVE)


def scores_of(reader, writer):
    rh, rl = split(reader)
    wh, wl = split(writer)
    return mm_nt(rh, wh) + (mm_nt(rh, wl) + mm_nt(rl, wh))


def forward_kernel(
    sizes,
    chunks,
    summed_ref,
    gate_ref,
    raw_ref,
    cum_ref,
    masks_ref,
    seg_row_ref,
    incoming_ref,
    tokens_ref,
    cot_ref,
    weight_ref,
    gain_ref,
    skip_ref,
    heads_ref,
    output_ref,
    low_ref,
    out_low_ref,
    gate_grad_ref,
    ssm_grad_ref,
    starts_ref,
    dot_ref,
    sums_ref,
    wide_ref,
    state_grad_ref,
    state,
    prefix,
    active,
    mixed_in,
    factors,
    grads,
    inv,
):
    seqs, piece, inner, channels, heads = sizes
    c = pl.program_id(1)

    @pl.when((c == 0) & (pl.program_id(0) == 0))
    def _():
        sums_ref[...] = jnp.zeros_like(sums_ref)
        wide_ref[...] = jnp.zeros_like(wide_ref)

    @pl.when(c == 0)
    def _():
        state[...] = incoming_ref[0]
        prefix[...] = jnp.zeros_like(prefix)
        state_grad_ref[...] = jnp.zeros_like(state_grad_ref)

    def activate(i, carry):
        rows = pl.ds(pl.multiple_of(i * 16, 16), 16)
        values = summed_ref[rows]
        active[rows] = values * sigmoid(values)
        return carry

    lax.fori_loop(0, CHUNK // 16, activate, 0)
    lane = lax.broadcasted_iota(jnp.int32, (CHUNK, 128), 1)
    steps = jnp.where(lane < heads, softplus(raw_ref[...]), 0.0)
    cum = cum_ref[...]
    cum_t = jnp.transpose(cum)
    final = cum[CHUNK - 1 :]
    enter = jnp.exp(cum) * masks_ref[:, 4:5]
    tails = jnp.exp(final - cum) * steps * masks_ref[:, 5:6]
    from_start = jnp.exp(cum + prefix[0:1]) * masks_ref[:, 6:7]
    prefix[...] = prefix[...] + final
    for i, block in enumerate((steps, enter, tails, from_start)):
        factors[i] = spread(block, heads_ref)
    writer = active[:, inner : inner + 128]
    reader = active[:, inner + 128 : inner + 256]
    scores = scores_of(reader, writer)
    bias = mask_bias(masks_ref[:, 8:9], seg_row_ref[0:1])
    half = lax.broadcasted_iota(jnp.int32, (CHUNK, 128), 1) < 64
    state_low = state[...].astype(BF16)
    starts_ref[0] = state_low
    reader_low = reader.astype(BF16)
    for pair in range(heads // 2):
        at = slice(pair * 128, (pair + 1) * 128)
        moved = (active[:, at] * factors[0, :, at]).astype(BF16)
        zero = jnp.zeros_like(moved)
        one = (scores * decays_of(cum, cum_t, bias, 2 * pair)).astype(BF16)
        two = (scores * decays_of(cum, cum_t, bias, 2 * pair + 1)).astype(BF16)
        both = jnp.concatenate([one, two], axis=1)
        stacked = jnp.concatenate(
            [jnp.where(half, moved, zero), jnp.where(half, zero, moved)], axis=0
        )
        carried = mm(reader_low, state_low[:, at]) * factors[1, :, at]
        mixed_in[:, at] = mm(both, stacked) + carried
    weighted = (active[:, :inner] * factors[2]).astype(BF16)
    kept = jnp.exp(final) * masks_ref[CHUNK - 1 :, 4:5]
    kept = spread(jnp.broadcast_to(kept, (8, 128)), heads_ref)[0:1]
    state[...] = state[...] * kept + mm_tn(writer.astype(BF16), weighted)

    gain = gain_ref[...]
    skip = skip_ref[...]

    def gating(i, carry):
        rows = pl.ds(pl.multiple_of(i * 16, 16), 16)
        gate = gate_ref[rows]
        mixer = mixed_in[rows] + skip * active[rows, :inner]
        gated = mixer * gate * sigmoid(gate)
        scale = lax.rsqrt(jnp.mean(gated * gated, axis=-1, keepdims=True) + EPS)
        inv[rows] = jnp.broadcast_to(scale, (16, 128))
        low_ref[rows] = (gated * scale * gain).astype(BF16)
        return carry

    lax.fori_loop(0, CHUNK // 16, gating, 0)
    mixed = mm(low_ref[...], weight_ref[...])
    block_out = tokens_ref[...].astype(F32) + mixed
    output_ref[...] = block_out.astype(BF16)
    valid = masks_ref[:, 9:10]
    for i, block in enumerate((block_out, mixed)):
        squares = jnp.sum(valid * block * block, axis=0, keepdims=True)
        for at in range(0, squares.shape[1], 128):
            sums_ref[i : i + 1] += squares[:, at : at + 128]
    sums_ref[2:3, :16] += jnp.sum(masks_ref[...], axis=0, keepdims=True)
    out_low = (cot_ref[...].astype(F32) * valid).astype(BF16)
    out_low_ref[...] = out_low
    grads[...] = mm_nt(out_low, weight_ref[...])

    def backing(i, carry):
        gain_sum, skip_sum = carry
        rows = pl.ds(pl.multiple_of(i * 16, 16), 16)
        gate = gate_ref[rows]
        turned = sigmoid(gate)
        silu = gate * turned
        signal = active[rows, :inner]
        mixer = mixed_in[rows] + skip * signal
        gated = mixer * silu
        scale = inv[rows, 0:1]
        grad = grads[rows]
        gain_sum = gain_sum + grad * gated * scale
        grad = grad * gain
        inside = jnp.mean(grad * gated, axis=-1, keepdims=True)
        gated_grad = scale * grad - gated * (scale * scale * scale * inside)
        ssm_grad = gated_grad * silu
        ssm_grad_ref[rows] = ssm_grad
        grads[rows] = ssm_grad
        skip_sum = skip_sum + ssm_grad * signal
        gate_grad_ref[rows] = (gated_grad * mixer * turned * (1.0 + gate * (1.0 - turned))).astype(
            BF16
        )
        return gain_sum, skip_sum

    start = jnp.zeros((16, inner), F32)
    gain_sum, skip_sum = lax.fori_loop(0, CHUNK // 16, backing, (start, start))
    wide_ref[0:1] += jnp.sum(gain_sum, axis=0, keepdims=True)
    wide_ref[1:2] += jnp.sum(skip_sum, axis=0, keepdims=True)
    reader_t = jnp.transpose(reader_low)
    for pair in range(heads // 2):
        at = slice(pair * 128, (pair + 1) * 128)
        state_grad_ref[0, :, at] += mm(
            reader_t, (grads[:, at] * factors[3, :, at]).astype(BF16)
        )
        mixed_in[:, at] = mixed_in[:, at] * grads[:, at].astype(BF16).astype(F32)
    dot_ref[...] = gather_heads(mixed_in[...], heads_ref)


def forward(
    summed, gate, raw, cum, masks, seg_row, incoming, tokens, cot, weight, gain, skip, heads_map, sizes
):
    seqs, piece, inner, channels, heads = sizes
    total, model = tokens.shape
    chunks = piece // CHUNK
    full = lambda *shape: pl.BlockSpec(shape, lambda n, c: (0,) * len(shape))
    rows = lambda width: pl.BlockSpec((CHUNK, width), lambda n, c: (n * chunks + c, 0))
    each = lambda depth: pl.BlockSpec((1, depth, inner), lambda n, c: (n, 0, 0))
    shape = jax.ShapeDtypeStruct
    return pl.pallas_call(
        functools.partial(forward_kernel, sizes, chunks),
        grid=(seqs, chunks),
        in_specs=[
            rows(channels),
            rows(inner),
            rows(128),
            rows(128),
            rows(16),
            pl.BlockSpec((1, CHUNK), lambda n, c: (0, n * chunks + c)),
            each(128),
            rows(model),
            rows(model),
            full(inner, model),
            full(1, inner),
            full(1, inner),
            full(128, inner),
        ],
        out_specs=(
            rows(model),
            rows(inner),
            rows(model),
            rows(inner),
            rows(inner),
            pl.BlockSpec((1, 128, inner), lambda n, c: (n * chunks + c, 0, 0)),
            rows(128),
            full(8, 128),
            full(8, inner),
            each(128),
        ),
        out_shape=(
            shape((total, model), BF16),
            shape((total, inner), BF16),
            shape((total, model), BF16),
            shape((total, inner), BF16),
            shape((total, inner), F32),
            shape((seqs * chunks, 128, inner), BF16),
            shape((total, 128), F32),
            shape((8, 128), F32),
            shape((8, inner), F32),
            shape((seqs, 128, inner), F32),
        ),
        scratch_shapes=[
            pltpu.VMEM((128, inner), F32),
            pltpu.VMEM((8, 128), F32),
            pltpu.VMEM((CHUNK, channels), F32),
            pltpu.VMEM((CHUNK, inner), F32),
            pltpu.VMEM((4, CHUNK, inner), F32),
            pltpu.VMEM((CHUNK, inner), F32),
            pltpu.VMEM((CHUNK, 128), F32),
        ],
        compiler_params=pltpu.CompilerParams(vmem_limit_bytes=48 * 1024 * 1024),
        name="forward",
    )(summed, gate, raw, cum, masks, seg_row, incoming, tokens, cot, weight, gain, skip, heads_map)


def backward_kernel(
    sizes,
    chunks,
    summed_ref,
    conv_ref,
    halo_ref,
    raw_ref,
    cum_ref,
    masks_ref,
    seg_row_ref,
    later_ref,
    ssm_grad_ref,
    starts_ref,
    dot_ref,
    taps_ref,
    a_log_ref,
    skip_ref,
    heads_ref,
    proj_grad_ref,
    tail_ref,
    rim_ref,
    conv_sums_ref,
    head_sums_ref,
    state_grad,
    after,
    active,
    factors,
    moved_grad,
    shifted_rows,
    all_grad,
    rims,
    rims_in,
    rim_send,
    rim_recv,
):
    seqs, piece, inner, channels, heads = sizes
    n, c = pl.program_id(0), pl.program_id(1)
    turn, pieces = lax.axis_index("seq"), lax.axis_size("seq")
    barrier = pltpu.get_barrier_semaphore()
    rim_copy = pltpu.make_async_remote_copy(
        src_ref=rims,
        dst_ref=rims_in,
        send_sem=rim_send,
        recv_sem=rim_recv,
        device_id={"seq": lax.rem(turn + pieces - 1, pieces)},
        device_id_type=pl.DeviceIdType.MESH,
    )

    @pl.when((c == 0) & (n == 0) & (turn < pieces - 1))
    def _():
        pl.semaphore_signal(
            barrier, inc=1, device_id={"seq": turn + 1}, device_id_type=pl.DeviceIdType.MESH
        )

    @pl.when((c == 0) & (n == 0) & (turn > 0))
    def _():
        pl.semaphore_wait(barrier, 1)

    @pl.when((c == 0) & (n == 0))
    def _():
        conv_sums_ref[...] = jnp.zeros_like(conv_sums_ref)
        head_sums_ref[...] = jnp.zeros_like(head_sums_ref)

    @pl.when(c == 0)
    def _():
        state_grad[...] = later_ref[0]
        after[...] = jnp.zeros_like(after)

    def activate(i, carry):
        rows = pl.ds(pl.multiple_of(i * 16, 16), 16)
        values = summed_ref[rows]
        active[rows] = values * sigmoid(values)
        return carry

    lax.fori_loop(0, CHUNK // 16, activate, 0)
    lane = lax.broadcasted_iota(jnp.int32, (CHUNK, 128), 1)
    raw = raw_ref[...]
    steps = jnp.where(lane < heads, softplus(raw), 0.0)
    cum = cum_ref[...]
    cum_t = jnp.transpose(cum)
    final = cum[CHUNK - 1 :]
    enter = jnp.exp(cum) * masks_ref[:, 4:5]
    tails = jnp.exp(final - cum) * masks_ref[:, 5:6]
    for i, block in enumerate((steps, enter, tails)):
        factors[i] = spread(block, heads_ref)
    writer = active[:, inner : inner + 128]
    reader = active[:, inner + 128 : inner + 256]
    scores = scores_of(reader, writer)
    bias = mask_bias(masks_ref[:, 8:9], seg_row_ref[0:1])
    half = lax.broadcasted_iota(jnp.int32, (CHUNK, 128), 1) < 64
    writer_low, reader_low = writer.astype(BF16), reader.astype(BF16)
    reader_t = jnp.transpose(reader_low)
    later = state_grad[...].astype(BF16)
    kept = jnp.exp(final) * masks_ref[CHUNK - 1 :, 4:5]
    kept = spread(jnp.broadcast_to(kept, (8, 128)), heads_ref)[0:1]
    scores_grad = jnp.zeros((CHUNK, CHUNK), F32)
    reader_grad = jnp.zeros((CHUNK, 128), F32)
    writer_grad = jnp.zeros((CHUNK, 128), F32)
    skip = skip_ref[...]
    for pair in range(heads // 2):
        at = slice(pair * 128, (pair + 1) * 128)
        signal = active[:, at]
        step_x = factors[0, :, at]
        moved = (signal * step_x).astype(BF16)
        grad = ssm_grad_ref[:, at]
        grad_low = grad.astype(BF16)
        zero = jnp.zeros_like(grad_low)
        stacked = jnp.concatenate(
            [jnp.where(half, grad_low, zero), jnp.where(half, zero, grad_low)], axis=0
        )
        both_grad = mm_nt(stacked, moved)
        one = decays_of(cum, cum_t, bias, 2 * pair)
        two = decays_of(cum, cum_t, bias, 2 * pair + 1)
        scores_grad = scores_grad + both_grad[:CHUNK] * one + both_grad[CHUNK:] * two
        both = jnp.concatenate([(scores * one).astype(BF16), (scores * two).astype(BF16)], axis=0)
        tail_x = factors[2, :, at]
        from_later = mm(writer_low, later[:, at])
        total = mm_tn(both, stacked) + from_later * tail_x
        weighted = (signal * step_x * tail_x).astype(BF16)
        entered = (grad * factors[1, :, at]).astype(BF16)
        start = starts_ref[0, :, at]
        reader_grad = reader_grad + mm_nt(entered, start)
        writer_grad = writer_grad + mm_nt(weighted, later[:, at])
        passed = jnp.sum(start.astype(F32) * later[:, at].astype(F32), axis=0, keepdims=True)
        factors[1, 0:1, at] = kept[:, at] * passed + jnp.sum(
            moved.astype(F32) * (from_later * tail_x), axis=0, keepdims=True
        )
        state_grad[:, at] = state_grad[:, at] * kept[:, at] + mm(reader_t, entered)
        moved_grad[:, at] = total * signal
        factors[2, :, at] = total * moved.astype(F32)
        all_grad[:, at] = total * step_x + skip[:, at] * grad
    sh, sl = split(scores_grad)
    reader_grad = reader_grad + mm(sh, writer_low) + mm(sl, writer_low)
    writer_grad = writer_grad + mm_tn(sh, reader_low) + mm_tn(sl, reader_low)
    all_grad[:, inner : inner + 128] = writer_grad
    all_grad[:, inner + 128 : inner + 256] = reader_grad
    step_grad = gather_heads(moved_grad[...], heads_ref)
    change = dot_ref[...] - gather_heads(factors[2], heads_ref)
    at_end = gather_heads(
        jnp.broadcast_to(factors[1, 0:1], (8, inner)), heads_ref
    )[0:1]
    row = lax.broadcasted_iota(jnp.int32, (CHUNK, 128), 0)
    change = change + jnp.where(row == CHUNK - 1, at_end, 0.0)
    decay_grad = exact_mm(triangle(CHUNK, True), change)
    rate = -jnp.exp(a_log_ref[...])
    raw_grad = jnp.where(lane < heads, (step_grad + decay_grad * rate) * sigmoid(raw), 0.0)
    head_sums_ref[0:1] += jnp.sum(raw_grad, axis=0, keepdims=True)
    head_sums_ref[1:2] += jnp.sum(decay_grad * steps * rate, axis=0, keepdims=True)
    proj_grad_ref[:, channels : channels + 128] = raw_grad.astype(BF16)
    proj_grad_ref[:, channels + 128 :] = jnp.zeros((CHUNK, 128), BF16)

    for block in range(channels // GATE_BLOCK):
        at = slice(block * GATE_BLOCK, (block + 1) * GATE_BLOCK)
        values = summed_ref[:, at]
        turned = sigmoid(values)
        grad = all_grad[:, at] * turned * (1.0 + values * (1.0 - turned))
        conv_sums_ref[4:5, at] += jnp.sum(grad, axis=0, keepdims=True)
        conv = conv_ref[:, at]
        result = grad * taps_ref[3:4, at]
        conv_sums_ref[3:4, at] += jnp.sum(grad * conv, axis=0, keepdims=True)
        rim = jnp.zeros((8, GATE_BLOCK), F32)
        shifted_rows[0:8] = jnp.zeros((8, GATE_BLOCK), F32)
        for k in range(3):
            shifted_rows[8 : 8 + CHUNK] = grad * masks_ref[:, k : k + 1]
            shifted_rows[8 + CHUNK :] = after[k, :, at]
            after[k, :, at] = shifted_rows[8:16]
            here = shifted_rows[11 - k : 11 - k + CHUNK]
            result = result + here * taps_ref[k : k + 1, at]
            conv_sums_ref[k : k + 1, at] += jnp.sum(here * conv, axis=0, keepdims=True)
            early = shifted_rows[3 - k : 11 - k]
            rim = rim + early * taps_ref[k : k + 1, at]

            @pl.when(c == chunks - 1)
            def _():
                conv_sums_ref[k : k + 1, at] += jnp.sum(
                    early * halo_ref[HALO - 8 :, at], axis=0, keepdims=True
                )

        proj_grad_ref[:, at] = result.astype(BF16)

        @pl.when(c == 0)
        def _():
            tail_ref[0, :, at] = result[CHUNK - 8 :]

        @pl.when(c == chunks - 1)
        def _():
            rims[n, :, at] = rim.astype(BF16)

    @pl.when((c == chunks - 1) & (n == seqs - 1))
    def _():
        @pl.when(turn > 0)
        def _():
            rim_copy.start()
            rim_copy.wait_send()

        @pl.when(turn < pieces - 1)
        def _():
            rim_copy.wait_recv()
            rim_ref[...] = rims_in[...]

        @pl.when(turn == pieces - 1)
        def _():
            rim_ref[...] = jnp.zeros_like(rim_ref)


def backward(
    summed,
    conv,
    halo,
    raw,
    cum,
    masks,
    seg_row,
    later,
    ssm_grad,
    starts,
    dots,
    taps,
    a_log,
    skip,
    heads_map,
    sizes,
):
    seqs, piece, inner, channels, heads = sizes
    total = summed.shape[0]
    chunks = piece // CHUNK
    full = lambda *shape: pl.BlockSpec(shape, lambda n, c: (0,) * len(shape))
    spot = lambda n, c: n * chunks + chunks - 1 - c
    rows = lambda width: pl.BlockSpec((CHUNK, width), lambda n, c: (spot(n, c), 0))
    each = lambda depth, width: pl.BlockSpec((1, depth, width), lambda n, c: (n, 0, 0))
    shape = jax.ShapeDtypeStruct
    return pl.pallas_call(
        functools.partial(backward_kernel, sizes, chunks),
        grid=(seqs, chunks),
        in_specs=[
            rows(channels),
            rows(channels),
            pl.BlockSpec((HALO, channels), lambda n, c: (n, 0)),
            rows(128),
            rows(128),
            rows(16),
            pl.BlockSpec((1, CHUNK), lambda n, c: (0, spot(n, c))),
            each(128, inner),
            rows(inner),
            pl.BlockSpec((1, 128, inner), lambda n, c: (spot(n, c), 0, 0)),
            rows(128),
            full(4, channels),
            full(1, 128),
            full(1, inner),
            full(128, inner),
        ],
        out_specs=(
            rows(channels + 256),
            each(8, channels),
            pl.BlockSpec(memory_space=pltpu.VMEM),
            full(8, channels),
            full(8, 128),
        ),
        out_shape=(
            shape((total, channels + 256), BF16),
            shape((seqs, 8, channels), F32),
            shape((seqs, 8, channels), BF16),
            shape((8, channels), F32),
            shape((8, 128), F32),
        ),
        scratch_shapes=[
            pltpu.VMEM((128, inner), F32),
            pltpu.VMEM((3, 8, channels), F32),
            pltpu.VMEM((CHUNK, channels), F32),
            pltpu.VMEM((3, CHUNK, inner), F32),
            pltpu.VMEM((CHUNK, inner), F32),
            pltpu.VMEM((CHUNK + 16, GATE_BLOCK), F32),
            pltpu.VMEM((CHUNK, channels), F32),
            pltpu.VMEM((seqs, 8, channels), BF16),
            pltpu.VMEM((seqs, 8, channels), BF16),
            pltpu.SemaphoreType.DMA,
            pltpu.SemaphoreType.DMA,
        ],
        compiler_params=pltpu.CompilerParams(
            collective_id=3, has_side_effects=True, vmem_limit_bytes=48 * 1024 * 1024
        ),
        name="backward",
    )(
        summed,
        conv,
        halo,
        raw,
        cum,
        masks,
        seg_row,
        later,
        ssm_grad,
        starts,
        dots,
        taps,
        a_log,
        skip,
        heads_map,
    )


def input_kernel(
    tokens_ref, out_low_ref, gate_grad_ref, proj_grad_ref, weight_ref, gain_ref, grad_ref, sums_ref
):
    inner = gate_grad_ref.shape[1]
    rest = weight_ref.shape[0] - inner

    @pl.when(pl.program_id(0) == 0)
    def _():
        sums_ref[...] = jnp.zeros_like(sums_ref)

    normed_grad = mm(gate_grad_ref[...], weight_ref[:inner]) + mm(
        proj_grad_ref[:, :rest], weight_ref[inner:]
    )
    values = tokens_ref[...].astype(F32)
    scale = lax.rsqrt(jnp.mean(values * values, axis=-1, keepdims=True) + EPS)
    sums_ref[0:1] += jnp.sum(normed_grad * values * scale, axis=0, keepdims=True)
    pushed = normed_grad * gain_ref[...]
    inside = jnp.mean(pushed * values, axis=-1, keepdims=True)
    grad_ref[...] = (
        out_low_ref[...].astype(F32)
        + scale * pushed
        - values * (scale * scale * scale * inside)
    ).astype(BF16)


def input_gradient(tokens, out_low, gate_grad, proj_grad, weight, gain):
    total, model = tokens.shape
    block = 128
    rows = lambda width: pl.BlockSpec((block, width), lambda i: (i, 0))
    full = lambda *shape: pl.BlockSpec(shape, lambda i: (0,) * len(shape))
    return pl.pallas_call(
        input_kernel,
        grid=(total // block,),
        in_specs=[
            rows(model),
            rows(model),
            rows(gate_grad.shape[1]),
            rows(proj_grad.shape[1]),
            full(*weight.shape),
            full(1, model),
        ],
        out_specs=(rows(model), full(8, model)),
        out_shape=(
            jax.ShapeDtypeStruct((total, model), BF16),
            jax.ShapeDtypeStruct((8, model), F32),
        ),
        compiler_params=pltpu.CompilerParams(vmem_limit_bytes=48 * 1024 * 1024),
        name="input_gradient",
    )(tokens, out_low, gate_grad, proj_grad, weight, gain)


def weight_kernel(counts, out_low_ref, normed_ref, low_ref, gate_grad_ref, proj_grad_ref, grad_ref, turned):
    low_count, gate_count = counts
    step = pl.program_id(0)

    @pl.when(step == 0)
    def _():
        turned[0] = jnp.transpose(out_low_ref[...])
        turned[1] = jnp.transpose(normed_ref[...])

    def put(result):
        grad_ref[0] = result[:, :LANES].astype(BF16)
        grad_ref[1] = result[:, LANES:].astype(BF16)

    @pl.when(step < low_count)
    def _():
        put(mm(turned[0], low_ref[...]))

    @pl.when((step >= low_count) & (step < low_count + gate_count))
    def _():
        put(mm(turned[1], gate_grad_ref[...]))

    @pl.when(step >= low_count + gate_count)
    def _():
        put(mm(turned[1], proj_grad_ref[...]))


def weight_gradient(out_low, normed, low, gate_grad, proj_grad):
    total, model = normed.shape
    wide = 2 * LANES
    low_count, gate_count, proj_count = (a.shape[1] // wide for a in (low, gate_grad, proj_grad))
    full = lambda *shape: pl.BlockSpec(shape, lambda j: (0,) * len(shape))

    def columns(before, count):
        return pl.BlockSpec((total, wide), lambda j: (0, jnp.clip(j - before, 0, count - 1)))

    return pl.pallas_call(
        functools.partial(weight_kernel, (low_count, gate_count)),
        grid=(low_count + gate_count + proj_count,),
        in_specs=[
            full(total, model),
            full(total, model),
            columns(0, low_count),
            columns(low_count, gate_count),
            columns(low_count + gate_count, proj_count),
        ],
        out_specs=pl.BlockSpec((2, model, LANES), lambda j: (j, 0, 0)),
        out_shape=jax.ShapeDtypeStruct(
            (2 * (low_count + gate_count + proj_count), model, LANES), BF16
        ),
        scratch_shapes=[pltpu.VMEM((2, model, total), BF16)],
        compiler_params=pltpu.CompilerParams(vmem_limit_bytes=48 * 1024 * 1024),
        name="weight_gradient",
    )(out_low, normed, low, gate_grad, proj_grad)


def piece_kernel(
    counts, spot_ref, out_weight_ref, weight_ref, out_momentum_ref, momentum_ref, w_ref, m_ref, turned
):
    out_tiles, places, limit = counts
    tile = pl.program_id(0) * places + spot_ref[0]
    rows = m_ref.shape[1]
    mine = pl.ds(pl.multiple_of(spot_ref[1] * rows, 16), rows)

    @pl.when(tile < out_tiles)
    def _():
        turned[...] = jnp.transpose(out_weight_ref[...])
        w_ref[0] = turned[mine]
        m_ref[0] = out_momentum_ref[...]

    @pl.when(tile >= out_tiles)
    def _():
        turned[...] = jnp.transpose(weight_ref[...])
        w_ref[0] = turned[mine]
        m_ref[0] = momentum_ref[...]


def owned(spot, out_weight, weight_t, out_momentum_t, momentum, flows, places):
    inner, model = out_weight.shape
    rows, width = momentum.shape
    out_tiles, in_tiles = inner // LANES, -(-width // LANES)

    def out_at(f, spot):
        return jnp.clip(f * places + spot[0], 0, out_tiles - 1)

    def in_at(f, spot):
        return jnp.clip(f * places + spot[0] - out_tiles, 0, in_tiles - 1)

    piece = pl.BlockSpec((1, rows, LANES), lambda f, spot: (f, 0, 0))
    return pl.pallas_call(
        functools.partial(piece_kernel, (out_tiles, places, width)),
        grid_spec=pltpu.PrefetchScalarGridSpec(
            num_scalar_prefetch=1,
            grid=(flows,),
            in_specs=[
                pl.BlockSpec((LANES, model), lambda f, spot: (out_at(f, spot), 0)),
                pl.BlockSpec((LANES, model), lambda f, spot: (in_at(f, spot), 0)),
                pl.BlockSpec((rows, LANES), lambda f, spot: (0, out_at(f, spot))),
                pl.BlockSpec((rows, LANES), lambda f, spot: (0, in_at(f, spot))),
            ],
            out_specs=(piece, piece),
            scratch_shapes=[pltpu.VMEM((model, LANES), BF16)],
        ),
        out_shape=(
            jax.ShapeDtypeStruct((flows, rows, LANES), BF16),
            jax.ShapeDtypeStruct((flows, rows, LANES), F32),
        ),
        name="owned",
    )(spot, out_weight, weight_t, out_momentum_t, momentum)


def finish_kernel(
    out_steps,
    gathered_ref,
    out_momentum_ref,
    momentum_ref,
    out_weight_ref,
    weight_ref,
    new_out_momentum_ref,
    new_momentum_ref,
):
    group, slots, rows, _ = gathered_ref.shape
    step = pl.program_id(0)

    def write(weights, old, new):
        for i in range(group):
            at = slice(i * LANES, (i + 1) * LANES)
            tile = gathered_ref[i, : slots - 1].reshape((slots - 1) * rows, LANES)
            weights[at] = jnp.transpose(tile)
            new[:, at] = 0.5 * old[:, at] + gathered_ref[i, slots - 1].astype(F32)

    @pl.when(step < out_steps)
    def _():
        write(out_weight_ref, out_momentum_ref, new_out_momentum_ref)

    @pl.when(step >= out_steps)
    def _():
        write(weight_ref, momentum_ref, new_momentum_ref)


def finish(gathered, out_momentum_t, momentum, group=4):
    tiles, slots, rows, _ = gathered.shape
    width, inner = momentum.shape[1], out_momentum_t.shape[1]
    model = (slots - 1) * rows
    wide = group * LANES
    out_steps, in_steps = inner // wide, -(-width // wide)
    out_at = lambda j: jnp.minimum(j, out_steps - 1)
    in_at = lambda j: jnp.maximum(j - out_steps, 0)
    by_column = [
        pl.BlockSpec((rows, wide), lambda j: (0, out_at(j))),
        pl.BlockSpec((rows, wide), lambda j: (0, in_at(j))),
    ]
    shape = jax.ShapeDtypeStruct
    return pl.pallas_call(
        functools.partial(finish_kernel, out_steps),
        grid=(out_steps + in_steps,),
        in_specs=[pl.BlockSpec((group, slots, rows, LANES), lambda j: (j, 0, 0, 0))] + by_column,
        out_specs=[
            pl.BlockSpec((wide, model), lambda j: (out_at(j), 0)),
            pl.BlockSpec((wide, model), lambda j: (in_at(j), 0)),
        ]
        + by_column,
        out_shape=(
            shape((inner, model), BF16),
            shape((width, model), BF16),
            shape((rows, inner), F32),
            shape((rows, width), F32),
        ),
        name="finish",
    )(gathered, out_momentum_t, momentum)


def local(
    tokens,
    cotangent,
    segment_ids,
    doc_starts,
    valid_mask,
    step_number,
    learn_rate,
    norm_gain,
    in_weight,
    conv_weight,
    conv_bias,
    dt_bias,
    a_log,
    skip_d,
    gate_gain,
    out_weight,
    in_momentum,
    out_momentum,
):
    seqs, piece, model_width = tokens.shape
    heads = dt_bias.shape[0]
    tap_count, channels = conv_weight.shape
    inner_width = gate_gain.shape[0]
    proj_width = in_weight.shape[1]
    total = seqs * piece
    sizes = (seqs, piece, inner_width, channels, heads)
    places, pieces = lax.axis_size("dp"), lax.axis_size("seq")
    turn = lax.axis_index("seq")
    seg = segment_ids.astype(F32)
    sent = jnp.concatenate(
        [
            tokens[:, piece - HALO :],
            jnp.broadcast_to(seg[:, piece - HALO :, None], (seqs, HALO, LANES)).astype(BF16),
        ],
        axis=2,
    )
    route = [(i, i + 1) for i in range(pieces - 1)]
    arrived = lax.ppermute(sent, "seq", route)
    halo = arrived[:, :, :model_width].reshape(seqs * HALO, model_width)
    early_seg = jnp.where(turn == 0, -1.0, arrived[:, :, model_width].astype(F32))
    seg_pad = jnp.concatenate([early_seg, seg], axis=1)
    seg_row = seg.reshape(1, total)
    heads_map = (
        lax.broadcasted_iota(jnp.int32, (LANES, inner_width), 0)
        == lax.broadcasted_iota(jnp.int32, (LANES, inner_width), 1) // (inner_width // heads)
    ).astype(BF16)

    def lanes(values):
        return jnp.pad(values, (0, LANES - heads)).reshape(1, LANES)

    flat_tokens = tokens.reshape(total, model_width)
    weight_t = jnp.transpose(in_weight)
    out_momentum_t = jnp.transpose(out_momentum)
    flat_cot = cotangent.reshape(total, model_width)
    bias_row, decay_row = lanes(dt_bias), lanes(a_log)
    skip_row = jnp.repeat(skip_d, inner_width // heads).reshape(1, inner_width)
    gain_row = gate_gain.reshape(1, inner_width)
    normed, masks, gate, conv, conv_halo, summed, raw, cum, fresh, keep = front(
        flat_tokens,
        halo,
        norm_gain.reshape(1, model_width),
        weight_t,
        conv_weight,
        conv_bias.reshape(1, channels),
        seg_pad,
        valid_mask,
        bias_row,
        decay_row,
        heads_map,
        sizes,
    )
    incoming = chain(fresh, keep, 1)
    output, low, out_low, gate_grad, ssm_grad, starts, dots, squares, wide, state_grad = forward(
        summed,
        gate,
        raw,
        cum,
        masks,
        seg_row,
        incoming,
        flat_tokens,
        flat_cot,
        out_weight,
        gain_row,
        skip_row,
        heads_map,
        sizes,
    )
    later = chain(state_grad, keep, -1)
    proj_grad, tail, rim, conv_sums, head_sums = backward(
        summed,
        conv,
        conv_halo,
        raw,
        cum,
        masks,
        seg_row,
        later,
        ssm_grad,
        starts,
        dots,
        conv_weight,
        decay_row,
        skip_row,
        heads_map,
        sizes,
    )
    fixed = (tail + rim.astype(F32)).astype(BF16)
    proj_grad = (
        proj_grad.reshape(seqs, piece, -1)
        .at[:, piece - 8 :, :channels]
        .set(fixed)
        .reshape(total, -1)
    )
    input_grad, gain_sums = input_gradient(
        flat_tokens, out_low, gate_grad, proj_grad, weight_t, norm_gain.reshape(1, model_width)
    )
    grad_tiles = weight_gradient(out_low, normed, low, gate_grad, proj_grad)
    share_rows = model_width // pieces
    flows = -(-grad_tiles.shape[0] // places)
    grad_tiles = jnp.pad(
        grad_tiles, ((0, flows * places - grad_tiles.shape[0]), (0, 0), (0, 0))
    )
    grads = grad_tiles.reshape(flows, places, pieces, share_rows, LANES)
    step_float = step_number[0].astype(F32)
    rate_now = learn_rate[0] * step_float / (step_float + 16.0)
    spot = jnp.stack([lax.axis_index("dp"), turn]).astype(jnp.int32)
    own_weight, own_momentum = owned(
        spot, out_weight, weight_t, out_momentum_t, in_momentum, flows, places
    )
    gathered, totals = exchange(
        rate_now.reshape(1),
        grads,
        own_weight,
        own_momentum,
        (conv_sums, wide, head_sums, gain_sums, squares),
    )
    new_out_weight, new_weight_t, new_out_momentum_t, new_in_momentum = finish(
        gathered.reshape(flows * places, pieces + 1, share_rows, LANES),
        out_momentum_t,
        in_momentum,
    )
    new_in_weight = jnp.transpose(new_weight_t)
    new_out_momentum = jnp.transpose(new_out_momentum_t)
    conv_weight_total = totals[:tap_count]
    conv_bias_total = totals[tap_count]
    gate_gain_total = totals[5, :inner_width]
    skip_total = totals[6, :inner_width].reshape(heads, -1).sum(axis=1)
    norm_gain_total = totals[7, :model_width]
    dt_bias_total = totals[5, inner_width : inner_width + heads]
    a_log_total = totals[6, inner_width : inner_width + heads]
    out_square_total = totals[5, inner_width + LANES :].sum()
    mix_square_total = totals[6, inner_width + LANES :].sum()
    valid_total = totals[7, inner_width + LANES + 9]
    denominator = jnp.maximum(valid_total, 1.0) * model_width
    output_rms = jnp.sqrt(out_square_total / denominator).reshape(1)
    mixer_rms = jnp.sqrt(mix_square_total / denominator).reshape(1)
    return (
        output.reshape(tokens.shape),
        input_grad.reshape(tokens.shape),
        new_in_weight,
        new_out_weight,
        new_in_momentum,
        new_out_momentum,
        norm_gain_total,
        conv_weight_total,
        conv_bias_total,
        dt_bias_total,
        a_log_total,
        skip_total,
        gate_gain_total,
        output_rms,
        mixer_rms,
    )


def solution(mesh):
    placed = (
        P("dp", "seq", None),
        P("dp", "seq", None),
        P("dp", "seq"),
        P("dp", "seq"),
        P("dp", "seq"),
        P(),
        P(),
        P(),
        P(),
        P(),
        P(),
        P(),
        P(),
        P(),
        P(),
        P(),
        P("seq", None),
        P(None, "seq"),
    )
    return jax.shard_map(
        local,
        mesh=mesh,
        in_specs=placed,
        out_specs=(
            P("dp", "seq", None),
            P("dp", "seq", None),
            P(),
            P(),
            P("seq", None),
            P(None, "seq"),
            P(),
            P(),
            P(),
            P(),
            P(),
            P(),
            P(),
            P(),
            P(),
        ),
        check_vma=False,
    )
```

```python
import functools

import jax
import jax.numpy as jnp
from jax import lax
from jax.experimental import pallas as pl
from jax.experimental.pallas import tpu as pltpu
from jax.sharding import PartitionSpec as P

CHUNK = 128
HALO = 16
GATE_BLOCK = 256
EPS = 1e-05
NEGATIVE = -1e30
F32, BF16 = jnp.float32, jnp.bfloat16
LANES = 128
MESH = pl.DeviceIdType.MESH


def remote(src, dst, send, recv, target):
    return pltpu.make_async_remote_copy(
        src_ref=src,
        dst_ref=dst,
        send_sem=send,
        recv_sem=recv,
        device_id=target,
        device_id_type=MESH,
    )


def greet(targets):
    barrier = pltpu.get_barrier_semaphore()
    for target in targets:
        pl.semaphore_signal(barrier, inc=1, device_id=target, device_id_type=MESH)
    pl.semaphore_wait(barrier, len(targets))


class Exchange:
    def __init__(self, bits, pieces, flows):
        self.bits, self.pieces, self.flows = bits, pieces, flows
        self.parts = 2 if pieces % 2 == 0 else 1
        self.place, self.turn = lax.axis_index("dp"), lax.axis_index("seq")
        self.own = [(self.place // (1 << b)) % 2 for b in range(bits)]
        self.partner = [
            {"dp": self.place + (1 - 2 * self.own[b]) * (1 << b)} for b in range(bits)
        ]
        self.others = [{"seq": lax.rem(self.turn + j, pieces)} for j in range(pieces)]
        self.mine = self.index_of({b: self.own[b] for b in range(bits)})

    def index_of(self, fixed):
        return tuple(fixed.get(b, slice(None)) for b in range(self.bits - 1, -1, -1))

    def order_of(self, f, h):
        rest = list(range(1, self.bits))
        shift = (f + h) % max(len(rest), 1)
        return [0] + rest[shift:] + rest[:shift]

    def share(self, h, extra=0):
        half = self.pieces // self.parts
        return pl.ds(h * half, half + (extra if h == self.parts - 1 else 0))

    def held(self, f, h, k, other):
        order = self.order_of(f, h)
        bit = order[k]
        value = 1 - self.own[bit] if other else self.own[bit]
        free = [b for b in range(self.bits - 1, -1, -1) if b not in order[:k]]
        source = self.grad if k == 0 else self.halves[k - 1]
        return source.at[
            (f,) + tuple(value if b == bit else slice(None) for b in free) + (self.share(h),)
        ]

    def landing(self, f, h, k):
        free = self.bits - k - 1
        return self.halves[k].at[(f,) + (slice(None),) * free + (self.share(h),)]

    def rs_copy(self, f, h, k):
        return remote(
            self.held(f, h, k, True),
            self.landing(f, h, k),
            self.rs_send.at[f, h, k],
            self.rs_recv.at[f, h, k],
            self.partner[self.order_of(f, h)[k]],
        )

    def rs_begin(self, k, flow=None):
        for f in range(self.flows) if flow is None else (flow,):
            for h in range(self.parts):
                self.rs_copy(f, h, k).start()

    def rs_end(self, k, then=None):
        for f in range(self.flows):
            for h in range(self.parts):
                self.rs_copy(f, h, k).wait_recv()
                kept, into = self.held(f, h, k, False), self.landing(f, h, k)
                left = self.bits - k - 1
                for count in range(1 << left):
                    spot = tuple((count >> (left - 1 - i)) & 1 for i in range(left))

                    def body(p, carry, spot=spot, kept=kept, into=into):
                        into[spot + (p,)] = (
                            kept[spot + (p,)].astype(F32) + into[spot + (p,)].astype(F32)
                        ).astype(BF16)
                        return carry

                    lax.fori_loop(0, self.pieces // self.parts, body, 0)
                if k + 1 < self.bits and then:
                    self.rs_copy(f, h, k + 1).start()
            if k + 1 == self.bits and then:
                self.zs_begin(f)

    def rs_done(self, k):
        for f in range(self.flows):
            for h in range(self.parts):
                self.rs_copy(f, h, k).wait_send()

    def zs_copy(self, f, j):
        return remote(
            self.halves[self.bits - 1].at[f, lax.rem(self.turn + j, self.pieces)],
            self.piece_parts.at[f, j],
            self.zs_send.at[f, j],
            self.zs_recv.at[f, j],
            self.others[j],
        )

    def zs_begin(self, flow=None):
        for f in range(self.flows) if flow is None else (flow,):
            for j in range(1, self.pieces):
                self.zs_copy(f, j).start()

    def zs_end(self, rate, weight, momentum, put):
        for f in range(self.flows):
            for j in range(1, self.pieces):
                self.zs_copy(f, j).wait_recv()
            total = self.halves[self.bits - 1][f, self.turn].astype(F32)
            for j in range(1, self.pieces):
                total = total + self.piece_parts[f, j].astype(F32)
            summed = total.astype(BF16)
            moved = 0.5 * momentum[f] + summed.astype(F32)
            put(f, summed, (weight[f].astype(F32) - rate * moved).astype(BF16))

    def zs_done(self):
        for f in range(self.flows):
            for j in range(1, self.pieces):
                self.zs_copy(f, j).wait_send()

    def put(self, f, summed, updated):
        self.gathered[(f,) + self.mine + (self.pieces,)] = summed
        self.gathered[(f,) + self.mine + (self.turn,)] = updated

    def zg_copy(self, f, j):
        spot = self.gathered.at[(f,) + self.mine + (self.turn,)]
        return remote(spot, spot, self.zg_send.at[f, j], self.zg_recv.at[f, j], self.others[j])

    def zg_begin(self, flow=None):
        for f in range(self.flows) if flow is None else (flow,):
            for j in range(1, self.pieces):
                self.zg_copy(f, j).start()

    def zg_end(self):
        for f in range(self.flows):
            for j in range(1, self.pieces):
                self.zg_copy(f, j).wait_recv()
            for h in range(self.parts):
                self.ag_copy(f, h, self.bits - 1).start()

    def zg_done(self):
        for f in range(self.flows):
            for j in range(1, self.pieces):
                self.zg_copy(f, j).wait_send()

    def ag_copy(self, f, h, k):
        order = self.order_of(f, h)
        fixed = {order[i]: self.own[order[i]] for i in range(k + 1)}
        spot = self.gathered.at[(f,) + self.index_of(fixed) + (self.share(h, 1),)]
        return remote(
            spot,
            spot,
            self.ag_send.at[f, h, k],
            self.ag_recv.at[f, h, k],
            self.partner[order[k]],
        )

    def ag_end(self, k):
        for f in range(self.flows):
            for h in range(self.parts):
                self.ag_copy(f, h, k).wait_recv()
                if k > 0:
                    self.ag_copy(f, h, k - 1).start()

    def ag_done(self):
        for k in range(self.bits):
            for f in range(self.flows):
                for h in range(self.parts):
                    self.ag_copy(f, h, k).wait_send()


def dma_semaphores(*shape):
    return [pltpu.SemaphoreType.DMA(shape)] * 2


def part_count(pieces):
    return 2 if pieces % 2 == 0 else 1


def half_shape(bits, pieces, flows, rows, k):
    return (flows,) + (2,) * (bits - k - 1) + (pieces, rows, LANES)


def mm(a, b):
    return jnp.dot(a, b, preferred_element_type=F32)


def mm_nt(a, b):
    return lax.dot_general(a, b, (((1,), (1,)), ((), ())), preferred_element_type=F32)


def mm_tn(a, b):
    return lax.dot_general(a, b, (((0,), (0,)), ((), ())), preferred_element_type=F32)


def split(a):
    high = a.astype(BF16)
    return high, (a - high.astype(F32)).astype(BF16)


def exact_mm(a, b):
    return jnp.dot(a, b, preferred_element_type=F32, precision=lax.Precision.HIGHEST)


def spread(a, heads_ref):
    high, low = split(a)
    return mm(high, heads_ref[...]) + mm(low, heads_ref[...])


def gather_heads(a, heads_ref):
    high, low = split(a)
    return mm_nt(high, heads_ref[...]) + mm_nt(low, heads_ref[...])


def sigmoid(v):
    return 1.0 / (1.0 + jnp.exp(-v))


def softplus(v):
    return jnp.maximum(v, 0.0) + jnp.log1p(jnp.exp(-jnp.abs(v)))


def triangle(size, upper):
    row = lax.broadcasted_iota(jnp.int32, (size, size), 0)
    column = lax.broadcasted_iota(jnp.int32, (size, size), 1)
    return ((row <= column) if upper else (row >= column)).astype(F32)


def front_kernel(
    sizes,
    tokens_ref,
    halo_ref,
    gain_ref,
    weight_ref,
    taps_ref,
    bias_ref,
    seg_ref,
    valid_ref,
    dt_bias_ref,
    a_log_ref,
    heads_ref,
    normed_ref,
    masks_ref,
    gate_ref,
    conv_ref,
    halo_out_ref,
    summed_ref,
    raw_ref,
    cum_ref,
    state_ref,
    keep_ref,
    padded,
    product,
    active,
):
    seqs, piece, inner, channels, heads = sizes
    gate_blocks, conv_blocks = inner // GATE_BLOCK, channels // GATE_BLOCK
    step = pl.program_id(0)
    stride = piece + HALO

    @pl.when(step == 0)
    def _():
        gain = gain_ref[...]
        for n in range(seqs):
            padded_seg = seg_ref[n : n + 1]
            seg = padded_seg[:, HALO:]

            def over_chunks(at):
                return jnp.concatenate(
                    [
                        jnp.broadcast_to(
                            padded_seg[:, c * CHUNK + at : c * CHUNK + at + 1], (1, CHUNK)
                        )
                        for c in range(piece // CHUNK)
                    ],
                    axis=1,
                )

            others = [padded_seg[:, HALO - 3 + k : HALO - 3 + k + piece] for k in range(4)] + [
                over_chunks(HALO - 1),
                over_chunks(HALO + CHUNK - 1),
                jnp.broadcast_to(padded_seg[:, HALO - 1 : HALO], (1, piece)),
                jnp.broadcast_to(padded_seg[:, HALO + piece - 1 :], (1, piece)),
            ]
            lines = [(other == seg).astype(F32) for other in others] + [
                seg,
                valid_ref[n : n + 1].astype(F32),
            ]
            lines = lines + [jnp.zeros_like(seg)] * (16 - len(lines))
            masks_ref[pl.ds(n * piece, piece)] = jnp.transpose(jnp.concatenate(lines, axis=0))
            for source, start, to, count in (
                (halo_ref, n * HALO, n * stride, HALO),
                (tokens_ref, n * piece, n * stride + HALO, piece),
            ):

                def body(i, carry):
                    values = source[pl.ds(pl.multiple_of(start + i * 16, 16), 16)].astype(F32)
                    scale = lax.rsqrt(jnp.mean(values * values, axis=-1, keepdims=True) + EPS)
                    low = (values * scale * gain).astype(BF16)
                    padded[pl.ds(pl.multiple_of(to + i * 16, 16), 16)] = low
                    return carry

                lax.fori_loop(0, count // 16, body, 0)
            normed_ref[pl.ds(n * piece, piece)] = padded[pl.ds(n * stride + HALO, piece)]

    product[...] = mm_nt(padded[...], weight_ref[...])

    @pl.when(step < gate_blocks)
    def _():
        for n in range(seqs):
            gate_ref[pl.ds(n * piece, piece)] = product[pl.ds(n * stride + HALO, piece)]

    @pl.when((step >= gate_blocks) & (step < gate_blocks + conv_blocks))
    def _():
        at = pl.multiple_of((step - gate_blocks) * GATE_BLOCK, GATE_BLOCK)
        for n in range(seqs):
            conv_ref[pl.ds(n * piece, piece)] = product[pl.ds(n * stride + HALO, piece)]
            halo_out_ref[pl.ds(n * HALO, HALO)] = product[pl.ds(n * stride, HALO)]
            for i in range(piece // 64):
                rows = pl.ds(n * piece + i * 64, 64)
                total = jnp.broadcast_to(bias_ref[...], (64, GATE_BLOCK))
                for k in range(4):
                    source = product[pl.ds(n * stride + HALO - 3 + k + i * 64, 64)]
                    total = total + source * masks_ref[rows, k : k + 1] * taps_ref[k : k + 1]
                summed_ref[rows] = total
                active[rows, pl.ds(at, GATE_BLOCK)] = (total * sigmoid(total)).astype(BF16)

    @pl.when(step == gate_blocks + conv_blocks)
    def _():
        lane = lax.broadcasted_iota(jnp.int32, (piece, 128), 1)
        lower = triangle(CHUNK, False)
        for n in range(seqs):
            rows = pl.ds(n * piece, piece)
            raw = jnp.where(lane < heads, product[pl.ds(n * stride + HALO, piece), :128], 0.0)
            raw = raw + dt_bias_ref[...]
            raw_ref[rows] = raw
            steps = jnp.where(lane < heads, softplus(raw), 0.0)
            decay = -jnp.exp(a_log_ref[...]) * steps
            total = jnp.zeros((1, 128), F32)
            pieces = []
            for c in range(piece // CHUNK):
                cumulative = exact_mm(lower, decay[c * CHUNK : (c + 1) * CHUNK])
                cum_ref[pl.ds(n * piece + c * CHUNK, CHUNK)] = cumulative
                pieces.append(cumulative + total)
                total = total + cumulative[CHUNK - 1 :]
            whole = jnp.concatenate(pieces, axis=0) if len(pieces) > 1 else pieces[0]
            tails = jnp.exp(total - whole) * steps * masks_ref[rows, 7:8]
            weighted = (spread(tails, heads_ref) * active[rows, :inner].astype(F32)).astype(BF16)
            state_ref[n] = mm_tn(active[rows, inner : inner + 128], weighted)
            last = masks_ref[n * piece + piece - 1 : n * piece + piece, 6:7]
            keep = jnp.exp(total) * last
            keep_ref[n] = spread(jnp.broadcast_to(keep, (8, 128)), heads_ref)


def front(tokens, halo, gain, weight, taps, bias, segs, valid, dt_bias, a_log, heads_map, sizes):
    seqs, piece, inner, channels, heads = sizes
    total, model = tokens.shape
    stride = seqs * (piece + HALO)
    gate_blocks, conv_blocks = inner // GATE_BLOCK, channels // GATE_BLOCK
    full = lambda *shape: pl.BlockSpec(shape, lambda j: (0,) * len(shape))

    def conv_at(j):
        return (0, jnp.clip(j - gate_blocks, 0, conv_blocks - 1))

    return pl.pallas_call(
        functools.partial(front_kernel, sizes),
        grid=(gate_blocks + conv_blocks + 1,),
        in_specs=[
            full(total, model),
            full(seqs * HALO, model),
            full(1, model),
            pl.BlockSpec((GATE_BLOCK, model), lambda j: (j, 0)),
            pl.BlockSpec((4, GATE_BLOCK), conv_at),
            pl.BlockSpec((1, GATE_BLOCK), conv_at),
            full(*segs.shape),
            full(*valid.shape),
            full(1, 128),
            full(1, 128),
            full(128, inner),
        ],
        out_specs=(
            full(total, model),
            full(total, 16),
            pl.BlockSpec((total, GATE_BLOCK), lambda j: (0, jnp.minimum(j, gate_blocks - 1))),
            pl.BlockSpec((total, GATE_BLOCK), conv_at),
            pl.BlockSpec((seqs * HALO, GATE_BLOCK), conv_at),
            pl.BlockSpec((total, GATE_BLOCK), conv_at),
            full(total, 128),
            full(total, 128),
            full(seqs, 128, inner),
            full(seqs, 8, inner),
        ),
        out_shape=(
            jax.ShapeDtypeStruct((total, model), BF16),
            jax.ShapeDtypeStruct((total, 16), F32),
            jax.ShapeDtypeStruct((total, inner), F32),
            jax.ShapeDtypeStruct((total, channels), F32),
            jax.ShapeDtypeStruct((seqs * HALO, channels), F32),
            jax.ShapeDtypeStruct((total, channels), F32),
            jax.ShapeDtypeStruct((total, 128), F32),
            jax.ShapeDtypeStruct((total, 128), F32),
            jax.ShapeDtypeStruct((seqs, 128, inner), F32),
            jax.ShapeDtypeStruct((seqs, 8, inner), F32),
        ),
        scratch_shapes=[
            pltpu.VMEM((stride, model), BF16),
            pltpu.VMEM((stride, GATE_BLOCK), F32),
            pltpu.VMEM((total, channels), BF16),
        ],
        compiler_params=pltpu.CompilerParams(vmem_limit_bytes=48 * 1024 * 1024),
        name="front",
    )(tokens, halo, gain, weight, taps, bias, segs, valid, dt_bias, a_log, heads_map)


def chain_kernel(ways, blocks, own_ref, keep_ref, out_ref, sent, taken, send, recv):
    size = lax.axis_size("seq")
    turn = lax.axis_index("seq")
    first = turn == (0 if ways > 0 else size - 1)
    final = turn == (size - 1 if ways > 0 else 0)
    ahead = {"seq": lax.rem(turn + ways + size, size)}
    behind = {"seq": lax.rem(turn - ways + size, size)}
    barrier = pltpu.get_barrier_semaphore()

    @pl.when(jnp.logical_not(first))
    def _():
        pl.semaphore_signal(
            barrier, inc=1, device_id=behind, device_id_type=pl.DeviceIdType.MESH
        )

    @pl.when(jnp.logical_not(final))
    def _():
        pl.semaphore_wait(barrier, 1)

    width = own_ref.shape[2] // blocks

    def copy(c):
        return pltpu.make_async_remote_copy(
            src_ref=sent.at[c],
            dst_ref=taken.at[c],
            send_sem=send.at[c],
            recv_sem=recv.at[c],
            device_id=ahead,
            device_id_type=pl.DeviceIdType.MESH,
        )

    @pl.when(first)
    def _():
        out_ref[...] = jnp.zeros_like(out_ref)
        for c in range(blocks):
            at = slice(c * width, (c + 1) * width)
            sent[c] = own_ref[:, :, at].astype(BF16)
            copy(c).start()

    @pl.when(jnp.logical_not(first))
    def _():
        for c in range(blocks):
            at = slice(c * width, (c + 1) * width)
            copy(c).wait_recv()

            @pl.when(jnp.logical_not(final))
            def _():
                sent[c] = (
                    own_ref[:, :, at] + keep_ref[:, 0:1, at] * taken[c].astype(F32)
                ).astype(BF16)
                copy(c).start()

            out_ref[:, :, at] = taken[c].astype(F32)

    @pl.when(jnp.logical_not(final))
    def _():
        for c in range(blocks):
            copy(c).wait_send()


def chain(own, keep, ways, blocks=6):
    seqs, depth, inner = own.shape
    vmem = pl.BlockSpec(memory_space=pltpu.VMEM)
    part = (blocks, seqs, depth, inner // blocks)
    return pl.pallas_call(
        functools.partial(chain_kernel, ways, blocks),
        out_shape=jax.ShapeDtypeStruct(own.shape, F32),
        in_specs=[vmem, vmem],
        out_specs=vmem,
        scratch_shapes=[pltpu.VMEM(part, BF16)] * 2 + [pltpu.SemaphoreType.DMA((blocks,))] * 2,
        compiler_params=pltpu.CompilerParams(
            collective_id=1 if ways > 0 else 2,
            has_side_effects=True,
            vmem_limit_bytes=32 * 1024 * 1024,
        ),
        name="chain",
    )(own, keep)


def decays_of(cum, cum_t, bias, h):
    return jnp.exp(cum[:, h : h + 1] - cum_t[h : h + 1, :] + bias)


def mask_bias(seg_col, seg_row):
    row = lax.broadcasted_iota(jnp.int32, (CHUNK, CHUNK), 0)
    column = lax.broadcasted_iota(jnp.int32, (CHUNK, CHUNK), 1)
    return jnp.where((row >= column) & (seg_col == seg_row), 0.0, NEGATIVE)


def scores_of(reader, writer):
    rh, rl = split(reader)
    wh, wl = split(writer)
    return mm_nt(rh, wh) + (mm_nt(rh, wl) + mm_nt(rl, wh))


def forward_kernel(
    sizes,
    chunks,
    summed_ref,
    gate_ref,
    raw_ref,
    cum_ref,
    masks_ref,
    seg_row_ref,
    incoming_ref,
    tokens_ref,
    cot_ref,
    weight_ref,
    gain_ref,
    skip_ref,
    heads_ref,
    output_ref,
    low_ref,
    out_low_ref,
    gate_grad_ref,
    ssm_grad_ref,
    starts_ref,
    dot_ref,
    sums_ref,
    wide_ref,
    state_grad_ref,
    state,
    prefix,
    active,
    mixed_in,
    factors,
    grads,
    inv,
):
    seqs, piece, inner, channels, heads = sizes
    c = pl.program_id(1)

    @pl.when((c == 0) & (pl.program_id(0) == 0))
    def _():
        sums_ref[...] = jnp.zeros_like(sums_ref)
        wide_ref[...] = jnp.zeros_like(wide_ref)

    @pl.when(c == 0)
    def _():
        state[...] = incoming_ref[0]
        prefix[...] = jnp.zeros_like(prefix)
        state_grad_ref[...] = jnp.zeros_like(state_grad_ref)

    def activate(i, carry):
        rows = pl.ds(pl.multiple_of(i * 16, 16), 16)
        values = summed_ref[rows]
        active[rows] = values * sigmoid(values)
        return carry

    lax.fori_loop(0, CHUNK // 16, activate, 0)
    lane = lax.broadcasted_iota(jnp.int32, (CHUNK, 128), 1)
    steps = jnp.where(lane < heads, softplus(raw_ref[...]), 0.0)
    cum = cum_ref[...]
    cum_t = jnp.transpose(cum)
    final = cum[CHUNK - 1 :]
    enter = jnp.exp(cum) * masks_ref[:, 4:5]
    tails = jnp.exp(final - cum) * steps * masks_ref[:, 5:6]
    from_start = jnp.exp(cum + prefix[0:1]) * masks_ref[:, 6:7]
    prefix[...] = prefix[...] + final
    for i, block in enumerate((steps, enter, tails, from_start)):
        factors[i] = spread(block, heads_ref)
    writer = active[:, inner : inner + 128]
    reader = active[:, inner + 128 : inner + 256]
    scores = scores_of(reader, writer)
    bias = mask_bias(masks_ref[:, 8:9], seg_row_ref[0:1])
    half = lax.broadcasted_iota(jnp.int32, (CHUNK, 128), 1) < 64
    state_low = state[...].astype(BF16)
    starts_ref[0] = state_low
    reader_low = reader.astype(BF16)
    for pair in range(heads // 2):
        at = slice(pair * 128, (pair + 1) * 128)
        moved = (active[:, at] * factors[0, :, at]).astype(BF16)
        zero = jnp.zeros_like(moved)
        one = (scores * decays_of(cum, cum_t, bias, 2 * pair)).astype(BF16)
        two = (scores * decays_of(cum, cum_t, bias, 2 * pair + 1)).astype(BF16)
        both = jnp.concatenate([one, two], axis=1)
        stacked = jnp.concatenate(
            [jnp.where(half, moved, zero), jnp.where(half, zero, moved)], axis=0
        )
        carried = mm(reader_low, state_low[:, at]) * factors[1, :, at]
        mixed_in[:, at] = mm(both, stacked) + carried
    weighted = (active[:, :inner] * factors[2]).astype(BF16)
    kept = jnp.exp(final) * masks_ref[CHUNK - 1 :, 4:5]
    kept = spread(jnp.broadcast_to(kept, (8, 128)), heads_ref)[0:1]
    state[...] = state[...] * kept + mm_tn(writer.astype(BF16), weighted)

    gain = gain_ref[...]
    skip = skip_ref[...]

    def gating(i, carry):
        rows = pl.ds(pl.multiple_of(i * 16, 16), 16)
        gate = gate_ref[rows]
        mixer = mixed_in[rows] + skip * active[rows, :inner]
        gated = mixer * gate * sigmoid(gate)
        scale = lax.rsqrt(jnp.mean(gated * gated, axis=-1, keepdims=True) + EPS)
        inv[rows] = jnp.broadcast_to(scale, (16, 128))
        low_ref[rows] = (gated * scale * gain).astype(BF16)
        return carry

    lax.fori_loop(0, CHUNK // 16, gating, 0)
    mixed = mm(low_ref[...], weight_ref[...])
    block_out = tokens_ref[...].astype(F32) + mixed
    output_ref[...] = block_out.astype(BF16)
    valid = masks_ref[:, 9:10]
    for i, block in enumerate((block_out, mixed)):
        squares = jnp.sum(valid * block * block, axis=0, keepdims=True)
        for at in range(0, squares.shape[1], 128):
            sums_ref[i : i + 1] += squares[:, at : at + 128]
    sums_ref[2:3, :16] += jnp.sum(masks_ref[...], axis=0, keepdims=True)
    out_low = (cot_ref[...].astype(F32) * valid).astype(BF16)
    out_low_ref[...] = out_low
    grads[...] = mm_nt(out_low, weight_ref[...])

    def backing(i, carry):
        gain_sum, skip_sum = carry
        rows = pl.ds(pl.multiple_of(i * 16, 16), 16)
        gate = gate_ref[rows]
        turned = sigmoid(gate)
        silu = gate * turned
        signal = active[rows, :inner]
        mixer = mixed_in[rows] + skip * signal
        gated = mixer * silu
        scale = inv[rows, 0:1]
        grad = grads[rows]
        gain_sum = gain_sum + grad * gated * scale
        grad = grad * gain
        inside = jnp.mean(grad * gated, axis=-1, keepdims=True)
        gated_grad = scale * grad - gated * (scale * scale * scale * inside)
        ssm_grad = gated_grad * silu
        ssm_grad_ref[rows] = ssm_grad
        grads[rows] = ssm_grad
        skip_sum = skip_sum + ssm_grad * signal
        gate_grad_ref[rows] = (gated_grad * mixer * turned * (1.0 + gate * (1.0 - turned))).astype(
            BF16
        )
        return gain_sum, skip_sum

    start = jnp.zeros((16, inner), F32)
    gain_sum, skip_sum = lax.fori_loop(0, CHUNK // 16, backing, (start, start))
    wide_ref[0:1] += jnp.sum(gain_sum, axis=0, keepdims=True)
    wide_ref[1:2] += jnp.sum(skip_sum, axis=0, keepdims=True)
    reader_t = jnp.transpose(reader_low)
    for pair in range(heads // 2):
        at = slice(pair * 128, (pair + 1) * 128)
        state_grad_ref[0, :, at] += mm(
            reader_t, (grads[:, at] * factors[3, :, at]).astype(BF16)
        )
        mixed_in[:, at] = mixed_in[:, at] * grads[:, at].astype(BF16).astype(F32)
    dot_ref[...] = gather_heads(mixed_in[...], heads_ref)


def forward(
    summed, gate, raw, cum, masks, seg_row, incoming, tokens, cot, weight, gain, skip, heads_map, sizes
):
    seqs, piece, inner, channels, heads = sizes
    total, model = tokens.shape
    chunks = piece // CHUNK
    full = lambda *shape: pl.BlockSpec(shape, lambda n, c: (0,) * len(shape))
    rows = lambda width: pl.BlockSpec((CHUNK, width), lambda n, c: (n * chunks + c, 0))
    each = lambda depth: pl.BlockSpec((1, depth, inner), lambda n, c: (n, 0, 0))
    shape = jax.ShapeDtypeStruct
    return pl.pallas_call(
        functools.partial(forward_kernel, sizes, chunks),
        grid=(seqs, chunks),
        in_specs=[
            rows(channels),
            rows(inner),
            rows(128),
            rows(128),
            rows(16),
            pl.BlockSpec((1, CHUNK), lambda n, c: (0, n * chunks + c)),
            each(128),
            rows(model),
            rows(model),
            full(inner, model),
            full(1, inner),
            full(1, inner),
            full(128, inner),
        ],
        out_specs=(
            rows(model),
            rows(inner),
            rows(model),
            rows(inner),
            rows(inner),
            pl.BlockSpec((1, 128, inner), lambda n, c: (n * chunks + c, 0, 0)),
            rows(128),
            full(8, 128),
            full(8, inner),
            each(128),
        ),
        out_shape=(
            shape((total, model), BF16),
            shape((total, inner), BF16),
            shape((total, model), BF16),
            shape((total, inner), BF16),
            shape((total, inner), F32),
            shape((seqs * chunks, 128, inner), BF16),
            shape((total, 128), F32),
            shape((8, 128), F32),
            shape((8, inner), F32),
            shape((seqs, 128, inner), F32),
        ),
        scratch_shapes=[
            pltpu.VMEM((128, inner), F32),
            pltpu.VMEM((8, 128), F32),
            pltpu.VMEM((CHUNK, channels), F32),
            pltpu.VMEM((CHUNK, inner), F32),
            pltpu.VMEM((4, CHUNK, inner), F32),
            pltpu.VMEM((CHUNK, inner), F32),
            pltpu.VMEM((CHUNK, 128), F32),
        ],
        compiler_params=pltpu.CompilerParams(vmem_limit_bytes=48 * 1024 * 1024),
        name="forward",
    )(summed, gate, raw, cum, masks, seg_row, incoming, tokens, cot, weight, gain, skip, heads_map)


def backward_kernel(
    sizes,
    dims,
    rate_ref,
    summed_all,
    conv_all,
    halo_all,
    raw_all,
    cum_all,
    masks_all,
    seg_row_all,
    later_ref,
    ssm_grad_all,
    starts_all,
    dot_all,
    taps_ref,
    a_log_ref,
    skip_ref,
    heads_ref,
    half_ref,
    weight_ref,
    momentum_ref,
    proj_grad_all,
    conv_sums_ref,
    head_sums_ref,
    piece_ref,
    state_grad,
    after,
    active,
    factors,
    moved_grad,
    shifted_rows,
    all_grad,
    rims,
    rims_in,
    tails_out,
    *scratch,
):
    seqs, piece, inner, channels, heads = sizes
    bits, pieces, flows = dims
    chunks = piece // CHUNK
    ex = Exchange(bits, pieces, flows)
    ex.halves = [half_ref] + list(scratch[: bits - 1])
    (ex.piece_parts, ex.rs_send, ex.rs_recv, ex.zs_send, ex.zs_recv) = scratch[bits - 1 : bits + 4]
    rim_send, rim_recv = scratch[bits + 4 :]
    turn = ex.turn
    rim_copy = remote(
        rims, rims_in, rim_send, rim_recv, {"seq": lax.rem(turn + pieces - 1, pieces)}
    )
    greet(ex.partner[1:] + ex.others[1:])
    conv_sums_ref[...] = jnp.zeros_like(conv_sums_ref)
    head_sums_ref[...] = jnp.zeros_like(head_sums_ref)
    slots = 2 * seqs * chunks
    starts_at = [0, 3, 5] if (bits, slots) == (3, 8) else [i * slots // bits for i in range(bits)]

    def begin(k):
        if k < bits:
            ex.rs_begin(k)
        else:
            ex.zs_begin()

    def hook(spot):
        for i, at in enumerate(starts_at):

            @pl.when(spot == at)
            def _(i=i):
                if i > 0:
                    ex.rs_end(i)
                begin(i + 1)

    def one_chunk(index, carry):
        n, c = index // chunks, lax.rem(index, chunks)
        spot = n * chunks + chunks - 1 - c
        rows_at = pl.ds(pl.multiple_of(spot * CHUNK, CHUNK), CHUNK)
        summed_ref, conv_ref = summed_all.at[rows_at], conv_all.at[rows_at]
        halo_ref = halo_all.at[pl.ds(pl.multiple_of(n * HALO, HALO), HALO)]
        raw_ref, cum_ref, masks_ref = raw_all.at[rows_at], cum_all.at[rows_at], masks_all.at[rows_at]
        seg_row = seg_row_all[0:1, rows_at]
        ssm_grad_ref, dot_ref = ssm_grad_all.at[rows_at], dot_all.at[rows_at]
        starts_ref = starts_all.at[pl.ds(spot, 1)]
        proj_grad_ref = proj_grad_all.at[rows_at]

        @pl.when(c == 0)
        def _():
            state_grad[...] = later_ref[n]
            after[...] = jnp.zeros_like(after)

        def activate(i, carry):
            rows = pl.ds(pl.multiple_of(i * 16, 16), 16)
            values = summed_ref[rows]
            active[rows] = values * sigmoid(values)
            return carry

        lax.fori_loop(0, CHUNK // 16, activate, 0)
        lane = lax.broadcasted_iota(jnp.int32, (CHUNK, 128), 1)
        raw = raw_ref[...]
        steps = jnp.where(lane < heads, softplus(raw), 0.0)
        cum = cum_ref[...]
        cum_t = jnp.transpose(cum)
        final = cum[CHUNK - 1 :]
        enter = jnp.exp(cum) * masks_ref[:, 4:5]
        tails = jnp.exp(final - cum) * masks_ref[:, 5:6]
        for i, block in enumerate((steps, enter, tails)):
            factors[i] = spread(block, heads_ref)
        writer = active[:, inner : inner + 128]
        reader = active[:, inner + 128 : inner + 256]
        scores = scores_of(reader, writer)
        bias = mask_bias(masks_ref[:, 8:9], seg_row)
        half = lax.broadcasted_iota(jnp.int32, (CHUNK, 128), 1) < 64
        writer_low, reader_low = writer.astype(BF16), reader.astype(BF16)
        reader_t = jnp.transpose(reader_low)
        later = state_grad[...].astype(BF16)
        kept = jnp.exp(final) * masks_ref[CHUNK - 1 :, 4:5]
        kept = spread(jnp.broadcast_to(kept, (8, 128)), heads_ref)[0:1]
        scores_grad = jnp.zeros((CHUNK, CHUNK), F32)
        reader_grad = jnp.zeros((CHUNK, 128), F32)
        writer_grad = jnp.zeros((CHUNK, 128), F32)
        skip = skip_ref[...]
        hook(2 * index)
        for pair in range(heads // 2):
            if pair == heads // 4:
                hook(2 * index + 1)
            at = slice(pair * 128, (pair + 1) * 128)
            signal = active[:, at]
            step_x = factors[0, :, at]
            moved = (signal * step_x).astype(BF16)
            grad = ssm_grad_ref[:, at]
            grad_low = grad.astype(BF16)
            zero = jnp.zeros_like(grad_low)
            stacked = jnp.concatenate(
                [jnp.where(half, grad_low, zero), jnp.where(half, zero, grad_low)], axis=0
            )
            both_grad = mm_nt(stacked, moved)
            one = decays_of(cum, cum_t, bias, 2 * pair)
            two = decays_of(cum, cum_t, bias, 2 * pair + 1)
            scores_grad = scores_grad + both_grad[:CHUNK] * one + both_grad[CHUNK:] * two
            both = jnp.concatenate([(scores * one).astype(BF16), (scores * two).astype(BF16)], axis=0)
            tail_x = factors[2, :, at]
            from_later = mm(writer_low, later[:, at])
            total = mm_tn(both, stacked) + from_later * tail_x
            weighted = (signal * step_x * tail_x).astype(BF16)
            entered = (grad * factors[1, :, at]).astype(BF16)
            start = starts_ref[0, :, at]
            reader_grad = reader_grad + mm_nt(entered, start)
            writer_grad = writer_grad + mm_nt(weighted, later[:, at])
            passed = jnp.sum(start.astype(F32) * later[:, at].astype(F32), axis=0, keepdims=True)
            factors[1, 0:1, at] = kept[:, at] * passed + jnp.sum(
                moved.astype(F32) * (from_later * tail_x), axis=0, keepdims=True
            )
            state_grad[:, at] = state_grad[:, at] * kept[:, at] + mm(reader_t, entered)
            moved_grad[:, at] = total * signal
            factors[2, :, at] = total * moved.astype(F32)
            all_grad[:, at] = total * step_x + skip[:, at] * grad
        sh, sl = split(scores_grad)
        reader_grad = reader_grad + mm(sh, writer_low) + mm(sl, writer_low)
        writer_grad = writer_grad + mm_tn(sh, reader_low) + mm_tn(sl, reader_low)
        all_grad[:, inner : inner + 128] = writer_grad
        all_grad[:, inner + 128 : inner + 256] = reader_grad
        step_grad = gather_heads(moved_grad[...], heads_ref)
        change = dot_ref[...] - gather_heads(factors[2], heads_ref)
        at_end = gather_heads(
            jnp.broadcast_to(factors[1, 0:1], (8, inner)), heads_ref
        )[0:1]
        row = lax.broadcasted_iota(jnp.int32, (CHUNK, 128), 0)
        change = change + jnp.where(row == CHUNK - 1, at_end, 0.0)
        decay_grad = exact_mm(triangle(CHUNK, True), change)
        rate = -jnp.exp(a_log_ref[...])
        raw_grad = jnp.where(lane < heads, (step_grad + decay_grad * rate) * sigmoid(raw), 0.0)
        head_sums_ref[0:1] += jnp.sum(raw_grad, axis=0, keepdims=True)
        head_sums_ref[1:2] += jnp.sum(decay_grad * steps * rate, axis=0, keepdims=True)
        proj_grad_ref[:, channels : channels + 128] = raw_grad.astype(BF16)
        proj_grad_ref[:, channels + 128 :] = jnp.zeros((CHUNK, 128), BF16)

        for block in range(channels // GATE_BLOCK):
            at = slice(block * GATE_BLOCK, (block + 1) * GATE_BLOCK)
            values = summed_ref[:, at]
            turned = sigmoid(values)
            grad = all_grad[:, at] * turned * (1.0 + values * (1.0 - turned))
            conv_sums_ref[4:5, at] += jnp.sum(grad, axis=0, keepdims=True)
            conv = conv_ref[:, at]
            result = grad * taps_ref[3:4, at]
            conv_sums_ref[3:4, at] += jnp.sum(grad * conv, axis=0, keepdims=True)
            rim = jnp.zeros((8, GATE_BLOCK), F32)
            shifted_rows[0:8] = jnp.zeros((8, GATE_BLOCK), F32)
            for k in range(3):
                shifted_rows[8 : 8 + CHUNK] = grad * masks_ref[:, k : k + 1]
                shifted_rows[8 + CHUNK :] = after[k, :, at]
                after[k, :, at] = shifted_rows[8:16]
                here = shifted_rows[11 - k : 11 - k + CHUNK]
                result = result + here * taps_ref[k : k + 1, at]
                conv_sums_ref[k : k + 1, at] += jnp.sum(here * conv, axis=0, keepdims=True)
                early = shifted_rows[3 - k : 11 - k]
                rim = rim + early * taps_ref[k : k + 1, at]

                @pl.when(c == chunks - 1)
                def _():
                    conv_sums_ref[k : k + 1, at] += jnp.sum(
                        early * halo_ref[HALO - 8 :, at], axis=0, keepdims=True
                    )

            proj_grad_ref[:, at] = result.astype(BF16)

            @pl.when(c == 0)
            def _():
                tails_out[n, :, at] = result[CHUNK - 8 :]

            @pl.when(c == chunks - 1)
            def _():
                rims[n, :, at] = rim.astype(BF16)

        return carry

    lax.fori_loop(0, seqs * chunks, one_chunk, 0)

    @pl.when(turn > 0)
    def _():
        rim_copy.start()

    def put(f, summed, updated):
        piece_ref[f, 0] = summed
        piece_ref[f, 1] = updated

    ex.zs_end(rate_ref[0], weight_ref, momentum_ref, put)

    @pl.when(turn < pieces - 1)
    def _():
        rim_copy.wait_recv()
        for n in range(seqs):
            for at in range(0, channels, GATE_BLOCK):
                columns = slice(at, at + GATE_BLOCK)
                rows = slice((n + 1) * piece - 8, (n + 1) * piece)
                proj_grad_all[rows, columns] = (
                    tails_out[n, :, columns] + rims_in[n, :, columns].astype(F32)
                ).astype(BF16)

    @pl.when(turn > 0)
    def _():
        rim_copy.wait_send()

    for k in range(1, bits):
        ex.rs_done(k)
    ex.zs_done()


def backward(rate, inputs, half, weights, momenta, sizes, places, pieces):
    seqs, piece, inner, channels, heads = sizes
    total = inputs[0].shape[0]
    bits = places.bit_length() - 1
    flows, rows = half.shape[0], half.shape[-2]
    vmem = pl.BlockSpec(memory_space=pltpu.VMEM)
    shape = jax.ShapeDtypeStruct
    return pl.pallas_call(
        functools.partial(backward_kernel, sizes, (bits, pieces, flows)),
        in_specs=[pl.BlockSpec(memory_space=pltpu.SMEM)] + [vmem] * (len(inputs) + 3),
        out_specs=(vmem,) * 4,
        out_shape=(
            shape((total, channels + 256), BF16),
            shape((8, channels), F32),
            shape((8, 128), F32),
            shape((flows, 2, rows, LANES), BF16),
        ),
        scratch_shapes=[
            pltpu.VMEM((128, inner), F32),
            pltpu.VMEM((3, 8, channels), F32),
            pltpu.VMEM((CHUNK, channels), F32),
            pltpu.VMEM((3, CHUNK, inner), F32),
            pltpu.VMEM((CHUNK, inner), F32),
            pltpu.VMEM((CHUNK + 16, GATE_BLOCK), F32),
            pltpu.VMEM((CHUNK, channels), F32),
            pltpu.VMEM((seqs, 8, channels), BF16),
            pltpu.VMEM((seqs, 8, channels), BF16),
            pltpu.VMEM((seqs, 8, channels), F32),
        ]
        + [
            pltpu.VMEM(half_shape(bits, pieces, flows, rows, k), BF16) for k in range(1, bits)
        ]
        + [pltpu.VMEM((flows, pieces, rows, LANES), BF16)]
        + dma_semaphores(flows, part_count(pieces), bits)
        + dma_semaphores(flows, pieces)
        + [pltpu.SemaphoreType.DMA] * 2,
        compiler_params=pltpu.CompilerParams(
            collective_id=3, has_side_effects=True, vmem_limit_bytes=48 * 1024 * 1024
        ),
        name="backward",
    )(rate, *inputs, half, weights, momenta)


def turn_kernel(
    dims,
    own_ref,
    keep_ref,
    out_low_ref,
    normed_ref,
    low_ref,
    gate_grad_ref,
    later_ref,
    half_ref,
    sent,
    taken,
    turned,
    grad,
    send,
    recv,
    rs_send,
    rs_recv,
):
    bits, pieces, flows, blocks, real = dims
    places = 1 << bits
    ex = Exchange(bits, pieces, flows)
    ex.grad, ex.halves = grad, [half_ref]
    ex.rs_send, ex.rs_recv = rs_send, rs_recv
    turn = ex.turn
    first, final = turn == pieces - 1, turn == 0
    ahead, behind = lax.rem(turn + pieces - 1, pieces), lax.rem(turn + 1, pieces)
    barrier = pltpu.get_barrier_semaphore()
    pl.semaphore_signal(barrier, inc=1, device_id=ex.partner[0], device_id_type=MESH)

    @pl.when(jnp.logical_not(first))
    def _():
        pl.semaphore_signal(barrier, inc=1, device_id={"seq": behind}, device_id_type=MESH)

    @pl.when(final)
    def _():
        pl.semaphore_wait(barrier, 1)

    @pl.when(jnp.logical_not(final))
    def _():
        pl.semaphore_wait(barrier, 2)

    width = own_ref.shape[2] // blocks
    rows = grad.shape[-2]

    def copy(c):
        return remote(sent.at[c], taken.at[c], send.at[c], recv.at[c], {"seq": ahead})

    @pl.when(first)
    def _():
        later_ref[...] = jnp.zeros_like(later_ref)
        for c in range(blocks):
            sent[c] = own_ref[:, :, c * width : (c + 1) * width].astype(BF16)
            copy(c).start()

    turned[0] = jnp.transpose(out_low_ref[...])
    turned[1] = jnp.transpose(normed_ref[...])
    low_tiles = low_ref.shape[1] // LANES

    def store(tile, values):
        f, d = tile // places, tile % places
        spot = (f,) + tuple((d >> b) & 1 for b in range(bits - 1, -1, -1))
        for p in range(pieces):
            grad[spot + (p,)] = values[p * rows : (p + 1) * rows]

    def tiles(tile):
        if tile >= real:
            result = jnp.zeros((pieces * rows, 2 * LANES), F32)
        elif tile < low_tiles:
            result = mm(turned[0], low_ref[:, tile * LANES : (tile + 2) * LANES])
        else:
            at = (tile - low_tiles) * LANES
            result = mm(turned[1], gate_grad_ref[:, at : at + 2 * LANES])
        result = result.astype(BF16)
        store(tile, result[:, :LANES])
        store(tile + 1, result[:, LANES:])

    pairs = flows * places // 2
    done = 0
    for c in range(blocks):
        until = pairs * (c + 1) // blocks
        for pair in range(done, until):
            tiles(2 * pair)
            if (2 * pair + 2) % places == 0:
                ex.rs_begin(0, (2 * pair) // places)
        done = until

        @pl.when(jnp.logical_not(first))
        def _():
            at = slice(c * width, (c + 1) * width)
            copy(c).wait_recv()

            @pl.when(jnp.logical_not(final))
            def _():
                sent[c] = (
                    own_ref[:, :, at] + keep_ref[:, 0:1, at] * taken[c].astype(F32)
                ).astype(BF16)
                copy(c).start()

            later_ref[:, :, at] = taken[c].astype(F32)

    ex.rs_end(0)
    ex.rs_done(0)

    @pl.when(jnp.logical_not(final))
    def _():
        for c in range(blocks):
            copy(c).wait_send()


def turn_back(own, keep, out_low, normed, low, gate_grad, places, pieces, blocks=6):
    seqs, depth, inner = own.shape
    total, model = out_low.shape
    bits = places.bit_length() - 1
    assert places == 1 << bits and bits >= 1 and pieces >= 2
    real = 2 * inner // LANES
    flows = -(-real // places)
    rows = model // pieces
    vmem = pl.BlockSpec(memory_space=pltpu.VMEM)
    part = (blocks, seqs, depth, inner // blocks)
    return pl.pallas_call(
        functools.partial(turn_kernel, (bits, pieces, flows, blocks, real)),
        out_shape=(
            jax.ShapeDtypeStruct(own.shape, F32),
            jax.ShapeDtypeStruct(half_shape(bits, pieces, flows, rows, 0), BF16),
        ),
        in_specs=[vmem] * 6,
        out_specs=(vmem, vmem),
        scratch_shapes=[pltpu.VMEM(part, BF16)] * 2
        + [
            pltpu.VMEM((2, model, total), BF16),
            pltpu.VMEM(half_shape(bits, pieces, flows, rows, -1), BF16),
        ]
        + dma_semaphores(blocks)
        + dma_semaphores(flows, part_count(pieces), 1),
        compiler_params=pltpu.CompilerParams(
            collective_id=2, has_side_effects=True, vmem_limit_bytes=32 * 1024 * 1024
        ),
        name="turn_back",
    )(own, keep, out_low, normed, low, gate_grad)


def last_kernel(
    dims,
    rate_ref,
    tokens_ref,
    out_low_ref,
    normed_ref,
    gate_grad_ref,
    proj_grad_ref,
    weight_t_ref,
    gain_ref,
    piece_ref,
    weight_ref,
    momentum_ref,
    conv_sums_ref,
    wide_ref,
    head_sums_ref,
    squares_ref,
    input_grad_ref,
    gathered_a_ref,
    gathered_b_ref,
    small_out_ref,
    *scratch,
):
    bits, pieces, flows_a, flows_b, real = dims
    places = 1 << bits
    a, b = Exchange(bits, pieces, flows_a), Exchange(bits, pieces, flows_b)
    b.halves, scratch = scratch[:bits], scratch[bits:]
    (b.grad, b.piece_parts, turned, gain_sums, small_acc, small_in, small_parts) = scratch[:7]
    (b.rs_send, b.rs_recv, b.zs_send, b.zs_recv) = scratch[7:11]
    (b.zg_send, b.zg_recv, b.ag_send, b.ag_recv) = scratch[11:15]
    (a.zg_send, a.zg_recv, a.ag_send, a.ag_recv) = scratch[15:19]
    (sm_send, sm_recv, sz_send, sz_recv) = scratch[19:]
    a.gathered, b.gathered = gathered_a_ref, gathered_b_ref
    turn = a.turn
    rows = b.grad.shape[-2]
    greet(a.partner + a.others[1:])

    for f in range(flows_a):
        a.put(f, piece_ref[f, 0], piece_ref[f, 1])
        a.zg_begin(f)

    turned[...] = jnp.transpose(normed_ref[...])

    def tiles(tile):
        if tile >= real:
            result = jnp.zeros((pieces * rows, 2 * LANES), BF16)
        else:
            at = tile * LANES
            result = mm(turned[...], proj_grad_ref[:, at : at + 2 * LANES]).astype(BF16)
        for i in range(2):
            f, d = (tile + i) // places, (tile + i) % places
            spot = (f,) + tuple((d >> k) & 1 for k in range(bits - 1, -1, -1))
            for p in range(pieces):
                b.grad[spot + (p,)] = result[
                    p * rows : (p + 1) * rows, i * LANES : (i + 1) * LANES
                ]

    for f in range(flows_b):
        for d in range(0, places, 2):
            tiles(f * places + d)
        b.rs_begin(0, f)

    inner = gate_grad_ref.shape[1]
    rest = weight_t_ref.shape[0] - inner
    gain_sums[...] = jnp.zeros_like(gain_sums)

    def input_rows(i, carry):
        at = pl.ds(pl.multiple_of(i * 128, 128), 128)
        normed_grad = mm(gate_grad_ref[at], weight_t_ref[:inner]) + mm(
            proj_grad_ref[at, :rest], weight_t_ref[inner:]
        )
        values = tokens_ref[at].astype(F32)
        scale = lax.rsqrt(jnp.mean(values * values, axis=-1, keepdims=True) + EPS)
        gain_sums[0:1] += jnp.sum(normed_grad * values * scale, axis=0, keepdims=True)
        pushed = normed_grad * gain_ref[...]
        inside = jnp.mean(pushed * values, axis=-1, keepdims=True)
        input_grad_ref[at] = (
            out_low_ref[at].astype(F32)
            + scale * pushed
            - values * (scale * scale * scale * inside)
        ).astype(BF16)
        return carry

    blocks = tokens_ref.shape[0] // 128
    lax.fori_loop(0, blocks // 2, input_rows, 0)
    b.rs_end(0, then=True)
    lax.fori_loop(blocks // 2, blocks, input_rows, 0)

    def sm_copy(k):
        return remote(
            small_acc.at[k], small_in.at[k], sm_send.at[k], sm_recv.at[k], a.partner[k]
        )

    def sz_copy(j):
        return remote(
            small_acc.at[bits], small_parts.at[turn], sz_send.at[j], sz_recv.at[j], a.others[j]
        )

    model = gain_sums.shape[1]
    small_acc[0, 0:5] = conv_sums_ref[0:5]
    small_acc[0, 5:7, :inner] = wide_ref[0:2]
    small_acc[0, 5:7, inner : inner + 128] = head_sums_ref[0:2]
    small_acc[0, 5:8, inner + 128 :] = squares_ref[0:3]
    small_acc[0, 7:8, :model] = gain_sums[0:1]
    small_acc[0, 7:8, model : inner + 128] = jnp.zeros((1, inner + 128 - model), F32)
    sm_copy(0).start()

    def small_step(k):
        sm_copy(k).wait_recv()
        small_acc[k + 1] = small_acc[k] + small_in[k]
        if k + 1 < bits:
            sm_copy(k + 1).start()
        else:
            small_parts[turn] = small_acc[bits]
            for j in range(1, pieces):
                sz_copy(j).start()

    a.zg_end()
    for k in range(1, bits):
        b.rs_end(k, then=True)
        small_step(k - 1)
        if k == 1:
            a.ag_end(bits - 1)
    small_step(bits - 1)

    def put(f, summed, updated):
        b.put(f, summed, updated)
        b.zg_begin(f)

    b.zs_end(rate_ref[0], weight_ref, momentum_ref, put)
    for k in range(bits - 2, 0, -1):
        a.ag_end(k)
    b.zg_end()
    for k in range(bits - 1, 0, -1):
        b.ag_end(k)
    for j in range(1, pieces):
        sz_copy(j).wait_recv()
    whole = small_parts[0]
    for j in range(1, pieces):
        whole = whole + small_parts[j]
    small_out_ref[...] = whole
    a.ag_end(0)
    b.ag_end(0)
    for k in range(bits):
        sm_copy(k).wait_send()
        b.rs_done(k)
    for j in range(1, pieces):
        sz_copy(j).wait_send()
    b.zs_done()
    for ex in (a, b):
        ex.zg_done()
        ex.ag_done()


def last(
    rate,
    tokens,
    out_low,
    normed,
    gate_grad,
    proj_grad,
    weight_t,
    gain,
    piece,
    weights,
    momenta,
    sums,
    places,
    pieces,
):
    total, model = tokens.shape
    bits = places.bit_length() - 1
    real = proj_grad.shape[1] // LANES
    flows_a, flows_b = piece.shape[0], weights.shape[0]
    rows = model // pieces
    small = sums[0].shape
    parts = part_count(pieces)
    vmem = pl.BlockSpec(memory_space=pltpu.VMEM)
    shape = jax.ShapeDtypeStruct
    gathered = lambda flows: (flows,) + (2,) * bits + (pieces + 1, rows, LANES)
    sem = dma_semaphores
    return pl.pallas_call(
        functools.partial(last_kernel, (bits, pieces, flows_a, flows_b, real)),
        out_shape=(
            shape((total, model), BF16),
            shape(gathered(flows_a), BF16),
            shape(gathered(flows_b), BF16),
            shape(small, F32),
        ),
        in_specs=[pl.BlockSpec(memory_space=pltpu.SMEM)] + [vmem] * 14,
        out_specs=(vmem,) * 4,
        scratch_shapes=[
            pltpu.VMEM(half_shape(bits, pieces, flows_b, rows, k), BF16) for k in range(bits)
        ]
        + [
            pltpu.VMEM(half_shape(bits, pieces, flows_b, rows, -1), BF16),
            pltpu.VMEM((flows_b, pieces, rows, LANES), BF16),
            pltpu.VMEM((model, total), BF16),
            pltpu.VMEM((8, model), F32),
            pltpu.VMEM((bits + 1,) + small, F32),
            pltpu.VMEM((bits,) + small, F32),
            pltpu.VMEM((pieces,) + small, F32),
        ]
        + sem(flows_b, parts, bits)
        + sem(flows_b, pieces)
        + sem(flows_b, pieces)
        + sem(flows_b, parts, bits)
        + sem(flows_a, pieces)
        + sem(flows_a, parts, bits)
        + sem(bits)
        + sem(pieces),
        compiler_params=pltpu.CompilerParams(
            collective_id=0, has_side_effects=True, vmem_limit_bytes=48 * 1024 * 1024
        ),
        name="last",
    )(
        rate,
        tokens,
        out_low,
        normed,
        gate_grad,
        proj_grad,
        weight_t,
        gain,
        piece,
        weights,
        momenta,
        *sums,
    )


def piece_kernel(
    counts, spot_ref, out_weight_ref, weight_ref, out_momentum_ref, momentum_ref, w_ref, m_ref, turned
):
    out_tiles, tile_of = counts
    tile = tile_of(pl.program_id(0), spot_ref)
    rows = m_ref.shape[1]
    mine = pl.ds(pl.multiple_of(spot_ref[1] * rows, 16), rows)

    @pl.when(tile < out_tiles)
    def _():
        turned[...] = jnp.transpose(out_weight_ref[...])
        w_ref[0] = turned[mine]
        m_ref[0] = out_momentum_ref[...]

    @pl.when(tile >= out_tiles)
    def _():
        turned[...] = jnp.transpose(weight_ref[...])
        w_ref[0] = turned[mine]
        m_ref[0] = momentum_ref[...]


def owned(spot, out_weight, weight_t, out_momentum_t, momentum, flows_a, flows_b, places):
    inner, model = out_weight.shape
    rows, width = momentum.shape
    out_tiles, in_tiles = inner // LANES, -(-width // LANES)

    flows = flows_a + flows_b

    def tile_of(f, spot):
        early = jnp.minimum(f * places + spot[0], 2 * out_tiles - 1)
        late = 2 * out_tiles + (f - flows_a) * places + spot[0]
        return jnp.where(f < flows_a, early, late)

    def out_at(f, spot):
        return jnp.clip(tile_of(f, spot), 0, out_tiles - 1)

    def in_at(f, spot):
        return jnp.clip(tile_of(f, spot) - out_tiles, 0, in_tiles - 1)

    piece = pl.BlockSpec((1, rows, LANES), lambda f, spot: (f, 0, 0))
    return pl.pallas_call(
        functools.partial(piece_kernel, (out_tiles, tile_of)),
        grid_spec=pltpu.PrefetchScalarGridSpec(
            num_scalar_prefetch=1,
            grid=(flows,),
            in_specs=[
                pl.BlockSpec((LANES, model), lambda f, spot: (out_at(f, spot), 0)),
                pl.BlockSpec((LANES, model), lambda f, spot: (in_at(f, spot), 0)),
                pl.BlockSpec((rows, LANES), lambda f, spot: (0, out_at(f, spot))),
                pl.BlockSpec((rows, LANES), lambda f, spot: (0, in_at(f, spot))),
            ],
            out_specs=(piece, piece),
            scratch_shapes=[pltpu.VMEM((model, LANES), BF16)],
        ),
        out_shape=(
            jax.ShapeDtypeStruct((flows, rows, LANES), BF16),
            jax.ShapeDtypeStruct((flows, rows, LANES), F32),
        ),
        name="owned",
    )(spot, out_weight, weight_t, out_momentum_t, momentum)


def finish_kernel(
    out_steps,
    gathered_a_ref,
    gathered_b_ref,
    out_momentum_ref,
    momentum_ref,
    out_weight_ref,
    weight_ref,
    new_out_momentum_ref,
    new_momentum_ref,
):
    group, slots, rows, _ = gathered_a_ref.shape
    step = pl.program_id(0)

    def write(gathered_ref, weights, old, new):
        for i in range(group):
            at = slice(i * LANES, (i + 1) * LANES)
            tile = gathered_ref[i, : slots - 1].reshape((slots - 1) * rows, LANES)
            weights[at] = jnp.transpose(tile)
            new[:, at] = 0.5 * old[:, at] + gathered_ref[i, slots - 1].astype(F32)

    @pl.when(step < out_steps)
    def _():
        write(gathered_a_ref, out_weight_ref, out_momentum_ref, new_out_momentum_ref)

    @pl.when((step >= out_steps) & (step < 2 * out_steps))
    def _():
        write(gathered_a_ref, weight_ref, momentum_ref, new_momentum_ref)

    @pl.when(step >= 2 * out_steps)
    def _():
        write(gathered_b_ref, weight_ref, momentum_ref, new_momentum_ref)


def finish(gathered_a, gathered_b, out_momentum_t, momentum, group=4):
    _, slots, rows, _ = gathered_a.shape
    width, inner = momentum.shape[1], out_momentum_t.shape[1]
    model = (slots - 1) * rows
    wide = group * LANES
    out_steps, in_steps = inner // wide, -(-width // wide)
    out_at = lambda j: jnp.minimum(j, out_steps - 1)
    in_at = lambda j: jnp.maximum(j - out_steps, 0)
    by_column = [
        pl.BlockSpec((rows, wide), lambda j: (0, out_at(j))),
        pl.BlockSpec((rows, wide), lambda j: (0, in_at(j))),
    ]
    shape = jax.ShapeDtypeStruct
    return pl.pallas_call(
        functools.partial(finish_kernel, out_steps),
        grid=(out_steps + in_steps,),
        in_specs=[
            pl.BlockSpec(
                (group, slots, rows, LANES), lambda j: (jnp.minimum(j, 2 * out_steps - 1), 0, 0, 0)
            ),
            pl.BlockSpec(
                (group, slots, rows, LANES), lambda j: (jnp.maximum(j - 2 * out_steps, 0), 0, 0, 0)
            ),
        ]
        + by_column,
        out_specs=[
            pl.BlockSpec((wide, model), lambda j: (out_at(j), 0)),
            pl.BlockSpec((wide, model), lambda j: (in_at(j), 0)),
        ]
        + by_column,
        out_shape=(
            shape((inner, model), BF16),
            shape((width, model), BF16),
            shape((rows, inner), F32),
            shape((rows, width), F32),
        ),
        name="finish",
    )(gathered_a, gathered_b, out_momentum_t, momentum)


def local(
    tokens,
    cotangent,
    segment_ids,
    doc_starts,
    valid_mask,
    step_number,
    learn_rate,
    norm_gain,
    in_weight,
    conv_weight,
    conv_bias,
    dt_bias,
    a_log,
    skip_d,
    gate_gain,
    out_weight,
    in_momentum,
    out_momentum,
):
    seqs, piece, model_width = tokens.shape
    heads = dt_bias.shape[0]
    tap_count, channels = conv_weight.shape
    inner_width = gate_gain.shape[0]
    proj_width = in_weight.shape[1]
    total = seqs * piece
    sizes = (seqs, piece, inner_width, channels, heads)
    places, pieces = lax.axis_size("dp"), lax.axis_size("seq")
    turn = lax.axis_index("seq")
    seg = segment_ids.astype(F32)
    sent = jnp.concatenate(
        [
            tokens[:, piece - HALO :],
            jnp.broadcast_to(seg[:, piece - HALO :, None], (seqs, HALO, LANES)).astype(BF16),
        ],
        axis=2,
    )
    route = [(i, i + 1) for i in range(pieces - 1)]
    arrived = lax.ppermute(sent, "seq", route)
    halo = arrived[:, :, :model_width].reshape(seqs * HALO, model_width)
    early_seg = jnp.where(turn == 0, -1.0, arrived[:, :, model_width].astype(F32))
    seg_pad = jnp.concatenate([early_seg, seg], axis=1)
    seg_row = seg.reshape(1, total)
    heads_map = (
        lax.broadcasted_iota(jnp.int32, (LANES, inner_width), 0)
        == lax.broadcasted_iota(jnp.int32, (LANES, inner_width), 1) // (inner_width // heads)
    ).astype(BF16)

    def lanes(values):
        return jnp.pad(values, (0, LANES - heads)).reshape(1, LANES)

    flat_tokens = tokens.reshape(total, model_width)
    weight_t = jnp.transpose(in_weight)
    out_momentum_t = jnp.transpose(out_momentum)
    flat_cot = cotangent.reshape(total, model_width)
    bias_row, decay_row = lanes(dt_bias), lanes(a_log)
    skip_row = jnp.repeat(skip_d, inner_width // heads).reshape(1, inner_width)
    gain_row = gate_gain.reshape(1, inner_width)
    normed, masks, gate, conv, conv_halo, summed, raw, cum, fresh, keep = front(
        flat_tokens,
        halo,
        norm_gain.reshape(1, model_width),
        weight_t,
        conv_weight,
        conv_bias.reshape(1, channels),
        seg_pad,
        valid_mask,
        bias_row,
        decay_row,
        heads_map,
        sizes,
    )
    incoming = chain(fresh, keep, 1)
    output, low, out_low, gate_grad, ssm_grad, starts, dots, squares, wide, state_grad = forward(
        summed,
        gate,
        raw,
        cum,
        masks,
        seg_row,
        incoming,
        flat_tokens,
        flat_cot,
        out_weight,
        gain_row,
        skip_row,
        heads_map,
        sizes,
    )
    later, half = turn_back(state_grad, keep, out_low, normed, low, gate_grad, places, pieces)
    step_float = step_number[0].astype(F32)
    rate = (learn_rate[0] * step_float / (step_float + 16.0)).reshape(1)
    flows_a = half.shape[0]
    flows_b = -(-(channels + 2 * LANES) // (LANES * places))
    spot = jnp.stack([lax.axis_index("dp"), turn]).astype(jnp.int32)
    weights, momenta = owned(
        spot, out_weight, weight_t, out_momentum_t, in_momentum, flows_a, flows_b, places
    )
    proj_grad, conv_sums, head_sums, piece_a = backward(
        rate,
        (
            summed,
            conv,
            conv_halo,
            raw,
            cum,
            masks,
            seg_row,
            later,
            ssm_grad,
            starts,
            dots,
            conv_weight,
            decay_row,
            skip_row,
            heads_map,
        ),
        half,
        weights[:flows_a],
        momenta[:flows_a],
        sizes,
        places,
        pieces,
    )
    input_grad, gathered_a, gathered_b, totals = last(
        rate,
        flat_tokens,
        out_low,
        normed,
        gate_grad,
        proj_grad,
        weight_t,
        norm_gain.reshape(1, model_width),
        piece_a,
        weights[flows_a:],
        momenta[flows_a:],
        (conv_sums, wide, head_sums, squares),
        places,
        pieces,
    )
    share = (pieces + 1, model_width // pieces, LANES)
    new_out_weight, new_weight_t, new_out_momentum_t, new_in_momentum = finish(
        gathered_a.reshape((-1,) + share),
        gathered_b.reshape((-1,) + share),
        out_momentum_t,
        in_momentum,
    )
    new_in_weight = jnp.transpose(new_weight_t)
    new_out_momentum = jnp.transpose(new_out_momentum_t)
    conv_weight_total = totals[:tap_count]
    conv_bias_total = totals[tap_count]
    gate_gain_total = totals[5, :inner_width]
    skip_total = totals[6, :inner_width].reshape(heads, -1).sum(axis=1)
    norm_gain_total = totals[7, :model_width]
    dt_bias_total = totals[5, inner_width : inner_width + heads]
    a_log_total = totals[6, inner_width : inner_width + heads]
    out_square_total = totals[5, inner_width + LANES :].sum()
    mix_square_total = totals[6, inner_width + LANES :].sum()
    valid_total = totals[7, inner_width + LANES + 9]
    denominator = jnp.maximum(valid_total, 1.0) * model_width
    output_rms = jnp.sqrt(out_square_total / denominator).reshape(1)
    mixer_rms = jnp.sqrt(mix_square_total / denominator).reshape(1)
    return (
        output.reshape(tokens.shape),
        input_grad.reshape(tokens.shape),
        new_in_weight,
        new_out_weight,
        new_in_momentum,
        new_out_momentum,
        norm_gain_total,
        conv_weight_total,
        conv_bias_total,
        dt_bias_total,
        a_log_total,
        skip_total,
        gate_gain_total,
        output_rms,
        mixer_rms,
    )


def solution(mesh):
    placed = (
        P("dp", "seq", None),
        P("dp", "seq", None),
        P("dp", "seq"),
        P("dp", "seq"),
        P("dp", "seq"),
        P(),
        P(),
        P(),
        P(),
        P(),
        P(),
        P(),
        P(),
        P(),
        P(),
        P(),
        P("seq", None),
        P(None, "seq"),
    )
    return jax.shard_map(
        local,
        mesh=mesh,
        in_specs=placed,
        out_specs=(
            P("dp", "seq", None),
            P("dp", "seq", None),
            P(),
            P(),
            P("seq", None),
            P(None, "seq"),
            P(),
            P(),
            P(),
            P(),
            P(),
            P(),
            P(),
            P(),
            P(),
        ),
        check_vma=False,
    )
```

```python
import functools

import jax
import jax.numpy as jnp
from jax import lax
from jax.experimental import pallas as pl
from jax.experimental.pallas import tpu as pltpu
from jax.sharding import PartitionSpec as P

CHUNK = 128
HALO = 16
GATE_BLOCK = 256
EPS = 1e-05
NEGATIVE = -1e30
F32, BF16 = jnp.float32, jnp.bfloat16
LANES = 128
MESH = pl.DeviceIdType.MESH


def remote(src, dst, send, recv, target):
    return pltpu.make_async_remote_copy(
        src_ref=src,
        dst_ref=dst,
        send_sem=send,
        recv_sem=recv,
        device_id=target,
        device_id_type=MESH,
    )


def greet(targets):
    barrier = pltpu.get_barrier_semaphore()
    for target in targets:
        pl.semaphore_signal(barrier, inc=1, device_id=target, device_id_type=MESH)
    pl.semaphore_wait(barrier, len(targets))


def dma_semaphores(*shape):
    return [pltpu.SemaphoreType.DMA(shape)] * 2


def part_count(pieces):
    return 2 if pieces % 2 == 0 else 1


def half_shape(bits, pieces, flows, rows, k):
    return (flows,) + (2,) * (bits - k - 1) + (pieces, rows, LANES)


def mm(a, b):
    return jnp.dot(a, b, preferred_element_type=F32)


def mm_nt(a, b):
    return lax.dot_general(a, b, (((1,), (1,)), ((), ())), preferred_element_type=F32)


def mm_tn(a, b):
    return lax.dot_general(a, b, (((0,), (0,)), ((), ())), preferred_element_type=F32)


def split(a):
    high = a.astype(BF16)
    return high, (a - high.astype(F32)).astype(BF16)


def exact_mm(a, b):
    return jnp.dot(a, b, preferred_element_type=F32, precision=lax.Precision.HIGHEST)


def spread(a, heads_ref):
    high, low = split(a)
    return mm(high, heads_ref[...]) + mm(low, heads_ref[...])


def gather_heads(a, heads_ref):
    high, low = split(a)
    return mm_nt(high, heads_ref[...]) + mm_nt(low, heads_ref[...])


def sigmoid(v):
    return 1.0 / (1.0 + jnp.exp(-v))


def softplus(v):
    return jnp.maximum(v, 0.0) + jnp.log1p(jnp.exp(-jnp.abs(v)))


def triangle(size, upper):
    row = lax.broadcasted_iota(jnp.int32, (size, size), 0)
    column = lax.broadcasted_iota(jnp.int32, (size, size), 1)
    return ((row <= column) if upper else (row >= column)).astype(F32)


def front_kernel(
    sizes,
    tokens_ref,
    halo_ref,
    gain_ref,
    weight_ref,
    taps_ref,
    bias_ref,
    seg_ref,
    valid_ref,
    dt_bias_ref,
    a_log_ref,
    heads_ref,
    normed_ref,
    masks_ref,
    gate_ref,
    conv_ref,
    halo_out_ref,
    summed_ref,
    raw_ref,
    cum_ref,
    state_ref,
    keep_ref,
    padded,
    product,
    active,
):
    seqs, piece, inner, channels, heads = sizes
    gate_blocks, conv_blocks = inner // GATE_BLOCK, channels // GATE_BLOCK
    step = pl.program_id(0)
    stride = piece + HALO

    @pl.when(step == 0)
    def _():
        gain = gain_ref[...]
        for n in range(seqs):
            padded_seg = seg_ref[n : n + 1]
            seg = padded_seg[:, HALO:]

            def over_chunks(at):
                return jnp.concatenate(
                    [
                        jnp.broadcast_to(
                            padded_seg[:, c * CHUNK + at : c * CHUNK + at + 1], (1, CHUNK)
                        )
                        for c in range(piece // CHUNK)
                    ],
                    axis=1,
                )

            others = [padded_seg[:, HALO - 3 + k : HALO - 3 + k + piece] for k in range(4)] + [
                over_chunks(HALO - 1),
                over_chunks(HALO + CHUNK - 1),
                jnp.broadcast_to(padded_seg[:, HALO - 1 : HALO], (1, piece)),
                jnp.broadcast_to(padded_seg[:, HALO + piece - 1 :], (1, piece)),
            ]
            lines = [(other == seg).astype(F32) for other in others] + [
                seg,
                valid_ref[n : n + 1].astype(F32),
            ]
            lines = lines + [jnp.zeros_like(seg)] * (16 - len(lines))
            masks_ref[pl.ds(n * piece, piece)] = jnp.transpose(jnp.concatenate(lines, axis=0))
            for source, start, to, count in (
                (halo_ref, n * HALO, n * stride, HALO),
                (tokens_ref, n * piece, n * stride + HALO, piece),
            ):

                def body(i, carry):
                    values = source[pl.ds(pl.multiple_of(start + i * 16, 16), 16)].astype(F32)
                    scale = lax.rsqrt(jnp.mean(values * values, axis=-1, keepdims=True) + EPS)
                    low = (values * scale * gain).astype(BF16)
                    padded[pl.ds(pl.multiple_of(to + i * 16, 16), 16)] = low
                    return carry

                lax.fori_loop(0, count // 16, body, 0)
            normed_ref[pl.ds(n * piece, piece)] = padded[pl.ds(n * stride + HALO, piece)]

    product[...] = mm_nt(padded[...], weight_ref[...])

    @pl.when(step < gate_blocks)
    def _():
        for n in range(seqs):
            gate_ref[pl.ds(n * piece, piece)] = product[pl.ds(n * stride + HALO, piece)]

    @pl.when((step >= gate_blocks) & (step < gate_blocks + conv_blocks))
    def _():
        at = pl.multiple_of((step - gate_blocks) * GATE_BLOCK, GATE_BLOCK)
        for n in range(seqs):
            conv_ref[pl.ds(n * piece, piece)] = product[pl.ds(n * stride + HALO, piece)]
            halo_out_ref[pl.ds(n * HALO, HALO)] = product[pl.ds(n * stride, HALO)]
            for i in range(piece // 64):
                rows = pl.ds(n * piece + i * 64, 64)
                total = jnp.broadcast_to(bias_ref[...], (64, GATE_BLOCK))
                for k in range(4):
                    source = product[pl.ds(n * stride + HALO - 3 + k + i * 64, 64)]
                    total = total + source * masks_ref[rows, k : k + 1] * taps_ref[k : k + 1]
                summed_ref[rows] = total
                active[rows, pl.ds(at, GATE_BLOCK)] = (total * sigmoid(total)).astype(BF16)

    @pl.when(step == gate_blocks + conv_blocks)
    def _():
        lane = lax.broadcasted_iota(jnp.int32, (piece, 128), 1)
        lower = triangle(CHUNK, False)
        for n in range(seqs):
            rows = pl.ds(n * piece, piece)
            raw = jnp.where(lane < heads, product[pl.ds(n * stride + HALO, piece), :128], 0.0)
            raw = raw + dt_bias_ref[...]
            raw_ref[rows] = raw
            steps = jnp.where(lane < heads, softplus(raw), 0.0)
            decay = -jnp.exp(a_log_ref[...]) * steps
            total = jnp.zeros((1, 128), F32)
            pieces = []
            for c in range(piece // CHUNK):
                cumulative = exact_mm(lower, decay[c * CHUNK : (c + 1) * CHUNK])
                cum_ref[pl.ds(n * piece + c * CHUNK, CHUNK)] = cumulative
                pieces.append(cumulative + total)
                total = total + cumulative[CHUNK - 1 :]
            whole = jnp.concatenate(pieces, axis=0) if len(pieces) > 1 else pieces[0]
            tails = jnp.exp(total - whole) * steps * masks_ref[rows, 7:8]
            weighted = (spread(tails, heads_ref) * active[rows, :inner].astype(F32)).astype(BF16)
            state_ref[n] = mm_tn(active[rows, inner : inner + 128], weighted)
            last = masks_ref[n * piece + piece - 1 : n * piece + piece, 6:7]
            keep = jnp.exp(total) * last
            keep_ref[n] = spread(jnp.broadcast_to(keep, (8, 128)), heads_ref)


def front(tokens, halo, gain, weight, taps, bias, segs, valid, dt_bias, a_log, heads_map, sizes):
    seqs, piece, inner, channels, heads = sizes
    total, model = tokens.shape
    stride = seqs * (piece + HALO)
    gate_blocks, conv_blocks = inner // GATE_BLOCK, channels // GATE_BLOCK
    full = lambda *shape: pl.BlockSpec(shape, lambda j: (0,) * len(shape))

    def conv_at(j):
        return (0, jnp.clip(j - gate_blocks, 0, conv_blocks - 1))

    return pl.pallas_call(
        functools.partial(front_kernel, sizes),
        grid=(gate_blocks + conv_blocks + 1,),
        in_specs=[
            full(total, model),
            full(seqs * HALO, model),
            full(1, model),
            pl.BlockSpec((GATE_BLOCK, model), lambda j: (j, 0)),
            pl.BlockSpec((4, GATE_BLOCK), conv_at),
            pl.BlockSpec((1, GATE_BLOCK), conv_at),
            full(*segs.shape),
            full(*valid.shape),
            full(1, 128),
            full(1, 128),
            full(128, inner),
        ],
        out_specs=(
            full(total, model),
            full(total, 16),
            pl.BlockSpec((total, GATE_BLOCK), lambda j: (0, jnp.minimum(j, gate_blocks - 1))),
            pl.BlockSpec((total, GATE_BLOCK), conv_at),
            pl.BlockSpec((seqs * HALO, GATE_BLOCK), conv_at),
            pl.BlockSpec((total, GATE_BLOCK), conv_at),
            full(total, 128),
            full(total, 128),
            full(seqs, 128, inner),
            full(seqs, 8, inner),
        ),
        out_shape=(
            jax.ShapeDtypeStruct((total, model), BF16),
            jax.ShapeDtypeStruct((total, 16), F32),
            jax.ShapeDtypeStruct((total, inner), F32),
            jax.ShapeDtypeStruct((total, channels), F32),
            jax.ShapeDtypeStruct((seqs * HALO, channels), F32),
            jax.ShapeDtypeStruct((total, channels), F32),
            jax.ShapeDtypeStruct((total, 128), F32),
            jax.ShapeDtypeStruct((total, 128), F32),
            jax.ShapeDtypeStruct((seqs, 128, inner), F32),
            jax.ShapeDtypeStruct((seqs, 8, inner), F32),
        ),
        scratch_shapes=[
            pltpu.VMEM((stride, model), BF16),
            pltpu.VMEM((stride, GATE_BLOCK), F32),
            pltpu.VMEM((total, channels), BF16),
        ],
        compiler_params=pltpu.CompilerParams(vmem_limit_bytes=48 * 1024 * 1024),
        name="front",
    )(tokens, halo, gain, weight, taps, bias, segs, valid, dt_bias, a_log, heads_map)


def chain_kernel(ways, blocks, own_ref, keep_ref, out_ref, sent, taken, send, recv):
    size = lax.axis_size("seq")
    turn = lax.axis_index("seq")
    first = turn == (0 if ways > 0 else size - 1)
    final = turn == (size - 1 if ways > 0 else 0)
    ahead = {"seq": lax.rem(turn + ways + size, size)}
    behind = {"seq": lax.rem(turn - ways + size, size)}
    barrier = pltpu.get_barrier_semaphore()

    @pl.when(jnp.logical_not(first))
    def _():
        pl.semaphore_signal(
            barrier, inc=1, device_id=behind, device_id_type=pl.DeviceIdType.MESH
        )

    @pl.when(jnp.logical_not(final))
    def _():
        pl.semaphore_wait(barrier, 1)

    width = own_ref.shape[2] // blocks

    def copy(c):
        return pltpu.make_async_remote_copy(
            src_ref=sent.at[c],
            dst_ref=taken.at[c],
            send_sem=send.at[c],
            recv_sem=recv.at[c],
            device_id=ahead,
            device_id_type=pl.DeviceIdType.MESH,
        )

    @pl.when(first)
    def _():
        out_ref[...] = jnp.zeros_like(out_ref)
        for c in range(blocks):
            at = slice(c * width, (c + 1) * width)
            sent[c] = own_ref[:, :, at].astype(BF16)
            copy(c).start()

    @pl.when(jnp.logical_not(first))
    def _():
        for c in range(blocks):
            at = slice(c * width, (c + 1) * width)
            copy(c).wait_recv()

            @pl.when(jnp.logical_not(final))
            def _():
                sent[c] = (
                    own_ref[:, :, at] + keep_ref[:, 0:1, at] * taken[c].astype(F32)
                ).astype(BF16)
                copy(c).start()

            out_ref[:, :, at] = taken[c].astype(F32)

    @pl.when(jnp.logical_not(final))
    def _():
        for c in range(blocks):
            copy(c).wait_send()


def chain(own, keep, ways, blocks=6):
    seqs, depth, inner = own.shape
    vmem = pl.BlockSpec(memory_space=pltpu.VMEM)
    part = (blocks, seqs, depth, inner // blocks)
    return pl.pallas_call(
        functools.partial(chain_kernel, ways, blocks),
        out_shape=jax.ShapeDtypeStruct(own.shape, F32),
        in_specs=[vmem, vmem],
        out_specs=vmem,
        scratch_shapes=[pltpu.VMEM(part, BF16)] * 2 + [pltpu.SemaphoreType.DMA((blocks,))] * 2,
        compiler_params=pltpu.CompilerParams(
            collective_id=1 if ways > 0 else 2,
            has_side_effects=True,
            vmem_limit_bytes=32 * 1024 * 1024,
        ),
        name="chain",
    )(own, keep)


def decays_of(cum, cum_t, bias, h):
    return jnp.exp(cum[:, h : h + 1] - cum_t[h : h + 1, :] + bias)


def mask_bias(seg_col, seg_row):
    row = lax.broadcasted_iota(jnp.int32, (CHUNK, CHUNK), 0)
    column = lax.broadcasted_iota(jnp.int32, (CHUNK, CHUNK), 1)
    return jnp.where((row >= column) & (seg_col == seg_row), 0.0, NEGATIVE)


def scores_of(reader, writer):
    rh, rl = split(reader)
    wh, wl = split(writer)
    return mm_nt(rh, wh) + (mm_nt(rh, wl) + mm_nt(rl, wh))


def forward_kernel(
    sizes,
    chunks,
    summed_ref,
    gate_ref,
    raw_ref,
    cum_ref,
    masks_ref,
    seg_row_ref,
    incoming_ref,
    tokens_ref,
    cot_ref,
    weight_ref,
    gain_ref,
    skip_ref,
    heads_ref,
    output_ref,
    low_ref,
    out_low_ref,
    gate_grad_ref,
    ssm_grad_ref,
    starts_ref,
    dot_ref,
    sums_ref,
    wide_ref,
    state_grad_ref,
    state,
    prefix,
    active,
    mixed_in,
    factors,
    grads,
    inv,
):
    seqs, piece, inner, channels, heads = sizes
    c = pl.program_id(1)

    @pl.when((c == 0) & (pl.program_id(0) == 0))
    def _():
        sums_ref[...] = jnp.zeros_like(sums_ref)
        wide_ref[...] = jnp.zeros_like(wide_ref)

    @pl.when(c == 0)
    def _():
        state[...] = incoming_ref[0]
        prefix[...] = jnp.zeros_like(prefix)
        state_grad_ref[...] = jnp.zeros_like(state_grad_ref)

    def activate(i, carry):
        rows = pl.ds(pl.multiple_of(i * 16, 16), 16)
        values = summed_ref[rows]
        active[rows] = values * sigmoid(values)
        return carry

    lax.fori_loop(0, CHUNK // 16, activate, 0)
    lane = lax.broadcasted_iota(jnp.int32, (CHUNK, 128), 1)
    steps = jnp.where(lane < heads, softplus(raw_ref[...]), 0.0)
    cum = cum_ref[...]
    cum_t = jnp.transpose(cum)
    final = cum[CHUNK - 1 :]
    enter = jnp.exp(cum) * masks_ref[:, 4:5]
    tails = jnp.exp(final - cum) * steps * masks_ref[:, 5:6]
    from_start = jnp.exp(cum + prefix[0:1]) * masks_ref[:, 6:7]
    prefix[...] = prefix[...] + final
    for i, block in enumerate((steps, enter, tails, from_start)):
        factors[i] = spread(block, heads_ref)
    writer = active[:, inner : inner + 128]
    reader = active[:, inner + 128 : inner + 256]
    scores = scores_of(reader, writer)
    bias = mask_bias(masks_ref[:, 8:9], seg_row_ref[0:1])
    half = lax.broadcasted_iota(jnp.int32, (CHUNK, 128), 1) < 64
    state_low = state[...].astype(BF16)
    starts_ref[0] = state_low
    reader_low = reader.astype(BF16)
    for pair in range(heads // 2):
        at = slice(pair * 128, (pair + 1) * 128)
        moved = (active[:, at] * factors[0, :, at]).astype(BF16)
        zero = jnp.zeros_like(moved)
        one = (scores * decays_of(cum, cum_t, bias, 2 * pair)).astype(BF16)
        two = (scores * decays_of(cum, cum_t, bias, 2 * pair + 1)).astype(BF16)
        both = jnp.concatenate([one, two], axis=1)
        stacked = jnp.concatenate(
            [jnp.where(half, moved, zero), jnp.where(half, zero, moved)], axis=0
        )
        carried = mm(reader_low, state_low[:, at]) * factors[1, :, at]
        mixed_in[:, at] = mm(both, stacked) + carried
    weighted = (active[:, :inner] * factors[2]).astype(BF16)
    kept = jnp.exp(final) * masks_ref[CHUNK - 1 :, 4:5]
    kept = spread(jnp.broadcast_to(kept, (8, 128)), heads_ref)[0:1]
    state[...] = state[...] * kept + mm_tn(writer.astype(BF16), weighted)

    gain = gain_ref[...]
    skip = skip_ref[...]

    def gating(i, carry):
        rows = pl.ds(pl.multiple_of(i * 16, 16), 16)
        gate = gate_ref[rows]
        mixer = mixed_in[rows] + skip * active[rows, :inner]
        gated = mixer * gate * sigmoid(gate)
        scale = lax.rsqrt(jnp.mean(gated * gated, axis=-1, keepdims=True) + EPS)
        inv[rows] = jnp.broadcast_to(scale, (16, 128))
        low_ref[rows] = (gated * scale * gain).astype(BF16)
        return carry

    lax.fori_loop(0, CHUNK // 16, gating, 0)
    mixed = mm(low_ref[...], weight_ref[...])
    block_out = tokens_ref[...].astype(F32) + mixed
    output_ref[...] = block_out.astype(BF16)
    valid = masks_ref[:, 9:10]
    for i, block in enumerate((block_out, mixed)):
        squares = jnp.sum(valid * block * block, axis=0, keepdims=True)
        for at in range(0, squares.shape[1], 128):
            sums_ref[i : i + 1] += squares[:, at : at + 128]
    sums_ref[2:3, :16] += jnp.sum(masks_ref[...], axis=0, keepdims=True)
    out_low = (cot_ref[...].astype(F32) * valid).astype(BF16)
    out_low_ref[...] = out_low
    grads[...] = mm_nt(out_low, weight_ref[...])

    def backing(i, carry):
        gain_sum, skip_sum = carry
        rows = pl.ds(pl.multiple_of(i * 16, 16), 16)
        gate = gate_ref[rows]
        turned = sigmoid(gate)
        silu = gate * turned
        signal = active[rows, :inner]
        mixer = mixed_in[rows] + skip * signal
        gated = mixer * silu
        scale = inv[rows, 0:1]
        grad = grads[rows]
        gain_sum = gain_sum + grad * gated * scale
        grad = grad * gain
        inside = jnp.mean(grad * gated, axis=-1, keepdims=True)
        gated_grad = scale * grad - gated * (scale * scale * scale * inside)
        ssm_grad = gated_grad * silu
        ssm_grad_ref[rows] = ssm_grad
        grads[rows] = ssm_grad
        skip_sum = skip_sum + ssm_grad * signal
        gate_grad_ref[rows] = (gated_grad * mixer * turned * (1.0 + gate * (1.0 - turned))).astype(
            BF16
        )
        return gain_sum, skip_sum

    start = jnp.zeros((16, inner), F32)
    gain_sum, skip_sum = lax.fori_loop(0, CHUNK // 16, backing, (start, start))
    wide_ref[0:1] += jnp.sum(gain_sum, axis=0, keepdims=True)
    wide_ref[1:2] += jnp.sum(skip_sum, axis=0, keepdims=True)
    reader_t = jnp.transpose(reader_low)
    for pair in range(heads // 2):
        at = slice(pair * 128, (pair + 1) * 128)
        state_grad_ref[0, :, at] += mm(
            reader_t, (grads[:, at] * factors[3, :, at]).astype(BF16)
        )
        mixed_in[:, at] = mixed_in[:, at] * grads[:, at].astype(BF16).astype(F32)
    dot_ref[...] = gather_heads(mixed_in[...], heads_ref)


def forward(
    summed, gate, raw, cum, masks, seg_row, incoming, tokens, cot, weight, gain, skip, heads_map, sizes
):
    seqs, piece, inner, channels, heads = sizes
    total, model = tokens.shape
    chunks = piece // CHUNK
    full = lambda *shape: pl.BlockSpec(shape, lambda n, c: (0,) * len(shape))
    rows = lambda width: pl.BlockSpec((CHUNK, width), lambda n, c: (n * chunks + c, 0))
    each = lambda depth: pl.BlockSpec((1, depth, inner), lambda n, c: (n, 0, 0))
    shape = jax.ShapeDtypeStruct
    return pl.pallas_call(
        functools.partial(forward_kernel, sizes, chunks),
        grid=(seqs, chunks),
        in_specs=[
            rows(channels),
            rows(inner),
            rows(128),
            rows(128),
            rows(16),
            pl.BlockSpec((1, CHUNK), lambda n, c: (0, n * chunks + c)),
            each(128),
            rows(model),
            rows(model),
            full(inner, model),
            full(1, inner),
            full(1, inner),
            full(128, inner),
        ],
        out_specs=(
            rows(model),
            rows(inner),
            rows(model),
            rows(inner),
            rows(inner),
            pl.BlockSpec((1, 128, inner), lambda n, c: (n * chunks + c, 0, 0)),
            rows(128),
            full(8, 128),
            full(8, inner),
            each(128),
        ),
        out_shape=(
            shape((total, model), BF16),
            shape((total, inner), BF16),
            shape((total, model), BF16),
            shape((total, inner), BF16),
            shape((total, inner), F32),
            shape((seqs * chunks, 128, inner), BF16),
            shape((total, 128), F32),
            shape((8, 128), F32),
            shape((8, inner), F32),
            shape((seqs, 128, inner), F32),
        ),
        scratch_shapes=[
            pltpu.VMEM((128, inner), F32),
            pltpu.VMEM((8, 128), F32),
            pltpu.VMEM((CHUNK, channels), F32),
            pltpu.VMEM((CHUNK, inner), F32),
            pltpu.VMEM((4, CHUNK, inner), F32),
            pltpu.VMEM((CHUNK, inner), F32),
            pltpu.VMEM((CHUNK, 128), F32),
        ],
        compiler_params=pltpu.CompilerParams(vmem_limit_bytes=48 * 1024 * 1024),
        name="forward",
    )(summed, gate, raw, cum, masks, seg_row, incoming, tokens, cot, weight, gain, skip, heads_map)


TILE = 256


class Exchange:
    def __init__(self, bits, pieces, flows):
        self.bits, self.pieces, self.flows = bits, pieces, flows
        self.parts = part_count(pieces)
        self.place, self.turn = lax.axis_index("dp"), lax.axis_index("seq")
        self.own = [(self.place // (1 << b)) % 2 for b in range(bits)]
        self.partner = [
            {"dp": self.place + (1 - 2 * self.own[b]) * (1 << b)} for b in range(bits)
        ]
        self.others = [{"seq": lax.rem(self.turn + j, pieces)} for j in range(pieces)]
        self.mine = self.index_of({b: self.own[b] for b in range(bits)})

    def index_of(self, fixed):
        return tuple(fixed.get(b, slice(None)) for b in range(self.bits - 1, -1, -1))

    def spot_of(self, d):
        return tuple((d // (1 << b)) % 2 for b in range(self.bits - 1, -1, -1))

    def order_of(self, f, h):
        rest = list(range(1, self.bits))
        shift = (f + h) % max(len(rest), 1)
        return [0] + rest[shift:] + rest[:shift]

    def share(self, h, extra=0):
        half = self.pieces // self.parts
        return pl.ds(h * half, half + (extra if h == self.parts - 1 else 0))

    def held(self, f, h, k, other):
        order = self.order_of(f, h)
        bit = order[k]
        value = 1 - self.own[bit] if other else self.own[bit]
        free = [b for b in range(self.bits - 1, -1, -1) if b not in order[:k]]
        source = self.grad if k == 0 else self.halves[k - 1]
        return source.at[
            (f,) + tuple(value if b == bit else slice(None) for b in free) + (self.share(h),)
        ]

    def landing(self, f, h, k):
        free = self.bits - k - 1
        return self.halves[k].at[(f,) + (slice(None),) * free + (self.share(h),)]

    def rs_copy(self, f, h, k):
        return remote(
            self.held(f, h, k, True),
            self.landing(f, h, k),
            self.rs_send.at[f, h, k],
            self.rs_recv.at[f, h, k],
            self.partner[self.order_of(f, h)[k]],
        )

    def rs_begin(self, f):
        for h in range(self.parts):
            self.rs_copy(f, h, 0).start()

    def rs_end(self, f, k):
        for h in range(self.parts):
            self.rs_copy(f, h, k).wait_recv()
            kept, into = self.held(f, h, k, False), self.landing(f, h, k)
            left = self.bits - k - 1
            for count in range(1 << left):
                spot = tuple((count >> (left - 1 - i)) & 1 for i in range(left))

                def body(p, carry, spot=spot, kept=kept, into=into):
                    into[spot + (p,)] = (
                        kept[spot + (p,)].astype(F32) + into[spot + (p,)].astype(F32)
                    ).astype(BF16)
                    return carry

                lax.fori_loop(0, self.pieces // self.parts, body, 0)
            if k + 1 < self.bits:
                self.rs_copy(f, h, k + 1).start()
        if k + 1 == self.bits:
            for j in range(1, self.pieces):
                self.zs_copy(f, j).start()

    def zs_copy(self, f, j):
        return remote(
            self.halves[self.bits - 1].at[f, lax.rem(self.turn + j, self.pieces)],
            self.piece_parts.at[f, j],
            self.zs_send.at[f, j],
            self.zs_recv.at[f, j],
            self.others[j],
        )

    def zs_end(self, f, rate, weight, momentum):
        for j in range(1, self.pieces):
            self.zs_copy(f, j).wait_recv()
        total = self.halves[self.bits - 1][f, self.turn].astype(F32)
        for j in range(1, self.pieces):
            total = total + self.piece_parts[f, j].astype(F32)
        summed = total.astype(BF16)
        moved = 0.5 * momentum + summed.astype(F32)
        self.gathered[(f,) + self.mine + (self.pieces,)] = summed
        self.gathered[(f,) + self.mine + (self.turn,)] = (
            weight.astype(F32) - rate * moved
        ).astype(BF16)
        for j in range(1, self.pieces):
            self.zg_copy(f, j).start()

    def zg_copy(self, f, j):
        spot = self.gathered.at[(f,) + self.mine + (self.turn,)]
        return remote(spot, spot, self.zg_send.at[f, j], self.zg_recv.at[f, j], self.others[j])

    def zg_end(self, f):
        for j in range(1, self.pieces):
            self.zg_copy(f, j).wait_recv()
        for h in range(self.parts):
            self.ag_copy(f, h, self.bits - 1).start()

    def ag_copy(self, f, h, k):
        order = self.order_of(f, h)
        fixed = {order[i]: self.own[order[i]] for i in range(k + 1)}
        spot = self.gathered.at[(f,) + self.index_of(fixed) + (self.share(h, 1),)]
        return remote(
            spot,
            spot,
            self.ag_send.at[f, h, k],
            self.ag_recv.at[f, h, k],
            self.partner[order[k]],
        )

    def ag_end(self, f, k):
        for h in range(self.parts):
            self.ag_copy(f, h, k).wait_recv()
            if k > 0:
                self.ag_copy(f, h, k - 1).start()

    def tiles_sent(self):
        for f in range(self.flows):
            for h in range(self.parts):
                self.rs_copy(f, h, 0).wait_send()

    def sent(self):
        for f in range(self.flows):
            for h in range(self.parts):
                for k in range(self.bits):
                    if k > 0:
                        self.rs_copy(f, h, k).wait_send()
                    self.ag_copy(f, h, k).wait_send()
            for j in range(1, self.pieces):
                self.zs_copy(f, j).wait_send()
                self.zg_copy(f, j).wait_send()

    def actions(self, f, rate, weights, momenta, after):
        steps = [functools.partial(self.rs_end, f, k) for k in range(self.bits)]
        steps.append(lambda: self.zs_end(f, rate, weights[f], momenta[f]))
        steps.append(functools.partial(self.zg_end, f))
        steps += [functools.partial(self.ag_end, f, k) for k in range(self.bits - 1, 0, -1)]

        def finish():
            self.ag_end(f, 0)
            after(f)

        return steps + [finish]


def exchange_scratch(bits, pieces, flows, rows, first=-1):
    parts = part_count(pieces)
    return (
        [pltpu.VMEM(half_shape(bits, pieces, flows, rows, k), BF16) for k in range(first, bits)]
        + [
            pltpu.VMEM((flows, pieces, rows, LANES), BF16),
            pltpu.VMEM((flows,) + (2,) * bits + (pieces + 1, rows, LANES), BF16),
        ]
        + dma_semaphores(flows, parts, bits)
        + dma_semaphores(flows, pieces)
        + dma_semaphores(flows, pieces)
        + dma_semaphores(flows, parts, bits)
        + [pltpu.SemaphoreType.DMA((flows,))]
    )


def give(ex, scratch, grad=None):
    if grad is None:
        grad, scratch = scratch[0], scratch[1:]
    ex.grad, ex.halves = grad, scratch[: ex.bits]
    scratch = scratch[ex.bits :]
    (ex.piece_parts, ex.gathered, ex.rs_send, ex.rs_recv, ex.zs_send, ex.zs_recv) = scratch[:6]
    (ex.zg_send, ex.zg_recv, ex.ag_send, ex.ag_recv, ex.out_sem) = scratch[6:11]
    return scratch[11:]


def tail_kernel(sizes, dims, *refs):
    seqs, piece, inner, channels, heads = sizes
    bits, pieces, flows_a, flows_b, split_rows, blocks = dims
    (
        rate_ref,
        summed_ref,
        conv_ref,
        halo_ref,
        taps_ref,
        ssm_grad_ref,
        starts_ref,
        heads_ref,
        skip_ref,
        summed_rw_ref,
        raw_ref,
        cum_ref,
        masks_ref,
        seg_row_ref,
        dot_ref,
        a_log_ref,
        own_ref,
        keep_ref,
        out_low_ref,
        normed_ref,
        low_ref,
        gate_grad_ref,
        weight_t_ref,
        tokens_ref,
        gain_ref,
        weight_ref,
        momentum_ref,
        wide_ref,
        squares_ref,
        input_grad_ref,
        small_out_ref,
        out_a_ref,
        out_b_ref,
    ) = refs[:33]
    scratch = refs[33:]
    a, b = Exchange(bits, pieces, flows_a), Exchange(bits, pieces, flows_b)
    scratch = give(a, scratch)
    scratch = give(b, scratch, a.grad)
    (
        sent,
        taken,
        chain_send,
        chain_recv,
        later,
        out_turned,
        normed_turned,
        writer_low,
        reader_low,
        reader_turned,
        scores,
        cum_turned,
        biases,
        scores_grad,
        reader_grad,
        writer_grad,
        active,
        bent,
        step_x,
        cum_x,
        total,
        state_grad,
        ends,
        step_sum,
        move_sum,
        end_sum,
        shifted_rows,
        proj_grad,
        tails,
        rims,
        rims_in,
        rim_send,
        rim_recv,
        conv_sums,
        head_sums,
        gain_sums,
        small_acc,
        small_in,
        small_parts,
        sm_send,
        sm_recv,
        sz_send,
        sz_recv,
    ) = scratch
    j = pl.program_id(0)
    steps = inner // TILE
    final_step = steps + 1
    places = 1 << bits
    per_flow = places // split_rows
    turn = a.turn
    chunk_count = seqs * piece // CHUNK
    rows = a.grad.shape[-2]
    chunks = piece // CHUNK
    rate = rate_ref[0]
    real = 2 * inner // LANES

    def out_copy(ex, out, f):
        return pltpu.make_async_copy(ex.gathered.at[f], out.at[f], ex.out_sem.at[f])

    a_actions = [
        a.actions(f, rate, weight_ref, momentum_ref, lambda f: out_copy(a, out_a_ref, f).start())
        for f in range(flows_a)
    ]
    late = [weight_ref.at[pl.ds(flows_a, flows_b)], momentum_ref.at[pl.ds(flows_a, flows_b)]]
    b_actions = [
        b.actions(f, rate, *late, lambda f: out_copy(b, out_b_ref, f).start())
        for f in range(flows_b)
    ]

    def store(ex, tile, values):
        for part in range(split_rows):
            d = (tile % per_flow) * split_rows + part
            spot = (tile // per_flow,) + ex.spot_of(d)
            for p in range(pieces):
                at = (p * split_rows + part) * rows
                ex.grad[spot + (p,)] = values[at : at + rows]

    def rim_copy(slot):
        return remote(
            rims.at[slot],
            rims_in.at[slot],
            rim_send.at[slot],
            rim_recv.at[slot],
            {"seq": lax.rem(turn + pieces - 1, pieces)},
        )

    def fix_rim(slot, at):
        @pl.when(turn < pieces - 1)
        def _():
            rim_copy(slot).wait_recv()
            for n in range(seqs):
                proj_grad[(n + 1) * piece - 8 : (n + 1) * piece, at] = (
                    tails[n] + rims_in[slot, n].astype(F32)
                ).astype(BF16)

    def conv_back(slot, at):
        for n in range(seqs):
            here_rows = pl.ds(n * piece, piece)
            grad = total[here_rows] * bent[here_rows]
            conv = conv_ref[here_rows]
            sums = [None] * 5
            sums[4] = jnp.sum(grad, axis=0, keepdims=True)
            sums[3] = jnp.sum(grad * conv, axis=0, keepdims=True)
            result = grad * taps_ref[3:4]
            rim = jnp.zeros((8, TILE), F32)
            shifted_rows[0:8] = jnp.zeros((8, TILE), F32)
            shifted_rows[8 + piece :] = jnp.zeros((8, TILE), F32)
            for k in range(3):
                shifted_rows[8 : 8 + piece] = grad * masks_ref[here_rows, k : k + 1]
                here = shifted_rows[11 - k : 11 - k + piece]
                result = result + here * taps_ref[k : k + 1]
                early = shifted_rows[3 - k : 11 - k]
                rim = rim + early * taps_ref[k : k + 1]
                sums[k] = jnp.sum(here * conv, axis=0, keepdims=True) + jnp.sum(
                    early * halo_ref[(n + 1) * HALO - 8 : (n + 1) * HALO], axis=0, keepdims=True
                )
            for i in range(5):
                if n == 0:
                    conv_sums[i : i + 1, at] = sums[i]
                else:
                    conv_sums[i : i + 1, at] += sums[i]
            proj_grad[here_rows, at] = result.astype(BF16)
            tails[n] = result[piece - 8 :]
            rims[slot, n] = rim.astype(BF16)

        @pl.when(turn > 0)
        def _():
            rim_copy(slot).start()

    @pl.when(j == 0)
    def _():
        greet(a.partner + a.others[1:])
        first, final = turn == pieces - 1, turn == 0
        width = inner // blocks

        def copy(c):
            ahead = {"seq": lax.rem(turn + pieces - 1, pieces)}
            return remote(sent.at[c], taken.at[c], chain_send.at[c], chain_recv.at[c], ahead)

        @pl.when(first)
        def _():
            later[...] = jnp.zeros_like(later)
            for c in range(blocks):
                sent[c] = own_ref[:, :, c * width : (c + 1) * width].astype(BF16)
                copy(c).start()

        out_turned[...] = jnp.transpose(out_low_ref[...])
        normed_turned[...] = jnp.transpose(normed_ref[...])
        low_tiles = inner // LANES

        def tiles(tile):
            if tile >= real:
                result = jnp.zeros((out_turned.shape[0], 2 * LANES), BF16)
            elif tile < low_tiles:
                at = tile * LANES
                result = mm(out_turned[...], low_ref[:, at : at + 2 * LANES]).astype(BF16)
            else:
                at = (tile - low_tiles) * LANES
                result = mm(normed_turned[...], gate_grad_ref[:, at : at + 2 * LANES])
                result = result.astype(BF16)
            store(a, tile, result[:, :LANES])
            store(a, tile + 1, result[:, LANES:])

        pairs = flows_a * per_flow // 2
        done = 0
        for c in range(blocks):
            until = pairs * (c + 1) // blocks
            for pair in range(done, until):
                tiles(2 * pair)
                if (2 * pair + 2) % per_flow == 0:
                    a.rs_begin(2 * pair // per_flow)
            done = until

            @pl.when(jnp.logical_not(first))
            def _():
                at = slice(c * width, (c + 1) * width)
                copy(c).wait_recv()

                @pl.when(jnp.logical_not(final))
                def _():
                    sent[c] = (
                        own_ref[:, :, at] + keep_ref[:, 0:1, at] * taken[c].astype(F32)
                    ).astype(BF16)
                    copy(c).start()

                later[:, :, at] = taken[c].astype(F32)

        for f in range(flows_a):
            a_actions[f][0]()
        a.tiles_sent()
        for ck in range(chunk_count):
            at = slice(ck * CHUNK, (ck + 1) * CHUNK)
            values = summed_rw_ref[at]
            values = values * sigmoid(values)
            writer, reader = values[:, :128], values[:, 128:]
            scores[ck] = scores_of(reader, writer)
            writer_low[at] = writer.astype(BF16)
            reader_low[at] = reader.astype(BF16)
            reader_turned[ck] = jnp.transpose(reader.astype(BF16))
            cum_turned[ck] = jnp.transpose(cum_ref[at])
            biases[ck] = mask_bias(masks_ref[at, 8:9], seg_row_ref[0:1, at])
        for ref in (
            scores_grad,
            reader_grad,
            writer_grad,
            step_sum,
            move_sum,
            end_sum,
            ends,
            gain_sums,
        ):
            ref[...] = jnp.zeros_like(ref)

        @pl.when(jnp.logical_not(final))
        def _():
            for c in range(blocks):
                copy(c).wait_send()

    agenda = {}

    def plan(step, act):
        agenda.setdefault(min(max(step, 1), steps), []).append(act)

    last_b = [((f + 1) * per_flow * LANES - 1) // TILE + 1 for f in range(flows_b)]
    a_steps = {1: 3, 2: 4} if bits == 3 else {k: 1 + k for k in range(1, bits)}
    a_done = b_ready = None
    for k in range(1, bits):
        for f in range(flows_a):
            plan(a_steps[k], a_actions[f][k])
    b_taken = []
    for f in range(flows_b):
        taken_steps = 0
        if last_b[f] + 1 <= steps:
            plan(last_b[f] + 1, functools.partial(b.rs_begin, f))
            for i in range(bits):
                if last_b[f] + 2 + i <= steps:
                    plan(last_b[f] + 2 + i, b_actions[f][i])
                    taken_steps = i + 1
            b_taken.append(taken_steps)
        else:
            b_taken.append(None)

    def weight_tiles(tile, at):
        result = mm(normed_turned[...], proj_grad[:, at]).astype(BF16)
        store(b, tile, result[:, :LANES])
        store(b, tile + 1, result[:, LANES:])

    @pl.when((j > 0) & (j < final_step))
    def _():
        at = pl.ds(pl.multiple_of((j - 1) * TILE, TILE), TILE)

        @pl.when(j > 1)
        def _():
            before = pl.ds(pl.multiple_of((j - 2) * TILE, TILE), TILE)
            fix_rim(j - 2, before)
            weight_tiles((j - 2) * (TILE // LANES), before)

        def activate(i, carry):
            rows_at = pl.ds(pl.multiple_of(i * 32, 32), 32)
            values = summed_ref[rows_at]
            turned = sigmoid(values)
            active[rows_at] = values * turned
            bent[rows_at] = turned * (1.0 + values * (1.0 - turned))
            return carry

        lax.fori_loop(0, seqs * piece // 32, activate, 0)
        raw = raw_ref[...]
        lane = lax.broadcasted_iota(jnp.int32, raw.shape, 1)
        step_x[...] = spread(jnp.where(lane < heads, softplus(raw), 0.0), heads_ref)
        cum = cum_ref[...]
        high, low = split(cum)
        lowest = (cum - high.astype(F32) - low.astype(F32)).astype(BF16)
        cum_x[...] = (
            mm(high, heads_ref[...]) + mm(low, heads_ref[...]) + mm(lowest, heads_ref[...])
        )
        half = lax.broadcasted_iota(jnp.int32, (CHUNK, 128), 1) < 64
        head = (j - 1) * (TILE // 64)
        skip = skip_ref[...]
        for n in range(seqs):
            state_grad[...] = later[n, :, at]
            for c in range(chunks - 1, -1, -1):
                ck = n * chunks + c
                here = slice(ck * CHUNK, (ck + 1) * CHUNK)
                cum_here = cum_x[here]
                final_cum = cum_here[CHUNK - 1 :]
                enter_x = jnp.exp(cum_here) * masks_ref[here, 4:5]
                tail_x = jnp.exp(final_cum - cum_here) * masks_ref[here, 5:6]
                kept = jnp.exp(final_cum) * masks_ref[(ck + 1) * CHUNK - 1 : (ck + 1) * CHUNK, 4:5]
                signal = active[here]
                grad = ssm_grad_ref[here]
                moved = (signal * step_x[here]).astype(BF16)
                grad_low = grad.astype(BF16)
                later_low = state_grad[...].astype(BF16)
                from_later = mm(writer_low[here], later_low) * tail_x
                parts = []
                score = scores[ck]
                bias = biases[ck]
                grad_of_scores = scores_grad[ck]
                for pair in range(TILE // 128):
                    col = slice(pair * 128, (pair + 1) * 128)
                    ones = []
                    for i in range(2):
                        lane_at = pair * 128 + i * 64
                        ones.append(
                            jnp.exp(
                                cum_here[:, lane_at : lane_at + 1]
                                - cum_turned[ck, pl.ds(head + 2 * pair + i, 1), :]
                                + bias
                            )
                        )
                    zero = jnp.zeros((CHUNK, 128), BF16)
                    stacked = jnp.concatenate(
                        [
                            jnp.where(half, grad_low[:, col], zero),
                            jnp.where(half, zero, grad_low[:, col]),
                        ],
                        axis=0,
                    )
                    both_grad = mm_nt(stacked, moved[:, col])
                    grad_of_scores = (
                        grad_of_scores + both_grad[:CHUNK] * ones[0] + both_grad[CHUNK:] * ones[1]
                    )
                    both = jnp.concatenate([(score * one).astype(BF16) for one in ones], axis=0)
                    parts.append(mm_tn(both, stacked))
                scores_grad[ck] = grad_of_scores
                moved_grad = jnp.concatenate(parts, axis=1) + from_later
                wide_moved = moved.astype(F32)
                weighted = (wide_moved * tail_x).astype(BF16)
                entered = (grad * enter_x).astype(BF16)
                start = starts_ref[ck]
                reader_grad[here] += mm_nt(entered, start)
                writer_grad[here] += mm_nt(weighted, later_low)
                passed = jnp.sum(
                    start.astype(F32) * later_low.astype(F32), axis=0, keepdims=True
                )
                ends[ck : ck + 1] = kept * passed + jnp.sum(
                    wide_moved * from_later, axis=0, keepdims=True
                )
                state_grad[...] = state_grad[...] * kept + mm(reader_turned[ck], entered)
                step_sum[here] += gather_heads(moved_grad * signal, heads_ref)
                move_sum[here] += gather_heads(moved_grad * wide_moved, heads_ref)
                total[here] = moved_grad * step_x[here] + skip * grad
        end_sum[...] += gather_heads(ends[...], heads_ref)
        conv_back(j - 1, at)
        for step in sorted(agenda):

            @pl.when(j == step)
            def _(step=step):
                for act in agenda[step]:
                    act()

    @pl.when(j == final_step)
    def _():
        before = slice((steps - 1) * TILE, steps * TILE)
        fix_rim(steps - 1, before)
        weight_tiles((steps - 1) * (TILE // LANES), before)
        pending = []
        for f in range(flows_b):
            if last_b[f] == steps and b_taken[f] is None:
                b.rs_begin(f)
                b_taken[f] = 0
        at = slice(inner, channels)
        lane = lax.broadcasted_iota(jnp.int32, (CHUNK, 128), 1)
        row = lax.broadcasted_iota(jnp.int32, (CHUNK, 128), 0)
        upper = triangle(CHUNK, True)
        decay_rate = -jnp.exp(a_log_ref[...])
        raw_sum = jnp.zeros((1, 128), F32)
        decay_sum = jnp.zeros((1, 128), F32)
        values = summed_rw_ref[...]
        turned = sigmoid(values)
        bent[...] = turned * (1.0 + values * (1.0 - turned))
        for ck in range(chunk_count):
            here = slice(ck * CHUNK, (ck + 1) * CHUNK)
            high, low = split(scores_grad[ck])
            total[here, 128:] = (
                reader_grad[here] + mm(high, writer_low[here]) + mm(low, writer_low[here])
            )
            total[here, :128] = (
                writer_grad[here] + mm_tn(high, reader_low[here]) + mm_tn(low, reader_low[here])
            )
            raw = raw_ref[here]
            taken_steps = jnp.where(lane < heads, softplus(raw), 0.0)
            change = dot_ref[here] - move_sum[here]
            change = change + jnp.where(row == CHUNK - 1, end_sum[ck : ck + 1], 0.0)
            decay_grad = exact_mm(upper, change)
            raw_grad = jnp.where(
                lane < heads, (step_sum[here] + decay_grad * decay_rate) * sigmoid(raw), 0.0
            )
            raw_sum = raw_sum + jnp.sum(raw_grad, axis=0, keepdims=True)
            decay_sum = decay_sum + jnp.sum(
                decay_grad * taken_steps * decay_rate, axis=0, keepdims=True
            )
            proj_grad[here, channels : channels + 128] = raw_grad.astype(BF16)
            proj_grad[here, channels + 128 :] = jnp.zeros((CHUNK, 128), BF16)
        head_sums[0:1] = raw_sum
        head_sums[1:2] = decay_sum
        conv_back(steps, at)
        fix_rim(steps, at)
        for tile in range(inner // LANES, flows_b * per_flow, 2):
            if tile * LANES < channels + 256:
                weight_tiles(tile, slice(tile * LANES, (tile + 2) * LANES))
            else:
                for i in range(2):
                    store(b, tile + i, jnp.zeros((pieces * split_rows * rows, LANES), BF16))
        for f in range(flows_b):
            if b_taken[f] is None:
                b.rs_begin(f)
                b_taken[f] = 0

        rest = weight_t_ref.shape[0] - inner

        def input_rows(i, carry):
            rows_at = pl.ds(pl.multiple_of(i * 128, 128), 128)
            normed_grad = mm(gate_grad_ref[rows_at], weight_t_ref[:inner]) + mm(
                proj_grad[rows_at, :rest], weight_t_ref[inner:]
            )
            values = tokens_ref[rows_at].astype(F32)
            scale = lax.rsqrt(jnp.mean(values * values, axis=-1, keepdims=True) + EPS)
            gain_sums[0:1] += jnp.sum(normed_grad * values * scale, axis=0, keepdims=True)
            pushed = normed_grad * gain_ref[...]
            inside = jnp.mean(pushed * values, axis=-1, keepdims=True)
            input_grad_ref[rows_at] = (
                out_low_ref[rows_at].astype(F32)
                + scale * pushed
                - values * (scale * scale * scale * inside)
            ).astype(BF16)
            return carry

        def sm_copy(k):
            return remote(
                small_acc.at[k], small_in.at[k], sm_send.at[k], sm_recv.at[k], a.partner[k]
            )

        def sz_copy(k):
            return remote(
                small_acc.at[bits],
                small_parts.at[turn],
                sz_send.at[k],
                sz_recv.at[k],
                a.others[k],
            )

        def small_begin():
            model = gain_sums.shape[1]
            small_acc[0, 0:5] = conv_sums[0:5]
            small_acc[0, 5:7, :inner] = wide_ref[0:2]
            small_acc[0, 5:7, inner : inner + 128] = head_sums[0:2]
            small_acc[0, 5:8, inner + 128 :] = squares_ref[0:3]
            small_acc[0, 7:8, :model] = gain_sums[0:1]
            small_acc[0, 7:8, model : inner + 128] = jnp.zeros((1, inner + 128 - model), F32)
            sm_copy(0).start()

        def small_step(k):
            sm_copy(k).wait_recv()
            small_acc[k + 1] = small_acc[k] + small_in[k]
            if k + 1 < bits:
                sm_copy(k + 1).start()
            else:
                small_parts[turn] = small_acc[bits]
                for i in range(1, pieces):
                    sz_copy(i).start()

        def small_end():
            for i in range(1, pieces):
                sz_copy(i).wait_recv()
            whole = small_parts[0]
            for i in range(1, pieces):
                whole = whole + small_parts[i]
            small_out_ref[...] = whole

        lines = [a_actions[f][bits:] for f in range(flows_a)]
        lines += [b_actions[f][b_taken[f] :] for f in range(flows_b)]
        blocks_of_rows = tokens_ref.shape[0] // 128
        extra = [
            lambda: lax.fori_loop(0, blocks_of_rows // 2, input_rows, 0),
            lambda: lax.fori_loop(blocks_of_rows // 2, blocks_of_rows, input_rows, 0),
            small_begin,
        ]
        extra += [functools.partial(small_step, k) for k in range(bits)] + [small_end]
        while any(lines) or extra:
            if extra:
                extra.pop(0)()
            for line in lines:
                if line:
                    line.pop(0)()
        b.tiles_sent()
        a.sent()
        b.sent()
        for k in range(bits):
            sm_copy(k).wait_send()
        for i in range(1, pieces):
            sz_copy(i).wait_send()

        @pl.when(turn > 0)
        def _():
            for slot in range(steps + 1):
                rim_copy(slot).wait_send()

        for f in range(flows_a):
            out_copy(a, out_a_ref, f).wait()
        for f in range(flows_b):
            out_copy(b, out_b_ref, f).wait()


def row_split(places, rows):
    return 2 if places > 2 and rows % 32 == 0 else 1


def tail(
    rate,
    tiled,
    summed_rw_source,
    whole,
    weights,
    momenta,
    wide,
    squares,
    sizes,
    places,
    pieces,
    flows,
    blocks=6,
):
    seqs, piece, inner, channels, heads = sizes
    summed, conv, halo, taps, ssm_grad, starts, heads_map, skip = tiled
    total_rows = summed.shape[0]
    own = whole[6]
    tokens, weight_t = whole[13], whole[12]
    model = tokens.shape[1]
    flows_a, flows_b = flows
    assert flows_b <= flows_a
    bits = places.bit_length() - 1
    assert places == 1 << bits and bits >= 1 and pieces >= 2
    share = model // pieces
    split_rows = row_split(places, share)
    rows = share // split_rows
    steps = inner // TILE
    small = (8, channels)
    shape = jax.ShapeDtypeStruct
    any_space = pl.BlockSpec(memory_space=pl.ANY)
    sem = dma_semaphores

    def constant(array):
        count = array.ndim
        return pl.BlockSpec(
            array.shape, lambda j: (0,) * count, pipeline_mode=pl.Buffered(1)
        )

    def columns(height, last):
        return pl.BlockSpec((height, TILE), lambda j: (0, jnp.clip(j - 1, 0, last)))

    gathered = lambda count: (count,) + (2,) * bits + (pieces + 1, rows, LANES)
    chunk_count = total_rows // CHUNK
    square = (chunk_count, CHUNK, CHUNK)
    per_tile = (total_rows, TILE)
    per_head = (total_rows, 128)
    constants = list(whole) + [weights, momenta, wide, squares]
    return pl.pallas_call(
        functools.partial(
            tail_kernel, sizes, (bits, pieces, flows_a, flows_b, split_rows, blocks)
        ),
        grid=(steps + 2,),
        in_specs=[
            pl.BlockSpec(memory_space=pltpu.SMEM),
            columns(total_rows, steps),
            columns(total_rows, steps),
            columns(halo.shape[0], steps),
            columns(4, steps),
            columns(total_rows, steps - 1),
            pl.BlockSpec(
                (chunk_count, 128, TILE), lambda j: (0, 0, jnp.clip(j - 1, 0, steps - 1))
            ),
            columns(128, steps - 1),
            columns(1, steps - 1),
            pl.BlockSpec((total_rows, TILE), lambda j: (0, steps), pipeline_mode=pl.Buffered(1)),
        ]
        + [constant(array) for array in constants],
        out_specs=(
            pl.BlockSpec((total_rows, model), lambda j: (0, 0)),
            pl.BlockSpec(small, lambda j: (0, 0)),
            any_space,
            any_space,
        ),
        out_shape=(
            shape((total_rows, model), BF16),
            shape(small, F32),
            shape(gathered(flows_a), BF16),
            shape(gathered(flows_b), BF16),
        ),
        scratch_shapes=exchange_scratch(bits, pieces, flows_a, rows)
        + exchange_scratch(bits, pieces, flows_b, rows, 0)
        + [pltpu.VMEM((blocks, seqs, 128, inner // blocks), BF16)] * 2
        + sem(blocks)
        + [
            pltpu.VMEM((seqs, 128, inner), F32),
            pltpu.VMEM((model, total_rows), BF16),
            pltpu.VMEM((model, total_rows), BF16),
            pltpu.VMEM(per_head, BF16),
            pltpu.VMEM(per_head, BF16),
            pltpu.VMEM(square, BF16),
            pltpu.VMEM(square, F32),
            pltpu.VMEM(square, F32),
            pltpu.VMEM(square, F32),
            pltpu.VMEM(square, F32),
            pltpu.VMEM(per_head, F32),
            pltpu.VMEM(per_head, F32),
            pltpu.VMEM(per_tile, F32),
            pltpu.VMEM(per_tile, F32),
            pltpu.VMEM(per_tile, F32),
            pltpu.VMEM(per_tile, F32),
            pltpu.VMEM(per_tile, F32),
            pltpu.VMEM((128, TILE), F32),
            pltpu.VMEM((max(chunk_count, 8), TILE), F32),
            pltpu.VMEM(per_head, F32),
            pltpu.VMEM(per_head, F32),
            pltpu.VMEM((max(chunk_count, 8), 128), F32),
            pltpu.VMEM((piece + 16, TILE), F32),
            pltpu.VMEM((total_rows, channels + 256), BF16),
            pltpu.VMEM((seqs, 8, TILE), F32),
            pltpu.VMEM((steps + 1, seqs, 8, TILE), BF16),
            pltpu.VMEM((steps + 1, seqs, 8, TILE), BF16),
        ]
        + sem(steps + 1)
        + [
            pltpu.VMEM(small, F32),
            pltpu.VMEM((8, 128), F32),
            pltpu.VMEM((8, model), F32),
            pltpu.VMEM((bits + 1,) + small, F32),
            pltpu.VMEM((bits,) + small, F32),
            pltpu.VMEM((pieces,) + small, F32),
        ]
        + sem(bits)
        + sem(pieces),
        compiler_params=pltpu.CompilerParams(
            collective_id=2, has_side_effects=True, vmem_limit_bytes=62 * 1024 * 1024
        ),
        name="tail",
    )(rate, *tiled, summed_rw_source, *constants)


def piece_kernel(
    counts, spot_ref, out_weight_ref, weight_ref, out_momentum_ref, momentum_ref, w_ref, m_ref, turned
):
    out_tiles, tile_of, split_rows = counts
    tile = tile_of(pl.program_id(0), spot_ref)
    rows = m_ref.shape[1]
    part = lax.rem(spot_ref[0], split_rows)
    mine = pl.ds(pl.multiple_of((spot_ref[1] * split_rows + part) * rows, 16), rows)
    half = pl.ds(pl.multiple_of(part * rows, 16), rows)

    @pl.when(tile < out_tiles)
    def _():
        turned[...] = jnp.transpose(out_weight_ref[...])
        w_ref[0] = turned[mine]
        m_ref[0] = out_momentum_ref[half]

    @pl.when(tile >= out_tiles)
    def _():
        turned[...] = jnp.transpose(weight_ref[...])
        w_ref[0] = turned[mine]
        m_ref[0] = momentum_ref[half]


def owned(spot, out_weight, weight_t, out_momentum_t, momentum, flows_a, flows_b, places):
    inner, model = out_weight.shape
    share, width = momentum.shape
    out_tiles, in_tiles = inner // LANES, -(-width // LANES)
    split_rows = row_split(places, share)
    rows, per_flow = share // split_rows, places // split_rows

    flows = flows_a + flows_b

    def tile_of(f, spot):
        early = jnp.minimum(f * per_flow + spot[0] // split_rows, 2 * out_tiles - 1)
        late = 2 * out_tiles + (f - flows_a) * per_flow + spot[0] // split_rows
        return jnp.where(f < flows_a, early, late)

    def out_at(f, spot):
        return jnp.clip(tile_of(f, spot), 0, out_tiles - 1)

    def in_at(f, spot):
        return jnp.clip(tile_of(f, spot) - out_tiles, 0, in_tiles - 1)

    piece = pl.BlockSpec((1, rows, LANES), lambda f, spot: (f, 0, 0))
    return pl.pallas_call(
        functools.partial(piece_kernel, (out_tiles, tile_of, split_rows)),
        grid_spec=pltpu.PrefetchScalarGridSpec(
            num_scalar_prefetch=1,
            grid=(flows,),
            in_specs=[
                pl.BlockSpec((LANES, model), lambda f, spot: (out_at(f, spot), 0)),
                pl.BlockSpec((LANES, model), lambda f, spot: (in_at(f, spot), 0)),
                pl.BlockSpec((share, LANES), lambda f, spot: (0, out_at(f, spot))),
                pl.BlockSpec((share, LANES), lambda f, spot: (0, in_at(f, spot))),
            ],
            out_specs=(piece, piece),
            scratch_shapes=[pltpu.VMEM((model, LANES), BF16)],
        ),
        out_shape=(
            jax.ShapeDtypeStruct((flows, rows, LANES), BF16),
            jax.ShapeDtypeStruct((flows, rows, LANES), F32),
        ),
        name="owned",
    )(spot, out_weight, weight_t, out_momentum_t, momentum)


def finish_kernel(
    out_steps,
    split_rows,
    gathered_a_ref,
    gathered_b_ref,
    out_momentum_ref,
    momentum_ref,
    out_weight_ref,
    weight_ref,
    new_out_momentum_ref,
    new_momentum_ref,
    joined,
):
    group, slots, rows, _ = gathered_a_ref.shape
    step = pl.program_id(0)

    def write(gathered_ref, weights, old, new):
        for i in range(group // split_rows):
            at = slice(i * LANES, (i + 1) * LANES)
            for part in range(split_rows):
                for p in range(slots - 1):
                    to = (p * split_rows + part) * rows
                    joined[to : to + rows] = gathered_ref[i * split_rows + part, p]
                own = slice(part * rows, (part + 1) * rows)
                summed = gathered_ref[i * split_rows + part, slots - 1].astype(F32)
                new[own, at] = 0.5 * old[own, at] + summed
            weights[at] = jnp.transpose(joined[...])

    @pl.when(step < out_steps)
    def _():
        write(gathered_a_ref, out_weight_ref, out_momentum_ref, new_out_momentum_ref)

    @pl.when((step >= out_steps) & (step < 2 * out_steps))
    def _():
        write(gathered_a_ref, weight_ref, momentum_ref, new_momentum_ref)

    @pl.when(step >= 2 * out_steps)
    def _():
        write(gathered_b_ref, weight_ref, momentum_ref, new_momentum_ref)


def finish(gathered_a, gathered_b, out_momentum_t, momentum, split_rows, group=4):
    _, slots, rows, _ = gathered_a.shape
    share, width = momentum.shape
    inner = out_momentum_t.shape[1]
    model = (slots - 1) * share
    wide = group * LANES
    group = group * split_rows
    out_steps, in_steps = inner // wide, -(-width // wide)
    out_at = lambda j: jnp.minimum(j, out_steps - 1)
    in_at = lambda j: jnp.maximum(j - out_steps, 0)
    by_column = [
        pl.BlockSpec((share, wide), lambda j: (0, out_at(j))),
        pl.BlockSpec((share, wide), lambda j: (0, in_at(j))),
    ]
    shape = jax.ShapeDtypeStruct
    return pl.pallas_call(
        functools.partial(finish_kernel, out_steps, split_rows),
        grid=(out_steps + in_steps,),
        in_specs=[
            pl.BlockSpec(
                (group, slots, rows, LANES), lambda j: (jnp.minimum(j, 2 * out_steps - 1), 0, 0, 0)
            ),
            pl.BlockSpec(
                (group, slots, rows, LANES), lambda j: (jnp.maximum(j - 2 * out_steps, 0), 0, 0, 0)
            ),
        ]
        + by_column,
        out_specs=[
            pl.BlockSpec((wide, model), lambda j: (out_at(j), 0)),
            pl.BlockSpec((wide, model), lambda j: (in_at(j), 0)),
        ]
        + by_column,
        out_shape=(
            shape((inner, model), BF16),
            shape((width, model), BF16),
            shape((share, inner), F32),
            shape((share, width), F32),
        ),
        scratch_shapes=[pltpu.VMEM((model, LANES), BF16)],
        name="finish",
    )(gathered_a, gathered_b, out_momentum_t, momentum)


def local(
    tokens,
    cotangent,
    segment_ids,
    doc_starts,
    valid_mask,
    step_number,
    learn_rate,
    norm_gain,
    in_weight,
    conv_weight,
    conv_bias,
    dt_bias,
    a_log,
    skip_d,
    gate_gain,
    out_weight,
    in_momentum,
    out_momentum,
):
    seqs, piece, model_width = tokens.shape
    heads = dt_bias.shape[0]
    tap_count, channels = conv_weight.shape
    inner_width = gate_gain.shape[0]
    proj_width = in_weight.shape[1]
    total = seqs * piece
    sizes = (seqs, piece, inner_width, channels, heads)
    places, pieces = lax.axis_size("dp"), lax.axis_size("seq")
    turn = lax.axis_index("seq")
    seg = segment_ids.astype(F32)
    sent = jnp.concatenate(
        [
            tokens[:, piece - HALO :],
            jnp.broadcast_to(seg[:, piece - HALO :, None], (seqs, HALO, LANES)).astype(BF16),
        ],
        axis=2,
    )
    route = [(i, i + 1) for i in range(pieces - 1)]
    arrived = lax.ppermute(sent, "seq", route)
    halo = arrived[:, :, :model_width].reshape(seqs * HALO, model_width)
    early_seg = jnp.where(turn == 0, -1.0, arrived[:, :, model_width].astype(F32))
    seg_pad = jnp.concatenate([early_seg, seg], axis=1)
    seg_row = seg.reshape(1, total)
    heads_map = (
        lax.broadcasted_iota(jnp.int32, (LANES, inner_width), 0)
        == lax.broadcasted_iota(jnp.int32, (LANES, inner_width), 1) // (inner_width // heads)
    ).astype(BF16)

    def lanes(values):
        return jnp.pad(values, (0, LANES - heads)).reshape(1, LANES)

    flat_tokens = tokens.reshape(total, model_width)
    weight_t = jnp.transpose(in_weight)
    out_momentum_t = jnp.transpose(out_momentum)
    flat_cot = cotangent.reshape(total, model_width)
    bias_row, decay_row = lanes(dt_bias), lanes(a_log)
    skip_row = jnp.repeat(skip_d, inner_width // heads).reshape(1, inner_width)
    gain_row = gate_gain.reshape(1, inner_width)
    normed, masks, gate, conv, conv_halo, summed, raw, cum, fresh, keep = front(
        flat_tokens,
        halo,
        norm_gain.reshape(1, model_width),
        weight_t,
        conv_weight,
        conv_bias.reshape(1, channels),
        seg_pad,
        valid_mask,
        bias_row,
        decay_row,
        heads_map,
        sizes,
    )
    incoming = chain(fresh, keep, 1)
    output, low, out_low, gate_grad, ssm_grad, starts, dots, squares, wide, state_grad = forward(
        summed,
        gate,
        raw,
        cum,
        masks,
        seg_row,
        incoming,
        flat_tokens,
        flat_cot,
        out_weight,
        gain_row,
        skip_row,
        heads_map,
        sizes,
    )
    step_float = step_number[0].astype(F32)
    rate = (learn_rate[0] * step_float / (step_float + 16.0)).reshape(1)
    share_rows = model_width // pieces
    split_rows = row_split(places, share_rows)
    per_flow = places // split_rows
    flows_a = -(-2 * inner_width // (LANES * per_flow))
    flows_b = -(-(channels + 2 * LANES) // (LANES * per_flow))
    spot = jnp.stack([lax.axis_index("dp"), turn]).astype(jnp.int32)
    weights, momenta = owned(
        spot, out_weight, weight_t, out_momentum_t, in_momentum, flows_a, flows_b, places
    )
    input_grad, totals, gathered_a, gathered_b = tail(
        rate,
        (summed, conv, conv_halo, conv_weight, ssm_grad, starts, heads_map, skip_row),
        summed,
        (
            raw,
            cum,
            masks,
            seg_row,
            dots,
            decay_row,
            state_grad,
            keep,
            out_low,
            normed,
            low,
            gate_grad,
            weight_t,
            flat_tokens,
            norm_gain.reshape(1, model_width),
        ),
        weights,
        momenta,
        wide,
        squares,
        sizes,
        places,
        pieces,
        (flows_a, flows_b),
    )
    share = (pieces + 1, share_rows // split_rows, LANES)
    new_out_weight, new_weight_t, new_out_momentum_t, new_in_momentum = finish(
        gathered_a.reshape((-1,) + share),
        gathered_b.reshape((-1,) + share),
        out_momentum_t,
        in_momentum,
        split_rows,
    )
    new_in_weight = jnp.transpose(new_weight_t)
    new_out_momentum = jnp.transpose(new_out_momentum_t)
    conv_weight_total = totals[:tap_count]
    conv_bias_total = totals[tap_count]
    gate_gain_total = totals[5, :inner_width]
    skip_total = totals[6, :inner_width].reshape(heads, -1).sum(axis=1)
    norm_gain_total = totals[7, :model_width]
    dt_bias_total = totals[5, inner_width : inner_width + heads]
    a_log_total = totals[6, inner_width : inner_width + heads]
    out_square_total = totals[5, inner_width + LANES :].sum()
    mix_square_total = totals[6, inner_width + LANES :].sum()
    valid_total = totals[7, inner_width + LANES + 9]
    denominator = jnp.maximum(valid_total, 1.0) * model_width
    output_rms = jnp.sqrt(out_square_total / denominator).reshape(1)
    mixer_rms = jnp.sqrt(mix_square_total / denominator).reshape(1)
    return (
        output.reshape(tokens.shape),
        input_grad.reshape(tokens.shape),
        new_in_weight,
        new_out_weight,
        new_in_momentum,
        new_out_momentum,
        norm_gain_total,
        conv_weight_total,
        conv_bias_total,
        dt_bias_total,
        a_log_total,
        skip_total,
        gate_gain_total,
        output_rms,
        mixer_rms,
    )


def solution(mesh):
    placed = (
        P("dp", "seq", None),
        P("dp", "seq", None),
        P("dp", "seq"),
        P("dp", "seq"),
        P("dp", "seq"),
        P(),
        P(),
        P(),
        P(),
        P(),
        P(),
        P(),
        P(),
        P(),
        P(),
        P(),
        P("seq", None),
        P(None, "seq"),
    )
    return jax.shard_map(
        local,
        mesh=mesh,
        in_specs=placed,
        out_specs=(
            P("dp", "seq", None),
            P("dp", "seq", None),
            P(),
            P(),
            P("seq", None),
            P(None, "seq"),
            P(),
            P(),
            P(),
            P(),
            P(),
            P(),
            P(),
            P(),
            P(),
        ),
        check_vma=False,
    )
```

```python
import functools

import jax
import jax.numpy as jnp
from jax import lax
from jax.experimental import pallas as pl
from jax.experimental.pallas import tpu as pltpu
from jax.sharding import PartitionSpec as P

CHUNK = 128
HALO = 16
GATE_BLOCK = 256
EPS = 1e-05
NEGATIVE = -1e30
F32, BF16 = jnp.float32, jnp.bfloat16
LANES = 128
MESH = pl.DeviceIdType.MESH


def remote(src, dst, send, recv, target):
    return pltpu.make_async_remote_copy(
        src_ref=src,
        dst_ref=dst,
        send_sem=send,
        recv_sem=recv,
        device_id=target,
        device_id_type=MESH,
    )


def greet(targets):
    barrier = pltpu.get_barrier_semaphore()
    for target in targets:
        pl.semaphore_signal(barrier, inc=1, device_id=target, device_id_type=MESH)
    pl.semaphore_wait(barrier, len(targets))


def dma_semaphores(*shape):
    return [pltpu.SemaphoreType.DMA(shape)] * 2


def part_count(pieces):
    return 2 if pieces % 2 == 0 else 1


def half_shape(bits, pieces, flows, rows, k):
    return (flows,) + (2,) * (bits - k - 1) + (pieces, rows, LANES)


def mm(a, b):
    return jnp.dot(a, b, preferred_element_type=F32)


def mm_nt(a, b):
    return lax.dot_general(a, b, (((1,), (1,)), ((), ())), preferred_element_type=F32)


def mm_tn(a, b):
    return lax.dot_general(a, b, (((0,), (0,)), ((), ())), preferred_element_type=F32)


def split(a):
    high = a.astype(BF16)
    return high, (a - high.astype(F32)).astype(BF16)


def exact_mm(a, b):
    return jnp.dot(a, b, preferred_element_type=F32, precision=lax.Precision.HIGHEST)


def spread(a, heads_ref):
    high, low = split(a)
    return mm(high, heads_ref[...]) + mm(low, heads_ref[...])


def gather_heads(a, heads_ref):
    high, low = split(a)
    return mm_nt(high, heads_ref[...]) + mm_nt(low, heads_ref[...])


def sigmoid(v):
    return 1.0 / (1.0 + jnp.exp(-v))


def gate_of(v):
    return 0.5 + 0.5 * jnp.tanh(0.5 * v)


def softplus(v):
    return jnp.maximum(v, 0.0) + jnp.log1p(jnp.exp(-jnp.abs(v)))


def triangle(size, upper):
    row = lax.broadcasted_iota(jnp.int32, (size, size), 0)
    column = lax.broadcasted_iota(jnp.int32, (size, size), 1)
    return ((row <= column) if upper else (row >= column)).astype(F32)


def front_kernel(
    sizes,
    tokens_ref,
    halo_ref,
    gain_ref,
    weight_ref,
    taps_ref,
    bias_ref,
    seg_ref,
    valid_ref,
    dt_bias_ref,
    a_log_ref,
    heads_ref,
    normed_ref,
    masks_ref,
    gate_ref,
    conv_ref,
    halo_out_ref,
    summed_ref,
    raw_ref,
    cum_ref,
    state_ref,
    keep_ref,
    padded,
    product,
    active,
):
    seqs, piece, inner, channels, heads = sizes
    gate_blocks, conv_blocks = inner // GATE_BLOCK, channels // GATE_BLOCK
    step = pl.program_id(0)
    stride = piece + HALO

    @pl.when(step == 0)
    def _():
        gain = gain_ref[...]
        for n in range(seqs):
            padded_seg = seg_ref[n : n + 1]
            seg = padded_seg[:, HALO:]

            def over_chunks(at):
                return jnp.concatenate(
                    [
                        jnp.broadcast_to(
                            padded_seg[:, c * CHUNK + at : c * CHUNK + at + 1], (1, CHUNK)
                        )
                        for c in range(piece // CHUNK)
                    ],
                    axis=1,
                )

            others = [padded_seg[:, HALO - 3 + k : HALO - 3 + k + piece] for k in range(4)] + [
                over_chunks(HALO - 1),
                over_chunks(HALO + CHUNK - 1),
                jnp.broadcast_to(padded_seg[:, HALO - 1 : HALO], (1, piece)),
                jnp.broadcast_to(padded_seg[:, HALO + piece - 1 :], (1, piece)),
            ]
            lines = [(other == seg).astype(F32) for other in others] + [
                seg,
                valid_ref[n : n + 1].astype(F32),
            ]
            lines = lines + [jnp.zeros_like(seg)] * (16 - len(lines))
            masks_ref[pl.ds(n * piece, piece)] = jnp.transpose(jnp.concatenate(lines, axis=0))
            for source, start, to, count in (
                (halo_ref, n * HALO, n * stride, HALO),
                (tokens_ref, n * piece, n * stride + HALO, piece),
            ):

                def body(i, carry):
                    values = source[pl.ds(pl.multiple_of(start + i * 16, 16), 16)].astype(F32)
                    scale = lax.rsqrt(jnp.mean(values * values, axis=-1, keepdims=True) + EPS)
                    low = (values * scale * gain).astype(BF16)
                    padded[pl.ds(pl.multiple_of(to + i * 16, 16), 16)] = low
                    return carry

                lax.fori_loop(0, count // 16, body, 0)
            normed_ref[pl.ds(n * piece, piece)] = padded[pl.ds(n * stride + HALO, piece)]

    product[...] = mm_nt(padded[...], weight_ref[...])

    @pl.when(step < gate_blocks)
    def _():
        for n in range(seqs):
            gate_ref[pl.ds(n * piece, piece)] = product[pl.ds(n * stride + HALO, piece)]

    @pl.when((step >= gate_blocks) & (step < gate_blocks + conv_blocks))
    def _():
        at = pl.multiple_of((step - gate_blocks) * GATE_BLOCK, GATE_BLOCK)
        for n in range(seqs):
            conv_ref[pl.ds(n * piece, piece)] = product[pl.ds(n * stride + HALO, piece)]
            halo_out_ref[pl.ds(n * HALO, HALO)] = product[pl.ds(n * stride, HALO)]
            for i in range(piece // 64):
                rows = pl.ds(n * piece + i * 64, 64)
                total = jnp.broadcast_to(bias_ref[...], (64, GATE_BLOCK))
                for k in range(4):
                    source = product[pl.ds(n * stride + HALO - 3 + k + i * 64, 64)]
                    total = total + source * masks_ref[rows, k : k + 1] * taps_ref[k : k + 1]
                summed_ref[rows] = total
                active[rows, pl.ds(at, GATE_BLOCK)] = (total * gate_of(total)).astype(BF16)

    @pl.when(step == gate_blocks + conv_blocks)
    def _():
        lane = lax.broadcasted_iota(jnp.int32, (piece, 128), 1)
        lower = triangle(CHUNK, False)
        for n in range(seqs):
            rows = pl.ds(n * piece, piece)
            raw = jnp.where(lane < heads, product[pl.ds(n * stride + HALO, piece), :128], 0.0)
            raw = raw + dt_bias_ref[...]
            raw_ref[rows] = raw
            steps = jnp.where(lane < heads, softplus(raw), 0.0)
            decay = -jnp.exp(a_log_ref[...]) * steps
            total = jnp.zeros((1, 128), F32)
            pieces = []
            for c in range(piece // CHUNK):
                cumulative = exact_mm(lower, decay[c * CHUNK : (c + 1) * CHUNK])
                cum_ref[pl.ds(n * piece + c * CHUNK, CHUNK)] = cumulative
                pieces.append(cumulative + total)
                total = total + cumulative[CHUNK - 1 :]
            whole = jnp.concatenate(pieces, axis=0) if len(pieces) > 1 else pieces[0]
            tails = jnp.exp(total - whole) * steps * masks_ref[rows, 7:8]
            weighted = (spread(tails, heads_ref) * active[rows, :inner].astype(F32)).astype(BF16)
            state_ref[n] = mm_tn(active[rows, inner : inner + 128], weighted)
            last = masks_ref[n * piece + piece - 1 : n * piece + piece, 6:7]
            keep = jnp.exp(total) * last
            keep_ref[n] = spread(jnp.broadcast_to(keep, (8, 128)), heads_ref)


def front(tokens, halo, gain, weight, taps, bias, segs, valid, dt_bias, a_log, heads_map, sizes):
    seqs, piece, inner, channels, heads = sizes
    total, model = tokens.shape
    stride = seqs * (piece + HALO)
    gate_blocks, conv_blocks = inner // GATE_BLOCK, channels // GATE_BLOCK
    full = lambda *shape: pl.BlockSpec(shape, lambda j: (0,) * len(shape))

    def conv_at(j):
        return (0, jnp.clip(j - gate_blocks, 0, conv_blocks - 1))

    return pl.pallas_call(
        functools.partial(front_kernel, sizes),
        grid=(gate_blocks + conv_blocks + 1,),
        in_specs=[
            full(total, model),
            full(seqs * HALO, model),
            full(1, model),
            pl.BlockSpec((GATE_BLOCK, model), lambda j: (j, 0)),
            pl.BlockSpec((4, GATE_BLOCK), conv_at),
            pl.BlockSpec((1, GATE_BLOCK), conv_at),
            full(*segs.shape),
            full(*valid.shape),
            full(1, 128),
            full(1, 128),
            full(128, inner),
        ],
        out_specs=(
            full(total, model),
            full(total, 16),
            pl.BlockSpec((total, GATE_BLOCK), lambda j: (0, jnp.minimum(j, gate_blocks - 1))),
            pl.BlockSpec((total, GATE_BLOCK), conv_at),
            pl.BlockSpec((seqs * HALO, GATE_BLOCK), conv_at),
            pl.BlockSpec((total, GATE_BLOCK), conv_at),
            full(total, 128),
            full(total, 128),
            full(seqs, 128, inner),
            full(seqs, 8, inner),
        ),
        out_shape=(
            jax.ShapeDtypeStruct((total, model), BF16),
            jax.ShapeDtypeStruct((total, 16), F32),
            jax.ShapeDtypeStruct((total, inner), F32),
            jax.ShapeDtypeStruct((total, channels), F32),
            jax.ShapeDtypeStruct((seqs * HALO, channels), F32),
            jax.ShapeDtypeStruct((total, channels), F32),
            jax.ShapeDtypeStruct((total, 128), F32),
            jax.ShapeDtypeStruct((total, 128), F32),
            jax.ShapeDtypeStruct((seqs, 128, inner), F32),
            jax.ShapeDtypeStruct((seqs, 8, inner), F32),
        ),
        scratch_shapes=[
            pltpu.VMEM((stride, model), BF16),
            pltpu.VMEM((stride, GATE_BLOCK), F32),
            pltpu.VMEM((total, channels), BF16),
        ],
        compiler_params=pltpu.CompilerParams(vmem_limit_bytes=48 * 1024 * 1024),
        name="front",
    )(tokens, halo, gain, weight, taps, bias, segs, valid, dt_bias, a_log, heads_map)


def chain_kernel(ways, blocks, own_ref, keep_ref, out_ref, sent, taken, send, recv):
    size = lax.axis_size("seq")
    turn = lax.axis_index("seq")
    first = turn == (0 if ways > 0 else size - 1)
    final = turn == (size - 1 if ways > 0 else 0)
    ahead = {"seq": lax.rem(turn + ways + size, size)}
    behind = {"seq": lax.rem(turn - ways + size, size)}
    barrier = pltpu.get_barrier_semaphore()

    @pl.when(jnp.logical_not(first))
    def _():
        pl.semaphore_signal(
            barrier, inc=1, device_id=behind, device_id_type=pl.DeviceIdType.MESH
        )

    @pl.when(jnp.logical_not(final))
    def _():
        pl.semaphore_wait(barrier, 1)

    width = own_ref.shape[2] // blocks

    def copy(c):
        return pltpu.make_async_remote_copy(
            src_ref=sent.at[c],
            dst_ref=taken.at[c],
            send_sem=send.at[c],
            recv_sem=recv.at[c],
            device_id=ahead,
            device_id_type=pl.DeviceIdType.MESH,
        )

    @pl.when(first)
    def _():
        out_ref[...] = jnp.zeros_like(out_ref)
        for c in range(blocks):
            at = slice(c * width, (c + 1) * width)
            sent[c] = own_ref[:, :, at].astype(BF16)
            copy(c).start()

    @pl.when(jnp.logical_not(first))
    def _():
        for c in range(blocks):
            at = slice(c * width, (c + 1) * width)
            copy(c).wait_recv()

            @pl.when(jnp.logical_not(final))
            def _():
                sent[c] = (
                    own_ref[:, :, at] + keep_ref[:, 0:1, at] * taken[c].astype(F32)
                ).astype(BF16)
                copy(c).start()

            out_ref[:, :, at] = taken[c].astype(F32)

    @pl.when(jnp.logical_not(final))
    def _():
        for c in range(blocks):
            copy(c).wait_send()


def chain(own, keep, ways, blocks=6):
    seqs, depth, inner = own.shape
    vmem = pl.BlockSpec(memory_space=pltpu.VMEM)
    part = (blocks, seqs, depth, inner // blocks)
    return pl.pallas_call(
        functools.partial(chain_kernel, ways, blocks),
        out_shape=jax.ShapeDtypeStruct(own.shape, F32),
        in_specs=[vmem, vmem],
        out_specs=vmem,
        scratch_shapes=[pltpu.VMEM(part, BF16)] * 2 + [pltpu.SemaphoreType.DMA((blocks,))] * 2,
        compiler_params=pltpu.CompilerParams(
            collective_id=1 if ways > 0 else 2,
            has_side_effects=True,
            vmem_limit_bytes=32 * 1024 * 1024,
        ),
        name="chain",
    )(own, keep)


def decays_of(cum, cum_t, bias, h):
    return jnp.exp(cum[:, h : h + 1] - cum_t[h : h + 1, :] + bias)


def mask_bias(seg_col, seg_row):
    row = lax.broadcasted_iota(jnp.int32, (CHUNK, CHUNK), 0)
    column = lax.broadcasted_iota(jnp.int32, (CHUNK, CHUNK), 1)
    return jnp.where((row >= column) & (seg_col == seg_row), 0.0, NEGATIVE)


def scores_of(reader, writer):
    rh, rl = split(reader)
    wh, wl = split(writer)
    return mm_nt(rh, wh) + (mm_nt(rh, wl) + mm_nt(rl, wh))


def forward_kernel(
    sizes,
    chunks,
    summed_ref,
    gate_ref,
    raw_ref,
    cum_ref,
    masks_ref,
    seg_row_ref,
    incoming_ref,
    tokens_ref,
    cot_ref,
    weight_ref,
    gain_ref,
    skip_ref,
    heads_ref,
    output_ref,
    low_ref,
    out_low_ref,
    gate_grad_ref,
    ssm_grad_ref,
    starts_ref,
    dot_ref,
    sums_ref,
    wide_ref,
    state_grad_ref,
    state,
    prefix,
    active,
    mixed_in,
    factors,
    grads,
    inv,
    totals,
):
    seqs, piece, inner, channels, heads = sizes
    c = pl.program_id(1)

    @pl.when((c == 0) & (pl.program_id(0) == 0))
    def _():
        sums_ref[...] = jnp.zeros_like(sums_ref)
        wide_ref[...] = jnp.zeros_like(wide_ref)

    @pl.when(c == 0)
    def _():
        state[...] = incoming_ref[0]
        prefix[...] = jnp.zeros_like(prefix)
        state_grad_ref[...] = jnp.zeros_like(state_grad_ref)

    def activate(i, carry):
        rows = pl.ds(pl.multiple_of(i * 16, 16), 16)
        values = summed_ref[rows]
        active[rows] = values * gate_of(values)
        return carry

    lax.fori_loop(0, CHUNK // 16, activate, 0)
    lane = lax.broadcasted_iota(jnp.int32, (CHUNK, 128), 1)
    steps = jnp.where(lane < heads, softplus(raw_ref[...]), 0.0)
    cum = cum_ref[...]
    cum_t = jnp.transpose(cum)
    final = cum[CHUNK - 1 :]
    enter = jnp.exp(cum) * masks_ref[:, 4:5]
    tails = jnp.exp(final - cum) * steps * masks_ref[:, 5:6]
    from_start = jnp.exp(cum + prefix[0:1]) * masks_ref[:, 6:7]
    prefix[...] = prefix[...] + final
    for i, block in enumerate((steps, enter, tails, from_start)):
        factors[i] = spread(block, heads_ref)
    writer = active[:, inner : inner + 128]
    reader = active[:, inner + 128 : inner + 256]
    scores = scores_of(reader, writer)
    bias = mask_bias(masks_ref[:, 8:9], seg_row_ref[0:1])
    half = lax.broadcasted_iota(jnp.int32, (CHUNK, 128), 1) < 64
    state_low = state[...].astype(BF16)
    starts_ref[0] = state_low
    reader_low = reader.astype(BF16)
    for pair in range(heads // 2):
        at = slice(pair * 128, (pair + 1) * 128)
        moved = (active[:, at] * factors[0, :, at]).astype(BF16)
        zero = jnp.zeros_like(moved)
        one = (scores * decays_of(cum, cum_t, bias, 2 * pair)).astype(BF16)
        two = (scores * decays_of(cum, cum_t, bias, 2 * pair + 1)).astype(BF16)
        both = jnp.concatenate([one, two], axis=1)
        stacked = jnp.concatenate(
            [jnp.where(half, moved, zero), jnp.where(half, zero, moved)], axis=0
        )
        carried = mm(reader_low, state_low[:, at]) * factors[1, :, at]
        mixed_in[:, at] = mm(both, stacked) + carried
    weighted = (active[:, :inner] * factors[2]).astype(BF16)
    kept = jnp.exp(final) * masks_ref[CHUNK - 1 :, 4:5]
    kept = spread(jnp.broadcast_to(kept, (8, 128)), heads_ref)[0:1]
    state[...] = state[...] * kept + mm_tn(writer.astype(BF16), weighted)

    gain = gain_ref[...]
    skip = skip_ref[...]

    column_blocks = [slice(at, at + 512) for at in range(0, inner, 512)]

    def gating(i, carry):
        rows = pl.ds(pl.multiple_of(i * 16, 16), 16)
        squares = jnp.zeros((16, 512), F32)
        for at in column_blocks:
            gate = gate_ref[rows, at]
            turned = gate_of(gate)
            mixer = mixed_in[rows, at] + skip[:, at] * active[rows, at]
            product = mixer * gate * turned
            factors[0, rows, at] = product
            factors[1, rows, at] = turned
            factors[2, rows, at] = mixer
            squares = squares + product * product
        mean = jnp.sum(squares, axis=-1, keepdims=True) / inner
        scale = lax.rsqrt(mean + EPS)
        inv[rows] = jnp.broadcast_to(scale, (16, 128))
        for at in column_blocks:
            low_ref[rows, at] = (factors[0, rows, at] * scale * gain[:, at]).astype(BF16)
        return carry

    lax.fori_loop(0, CHUNK // 16, gating, 0)
    mixed = mm(low_ref[...], weight_ref[...])
    block_out = tokens_ref[...].astype(F32) + mixed
    output_ref[...] = block_out.astype(BF16)
    valid = masks_ref[:, 9:10]
    for i, block in enumerate((block_out, mixed)):
        squares = jnp.sum(valid * block * block, axis=0, keepdims=True)
        for at in range(0, squares.shape[1], 128):
            sums_ref[i : i + 1] += squares[:, at : at + 128]
    sums_ref[2:3, :16] += jnp.sum(masks_ref[...], axis=0, keepdims=True)
    out_low = (cot_ref[...].astype(F32) * valid).astype(BF16)
    out_low_ref[...] = out_low
    grads[...] = mm_nt(out_low, weight_ref[...])

    @pl.when((c == 0) & (pl.program_id(0) == 0))
    def _():
        totals[...] = jnp.zeros_like(totals)

    def backing(i, carry):
        rows = pl.ds(pl.multiple_of(i * 16, 16), 16)
        scale = inv[rows, 0:1]
        inside = jnp.zeros((16, 512), F32)
        for at in column_blocks:
            grad = grads[rows, at]
            gated = factors[0, rows, at]
            totals[0, :, at] += grad * gated * scale
            inside = inside + grad * gain[:, at] * gated
        inside = jnp.sum(inside, axis=-1, keepdims=True) / inner
        inside = scale * scale * scale * inside
        for at in column_blocks:
            gate, turned = gate_ref[rows, at], factors[1, rows, at]
            gated_grad = scale * (grads[rows, at] * gain[:, at]) - factors[0, rows, at] * inside
            ssm_grad = gated_grad * (gate * turned)
            ssm_grad_ref[rows, at] = ssm_grad
            grads[rows, at] = ssm_grad
            totals[1, :, at] += ssm_grad * active[rows, at]
            gate_grad_ref[rows, at] = (
                gated_grad * factors[2, rows, at] * turned * (1.0 + gate * (1.0 - turned))
            ).astype(BF16)
        return carry

    lax.fori_loop(0, CHUNK // 16, backing, 0)

    @pl.when((c == chunks - 1) & (pl.program_id(0) == seqs - 1))
    def _():
        wide_ref[0:1] = jnp.sum(totals[0], axis=0, keepdims=True)
        skips = jnp.sum(totals[1], axis=0, keepdims=True)
        skips = gather_heads(jnp.broadcast_to(skips, (8, inner)), heads_ref)
        wide_ref[1:2, :128] = skips[0:1]

    reader_t = jnp.transpose(reader_low)
    for pair in range(heads // 2):
        at = slice(pair * 128, (pair + 1) * 128)
        state_grad_ref[0, :, at] += mm(
            reader_t, (grads[:, at] * factors[3, :, at]).astype(BF16)
        )
        mixed_in[:, at] = mixed_in[:, at] * grads[:, at].astype(BF16).astype(F32)
    dot_ref[...] = gather_heads(mixed_in[...], heads_ref)


def forward(
    summed, gate, raw, cum, masks, seg_row, incoming, tokens, cot, weight, gain, skip, heads_map, sizes
):
    seqs, piece, inner, channels, heads = sizes
    total, model = tokens.shape
    chunks = piece // CHUNK
    full = lambda *shape: pl.BlockSpec(shape, lambda n, c: (0,) * len(shape))
    rows = lambda width: pl.BlockSpec((CHUNK, width), lambda n, c: (n * chunks + c, 0))
    each = lambda depth: pl.BlockSpec((1, depth, inner), lambda n, c: (n, 0, 0))
    shape = jax.ShapeDtypeStruct
    return pl.pallas_call(
        functools.partial(forward_kernel, sizes, chunks),
        grid=(seqs, chunks),
        in_specs=[
            rows(channels),
            rows(inner),
            rows(128),
            rows(128),
            rows(16),
            pl.BlockSpec((1, CHUNK), lambda n, c: (0, n * chunks + c)),
            each(128),
            rows(model),
            rows(model),
            full(inner, model),
            full(1, inner),
            full(1, inner),
            full(128, inner),
        ],
        out_specs=(
            rows(model),
            rows(inner),
            rows(model),
            rows(inner),
            rows(inner),
            pl.BlockSpec((1, 128, inner), lambda n, c: (n * chunks + c, 0, 0)),
            rows(128),
            full(8, 128),
            full(8, inner),
            each(128),
        ),
        out_shape=(
            shape((total, model), BF16),
            shape((total, inner), BF16),
            shape((total, model), BF16),
            shape((total, inner), BF16),
            shape((total, inner), F32),
            shape((seqs * chunks, 128, inner), BF16),
            shape((total, 128), F32),
            shape((8, 128), F32),
            shape((8, inner), F32),
            shape((seqs, 128, inner), F32),
        ),
        scratch_shapes=[
            pltpu.VMEM((128, inner), F32),
            pltpu.VMEM((8, 128), F32),
            pltpu.VMEM((CHUNK, channels), F32),
            pltpu.VMEM((CHUNK, inner), F32),
            pltpu.VMEM((4, CHUNK, inner), F32),
            pltpu.VMEM((CHUNK, inner), F32),
            pltpu.VMEM((CHUNK, 128), F32),
            pltpu.VMEM((2, 16, inner), F32),
        ],
        compiler_params=pltpu.CompilerParams(vmem_limit_bytes=48 * 1024 * 1024),
        name="forward",
    )(summed, gate, raw, cum, masks, seg_row, incoming, tokens, cot, weight, gain, skip, heads_map)


TILE = 256


class Exchange:
    def __init__(self, bits, pieces, flows):
        self.bits, self.pieces, self.flows = bits, pieces, flows
        self.parts = part_count(pieces)
        self.place, self.turn = lax.axis_index("dp"), lax.axis_index("seq")
        self.own = [(self.place // (1 << b)) % 2 for b in range(bits)]
        self.partner = [
            {"dp": self.place + (1 - 2 * self.own[b]) * (1 << b)} for b in range(bits)
        ]
        self.others = [{"seq": lax.rem(self.turn + j, pieces)} for j in range(pieces)]
        self.mine = self.index_of({b: self.own[b] for b in range(bits)})

    def index_of(self, fixed):
        return tuple(fixed.get(b, slice(None)) for b in range(self.bits - 1, -1, -1))

    def spot_of(self, d):
        return tuple((d // (1 << b)) % 2 for b in range(self.bits - 1, -1, -1))

    def order_of(self, f, h):
        rest = list(range(1, self.bits))
        shift = (f + h) % max(len(rest), 1)
        return [0] + rest[shift:] + rest[:shift]

    def share(self, h, extra=0):
        half = self.pieces // self.parts
        return pl.ds(h * half, half + (extra if h == self.parts - 1 else 0))

    def held(self, f, h, k, other):
        order = self.order_of(f, h)
        bit = order[k]
        value = 1 - self.own[bit] if other else self.own[bit]
        free = [b for b in range(self.bits - 1, -1, -1) if b not in order[:k]]
        source = self.grad if k == 0 else self.halves[k - 1]
        return source.at[
            (f,) + tuple(value if b == bit else slice(None) for b in free) + (self.share(h),)
        ]

    def landing(self, f, h, k):
        free = self.bits - k - 1
        return self.halves[k].at[(f,) + (slice(None),) * free + (self.share(h),)]

    def rs_copy(self, f, h, k):
        return remote(
            self.held(f, h, k, True),
            self.landing(f, h, k),
            self.rs_send.at[f, h, k],
            self.rs_recv.at[f, h, k],
            self.partner[self.order_of(f, h)[k]],
        )

    def rs_begin(self, f):
        for h in range(self.parts):
            self.rs_copy(f, h, 0).start()

    def rs_end(self, f, k):
        for h in range(self.parts):
            self.rs_copy(f, h, k).wait_recv()
            kept, into = self.held(f, h, k, False), self.landing(f, h, k)
            left = self.bits - k - 1
            for count in range(1 << left):
                spot = tuple((count >> (left - 1 - i)) & 1 for i in range(left))

                def body(p, carry, spot=spot, kept=kept, into=into):
                    into[spot + (p,)] = (
                        kept[spot + (p,)].astype(F32) + into[spot + (p,)].astype(F32)
                    ).astype(BF16)
                    return carry

                lax.fori_loop(0, self.pieces // self.parts, body, 0)
            if k + 1 < self.bits:
                self.rs_copy(f, h, k + 1).start()
        if k + 1 == self.bits:
            for j in range(1, self.pieces):
                self.zs_copy(f, j).start()

    def zs_copy(self, f, j):
        return remote(
            self.halves[self.bits - 1].at[f, lax.rem(self.turn + j, self.pieces)],
            self.piece_parts.at[f, j],
            self.zs_send.at[f, j],
            self.zs_recv.at[f, j],
            self.others[j],
        )

    def zs_end(self, f, rate, weight, momentum):
        for j in range(1, self.pieces):
            self.zs_copy(f, j).wait_recv()
        total = self.halves[self.bits - 1][f, self.turn].astype(F32)
        for j in range(1, self.pieces):
            total = total + self.piece_parts[f, j].astype(F32)
        summed = total.astype(BF16)
        moved = 0.5 * momentum + summed.astype(F32)
        self.gathered[(f,) + self.mine + (self.pieces,)] = summed
        self.gathered[(f,) + self.mine + (self.turn,)] = (
            weight.astype(F32) - rate * moved
        ).astype(BF16)
        for j in range(1, self.pieces):
            self.zg_copy(f, j).start()

    def zg_copy(self, f, j):
        spot = self.gathered.at[(f,) + self.mine + (self.turn,)]
        return remote(spot, spot, self.zg_send.at[f, j], self.zg_recv.at[f, j], self.others[j])

    def zg_end(self, f):
        for j in range(1, self.pieces):
            self.zg_copy(f, j).wait_recv()
        for h in range(self.parts):
            self.ag_copy(f, h, self.bits - 1).start()

    def ag_copy(self, f, h, k):
        order = self.order_of(f, h)
        fixed = {order[i]: self.own[order[i]] for i in range(k + 1)}
        spot = self.gathered.at[(f,) + self.index_of(fixed) + (self.share(h, 1),)]
        return remote(
            spot,
            spot,
            self.ag_send.at[f, h, k],
            self.ag_recv.at[f, h, k],
            self.partner[order[k]],
        )

    def ag_end(self, f, k):
        for h in range(self.parts):
            self.ag_copy(f, h, k).wait_recv()
            if k > 0:
                self.ag_copy(f, h, k - 1).start()

    def tiles_sent(self):
        for f in range(self.flows):
            for h in range(self.parts):
                self.rs_copy(f, h, 0).wait_send()

    def sent(self):
        for f in range(self.flows):
            for h in range(self.parts):
                for k in range(self.bits):
                    if k > 0:
                        self.rs_copy(f, h, k).wait_send()
                    self.ag_copy(f, h, k).wait_send()
            for j in range(1, self.pieces):
                self.zs_copy(f, j).wait_send()
                self.zg_copy(f, j).wait_send()

    def actions(self, f, rate, weights, momenta, after):
        steps = [functools.partial(self.rs_end, f, k) for k in range(self.bits)]
        steps.append(lambda: self.zs_end(f, rate, weights[f], momenta[f]))
        steps.append(functools.partial(self.zg_end, f))
        steps += [functools.partial(self.ag_end, f, k) for k in range(self.bits - 1, 0, -1)]

        def finish():
            self.ag_end(f, 0)
            after(f)

        return steps + [finish]


def exchange_scratch(bits, pieces, flows, rows, first=-1):
    parts = part_count(pieces)
    return (
        [pltpu.VMEM(half_shape(bits, pieces, flows, rows, k), BF16) for k in range(first, bits)]
        + [
            pltpu.VMEM((flows, pieces, rows, LANES), BF16),
            pltpu.VMEM((flows,) + (2,) * bits + (pieces + 1, rows, LANES), BF16),
        ]
        + dma_semaphores(flows, parts, bits)
        + dma_semaphores(flows, pieces)
        + dma_semaphores(flows, pieces)
        + dma_semaphores(flows, parts, bits)
        + [pltpu.SemaphoreType.DMA((flows,))]
    )


def give(ex, scratch, grad=None):
    if grad is None:
        grad, scratch = scratch[0], scratch[1:]
    ex.grad, ex.halves = grad, scratch[: ex.bits]
    scratch = scratch[ex.bits :]
    (ex.piece_parts, ex.gathered, ex.rs_send, ex.rs_recv, ex.zs_send, ex.zs_recv) = scratch[:6]
    (ex.zg_send, ex.zg_recv, ex.ag_send, ex.ag_recv, ex.out_sem) = scratch[6:11]
    return scratch[11:]


def tail_kernel(sizes, dims, *refs):
    seqs, piece, inner, channels, heads = sizes
    bits, pieces, flows_a, flows_b, split_rows, blocks = dims
    (
        rate_ref,
        summed_ref,
        conv_ref,
        halo_ref,
        taps_ref,
        ssm_grad_ref,
        starts_ref,
        heads_ref,
        skip_ref,
        summed_rw_ref,
        raw_ref,
        cum_ref,
        masks_ref,
        seg_row_ref,
        dot_ref,
        a_log_ref,
        own_ref,
        keep_ref,
        out_low_ref,
        normed_ref,
        low_ref,
        gate_grad_ref,
        weight_t_ref,
        tokens_ref,
        gain_ref,
        weight_ref,
        momentum_ref,
        wide_ref,
        squares_ref,
        input_grad_ref,
        small_out_ref,
        out_a_ref,
        out_b_ref,
    ) = refs[:33]
    scratch = refs[33:]
    a, b = Exchange(bits, pieces, flows_a), Exchange(bits, pieces, flows_b)
    scratch = give(a, scratch)
    scratch = give(b, scratch, a.grad)
    (
        sent,
        taken,
        chain_send,
        chain_recv,
        later,
        out_turned,
        normed_turned,
        writer_low,
        reader_low,
        reader_turned,
        scores,
        cum_turned,
        biases,
        scores_grad,
        reader_grad,
        writer_grad,
        active,
        bent,
        step_x,
        cum_x,
        total,
        state_grad,
        ends,
        step_sum,
        move_sum,
        end_sum,
        shifted_rows,
        proj_grad,
        tails,
        rims,
        rims_in,
        rim_send,
        rim_recv,
        conv_sums,
        head_sums,
        gain_sums,
        small_acc,
        small_in,
        small_parts,
        sm_send,
        sm_recv,
        sz_send,
        sz_recv,
    ) = scratch
    j = pl.program_id(0)
    steps = inner // TILE
    final_step = steps + 1
    places = 1 << bits
    per_flow = places // split_rows
    turn = a.turn
    chunk_count = seqs * piece // CHUNK
    rows = a.grad.shape[-2]
    chunks = piece // CHUNK
    rate = rate_ref[0]
    real = 2 * inner // LANES

    def out_copy(ex, out, f):
        return pltpu.make_async_copy(ex.gathered.at[f], out.at[f], ex.out_sem.at[f])

    a_actions = [
        a.actions(f, rate, weight_ref, momentum_ref, lambda f: out_copy(a, out_a_ref, f).start())
        for f in range(flows_a)
    ]
    late = [weight_ref.at[pl.ds(flows_a, flows_b)], momentum_ref.at[pl.ds(flows_a, flows_b)]]
    b_actions = [
        b.actions(f, rate, *late, lambda f: out_copy(b, out_b_ref, f).start())
        for f in range(flows_b)
    ]

    def store(ex, tile, values):
        for part in range(split_rows):
            d = (tile % per_flow) * split_rows + part
            spot = (tile // per_flow,) + ex.spot_of(d)
            for p in range(pieces):
                at = (p * split_rows + part) * rows
                ex.grad[spot + (p,)] = values[at : at + rows]

    def rim_copy(slot):
        return remote(
            rims.at[slot],
            rims_in.at[slot],
            rim_send.at[slot],
            rim_recv.at[slot],
            {"seq": lax.rem(turn + pieces - 1, pieces)},
        )

    def fix_rim(slot, at):
        @pl.when(turn < pieces - 1)
        def _():
            rim_copy(slot).wait_recv()
            for n in range(seqs):
                proj_grad[(n + 1) * piece - 8 : (n + 1) * piece, at] = (
                    tails[n] + rims_in[slot, n].astype(F32)
                ).astype(BF16)

    def conv_back(slot, at):
        for n in range(seqs):
            here_rows = pl.ds(n * piece, piece)
            grad = total[here_rows] * bent[here_rows]
            conv = conv_ref[here_rows]
            sums = [None] * 5
            sums[4] = jnp.sum(grad, axis=0, keepdims=True)
            sums[3] = jnp.sum(grad * conv, axis=0, keepdims=True)
            result = grad * taps_ref[3:4]
            rim = jnp.zeros((8, TILE), F32)
            shifted_rows[0:8] = jnp.zeros((8, TILE), F32)
            shifted_rows[8 + piece :] = jnp.zeros((8, TILE), F32)
            for k in range(3):
                shifted_rows[8 : 8 + piece] = grad * masks_ref[here_rows, k : k + 1]
                here = shifted_rows[11 - k : 11 - k + piece]
                result = result + here * taps_ref[k : k + 1]
                early = shifted_rows[3 - k : 11 - k]
                rim = rim + early * taps_ref[k : k + 1]
                sums[k] = jnp.sum(here * conv, axis=0, keepdims=True) + jnp.sum(
                    early * halo_ref[(n + 1) * HALO - 8 : (n + 1) * HALO], axis=0, keepdims=True
                )
            for i in range(5):
                if n == 0:
                    conv_sums[i : i + 1, at] = sums[i]
                else:
                    conv_sums[i : i + 1, at] += sums[i]
            proj_grad[here_rows, at] = result.astype(BF16)
            tails[n] = result[piece - 8 :]
            rims[slot, n] = rim.astype(BF16)

        @pl.when(turn > 0)
        def _():
            rim_copy(slot).start()

    @pl.when(j == 0)
    def _():
        greet(a.partner + a.others[1:])
        first, final = turn == pieces - 1, turn == 0
        width = inner // blocks

        def copy(c):
            ahead = {"seq": lax.rem(turn + pieces - 1, pieces)}
            return remote(sent.at[c], taken.at[c], chain_send.at[c], chain_recv.at[c], ahead)

        @pl.when(first)
        def _():
            later[...] = jnp.zeros_like(later)
            for c in range(blocks):
                sent[c] = own_ref[:, :, c * width : (c + 1) * width].astype(BF16)
                copy(c).start()

        out_turned[...] = jnp.transpose(out_low_ref[...])
        normed_turned[...] = jnp.transpose(normed_ref[...])
        low_tiles = inner // LANES

        def tiles(tile):
            if tile >= real:
                result = jnp.zeros((out_turned.shape[0], 2 * LANES), BF16)
            elif tile < low_tiles:
                at = tile * LANES
                result = mm(out_turned[...], low_ref[:, at : at + 2 * LANES]).astype(BF16)
            else:
                at = (tile - low_tiles) * LANES
                result = mm(normed_turned[...], gate_grad_ref[:, at : at + 2 * LANES])
                result = result.astype(BF16)
            store(a, tile, result[:, :LANES])
            store(a, tile + 1, result[:, LANES:])

        pairs = flows_a * per_flow // 2
        done = 0
        for c in range(blocks):
            until = pairs * (c + 1) // blocks
            for pair in range(done, until):
                tiles(2 * pair)
                if (2 * pair + 2) % per_flow == 0:
                    a.rs_begin(2 * pair // per_flow)
            done = until

            @pl.when(jnp.logical_not(first))
            def _():
                at = slice(c * width, (c + 1) * width)
                copy(c).wait_recv()

                @pl.when(jnp.logical_not(final))
                def _():
                    sent[c] = (
                        own_ref[:, :, at] + keep_ref[:, 0:1, at] * taken[c].astype(F32)
                    ).astype(BF16)
                    copy(c).start()

                later[:, :, at] = taken[c].astype(F32)

        for f in range(flows_a):
            a_actions[f][0]()
        a.tiles_sent()
        for ck in range(chunk_count):
            at = slice(ck * CHUNK, (ck + 1) * CHUNK)
            values = summed_rw_ref[at]
            values = values * sigmoid(values)
            writer, reader = values[:, :128], values[:, 128:]
            scores[ck] = scores_of(reader, writer)
            writer_low[at] = writer.astype(BF16)
            reader_low[at] = reader.astype(BF16)
            reader_turned[ck] = jnp.transpose(reader.astype(BF16))
            cum_turned[ck] = jnp.transpose(cum_ref[at])
            biases[ck] = mask_bias(masks_ref[at, 8:9], seg_row_ref[0:1, at])
        for ref in (
            scores_grad,
            reader_grad,
            writer_grad,
            step_sum,
            move_sum,
            end_sum,
            ends,
            gain_sums,
        ):
            ref[...] = jnp.zeros_like(ref)

        @pl.when(jnp.logical_not(final))
        def _():
            for c in range(blocks):
                copy(c).wait_send()

    agenda = {}

    def plan(step, act):
        agenda.setdefault(min(max(step, 1), steps), []).append(act)

    last_b = [((f + 1) * per_flow * LANES - 1) // TILE + 1 for f in range(flows_b)]
    a_steps = {1: 3, 2: 4} if bits == 3 else {k: 1 + k for k in range(1, bits)}
    a_done = b_ready = None
    for k in range(1, bits):
        for f in range(flows_a):
            plan(a_steps[k], a_actions[f][k])
    b_taken = []
    for f in range(flows_b):
        taken_steps = 0
        if last_b[f] + 1 <= steps:
            plan(last_b[f] + 1, functools.partial(b.rs_begin, f))
            for i in range(bits):
                if last_b[f] + 2 + i <= steps:
                    plan(last_b[f] + 2 + i, b_actions[f][i])
                    taken_steps = i + 1
            b_taken.append(taken_steps)
        else:
            b_taken.append(None)

    def weight_tiles(tile, at):
        result = mm(normed_turned[...], proj_grad[:, at]).astype(BF16)
        store(b, tile, result[:, :LANES])
        store(b, tile + 1, result[:, LANES:])

    @pl.when((j > 0) & (j < final_step))
    def _():
        at = pl.ds(pl.multiple_of((j - 1) * TILE, TILE), TILE)

        @pl.when(j > 1)
        def _():
            before = pl.ds(pl.multiple_of((j - 2) * TILE, TILE), TILE)
            fix_rim(j - 2, before)
            weight_tiles((j - 2) * (TILE // LANES), before)

        def activate(i, carry):
            rows_at = pl.ds(pl.multiple_of(i * 32, 32), 32)
            values = summed_ref[rows_at]
            turned = gate_of(values)
            active[rows_at] = values * turned
            bent[rows_at] = turned * (1.0 + values * (1.0 - turned))
            return carry

        lax.fori_loop(0, seqs * piece // 32, activate, 0)
        raw = raw_ref[...]
        lane = lax.broadcasted_iota(jnp.int32, raw.shape, 1)
        step_x[...] = spread(jnp.where(lane < heads, softplus(raw), 0.0), heads_ref)
        cum = cum_ref[...]
        high, low = split(cum)
        lowest = (cum - high.astype(F32) - low.astype(F32)).astype(BF16)
        cum_x[...] = (
            mm(high, heads_ref[...]) + mm(low, heads_ref[...]) + mm(lowest, heads_ref[...])
        )
        half = lax.broadcasted_iota(jnp.int32, (CHUNK, 128), 1) < 64
        head = (j - 1) * (TILE // 64)
        skip = skip_ref[...]
        for n in range(seqs):
            state_grad[...] = later[n, :, at]
            for c in range(chunks - 1, -1, -1):
                ck = n * chunks + c
                here = slice(ck * CHUNK, (ck + 1) * CHUNK)
                cum_here = cum_x[here]
                final_cum = cum_here[CHUNK - 1 :]
                enter_x = jnp.exp(cum_here) * masks_ref[here, 4:5]
                tail_x = jnp.exp(final_cum - cum_here) * masks_ref[here, 5:6]
                kept = jnp.exp(final_cum) * masks_ref[(ck + 1) * CHUNK - 1 : (ck + 1) * CHUNK, 4:5]
                signal = active[here]
                grad = ssm_grad_ref[here]
                moved = (signal * step_x[here]).astype(BF16)
                grad_low = grad.astype(BF16)
                later_low = state_grad[...].astype(BF16)
                from_later = mm(writer_low[here], later_low) * tail_x
                parts = []
                score = scores[ck]
                bias = biases[ck]
                grad_of_scores = scores_grad[ck]
                for pair in range(TILE // 128):
                    col = slice(pair * 128, (pair + 1) * 128)
                    ones = []
                    for i in range(2):
                        lane_at = pair * 128 + i * 64
                        ones.append(
                            jnp.exp(
                                cum_here[:, lane_at : lane_at + 1]
                                - cum_turned[ck, pl.ds(head + 2 * pair + i, 1), :]
                                + bias
                            )
                        )
                    zero = jnp.zeros((CHUNK, 128), BF16)
                    stacked = jnp.concatenate(
                        [
                            jnp.where(half, grad_low[:, col], zero),
                            jnp.where(half, zero, grad_low[:, col]),
                        ],
                        axis=0,
                    )
                    both_grad = mm_nt(stacked, moved[:, col])
                    grad_of_scores = (
                        grad_of_scores + both_grad[:CHUNK] * ones[0] + both_grad[CHUNK:] * ones[1]
                    )
                    both = jnp.concatenate([(score * one).astype(BF16) for one in ones], axis=0)
                    parts.append(mm_tn(both, stacked))
                scores_grad[ck] = grad_of_scores
                moved_grad = jnp.concatenate(parts, axis=1) + from_later
                wide_moved = moved.astype(F32)
                weighted = (wide_moved * tail_x).astype(BF16)
                entered = (grad * enter_x).astype(BF16)
                start = starts_ref[ck]
                reader_grad[here] += mm_nt(entered, start)
                writer_grad[here] += mm_nt(weighted, later_low)
                passed = jnp.sum(
                    start.astype(F32) * later_low.astype(F32), axis=0, keepdims=True
                )
                ends[ck : ck + 1] = kept * passed + jnp.sum(
                    wide_moved * from_later, axis=0, keepdims=True
                )
                state_grad[...] = state_grad[...] * kept + mm(reader_turned[ck], entered)
                step_sum[here] += gather_heads(moved_grad * signal, heads_ref)
                move_sum[here] += gather_heads(moved_grad * wide_moved, heads_ref)
                total[here] = moved_grad * step_x[here] + skip * grad
        end_sum[...] += gather_heads(ends[...], heads_ref)
        conv_back(j - 1, at)
        for step in sorted(agenda):

            @pl.when(j == step)
            def _(step=step):
                for act in agenda[step]:
                    act()

    @pl.when(j == final_step)
    def _():
        before = slice((steps - 1) * TILE, steps * TILE)
        fix_rim(steps - 1, before)
        weight_tiles((steps - 1) * (TILE // LANES), before)
        pending = []
        for f in range(flows_b):
            if last_b[f] == steps and b_taken[f] is None:
                b.rs_begin(f)
                b_taken[f] = 0
        at = slice(inner, channels)
        lane = lax.broadcasted_iota(jnp.int32, (CHUNK, 128), 1)
        row = lax.broadcasted_iota(jnp.int32, (CHUNK, 128), 0)
        upper = triangle(CHUNK, True)
        decay_rate = -jnp.exp(a_log_ref[...])
        raw_sum = jnp.zeros((1, 128), F32)
        decay_sum = jnp.zeros((1, 128), F32)
        values = summed_rw_ref[...]
        turned = sigmoid(values)
        bent[...] = turned * (1.0 + values * (1.0 - turned))
        for ck in range(chunk_count):
            here = slice(ck * CHUNK, (ck + 1) * CHUNK)
            high, low = split(scores_grad[ck])
            total[here, 128:] = (
                reader_grad[here] + mm(high, writer_low[here]) + mm(low, writer_low[here])
            )
            total[here, :128] = (
                writer_grad[here] + mm_tn(high, reader_low[here]) + mm_tn(low, reader_low[here])
            )
            raw = raw_ref[here]
            taken_steps = jnp.where(lane < heads, softplus(raw), 0.0)
            change = dot_ref[here] - move_sum[here]
            change = change + jnp.where(row == CHUNK - 1, end_sum[ck : ck + 1], 0.0)
            decay_grad = exact_mm(upper, change)
            raw_grad = jnp.where(
                lane < heads, (step_sum[here] + decay_grad * decay_rate) * sigmoid(raw), 0.0
            )
            raw_sum = raw_sum + jnp.sum(raw_grad, axis=0, keepdims=True)
            decay_sum = decay_sum + jnp.sum(
                decay_grad * taken_steps * decay_rate, axis=0, keepdims=True
            )
            proj_grad[here, channels : channels + 128] = raw_grad.astype(BF16)
            proj_grad[here, channels + 128 :] = jnp.zeros((CHUNK, 128), BF16)
        head_sums[0:1] = raw_sum
        head_sums[1:2] = decay_sum
        conv_back(steps, at)
        fix_rim(steps, at)
        for tile in range(inner // LANES, flows_b * per_flow, 2):
            if tile * LANES < channels + 256:
                weight_tiles(tile, slice(tile * LANES, (tile + 2) * LANES))
            else:
                for i in range(2):
                    store(b, tile + i, jnp.zeros((pieces * split_rows * rows, LANES), BF16))
        for f in range(flows_b):
            if b_taken[f] is None:
                b.rs_begin(f)
                b_taken[f] = 0

        rest = weight_t_ref.shape[0] - inner

        def input_rows(i, carry):
            rows_at = pl.ds(pl.multiple_of(i * 128, 128), 128)
            normed_grad = mm(gate_grad_ref[rows_at], weight_t_ref[:inner]) + mm(
                proj_grad[rows_at, :rest], weight_t_ref[inner:]
            )
            values = tokens_ref[rows_at].astype(F32)
            scale = lax.rsqrt(jnp.mean(values * values, axis=-1, keepdims=True) + EPS)
            gain_sums[0:1] += jnp.sum(normed_grad * values * scale, axis=0, keepdims=True)
            pushed = normed_grad * gain_ref[...]
            inside = jnp.mean(pushed * values, axis=-1, keepdims=True)
            input_grad_ref[rows_at] = (
                out_low_ref[rows_at].astype(F32)
                + scale * pushed
                - values * (scale * scale * scale * inside)
            ).astype(BF16)
            return carry

        def sm_copy(k):
            return remote(
                small_acc.at[k], small_in.at[k], sm_send.at[k], sm_recv.at[k], a.partner[k]
            )

        def sz_copy(k):
            return remote(
                small_acc.at[bits],
                small_parts.at[turn],
                sz_send.at[k],
                sz_recv.at[k],
                a.others[k],
            )

        def small_begin():
            model = gain_sums.shape[1]
            small_acc[0, 0:5] = conv_sums[0:5]
            small_acc[0, 5:7, :inner] = wide_ref[0:2]
            small_acc[0, 5:7, inner : inner + 128] = head_sums[0:2]
            small_acc[0, 5:8, inner + 128 :] = squares_ref[0:3]
            small_acc[0, 7:8, :model] = gain_sums[0:1]
            small_acc[0, 7:8, model : inner + 128] = jnp.zeros((1, inner + 128 - model), F32)
            sm_copy(0).start()

        def small_step(k):
            sm_copy(k).wait_recv()
            small_acc[k + 1] = small_acc[k] + small_in[k]
            if k + 1 < bits:
                sm_copy(k + 1).start()
            else:
                small_parts[turn] = small_acc[bits]
                for i in range(1, pieces):
                    sz_copy(i).start()

        def small_end():
            for i in range(1, pieces):
                sz_copy(i).wait_recv()
            whole = small_parts[0]
            for i in range(1, pieces):
                whole = whole + small_parts[i]
            small_out_ref[...] = whole

        lines = [a_actions[f][bits:] for f in range(flows_a)]
        lines += [b_actions[f][b_taken[f] :] for f in range(flows_b)]
        blocks_of_rows = tokens_ref.shape[0] // 128
        extra = [
            lambda: lax.fori_loop(0, blocks_of_rows // 2, input_rows, 0),
            lambda: lax.fori_loop(blocks_of_rows // 2, blocks_of_rows, input_rows, 0),
            small_begin,
        ]
        extra += [functools.partial(small_step, k) for k in range(bits)] + [small_end]
        while any(lines) or extra:
            if extra:
                extra.pop(0)()
            for line in lines:
                if line:
                    line.pop(0)()
        b.tiles_sent()
        a.sent()
        b.sent()
        for k in range(bits):
            sm_copy(k).wait_send()
        for i in range(1, pieces):
            sz_copy(i).wait_send()

        @pl.when(turn > 0)
        def _():
            for slot in range(steps + 1):
                rim_copy(slot).wait_send()

        for f in range(flows_a):
            out_copy(a, out_a_ref, f).wait()
        for f in range(flows_b):
            out_copy(b, out_b_ref, f).wait()


def row_split(places, rows):
    return 2 if places > 2 and rows % 32 == 0 else 1


def tail(
    rate,
    tiled,
    summed_rw_source,
    whole,
    weights,
    momenta,
    wide,
    squares,
    sizes,
    places,
    pieces,
    flows,
    blocks=6,
):
    seqs, piece, inner, channels, heads = sizes
    summed, conv, halo, taps, ssm_grad, starts, heads_map, skip = tiled
    total_rows = summed.shape[0]
    own = whole[6]
    tokens, weight_t = whole[13], whole[12]
    model = tokens.shape[1]
    flows_a, flows_b = flows
    assert flows_b <= flows_a
    bits = places.bit_length() - 1
    assert places == 1 << bits and bits >= 1 and pieces >= 2
    share = model // pieces
    split_rows = row_split(places, share)
    rows = share // split_rows
    steps = inner // TILE
    small = (8, channels)
    shape = jax.ShapeDtypeStruct
    any_space = pl.BlockSpec(memory_space=pl.ANY)
    sem = dma_semaphores

    def constant(array):
        count = array.ndim
        return pl.BlockSpec(
            array.shape, lambda j: (0,) * count, pipeline_mode=pl.Buffered(1)
        )

    def columns(height, last):
        return pl.BlockSpec((height, TILE), lambda j: (0, jnp.clip(j - 1, 0, last)))

    gathered = lambda count: (count,) + (2,) * bits + (pieces + 1, rows, LANES)
    chunk_count = total_rows // CHUNK
    square = (chunk_count, CHUNK, CHUNK)
    per_tile = (total_rows, TILE)
    per_head = (total_rows, 128)
    constants = list(whole) + [weights, momenta, wide, squares]
    return pl.pallas_call(
        functools.partial(
            tail_kernel, sizes, (bits, pieces, flows_a, flows_b, split_rows, blocks)
        ),
        grid=(steps + 2,),
        in_specs=[
            pl.BlockSpec(memory_space=pltpu.SMEM),
            columns(total_rows, steps),
            columns(total_rows, steps),
            columns(halo.shape[0], steps),
            columns(4, steps),
            columns(total_rows, steps - 1),
            pl.BlockSpec(
                (chunk_count, 128, TILE), lambda j: (0, 0, jnp.clip(j - 1, 0, steps - 1))
            ),
            columns(128, steps - 1),
            columns(1, steps - 1),
            pl.BlockSpec((total_rows, TILE), lambda j: (0, steps), pipeline_mode=pl.Buffered(1)),
        ]
        + [constant(array) for array in constants],
        out_specs=(
            pl.BlockSpec((total_rows, model), lambda j: (0, 0)),
            pl.BlockSpec(small, lambda j: (0, 0)),
            any_space,
            any_space,
        ),
        out_shape=(
            shape((total_rows, model), BF16),
            shape(small, F32),
            shape(gathered(flows_a), BF16),
            shape(gathered(flows_b), BF16),
        ),
        scratch_shapes=exchange_scratch(bits, pieces, flows_a, rows)
        + exchange_scratch(bits, pieces, flows_b, rows, 0)
        + [pltpu.VMEM((blocks, seqs, 128, inner // blocks), BF16)] * 2
        + sem(blocks)
        + [
            pltpu.VMEM((seqs, 128, inner), F32),
            pltpu.VMEM((model, total_rows), BF16),
            pltpu.VMEM((model, total_rows), BF16),
            pltpu.VMEM(per_head, BF16),
            pltpu.VMEM(per_head, BF16),
            pltpu.VMEM(square, BF16),
            pltpu.VMEM(square, F32),
            pltpu.VMEM(square, F32),
            pltpu.VMEM(square, F32),
            pltpu.VMEM(square, F32),
            pltpu.VMEM(per_head, F32),
            pltpu.VMEM(per_head, F32),
            pltpu.VMEM(per_tile, F32),
            pltpu.VMEM(per_tile, F32),
            pltpu.VMEM(per_tile, F32),
            pltpu.VMEM(per_tile, F32),
            pltpu.VMEM(per_tile, F32),
            pltpu.VMEM((128, TILE), F32),
            pltpu.VMEM((max(chunk_count, 8), TILE), F32),
            pltpu.VMEM(per_head, F32),
            pltpu.VMEM(per_head, F32),
            pltpu.VMEM((max(chunk_count, 8), 128), F32),
            pltpu.VMEM((piece + 16, TILE), F32),
            pltpu.VMEM((total_rows, channels + 256), BF16),
            pltpu.VMEM((seqs, 8, TILE), F32),
            pltpu.VMEM((steps + 1, seqs, 8, TILE), BF16),
            pltpu.VMEM((steps + 1, seqs, 8, TILE), BF16),
        ]
        + sem(steps + 1)
        + [
            pltpu.VMEM(small, F32),
            pltpu.VMEM((8, 128), F32),
            pltpu.VMEM((8, model), F32),
            pltpu.VMEM((bits + 1,) + small, F32),
            pltpu.VMEM((bits,) + small, F32),
            pltpu.VMEM((pieces,) + small, F32),
        ]
        + sem(bits)
        + sem(pieces),
        compiler_params=pltpu.CompilerParams(
            collective_id=2, has_side_effects=True, vmem_limit_bytes=62 * 1024 * 1024
        ),
        name="tail",
    )(rate, *tiled, summed_rw_source, *constants)


def piece_kernel(
    counts, spot_ref, out_weight_ref, weight_ref, out_momentum_ref, momentum_ref, w_ref, m_ref, turned
):
    out_tiles, tile_of, split_rows = counts
    tile = tile_of(pl.program_id(0), spot_ref)
    rows = m_ref.shape[1]
    part = lax.rem(spot_ref[0], split_rows)
    first = (spot_ref[1] * split_rows + part) * rows
    start = jnp.minimum(lax.div(first, 128) * 128, out_weight_ref.shape[1] - 256)
    window = pl.ds(pl.multiple_of(start, 128), 256)
    mine = pl.ds(pl.multiple_of(first - start, 16), rows)
    half = pl.ds(pl.multiple_of(part * rows, 16), rows)

    @pl.when(tile < out_tiles)
    def _():
        turned[...] = jnp.transpose(out_weight_ref[:, window])
        w_ref[0] = turned[mine]
        m_ref[0] = out_momentum_ref[half]

    @pl.when(tile >= out_tiles)
    def _():
        turned[...] = jnp.transpose(weight_ref[:, window])
        w_ref[0] = turned[mine]
        m_ref[0] = momentum_ref[half]


def owned(spot, out_weight, weight_t, out_momentum_t, momentum, flows_a, flows_b, places):
    inner, model = out_weight.shape
    share, width = momentum.shape
    out_tiles, in_tiles = inner // LANES, -(-width // LANES)
    split_rows = row_split(places, share)
    rows, per_flow = share // split_rows, places // split_rows

    flows = flows_a + flows_b

    def tile_of(f, spot):
        early = jnp.minimum(f * per_flow + spot[0] // split_rows, 2 * out_tiles - 1)
        late = 2 * out_tiles + (f - flows_a) * per_flow + spot[0] // split_rows
        return jnp.where(f < flows_a, early, late)

    def out_at(f, spot):
        return jnp.clip(tile_of(f, spot), 0, out_tiles - 1)

    def in_at(f, spot):
        return jnp.clip(tile_of(f, spot) - out_tiles, 0, in_tiles - 1)

    piece = pl.BlockSpec((1, rows, LANES), lambda f, spot: (f, 0, 0))
    return pl.pallas_call(
        functools.partial(piece_kernel, (out_tiles, tile_of, split_rows)),
        grid_spec=pltpu.PrefetchScalarGridSpec(
            num_scalar_prefetch=1,
            grid=(flows,),
            in_specs=[
                pl.BlockSpec((LANES, model), lambda f, spot: (out_at(f, spot), 0)),
                pl.BlockSpec((LANES, model), lambda f, spot: (in_at(f, spot), 0)),
                pl.BlockSpec((share, LANES), lambda f, spot: (0, out_at(f, spot))),
                pl.BlockSpec((share, LANES), lambda f, spot: (0, in_at(f, spot))),
            ],
            out_specs=(piece, piece),
            scratch_shapes=[pltpu.VMEM((256, LANES), BF16)],
        ),
        out_shape=(
            jax.ShapeDtypeStruct((flows, rows, LANES), BF16),
            jax.ShapeDtypeStruct((flows, rows, LANES), F32),
        ),
        name="owned",
    )(spot, out_weight, weight_t, out_momentum_t, momentum)


def finish_kernel(
    out_steps,
    split_rows,
    gathered_a_ref,
    gathered_b_ref,
    out_momentum_ref,
    momentum_ref,
    totals_ref,
    out_weight_ref,
    weight_ref,
    new_out_momentum_ref,
    new_momentum_ref,
    conv_weight_ref,
    conv_bias_ref,
    gate_gain_ref,
    norm_gain_ref,
    skip_ref,
    dt_bias_ref,
    a_log_ref,
    output_rms_ref,
    mixer_rms_ref,
    joined,
):
    group, slots, rows, _ = gathered_a_ref.shape
    step = pl.program_id(0)

    @pl.when(step == 0)
    def _():
        heads, inner, model = skip_ref.shape[0], gate_gain_ref.shape[0], norm_gain_ref.shape[0]
        side = inner + 128
        conv_weight_ref[...] = totals_ref[0:4]
        conv_bias_ref[...] = totals_ref[4]
        gate_gain_ref[...] = totals_ref[5, :inner]
        norm_gain_ref[...] = totals_ref[7, :model]
        skip_ref[...] = totals_ref[6, :heads]
        dt_bias_ref[...] = totals_ref[5, inner : inner + heads]
        a_log_ref[...] = totals_ref[6, inner : inner + heads]
        count = jnp.maximum(totals_ref[7:8, side + 9 : side + 10], 1.0) * model
        squares = jnp.sum(totals_ref[5:7, side:], axis=1, keepdims=True)
        output_rms_ref[...] = jnp.sqrt(squares[0:1] / count)
        mixer_rms_ref[...] = jnp.sqrt(squares[1:2] / count)

    def write(gathered_ref, weights, old, new):
        for i in range(group // split_rows):
            at = slice(i * LANES, (i + 1) * LANES)
            for part in range(split_rows):
                for p in range(slots - 1):
                    to = (p * split_rows + part) * rows
                    joined[to : to + rows] = gathered_ref[i * split_rows + part, p]
                own = slice(part * rows, (part + 1) * rows)
                summed = gathered_ref[i * split_rows + part, slots - 1].astype(F32)
                new[own, at] = 0.5 * old[own, at] + summed
            weights[at] = jnp.transpose(joined[...])

    @pl.when(step < out_steps)
    def _():
        write(gathered_a_ref, out_weight_ref, out_momentum_ref, new_out_momentum_ref)

    @pl.when((step >= out_steps) & (step < 2 * out_steps))
    def _():
        write(gathered_a_ref, weight_ref, momentum_ref, new_momentum_ref)

    @pl.when(step >= 2 * out_steps)
    def _():
        write(gathered_b_ref, weight_ref, momentum_ref, new_momentum_ref)


def finish(gathered_a, gathered_b, out_momentum_t, momentum, totals, heads, split_rows, group=4):
    _, slots, rows, _ = gathered_a.shape
    share, width = momentum.shape
    inner = out_momentum_t.shape[1]
    model = (slots - 1) * share
    wide = group * LANES
    group = group * split_rows
    out_steps, in_steps = inner // wide, -(-width // wide)
    out_at = lambda j: jnp.minimum(j, out_steps - 1)
    in_at = lambda j: jnp.maximum(j - out_steps, 0)
    by_column = [
        pl.BlockSpec((share, wide), lambda j: (0, out_at(j))),
        pl.BlockSpec((share, wide), lambda j: (0, in_at(j))),
    ]
    shape = jax.ShapeDtypeStruct
    smalls = [
        shape(size, F32)
        for size in (
            (4, totals.shape[1]),
            (totals.shape[1],),
            (inner,),
            (model,),
            (heads,),
            (heads,),
            (heads,),
            (1, 1),
            (1, 1),
        )
    ]
    return pl.pallas_call(
        functools.partial(finish_kernel, out_steps, split_rows),
        grid=(out_steps + in_steps,),
        in_specs=[
            pl.BlockSpec(
                (group, slots, rows, LANES), lambda j: (jnp.minimum(j, 2 * out_steps - 1), 0, 0, 0)
            ),
            pl.BlockSpec(
                (group, slots, rows, LANES), lambda j: (jnp.maximum(j - 2 * out_steps, 0), 0, 0, 0)
            ),
        ]
        + by_column
        + [pl.BlockSpec(totals.shape, lambda j: (0, 0))],
        out_specs=[
            pl.BlockSpec((wide, model), lambda j: (out_at(j), 0)),
            pl.BlockSpec((wide, model), lambda j: (in_at(j), 0)),
        ]
        + by_column
        + [
            pl.BlockSpec(small.shape, lambda j, count=len(small.shape): (0,) * count)
            for small in smalls
        ],
        out_shape=[
            shape((inner, model), BF16),
            shape((width, model), BF16),
            shape((share, inner), F32),
            shape((share, width), F32),
        ]
        + smalls,
        scratch_shapes=[pltpu.VMEM((model, LANES), BF16)],
        name="finish",
    )(gathered_a, gathered_b, out_momentum_t, momentum, totals)


def local(
    tokens,
    cotangent,
    segment_ids,
    doc_starts,
    valid_mask,
    step_number,
    learn_rate,
    norm_gain,
    in_weight,
    conv_weight,
    conv_bias,
    dt_bias,
    a_log,
    skip_d,
    gate_gain,
    out_weight,
    in_momentum,
    out_momentum,
):
    seqs, piece, model_width = tokens.shape
    heads = dt_bias.shape[0]
    tap_count, channels = conv_weight.shape
    inner_width = gate_gain.shape[0]
    proj_width = in_weight.shape[1]
    total = seqs * piece
    sizes = (seqs, piece, inner_width, channels, heads)
    places, pieces = lax.axis_size("dp"), lax.axis_size("seq")
    turn = lax.axis_index("seq")
    seg = segment_ids.astype(F32)
    sent = jnp.concatenate(
        [
            tokens[:, piece - HALO :],
            jnp.broadcast_to(seg[:, piece - HALO :, None], (seqs, HALO, LANES)).astype(BF16),
        ],
        axis=2,
    )
    route = [(i, i + 1) for i in range(pieces - 1)]
    arrived = lax.ppermute(sent, "seq", route)
    halo = arrived[:, :, :model_width].reshape(seqs * HALO, model_width)
    early_seg = jnp.where(turn == 0, -1.0, arrived[:, :, model_width].astype(F32))
    seg_pad = jnp.concatenate([early_seg, seg], axis=1)
    seg_row = seg.reshape(1, total)
    heads_map = (
        lax.broadcasted_iota(jnp.int32, (LANES, inner_width), 0)
        == lax.broadcasted_iota(jnp.int32, (LANES, inner_width), 1) // (inner_width // heads)
    ).astype(BF16)

    def lanes(values):
        return jnp.pad(values, (0, LANES - heads)).reshape(1, LANES)

    flat_tokens = tokens.reshape(total, model_width)
    weight_t = jnp.transpose(in_weight)
    out_momentum_t = jnp.transpose(out_momentum)
    flat_cot = cotangent.reshape(total, model_width)
    bias_row, decay_row = lanes(dt_bias), lanes(a_log)
    skip_row = jnp.repeat(skip_d, inner_width // heads).reshape(1, inner_width)
    gain_row = gate_gain.reshape(1, inner_width)
    normed, masks, gate, conv, conv_halo, summed, raw, cum, fresh, keep = front(
        flat_tokens,
        halo,
        norm_gain.reshape(1, model_width),
        weight_t,
        conv_weight,
        conv_bias.reshape(1, channels),
        seg_pad,
        valid_mask,
        bias_row,
        decay_row,
        heads_map,
        sizes,
    )
    incoming = chain(fresh, keep, 1)
    output, low, out_low, gate_grad, ssm_grad, starts, dots, squares, wide, state_grad = forward(
        summed,
        gate,
        raw,
        cum,
        masks,
        seg_row,
        incoming,
        flat_tokens,
        flat_cot,
        out_weight,
        gain_row,
        skip_row,
        heads_map,
        sizes,
    )
    step_float = step_number[0].astype(F32)
    rate = (learn_rate[0] * step_float / (step_float + 16.0)).reshape(1)
    share_rows = model_width // pieces
    split_rows = row_split(places, share_rows)
    per_flow = places // split_rows
    flows_a = -(-2 * inner_width // (LANES * per_flow))
    flows_b = -(-(channels + 2 * LANES) // (LANES * per_flow))
    spot = jnp.stack([lax.axis_index("dp"), turn]).astype(jnp.int32)
    weights, momenta = owned(
        spot, out_weight, weight_t, out_momentum_t, in_momentum, flows_a, flows_b, places
    )
    input_grad, totals, gathered_a, gathered_b = tail(
        rate,
        (summed, conv, conv_halo, conv_weight, ssm_grad, starts, heads_map, skip_row),
        summed,
        (
            raw,
            cum,
            masks,
            seg_row,
            dots,
            decay_row,
            state_grad,
            keep,
            out_low,
            normed,
            low,
            gate_grad,
            weight_t,
            flat_tokens,
            norm_gain.reshape(1, model_width),
        ),
        weights,
        momenta,
        wide,
        squares,
        sizes,
        places,
        pieces,
        (flows_a, flows_b),
    )
    share = (pieces + 1, share_rows // split_rows, LANES)
    (
        new_out_weight,
        new_weight_t,
        new_out_momentum_t,
        new_in_momentum,
        conv_weight_total,
        conv_bias_total,
        gate_gain_total,
        norm_gain_total,
        skip_total,
        dt_bias_total,
        a_log_total,
        output_rms,
        mixer_rms,
    ) = finish(
        gathered_a.reshape((-1,) + share),
        gathered_b.reshape((-1,) + share),
        out_momentum_t,
        in_momentum,
        totals,
        heads,
        split_rows,
    )
    new_in_weight = jnp.transpose(new_weight_t)
    new_out_momentum = jnp.transpose(new_out_momentum_t)
    output_rms, mixer_rms = output_rms.reshape(1), mixer_rms.reshape(1)
    return (
        output.reshape(tokens.shape),
        input_grad.reshape(tokens.shape),
        new_in_weight,
        new_out_weight,
        new_in_momentum,
        new_out_momentum,
        norm_gain_total,
        conv_weight_total,
        conv_bias_total,
        dt_bias_total,
        a_log_total,
        skip_total,
        gate_gain_total,
        output_rms,
        mixer_rms,
    )


def solution(mesh):
    placed = (
        P("dp", "seq", None),
        P("dp", "seq", None),
        P("dp", "seq"),
        P("dp", "seq"),
        P("dp", "seq"),
        P(),
        P(),
        P(),
        P(),
        P(),
        P(),
        P(),
        P(),
        P(),
        P(),
        P(),
        P("seq", None),
        P(None, "seq"),
    )
    return jax.shard_map(
        local,
        mesh=mesh,
        in_specs=placed,
        out_specs=(
            P("dp", "seq", None),
            P("dp", "seq", None),
            P(),
            P(),
            P("seq", None),
            P(None, "seq"),
            P(),
            P(),
            P(),
            P(),
            P(),
            P(),
            P(),
            P(),
            P(),
        ),
        check_vma=False,
    )
```

```python
import functools

import jax
import jax.numpy as jnp
from jax import lax
from jax.experimental import pallas as pl
from jax.experimental.pallas import tpu as pltpu
from jax.sharding import PartitionSpec as P

CHUNK = 128
HALO = 16
GATE_BLOCK = 256
EPS = 1e-05
NEGATIVE = -1e30
F32, BF16 = jnp.float32, jnp.bfloat16
LANES = 128
MESH = pl.DeviceIdType.MESH


def remote(src, dst, send, recv, target):
    return pltpu.make_async_remote_copy(
        src_ref=src,
        dst_ref=dst,
        send_sem=send,
        recv_sem=recv,
        device_id=target,
        device_id_type=MESH,
    )


def greet(targets):
    barrier = pltpu.get_barrier_semaphore()
    for target in targets:
        pl.semaphore_signal(barrier, inc=1, device_id=target, device_id_type=MESH)
    pl.semaphore_wait(barrier, len(targets))


def dma_semaphores(*shape):
    return [pltpu.SemaphoreType.DMA(shape)] * 2


def part_count(pieces):
    return 2 if pieces % 2 == 0 else 1


def half_shape(bits, pieces, flows, rows, k):
    return (flows,) + (2,) * (bits - k - 1) + (pieces, rows, LANES)


def mm(a, b):
    return jnp.dot(a, b, preferred_element_type=F32)


def mm_nt(a, b):
    return lax.dot_general(a, b, (((1,), (1,)), ((), ())), preferred_element_type=F32)


def mm_tn(a, b):
    return lax.dot_general(a, b, (((0,), (0,)), ((), ())), preferred_element_type=F32)


def split(a):
    high = a.astype(BF16)
    return high, (a - high.astype(F32)).astype(BF16)


def exact_mm(a, b):
    return jnp.dot(a, b, preferred_element_type=F32, precision=lax.Precision.HIGHEST)


def spread(a, heads_ref):
    high, low = split(a)
    return mm(high, heads_ref[...]) + mm(low, heads_ref[...])


def gather_heads(a, heads_ref):
    high, low = split(a)
    return mm_nt(high, heads_ref[...]) + mm_nt(low, heads_ref[...])


def sigmoid(v):
    return 1.0 / (1.0 + jnp.exp(-v))


def gate_of(v):
    return 0.5 + 0.5 * jnp.tanh(0.5 * v)


def softplus(v):
    return jnp.maximum(v, 0.0) + jnp.log1p(jnp.exp(-jnp.abs(v)))


def triangle(size, upper):
    row = lax.broadcasted_iota(jnp.int32, (size, size), 0)
    column = lax.broadcasted_iota(jnp.int32, (size, size), 1)
    return ((row <= column) if upper else (row >= column)).astype(F32)


def front_kernel(
    sizes,
    tokens_ref,
    halo_ref,
    gain_ref,
    weight_ref,
    taps_ref,
    bias_ref,
    seg_ref,
    valid_ref,
    dt_bias_ref,
    a_log_ref,
    heads_ref,
    normed_ref,
    masks_ref,
    gate_ref,
    conv_ref,
    halo_out_ref,
    summed_ref,
    raw_ref,
    cum_ref,
    state_ref,
    keep_ref,
    padded,
    product,
    active,
):
    seqs, piece, inner, channels, heads = sizes
    gate_blocks, conv_blocks = inner // GATE_BLOCK, channels // GATE_BLOCK
    step = pl.program_id(0)
    stride = piece + HALO

    @pl.when(step == 0)
    def _():
        gain = gain_ref[...]
        for n in range(seqs):
            padded_seg = seg_ref[n : n + 1]
            seg = padded_seg[:, HALO:]

            def over_chunks(at):
                return jnp.concatenate(
                    [
                        jnp.broadcast_to(
                            padded_seg[:, c * CHUNK + at : c * CHUNK + at + 1], (1, CHUNK)
                        )
                        for c in range(piece // CHUNK)
                    ],
                    axis=1,
                )

            others = [padded_seg[:, HALO - 3 + k : HALO - 3 + k + piece] for k in range(4)] + [
                over_chunks(HALO - 1),
                over_chunks(HALO + CHUNK - 1),
                jnp.broadcast_to(padded_seg[:, HALO - 1 : HALO], (1, piece)),
                jnp.broadcast_to(padded_seg[:, HALO + piece - 1 :], (1, piece)),
            ]
            lines = [(other == seg).astype(F32) for other in others] + [
                seg,
                valid_ref[n : n + 1].astype(F32),
            ]
            lines = lines + [jnp.zeros_like(seg)] * (16 - len(lines))
            masks_ref[pl.ds(n * piece, piece)] = jnp.transpose(jnp.concatenate(lines, axis=0))
            for source, start, to, count in (
                (halo_ref, n * HALO, n * stride, HALO),
                (tokens_ref, n * piece, n * stride + HALO, piece),
            ):

                def body(i, carry):
                    values = source[pl.ds(pl.multiple_of(start + i * 16, 16), 16)].astype(F32)
                    scale = lax.rsqrt(jnp.mean(values * values, axis=-1, keepdims=True) + EPS)
                    low = (values * scale * gain).astype(BF16)
                    padded[pl.ds(pl.multiple_of(to + i * 16, 16), 16)] = low
                    return carry

                lax.fori_loop(0, count // 16, body, 0)
            normed_ref[pl.ds(n * piece, piece)] = padded[pl.ds(n * stride + HALO, piece)]

    product[...] = mm_nt(padded[...], weight_ref[...])

    @pl.when(step < gate_blocks)
    def _():
        for n in range(seqs):
            gate_ref[pl.ds(n * piece, piece)] = product[pl.ds(n * stride + HALO, piece)]

    @pl.when((step >= gate_blocks) & (step < gate_blocks + conv_blocks))
    def _():
        at = pl.multiple_of((step - gate_blocks) * GATE_BLOCK, GATE_BLOCK)
        for n in range(seqs):
            conv_ref[pl.ds(n * piece, piece)] = product[pl.ds(n * stride + HALO, piece)]
            halo_out_ref[pl.ds(n * HALO, HALO)] = product[pl.ds(n * stride, HALO)]
            for i in range(piece // 64):
                rows = pl.ds(n * piece + i * 64, 64)
                total = jnp.broadcast_to(bias_ref[...], (64, GATE_BLOCK))
                for k in range(4):
                    source = product[pl.ds(n * stride + HALO - 3 + k + i * 64, 64)]
                    total = total + source * masks_ref[rows, k : k + 1] * taps_ref[k : k + 1]
                summed_ref[rows] = total
                active[rows, pl.ds(at, GATE_BLOCK)] = (total * gate_of(total)).astype(BF16)

    @pl.when(step == gate_blocks + conv_blocks)
    def _():
        lane = lax.broadcasted_iota(jnp.int32, (piece, 128), 1)
        lower = triangle(CHUNK, False)
        for n in range(seqs):
            rows = pl.ds(n * piece, piece)
            raw = jnp.where(lane < heads, product[pl.ds(n * stride + HALO, piece), :128], 0.0)
            raw = raw + dt_bias_ref[...]
            raw_ref[rows] = raw
            steps = jnp.where(lane < heads, softplus(raw), 0.0)
            decay = -jnp.exp(a_log_ref[...]) * steps
            total = jnp.zeros((1, 128), F32)
            pieces = []
            for c in range(piece // CHUNK):
                cumulative = exact_mm(lower, decay[c * CHUNK : (c + 1) * CHUNK])
                cum_ref[pl.ds(n * piece + c * CHUNK, CHUNK)] = cumulative
                pieces.append(cumulative + total)
                total = total + cumulative[CHUNK - 1 :]
            whole = jnp.concatenate(pieces, axis=0) if len(pieces) > 1 else pieces[0]
            tails = jnp.exp(total - whole) * steps * masks_ref[rows, 7:8]
            weighted = (spread(tails, heads_ref) * active[rows, :inner].astype(F32)).astype(BF16)
            state_ref[n] = mm_tn(active[rows, inner : inner + 128], weighted)
            last = masks_ref[n * piece + piece - 1 : n * piece + piece, 6:7]
            keep = jnp.exp(total) * last
            keep_ref[n] = spread(jnp.broadcast_to(keep, (8, 128)), heads_ref)


def front(tokens, halo, gain, weight, taps, bias, segs, valid, dt_bias, a_log, heads_map, sizes):
    seqs, piece, inner, channels, heads = sizes
    total, model = tokens.shape
    stride = seqs * (piece + HALO)
    gate_blocks, conv_blocks = inner // GATE_BLOCK, channels // GATE_BLOCK
    full = lambda *shape: pl.BlockSpec(shape, lambda j: (0,) * len(shape))

    def conv_at(j):
        return (0, jnp.clip(j - gate_blocks, 0, conv_blocks - 1))

    return pl.pallas_call(
        functools.partial(front_kernel, sizes),
        grid=(gate_blocks + conv_blocks + 1,),
        in_specs=[
            full(total, model),
            full(seqs * HALO, model),
            full(1, model),
            pl.BlockSpec((GATE_BLOCK, model), lambda j: (j, 0)),
            pl.BlockSpec((4, GATE_BLOCK), conv_at),
            pl.BlockSpec((1, GATE_BLOCK), conv_at),
            full(*segs.shape),
            full(*valid.shape),
            full(1, 128),
            full(1, 128),
            full(128, inner),
        ],
        out_specs=(
            full(total, model),
            full(total, 16),
            pl.BlockSpec((total, GATE_BLOCK), lambda j: (0, jnp.minimum(j, gate_blocks - 1))),
            pl.BlockSpec((total, GATE_BLOCK), conv_at),
            pl.BlockSpec((seqs * HALO, GATE_BLOCK), conv_at),
            pl.BlockSpec((total, GATE_BLOCK), conv_at),
            full(total, 128),
            full(total, 128),
            full(seqs, 128, inner),
            full(seqs, 8, inner),
        ),
        out_shape=(
            jax.ShapeDtypeStruct((total, model), BF16),
            jax.ShapeDtypeStruct((total, 16), F32),
            jax.ShapeDtypeStruct((total, inner), F32),
            jax.ShapeDtypeStruct((total, channels), F32),
            jax.ShapeDtypeStruct((seqs * HALO, channels), F32),
            jax.ShapeDtypeStruct((total, channels), F32),
            jax.ShapeDtypeStruct((total, 128), F32),
            jax.ShapeDtypeStruct((total, 128), F32),
            jax.ShapeDtypeStruct((seqs, 128, inner), F32),
            jax.ShapeDtypeStruct((seqs, 8, inner), F32),
        ),
        scratch_shapes=[
            pltpu.VMEM((stride, model), BF16),
            pltpu.VMEM((stride, GATE_BLOCK), F32),
            pltpu.VMEM((total, channels), BF16),
        ],
        compiler_params=pltpu.CompilerParams(vmem_limit_bytes=48 * 1024 * 1024),
        name="front",
    )(tokens, halo, gain, weight, taps, bias, segs, valid, dt_bias, a_log, heads_map)


def chain_kernel(ways, blocks, own_ref, keep_ref, out_ref, sent, taken, send, recv):
    size = lax.axis_size("seq")
    turn = lax.axis_index("seq")
    first = turn == (0 if ways > 0 else size - 1)
    final = turn == (size - 1 if ways > 0 else 0)
    ahead = {"seq": lax.rem(turn + ways + size, size)}
    behind = {"seq": lax.rem(turn - ways + size, size)}
    barrier = pltpu.get_barrier_semaphore()

    @pl.when(jnp.logical_not(first))
    def _():
        pl.semaphore_signal(
            barrier, inc=1, device_id=behind, device_id_type=pl.DeviceIdType.MESH
        )

    @pl.when(jnp.logical_not(final))
    def _():
        pl.semaphore_wait(barrier, 1)

    width = own_ref.shape[2] // blocks

    def copy(c):
        return pltpu.make_async_remote_copy(
            src_ref=sent.at[c],
            dst_ref=taken.at[c],
            send_sem=send.at[c],
            recv_sem=recv.at[c],
            device_id=ahead,
            device_id_type=pl.DeviceIdType.MESH,
        )

    @pl.when(first)
    def _():
        out_ref[...] = jnp.zeros_like(out_ref)
        for c in range(blocks):
            at = slice(c * width, (c + 1) * width)
            sent[c] = own_ref[:, :, at].astype(BF16)
            copy(c).start()

    @pl.when(jnp.logical_not(first))
    def _():
        for c in range(blocks):
            at = slice(c * width, (c + 1) * width)
            copy(c).wait_recv()

            @pl.when(jnp.logical_not(final))
            def _():
                sent[c] = (
                    own_ref[:, :, at] + keep_ref[:, 0:1, at] * taken[c].astype(F32)
                ).astype(BF16)
                copy(c).start()

            out_ref[:, :, at] = taken[c].astype(F32)

    @pl.when(jnp.logical_not(final))
    def _():
        for c in range(blocks):
            copy(c).wait_send()


def chain(own, keep, ways, blocks=6):
    seqs, depth, inner = own.shape
    vmem = pl.BlockSpec(memory_space=pltpu.VMEM)
    part = (blocks, seqs, depth, inner // blocks)
    return pl.pallas_call(
        functools.partial(chain_kernel, ways, blocks),
        out_shape=jax.ShapeDtypeStruct(own.shape, F32),
        in_specs=[vmem, vmem],
        out_specs=vmem,
        scratch_shapes=[pltpu.VMEM(part, BF16)] * 2 + [pltpu.SemaphoreType.DMA((blocks,))] * 2,
        compiler_params=pltpu.CompilerParams(
            collective_id=1 if ways > 0 else 2,
            has_side_effects=True,
            vmem_limit_bytes=32 * 1024 * 1024,
        ),
        name="chain",
    )(own, keep)


def decays_of(cum, cum_t, bias, h):
    return jnp.exp(cum[:, h : h + 1] - cum_t[h : h + 1, :] + bias)


def mask_bias(seg_col, seg_row):
    row = lax.broadcasted_iota(jnp.int32, (CHUNK, CHUNK), 0)
    column = lax.broadcasted_iota(jnp.int32, (CHUNK, CHUNK), 1)
    return jnp.where((row >= column) & (seg_col == seg_row), 0.0, NEGATIVE)


def scores_of(reader, writer):
    rh, rl = split(reader)
    wh, wl = split(writer)
    return mm_nt(rh, wh) + (mm_nt(rh, wl) + mm_nt(rl, wh))


def forward_kernel(
    sizes,
    chunks,
    summed_ref,
    gate_ref,
    raw_ref,
    cum_ref,
    masks_ref,
    seg_row_ref,
    incoming_ref,
    tokens_ref,
    cot_ref,
    weight_ref,
    gain_ref,
    skip_ref,
    heads_ref,
    output_ref,
    low_ref,
    out_low_ref,
    gate_grad_ref,
    ssm_grad_ref,
    starts_ref,
    dot_ref,
    sums_ref,
    wide_ref,
    state_grad_ref,
    state,
    prefix,
    active,
    mixed_in,
    factors,
    grads,
    inv,
    totals,
):
    seqs, piece, inner, channels, heads = sizes
    c = pl.program_id(1)

    @pl.when((c == 0) & (pl.program_id(0) == 0))
    def _():
        sums_ref[...] = jnp.zeros_like(sums_ref)
        wide_ref[...] = jnp.zeros_like(wide_ref)

    @pl.when(c == 0)
    def _():
        state[...] = incoming_ref[0]
        prefix[...] = jnp.zeros_like(prefix)
        state_grad_ref[...] = jnp.zeros_like(state_grad_ref)

    def activate(i, carry):
        rows = pl.ds(pl.multiple_of(i * 16, 16), 16)
        values = summed_ref[rows]
        active[rows] = values * gate_of(values)
        return carry

    lax.fori_loop(0, CHUNK // 16, activate, 0)
    lane = lax.broadcasted_iota(jnp.int32, (CHUNK, 128), 1)
    steps = jnp.where(lane < heads, softplus(raw_ref[...]), 0.0)
    cum = cum_ref[...]
    cum_t = jnp.transpose(cum)
    final = cum[CHUNK - 1 :]
    tails = jnp.exp(final - cum) * steps * masks_ref[:, 5:6]
    before = spread(jnp.exp(prefix[...]), heads_ref)[0:1]
    prefix[...] = prefix[...] + final
    for i, block in enumerate((steps, jnp.exp(cum), tails)):
        factors[i] = spread(block, heads_ref)
    factors[3] = factors[1] * before * masks_ref[:, 6:7]
    factors[1] = factors[1] * masks_ref[:, 4:5]
    writer = active[:, inner : inner + 128]
    reader = active[:, inner + 128 : inner + 256]
    scores = scores_of(reader, writer)
    bias = mask_bias(masks_ref[:, 8:9], seg_row_ref[0:1])
    half = lax.broadcasted_iota(jnp.int32, (CHUNK, 128), 1) < 64
    state_low = state[...].astype(BF16)
    starts_ref[0] = state_low
    reader_low = reader.astype(BF16)
    for pair in range(heads // 2):
        at = slice(pair * 128, (pair + 1) * 128)
        moved = (active[:, at] * factors[0, :, at]).astype(BF16)
        zero = jnp.zeros_like(moved)
        one = (scores * decays_of(cum, cum_t, bias, 2 * pair)).astype(BF16)
        two = (scores * decays_of(cum, cum_t, bias, 2 * pair + 1)).astype(BF16)
        both = jnp.concatenate([one, two], axis=1)
        stacked = jnp.concatenate(
            [jnp.where(half, moved, zero), jnp.where(half, zero, moved)], axis=0
        )
        carried = mm(reader_low, state_low[:, at]) * factors[1, :, at]
        mixed_in[:, at] = mm(both, stacked) + carried
    weighted = (active[:, :inner] * factors[2]).astype(BF16)
    kept = jnp.exp(final) * masks_ref[CHUNK - 1 :, 4:5]
    kept = spread(jnp.broadcast_to(kept, (8, 128)), heads_ref)[0:1]
    state[...] = state[...] * kept + mm_tn(writer.astype(BF16), weighted)

    gain = gain_ref[...]
    skip = skip_ref[...]

    column_blocks = [slice(at, at + 512) for at in range(0, inner, 512)]

    def gating(i, carry):
        rows = pl.ds(pl.multiple_of(i * 16, 16), 16)
        squares = jnp.zeros((16, 512), F32)
        for at in column_blocks:
            gate = gate_ref[rows, at]
            turned = gate_of(gate)
            mixer = mixed_in[rows, at] + skip[:, at] * active[rows, at]
            product = mixer * gate * turned
            factors[0, rows, at] = product
            factors[1, rows, at] = turned
            factors[2, rows, at] = mixer
            squares = squares + product * product
        mean = jnp.sum(squares, axis=-1, keepdims=True) / inner
        scale = lax.rsqrt(mean + EPS)
        inv[rows] = jnp.broadcast_to(scale, (16, 128))
        for at in column_blocks:
            low_ref[rows, at] = (factors[0, rows, at] * scale * gain[:, at]).astype(BF16)
        return carry

    lax.fori_loop(0, CHUNK // 16, gating, 0)
    mixed = mm(low_ref[...], weight_ref[...])
    block_out = tokens_ref[...].astype(F32) + mixed
    output_ref[...] = block_out.astype(BF16)
    valid = masks_ref[:, 9:10]
    for i, block in enumerate((block_out, mixed)):
        squares = jnp.sum(valid * block * block, axis=0, keepdims=True)
        for at in range(0, squares.shape[1], 128):
            sums_ref[i : i + 1] += squares[:, at : at + 128]
    sums_ref[2:3, :16] += jnp.sum(masks_ref[...], axis=0, keepdims=True)
    out_low = (cot_ref[...].astype(F32) * valid).astype(BF16)
    out_low_ref[...] = out_low
    grads[...] = mm_nt(out_low, weight_ref[...])

    @pl.when((c == 0) & (pl.program_id(0) == 0))
    def _():
        totals[...] = jnp.zeros_like(totals)

    def backing(i, carry):
        rows = pl.ds(pl.multiple_of(i * 16, 16), 16)
        scale = inv[rows, 0:1]
        inside = jnp.zeros((16, 512), F32)
        for at in column_blocks:
            grad = grads[rows, at]
            gated = factors[0, rows, at]
            totals[0, :, at] += grad * gated * scale
            inside = inside + grad * gain[:, at] * gated
        inside = jnp.sum(inside, axis=-1, keepdims=True) / inner
        inside = scale * scale * scale * inside
        for at in column_blocks:
            gate, turned = gate_ref[rows, at], factors[1, rows, at]
            gated_grad = scale * (grads[rows, at] * gain[:, at]) - factors[0, rows, at] * inside
            ssm_grad = gated_grad * (gate * turned)
            ssm_grad_ref[rows, at] = ssm_grad
            grads[rows, at] = ssm_grad
            totals[1, :, at] += ssm_grad * active[rows, at]
            gate_grad_ref[rows, at] = (
                gated_grad * factors[2, rows, at] * turned * (1.0 + gate * (1.0 - turned))
            ).astype(BF16)
        return carry

    lax.fori_loop(0, CHUNK // 16, backing, 0)

    @pl.when((c == chunks - 1) & (pl.program_id(0) == seqs - 1))
    def _():
        wide_ref[0:1] = jnp.sum(totals[0], axis=0, keepdims=True)
        skips = jnp.sum(totals[1], axis=0, keepdims=True)
        skips = gather_heads(jnp.broadcast_to(skips, (8, inner)), heads_ref)
        wide_ref[1:2, :128] = skips[0:1]

    reader_t = jnp.transpose(reader_low)
    for pair in range(heads // 2):
        at = slice(pair * 128, (pair + 1) * 128)
        state_grad_ref[0, :, at] += mm(
            reader_t, (grads[:, at] * factors[3, :, at]).astype(BF16)
        )
        mixed_in[:, at] = mixed_in[:, at] * grads[:, at].astype(BF16).astype(F32)
    dot_ref[...] = gather_heads(mixed_in[...], heads_ref)


def forward(
    summed, gate, raw, cum, masks, seg_row, incoming, tokens, cot, weight, gain, skip, heads_map, sizes
):
    seqs, piece, inner, channels, heads = sizes
    total, model = tokens.shape
    chunks = piece // CHUNK
    full = lambda *shape: pl.BlockSpec(shape, lambda n, c: (0,) * len(shape))
    rows = lambda width: pl.BlockSpec((CHUNK, width), lambda n, c: (n * chunks + c, 0))
    each = lambda depth: pl.BlockSpec((1, depth, inner), lambda n, c: (n, 0, 0))
    shape = jax.ShapeDtypeStruct
    return pl.pallas_call(
        functools.partial(forward_kernel, sizes, chunks),
        grid=(seqs, chunks),
        in_specs=[
            rows(channels),
            rows(inner),
            rows(128),
            rows(128),
            rows(16),
            pl.BlockSpec((1, CHUNK), lambda n, c: (0, n * chunks + c)),
            each(128),
            rows(model),
            rows(model),
            full(inner, model),
            full(1, inner),
            full(1, inner),
            full(128, inner),
        ],
        out_specs=(
            rows(model),
            rows(inner),
            rows(model),
            rows(inner),
            rows(inner),
            pl.BlockSpec((1, 128, inner), lambda n, c: (n * chunks + c, 0, 0)),
            rows(128),
            full(8, 128),
            full(8, inner),
            each(128),
        ),
        out_shape=(
            shape((total, model), BF16),
            shape((total, inner), BF16),
            shape((total, model), BF16),
            shape((total, inner), BF16),
            shape((total, inner), F32),
            shape((seqs * chunks, 128, inner), BF16),
            shape((total, 128), F32),
            shape((8, 128), F32),
            shape((8, inner), F32),
            shape((seqs, 128, inner), F32),
        ),
        scratch_shapes=[
            pltpu.VMEM((128, inner), F32),
            pltpu.VMEM((8, 128), F32),
            pltpu.VMEM((CHUNK, channels), F32),
            pltpu.VMEM((CHUNK, inner), F32),
            pltpu.VMEM((4, CHUNK, inner), F32),
            pltpu.VMEM((CHUNK, inner), F32),
            pltpu.VMEM((CHUNK, 128), F32),
            pltpu.VMEM((2, 16, inner), F32),
        ],
        compiler_params=pltpu.CompilerParams(vmem_limit_bytes=48 * 1024 * 1024),
        name="forward",
    )(summed, gate, raw, cum, masks, seg_row, incoming, tokens, cot, weight, gain, skip, heads_map)


TILE = 256


class Exchange:
    def __init__(self, bits, pieces, flows):
        self.bits, self.pieces, self.flows = bits, pieces, flows
        self.parts = part_count(pieces)
        self.place, self.turn = lax.axis_index("dp"), lax.axis_index("seq")
        self.own = [(self.place // (1 << b)) % 2 for b in range(bits)]
        self.partner = [
            {"dp": self.place + (1 - 2 * self.own[b]) * (1 << b)} for b in range(bits)
        ]
        self.others = [{"seq": lax.rem(self.turn + j, pieces)} for j in range(pieces)]
        self.mine = self.index_of({b: self.own[b] for b in range(bits)})

    def index_of(self, fixed):
        return tuple(fixed.get(b, slice(None)) for b in range(self.bits - 1, -1, -1))

    def spot_of(self, d):
        return tuple((d // (1 << b)) % 2 for b in range(self.bits - 1, -1, -1))

    def order_of(self, f, h):
        rest = list(range(1, self.bits))
        shift = (f + h) % max(len(rest), 1)
        return [0] + rest[shift:] + rest[:shift]

    def share(self, h, extra=0):
        half = self.pieces // self.parts
        return pl.ds(h * half, half + (extra if h == self.parts - 1 else 0))

    def held(self, f, h, k, other):
        order = self.order_of(f, h)
        bit = order[k]
        value = 1 - self.own[bit] if other else self.own[bit]
        free = [b for b in range(self.bits - 1, -1, -1) if b not in order[:k]]
        source = self.grad if k == 0 else self.halves[k - 1]
        return source.at[
            (f,) + tuple(value if b == bit else slice(None) for b in free) + (self.share(h),)
        ]

    def landing(self, f, h, k):
        free = self.bits - k - 1
        return self.halves[k].at[(f,) + (slice(None),) * free + (self.share(h),)]

    def rs_copy(self, f, h, k):
        return remote(
            self.held(f, h, k, True),
            self.landing(f, h, k),
            self.rs_send.at[f, h, k],
            self.rs_recv.at[f, h, k],
            self.partner[self.order_of(f, h)[k]],
        )

    def rs_begin(self, f):
        for h in range(self.parts):
            self.rs_copy(f, h, 0).start()

    def rs_end(self, f, k):
        for h in range(self.parts):
            self.rs_copy(f, h, k).wait_recv()
            kept, into = self.held(f, h, k, False), self.landing(f, h, k)
            left = self.bits - k - 1
            for count in range(1 << left):
                spot = tuple((count >> (left - 1 - i)) & 1 for i in range(left))

                def body(p, carry, spot=spot, kept=kept, into=into):
                    into[spot + (p,)] = (
                        kept[spot + (p,)].astype(F32) + into[spot + (p,)].astype(F32)
                    ).astype(BF16)
                    return carry

                lax.fori_loop(0, self.pieces // self.parts, body, 0)
            if k + 1 < self.bits:
                self.rs_copy(f, h, k + 1).start()
        if k + 1 == self.bits:
            for j in range(1, self.pieces):
                self.zs_copy(f, j).start()

    def zs_copy(self, f, j):
        return remote(
            self.halves[self.bits - 1].at[f, lax.rem(self.turn + j, self.pieces)],
            self.piece_parts.at[f, j],
            self.zs_send.at[f, j],
            self.zs_recv.at[f, j],
            self.others[j],
        )

    def zs_end(self, f, rate, weight, momentum):
        for j in range(1, self.pieces):
            self.zs_copy(f, j).wait_recv()
        total = self.halves[self.bits - 1][f, self.turn].astype(F32)
        for j in range(1, self.pieces):
            total = total + self.piece_parts[f, j].astype(F32)
        summed = total.astype(BF16)
        moved = 0.5 * momentum + summed.astype(F32)
        self.gathered[(f,) + self.mine + (self.pieces,)] = summed
        self.gathered[(f,) + self.mine + (self.turn,)] = (
            weight.astype(F32) - rate * moved
        ).astype(BF16)
        for j in range(1, self.pieces):
            self.zg_copy(f, j).start()

    def zg_copy(self, f, j):
        spot = self.gathered.at[(f,) + self.mine + (self.turn,)]
        return remote(spot, spot, self.zg_send.at[f, j], self.zg_recv.at[f, j], self.others[j])

    def zg_end(self, f):
        for j in range(1, self.pieces):
            self.zg_copy(f, j).wait_recv()
        for h in range(self.parts):
            self.ag_copy(f, h, self.bits - 1).start()

    def ag_copy(self, f, h, k):
        order = self.order_of(f, h)
        fixed = {order[i]: self.own[order[i]] for i in range(k + 1)}
        spot = self.gathered.at[(f,) + self.index_of(fixed) + (self.share(h, 1),)]
        return remote(
            spot,
            spot,
            self.ag_send.at[f, h, k],
            self.ag_recv.at[f, h, k],
            self.partner[order[k]],
        )

    def ag_end(self, f, k):
        for h in range(self.parts):
            self.ag_copy(f, h, k).wait_recv()
            if k > 0:
                self.ag_copy(f, h, k - 1).start()

    def tiles_sent(self):
        for f in range(self.flows):
            for h in range(self.parts):
                self.rs_copy(f, h, 0).wait_send()

    def sent(self):
        for f in range(self.flows):
            for h in range(self.parts):
                for k in range(self.bits):
                    if k > 0:
                        self.rs_copy(f, h, k).wait_send()
                    self.ag_copy(f, h, k).wait_send()
            for j in range(1, self.pieces):
                self.zs_copy(f, j).wait_send()
                self.zg_copy(f, j).wait_send()

    def actions(self, f, rate, weights, momenta, after):
        steps = [functools.partial(self.rs_end, f, k) for k in range(self.bits)]
        steps.append(lambda: self.zs_end(f, rate, weights[f], momenta[f]))
        steps.append(functools.partial(self.zg_end, f))
        steps += [functools.partial(self.ag_end, f, k) for k in range(self.bits - 1, 0, -1)]

        def finish():
            self.ag_end(f, 0)
            after(f)

        return steps + [finish]


def exchange_scratch(bits, pieces, flows, rows, first=-1):
    parts = part_count(pieces)
    return (
        [pltpu.VMEM(half_shape(bits, pieces, flows, rows, k), BF16) for k in range(first, bits)]
        + [
            pltpu.VMEM((flows, pieces, rows, LANES), BF16),
            pltpu.VMEM((flows,) + (2,) * bits + (pieces + 1, rows, LANES), BF16),
        ]
        + dma_semaphores(flows, parts, bits)
        + dma_semaphores(flows, pieces)
        + dma_semaphores(flows, pieces)
        + dma_semaphores(flows, parts, bits)
        + [pltpu.SemaphoreType.DMA((flows,))]
    )


def give(ex, scratch, grad=None):
    if grad is None:
        grad, scratch = scratch[0], scratch[1:]
    ex.grad, ex.halves = grad, scratch[: ex.bits]
    scratch = scratch[ex.bits :]
    (ex.piece_parts, ex.gathered, ex.rs_send, ex.rs_recv, ex.zs_send, ex.zs_recv) = scratch[:6]
    (ex.zg_send, ex.zg_recv, ex.ag_send, ex.ag_recv, ex.out_sem) = scratch[6:11]
    return scratch[11:]


def tail_kernel(sizes, dims, *refs):
    seqs, piece, inner, channels, heads = sizes
    bits, pieces, flows_a, flows_b, split_rows, blocks = dims
    (
        rate_ref,
        summed_ref,
        conv_ref,
        halo_ref,
        taps_ref,
        ssm_grad_ref,
        starts_ref,
        heads_ref,
        skip_ref,
        summed_rw_ref,
        raw_ref,
        cum_ref,
        masks_ref,
        seg_row_ref,
        dot_ref,
        a_log_ref,
        own_ref,
        keep_ref,
        out_low_ref,
        normed_ref,
        low_ref,
        gate_grad_ref,
        weight_t_hbm,
        tokens_ref,
        gain_ref,
        weight_ref,
        momentum_ref,
        wide_ref,
        squares_ref,
        input_grad_ref,
        small_out_ref,
        out_a_ref,
        out_b_ref,
    ) = refs[:33]
    scratch = refs[33:]
    a, b = Exchange(bits, pieces, flows_a), Exchange(bits, pieces, flows_b)
    scratch = give(a, scratch)
    scratch = give(b, scratch, a.grad)
    (
        sent,
        taken,
        chain_send,
        chain_recv,
        later,
        out_turned,
        normed_turned,
        writer_low,
        reader_low,
        reader_turned,
        scores,
        cum_turned,
        biases,
        scores_grad,
        reader_grad,
        writer_grad,
        active,
        bent,
        step_x,
        cum_x,
        total,
        state_grad,
        ends,
        step_sum,
        move_sum,
        end_sum,
        shifted_rows,
        proj_grad,
        tails,
        rims,
        rims_in,
        rim_send,
        rim_recv,
        conv_sums,
        head_sums,
        gain_sums,
        small_acc,
        small_in,
        small_parts,
        sm_send,
        sm_recv,
        sz_send,
        sz_recv,
        weight_t_ref,
        weight_sem,
    ) = scratch
    weight_copy = pltpu.make_async_copy(weight_t_hbm, weight_t_ref, weight_sem)
    j = pl.program_id(0)
    steps = inner // TILE
    final_step = steps + 1
    places = 1 << bits
    per_flow = places // split_rows
    turn = a.turn
    chunk_count = seqs * piece // CHUNK
    rows = a.grad.shape[-2]
    chunks = piece // CHUNK
    rate = rate_ref[0]
    real = 2 * inner // LANES

    def out_copy(ex, out, f):
        return pltpu.make_async_copy(ex.gathered.at[f], out.at[f], ex.out_sem.at[f])

    a_actions = [
        a.actions(f, rate, weight_ref, momentum_ref, lambda f: out_copy(a, out_a_ref, f).start())
        for f in range(flows_a)
    ]
    late = [weight_ref.at[pl.ds(flows_a, flows_b)], momentum_ref.at[pl.ds(flows_a, flows_b)]]
    b_actions = [
        b.actions(f, rate, *late, lambda f: out_copy(b, out_b_ref, f).start())
        for f in range(flows_b)
    ]

    def store(ex, tile, values):
        for part in range(split_rows):
            d = (tile % per_flow) * split_rows + part
            spot = (tile // per_flow,) + ex.spot_of(d)
            for p in range(pieces):
                at = (p * split_rows + part) * rows
                ex.grad[spot + (p,)] = values[at : at + rows]

    def rim_copy(slot):
        return remote(
            rims.at[slot],
            rims_in.at[slot],
            rim_send.at[slot],
            rim_recv.at[slot],
            {"seq": lax.rem(turn + pieces - 1, pieces)},
        )

    def fix_rim(slot, at):
        @pl.when(turn < pieces - 1)
        def _():
            rim_copy(slot).wait_recv()
            for n in range(seqs):
                proj_grad[(n + 1) * piece - 8 : (n + 1) * piece, at] = (
                    tails[n] + rims_in[slot, n].astype(F32)
                ).astype(BF16)

    def conv_back(slot, at):
        for n in range(seqs):
            here_rows = pl.ds(n * piece, piece)
            grad = total[here_rows] * bent[here_rows]
            conv = conv_ref[here_rows]
            sums = [None] * 5
            sums[4] = jnp.sum(grad, axis=0, keepdims=True)
            sums[3] = jnp.sum(grad * conv, axis=0, keepdims=True)
            result = grad * taps_ref[3:4]
            rim = jnp.zeros((8, TILE), F32)
            shifted_rows[0:8] = jnp.zeros((8, TILE), F32)
            shifted_rows[8 + piece :] = jnp.zeros((8, TILE), F32)
            for k in range(3):
                shifted_rows[8 : 8 + piece] = grad * masks_ref[here_rows, k : k + 1]
                here = shifted_rows[11 - k : 11 - k + piece]
                result = result + here * taps_ref[k : k + 1]
                early = shifted_rows[3 - k : 11 - k]
                rim = rim + early * taps_ref[k : k + 1]
                sums[k] = jnp.sum(here * conv, axis=0, keepdims=True) + jnp.sum(
                    early * halo_ref[(n + 1) * HALO - 8 : (n + 1) * HALO], axis=0, keepdims=True
                )
            for i in range(5):
                if n == 0:
                    conv_sums[i : i + 1, at] = sums[i]
                else:
                    conv_sums[i : i + 1, at] += sums[i]
            proj_grad[here_rows, at] = result.astype(BF16)
            tails[n] = result[piece - 8 :]
            rims[slot, n] = rim.astype(BF16)

        @pl.when(turn > 0)
        def _():
            rim_copy(slot).start()

    @pl.when(j == 0)
    def _():
        greet(a.partner + a.others[1:])
        first, final = turn == pieces - 1, turn == 0
        width = inner // blocks

        def copy(c):
            ahead = {"seq": lax.rem(turn + pieces - 1, pieces)}
            return remote(sent.at[c], taken.at[c], chain_send.at[c], chain_recv.at[c], ahead)

        @pl.when(first)
        def _():
            later[...] = jnp.zeros_like(later)
            for c in range(blocks):
                sent[c] = own_ref[:, :, c * width : (c + 1) * width].astype(BF16)
                copy(c).start()

        weight_copy.start()
        out_turned[...] = jnp.transpose(out_low_ref[...])
        normed_turned[...] = jnp.transpose(normed_ref[...])
        low_tiles = inner // LANES

        def tiles(tile):
            if tile >= real:
                result = jnp.zeros((out_turned.shape[0], 2 * LANES), BF16)
            elif tile < low_tiles:
                at = tile * LANES
                result = mm(out_turned[...], low_ref[:, at : at + 2 * LANES]).astype(BF16)
            else:
                at = (tile - low_tiles) * LANES
                result = mm(normed_turned[...], gate_grad_ref[:, at : at + 2 * LANES])
                result = result.astype(BF16)
            store(a, tile, result[:, :LANES])
            store(a, tile + 1, result[:, LANES:])

        pairs = flows_a * per_flow // 2
        done = 0
        for c in range(blocks):
            until = pairs * (c + 1) // blocks
            for pair in range(done, until):
                tiles(2 * pair)
                if (2 * pair + 2) % per_flow == 0:
                    a.rs_begin(2 * pair // per_flow)
            done = until

            @pl.when(jnp.logical_not(first))
            def _():
                at = slice(c * width, (c + 1) * width)
                copy(c).wait_recv()

                @pl.when(jnp.logical_not(final))
                def _():
                    sent[c] = (
                        own_ref[:, :, at] + keep_ref[:, 0:1, at] * taken[c].astype(F32)
                    ).astype(BF16)
                    copy(c).start()

                later[:, :, at] = taken[c].astype(F32)

        for f in range(flows_a):
            a_actions[f][0]()
        a.tiles_sent()
        for ck in range(chunk_count):
            at = slice(ck * CHUNK, (ck + 1) * CHUNK)
            values = summed_rw_ref[at]
            values = values * sigmoid(values)
            writer, reader = values[:, :128], values[:, 128:]
            scores[ck] = scores_of(reader, writer)
            writer_low[at] = writer.astype(BF16)
            reader_low[at] = reader.astype(BF16)
            reader_turned[ck] = jnp.transpose(reader.astype(BF16))
            cum_turned[ck] = jnp.transpose(cum_ref[at])
            biases[ck] = mask_bias(masks_ref[at, 8:9], seg_row_ref[0:1, at])
        for ref in (
            scores_grad,
            reader_grad,
            writer_grad,
            step_sum,
            move_sum,
            end_sum,
            ends,
            gain_sums,
        ):
            ref[...] = jnp.zeros_like(ref)

        @pl.when(jnp.logical_not(final))
        def _():
            for c in range(blocks):
                copy(c).wait_send()

    agenda = {}

    def plan(step, act):
        agenda.setdefault(min(max(step, 1), steps), []).append(act)

    last_b = [((f + 1) * per_flow * LANES - 1) // TILE + 1 for f in range(flows_b)]
    a_steps = {1: 3, 2: 4} if bits == 3 else {k: 1 + k for k in range(1, bits)}
    a_done = b_ready = None
    for k in range(1, bits):
        for f in range(flows_a):
            plan(a_steps[k], a_actions[f][k])
    b_taken = []
    for f in range(flows_b):
        taken_steps = 0
        if last_b[f] + 1 <= steps:
            plan(last_b[f] + 1, functools.partial(b.rs_begin, f))
            for i in range(bits):
                if last_b[f] + 2 + i <= steps:
                    plan(last_b[f] + 2 + i, b_actions[f][i])
                    taken_steps = i + 1
            b_taken.append(taken_steps)
        else:
            b_taken.append(None)

    def weight_tiles(tile, at):
        result = mm(normed_turned[...], proj_grad[:, at]).astype(BF16)
        store(b, tile, result[:, :LANES])
        store(b, tile + 1, result[:, LANES:])

    @pl.when((j > 0) & (j < final_step))
    def _():
        at = pl.ds(pl.multiple_of((j - 1) * TILE, TILE), TILE)

        @pl.when(j > 1)
        def _():
            before = pl.ds(pl.multiple_of((j - 2) * TILE, TILE), TILE)
            fix_rim(j - 2, before)
            weight_tiles((j - 2) * (TILE // LANES), before)

        def activate(i, carry):
            rows_at = pl.ds(pl.multiple_of(i * 32, 32), 32)
            values = summed_ref[rows_at]
            turned = gate_of(values)
            active[rows_at] = values * turned
            bent[rows_at] = turned * (1.0 + values * (1.0 - turned))
            return carry

        lax.fori_loop(0, seqs * piece // 32, activate, 0)
        raw = raw_ref[...]
        lane = lax.broadcasted_iota(jnp.int32, raw.shape, 1)
        step_x[...] = spread(jnp.where(lane < heads, softplus(raw), 0.0), heads_ref)
        cum = cum_ref[...]
        high, low = split(cum)
        lowest = (cum - high.astype(F32) - low.astype(F32)).astype(BF16)
        cum_x[...] = (
            mm(high, heads_ref[...]) + mm(low, heads_ref[...]) + mm(lowest, heads_ref[...])
        )
        half = lax.broadcasted_iota(jnp.int32, (CHUNK, 128), 1) < 64
        head = (j - 1) * (TILE // 64)
        skip = skip_ref[...]
        for n in range(seqs):
            state_grad[...] = later[n, :, at]
            for c in range(chunks - 1, -1, -1):
                ck = n * chunks + c
                here = slice(ck * CHUNK, (ck + 1) * CHUNK)
                cum_here = cum_x[here]
                final_cum = cum_here[CHUNK - 1 :]
                enter_x = jnp.exp(cum_here) * masks_ref[here, 4:5]
                tail_x = jnp.exp(final_cum - cum_here) * masks_ref[here, 5:6]
                kept = jnp.exp(final_cum) * masks_ref[(ck + 1) * CHUNK - 1 : (ck + 1) * CHUNK, 4:5]
                signal = active[here]
                grad = ssm_grad_ref[here]
                moved = (signal * step_x[here]).astype(BF16)
                grad_low = grad.astype(BF16)
                later_low = state_grad[...].astype(BF16)
                from_later = mm(writer_low[here], later_low) * tail_x
                parts = []
                score = scores[ck]
                bias = biases[ck]
                grad_of_scores = scores_grad[ck]
                for pair in range(TILE // 128):
                    col = slice(pair * 128, (pair + 1) * 128)
                    ones = []
                    for i in range(2):
                        lane_at = pair * 128 + i * 64
                        ones.append(
                            jnp.exp(
                                cum_here[:, lane_at : lane_at + 1]
                                - cum_turned[ck, pl.ds(head + 2 * pair + i, 1), :]
                                + bias
                            )
                        )
                    zero = jnp.zeros((CHUNK, 128), BF16)
                    stacked = jnp.concatenate(
                        [
                            jnp.where(half, grad_low[:, col], zero),
                            jnp.where(half, zero, grad_low[:, col]),
                        ],
                        axis=0,
                    )
                    both_grad = mm_nt(stacked, moved[:, col])
                    grad_of_scores = (
                        grad_of_scores + both_grad[:CHUNK] * ones[0] + both_grad[CHUNK:] * ones[1]
                    )
                    both = jnp.concatenate([(score * one).astype(BF16) for one in ones], axis=0)
                    parts.append(mm_tn(both, stacked))
                scores_grad[ck] = grad_of_scores
                moved_grad = jnp.concatenate(parts, axis=1) + from_later
                wide_moved = moved.astype(F32)
                weighted = (wide_moved * tail_x).astype(BF16)
                entered = (grad * enter_x).astype(BF16)
                start = starts_ref[ck]
                reader_grad[here] += mm_nt(entered, start)
                writer_grad[here] += mm_nt(weighted, later_low)
                passed = jnp.sum(
                    start.astype(F32) * later_low.astype(F32), axis=0, keepdims=True
                )
                ends[ck : ck + 1] = kept * passed + jnp.sum(
                    wide_moved * from_later, axis=0, keepdims=True
                )
                state_grad[...] = state_grad[...] * kept + mm(reader_turned[ck], entered)
                step_sum[here] += gather_heads(moved_grad * signal, heads_ref)
                move_sum[here] += gather_heads(moved_grad * wide_moved, heads_ref)
                total[here] = moved_grad * step_x[here] + skip * grad
        end_sum[...] += gather_heads(ends[...], heads_ref)
        conv_back(j - 1, at)
        for step in sorted(agenda):

            @pl.when(j == step)
            def _(step=step):
                for act in agenda[step]:
                    act()

    @pl.when(j == final_step)
    def _():
        before = slice((steps - 1) * TILE, steps * TILE)
        fix_rim(steps - 1, before)
        weight_tiles((steps - 1) * (TILE // LANES), before)
        pending = []
        for f in range(flows_b):
            if last_b[f] == steps and b_taken[f] is None:
                b.rs_begin(f)
                b_taken[f] = 0
        at = slice(inner, channels)
        lane = lax.broadcasted_iota(jnp.int32, (CHUNK, 128), 1)
        row = lax.broadcasted_iota(jnp.int32, (CHUNK, 128), 0)
        upper = triangle(CHUNK, True)
        decay_rate = -jnp.exp(a_log_ref[...])
        raw_sum = jnp.zeros((1, 128), F32)
        decay_sum = jnp.zeros((1, 128), F32)
        values = summed_rw_ref[...]
        turned = sigmoid(values)
        bent[...] = turned * (1.0 + values * (1.0 - turned))
        for ck in range(chunk_count):
            here = slice(ck * CHUNK, (ck + 1) * CHUNK)
            high, low = split(scores_grad[ck])
            total[here, 128:] = (
                reader_grad[here] + mm(high, writer_low[here]) + mm(low, writer_low[here])
            )
            total[here, :128] = (
                writer_grad[here] + mm_tn(high, reader_low[here]) + mm_tn(low, reader_low[here])
            )
            raw = raw_ref[here]
            taken_steps = jnp.where(lane < heads, softplus(raw), 0.0)
            change = dot_ref[here] - move_sum[here]
            change = change + jnp.where(row == CHUNK - 1, end_sum[ck : ck + 1], 0.0)
            decay_grad = exact_mm(upper, change)
            raw_grad = jnp.where(
                lane < heads, (step_sum[here] + decay_grad * decay_rate) * sigmoid(raw), 0.0
            )
            raw_sum = raw_sum + jnp.sum(raw_grad, axis=0, keepdims=True)
            decay_sum = decay_sum + jnp.sum(
                decay_grad * taken_steps * decay_rate, axis=0, keepdims=True
            )
            proj_grad[here, channels : channels + 128] = raw_grad.astype(BF16)
            proj_grad[here, channels + 128 :] = jnp.zeros((CHUNK, 128), BF16)
        head_sums[0:1] = raw_sum
        head_sums[1:2] = decay_sum
        conv_back(steps, at)
        fix_rim(steps, at)
        for tile in range(inner // LANES, flows_b * per_flow, 2):
            if tile * LANES < channels + 256:
                weight_tiles(tile, slice(tile * LANES, (tile + 2) * LANES))
            else:
                for i in range(2):
                    store(b, tile + i, jnp.zeros((pieces * split_rows * rows, LANES), BF16))
        for f in range(flows_b):
            if b_taken[f] is None:
                b.rs_begin(f)
                b_taken[f] = 0

        rest = weight_t_ref.shape[0] - inner
        weight_copy.wait()

        def input_rows(i, carry):
            rows_at = pl.ds(pl.multiple_of(i * 128, 128), 128)
            normed_grad = mm(gate_grad_ref[rows_at], weight_t_ref[:inner]) + mm(
                proj_grad[rows_at, :rest], weight_t_ref[inner:]
            )
            values = tokens_ref[rows_at].astype(F32)
            scale = lax.rsqrt(jnp.mean(values * values, axis=-1, keepdims=True) + EPS)
            gain_sums[0:1] += jnp.sum(normed_grad * values * scale, axis=0, keepdims=True)
            pushed = normed_grad * gain_ref[...]
            inside = jnp.mean(pushed * values, axis=-1, keepdims=True)
            input_grad_ref[rows_at] = (
                out_low_ref[rows_at].astype(F32)
                + scale * pushed
                - values * (scale * scale * scale * inside)
            ).astype(BF16)
            return carry

        def sm_copy(k):
            return remote(
                small_acc.at[k], small_in.at[k], sm_send.at[k], sm_recv.at[k], a.partner[k]
            )

        def sz_copy(k):
            return remote(
                small_acc.at[bits],
                small_parts.at[turn],
                sz_send.at[k],
                sz_recv.at[k],
                a.others[k],
            )

        def small_begin():
            model = gain_sums.shape[1]
            small_acc[0, 0:5] = conv_sums[0:5]
            small_acc[0, 5:7, :inner] = wide_ref[0:2]
            small_acc[0, 5:7, inner : inner + 128] = head_sums[0:2]
            small_acc[0, 5:8, inner + 128 :] = squares_ref[0:3]
            small_acc[0, 7:8, :model] = gain_sums[0:1]
            small_acc[0, 7:8, model : inner + 128] = jnp.zeros((1, inner + 128 - model), F32)
            sm_copy(0).start()

        def small_step(k):
            sm_copy(k).wait_recv()
            small_acc[k + 1] = small_acc[k] + small_in[k]
            if k + 1 < bits:
                sm_copy(k + 1).start()
            else:
                small_parts[turn] = small_acc[bits]
                for i in range(1, pieces):
                    sz_copy(i).start()

        def small_end():
            for i in range(1, pieces):
                sz_copy(i).wait_recv()
            whole = small_parts[0]
            for i in range(1, pieces):
                whole = whole + small_parts[i]
            small_out_ref[...] = whole

        lines = [a_actions[f][bits:] for f in range(flows_a)]
        lines += [b_actions[f][b_taken[f] :] for f in range(flows_b)]
        blocks_of_rows = tokens_ref.shape[0] // 128
        extra = [
            lambda: lax.fori_loop(0, blocks_of_rows // 2, input_rows, 0),
            lambda: lax.fori_loop(blocks_of_rows // 2, blocks_of_rows, input_rows, 0),
            small_begin,
        ]
        extra += [functools.partial(small_step, k) for k in range(bits)] + [small_end]
        while any(lines) or extra:
            if extra:
                extra.pop(0)()
            for line in lines[flows_a:] + lines[:flows_a]:
                if line:
                    line.pop(0)()
        b.tiles_sent()
        a.sent()
        b.sent()
        for k in range(bits):
            sm_copy(k).wait_send()
        for i in range(1, pieces):
            sz_copy(i).wait_send()

        @pl.when(turn > 0)
        def _():
            for slot in range(steps + 1):
                rim_copy(slot).wait_send()

        for f in range(flows_a):
            out_copy(a, out_a_ref, f).wait()
        for f in range(flows_b):
            out_copy(b, out_b_ref, f).wait()


def row_split(places, rows):
    return 2 if places > 2 and rows % 32 == 0 else 1


def tail(
    rate,
    tiled,
    summed_rw_source,
    whole,
    weights,
    momenta,
    wide,
    squares,
    sizes,
    places,
    pieces,
    flows,
    blocks=6,
):
    seqs, piece, inner, channels, heads = sizes
    summed, conv, halo, taps, ssm_grad, starts, heads_map, skip = tiled
    total_rows = summed.shape[0]
    own = whole[6]
    tokens, weight_t = whole[13], whole[12]
    model = tokens.shape[1]
    flows_a, flows_b = flows
    assert flows_b <= flows_a
    bits = places.bit_length() - 1
    assert places == 1 << bits and bits >= 1 and pieces >= 2
    share = model // pieces
    split_rows = row_split(places, share)
    rows = share // split_rows
    steps = inner // TILE
    small = (8, channels)
    shape = jax.ShapeDtypeStruct
    any_space = pl.BlockSpec(memory_space=pl.ANY)
    sem = dma_semaphores

    def constant(array):
        count = array.ndim
        return pl.BlockSpec(
            array.shape, lambda j: (0,) * count, pipeline_mode=pl.Buffered(1)
        )

    def columns(height, last):
        return pl.BlockSpec((height, TILE), lambda j: (0, jnp.clip(j - 1, 0, last)))

    gathered = lambda count: (count,) + (2,) * bits + (pieces + 1, rows, LANES)
    chunk_count = total_rows // CHUNK
    square = (chunk_count, CHUNK, CHUNK)
    per_tile = (total_rows, TILE)
    per_head = (total_rows, 128)
    constants = list(whole) + [weights, momenta, wide, squares]
    return pl.pallas_call(
        functools.partial(
            tail_kernel, sizes, (bits, pieces, flows_a, flows_b, split_rows, blocks)
        ),
        grid=(steps + 2,),
        in_specs=[
            pl.BlockSpec(memory_space=pltpu.SMEM),
            columns(total_rows, steps),
            columns(total_rows, steps),
            columns(halo.shape[0], steps),
            columns(4, steps),
            columns(total_rows, steps - 1),
            pl.BlockSpec(
                (chunk_count, 128, TILE), lambda j: (0, 0, jnp.clip(j - 1, 0, steps - 1))
            ),
            columns(128, steps - 1),
            columns(1, steps - 1),
            pl.BlockSpec((total_rows, TILE), lambda j: (0, steps), pipeline_mode=pl.Buffered(1)),
        ]
        + [any_space if array is weight_t else constant(array) for array in constants],
        out_specs=(
            pl.BlockSpec((total_rows, model), lambda j: (0, 0)),
            pl.BlockSpec(small, lambda j: (0, 0)),
            any_space,
            any_space,
        ),
        out_shape=(
            shape((total_rows, model), BF16),
            shape(small, F32),
            shape(gathered(flows_a), BF16),
            shape(gathered(flows_b), BF16),
        ),
        scratch_shapes=exchange_scratch(bits, pieces, flows_a, rows)
        + exchange_scratch(bits, pieces, flows_b, rows, 0)
        + [pltpu.VMEM((blocks, seqs, 128, inner // blocks), BF16)] * 2
        + sem(blocks)
        + [
            pltpu.VMEM((seqs, 128, inner), F32),
            pltpu.VMEM((model, total_rows), BF16),
            pltpu.VMEM((model, total_rows), BF16),
            pltpu.VMEM(per_head, BF16),
            pltpu.VMEM(per_head, BF16),
            pltpu.VMEM(square, BF16),
            pltpu.VMEM(square, F32),
            pltpu.VMEM(square, F32),
            pltpu.VMEM(square, F32),
            pltpu.VMEM(square, F32),
            pltpu.VMEM(per_head, F32),
            pltpu.VMEM(per_head, F32),
            pltpu.VMEM(per_tile, F32),
            pltpu.VMEM(per_tile, F32),
            pltpu.VMEM(per_tile, F32),
            pltpu.VMEM(per_tile, F32),
            pltpu.VMEM(per_tile, F32),
            pltpu.VMEM((128, TILE), F32),
            pltpu.VMEM((max(chunk_count, 8), TILE), F32),
            pltpu.VMEM(per_head, F32),
            pltpu.VMEM(per_head, F32),
            pltpu.VMEM((max(chunk_count, 8), 128), F32),
            pltpu.VMEM((piece + 16, TILE), F32),
            pltpu.VMEM((total_rows, channels + 256), BF16),
            pltpu.VMEM((seqs, 8, TILE), F32),
            pltpu.VMEM((steps + 1, seqs, 8, TILE), BF16),
            pltpu.VMEM((steps + 1, seqs, 8, TILE), BF16),
        ]
        + sem(steps + 1)
        + [
            pltpu.VMEM(small, F32),
            pltpu.VMEM((8, 128), F32),
            pltpu.VMEM((8, model), F32),
            pltpu.VMEM((bits + 1,) + small, F32),
            pltpu.VMEM((bits,) + small, F32),
            pltpu.VMEM((pieces,) + small, F32),
        ]
        + sem(bits)
        + sem(pieces)
        + [pltpu.VMEM(weight_t.shape, BF16), pltpu.SemaphoreType.DMA],
        compiler_params=pltpu.CompilerParams(
            collective_id=2, has_side_effects=True, vmem_limit_bytes=62 * 1024 * 1024
        ),
        name="tail",
    )(rate, *tiled, summed_rw_source, *constants)


def piece_kernel(
    counts, spot_ref, out_weight_ref, weight_ref, out_momentum_ref, momentum_ref, w_ref, m_ref, turned
):
    out_tiles, tile_of, split_rows = counts
    tile = tile_of(pl.program_id(0), spot_ref)
    rows = m_ref.shape[1]
    part = lax.rem(spot_ref[0], split_rows)
    first = (spot_ref[1] * split_rows + part) * rows
    start = jnp.minimum(lax.div(first, 128) * 128, out_weight_ref.shape[1] - 256)
    window = pl.ds(pl.multiple_of(start, 128), 256)
    mine = pl.ds(pl.multiple_of(first - start, 16), rows)
    half = pl.ds(pl.multiple_of(part * rows, 16), rows)

    @pl.when(tile < out_tiles)
    def _():
        turned[...] = jnp.transpose(out_weight_ref[:, window])
        w_ref[0] = turned[mine]
        m_ref[0] = out_momentum_ref[half]

    @pl.when(tile >= out_tiles)
    def _():
        turned[...] = jnp.transpose(weight_ref[:, window])
        w_ref[0] = turned[mine]
        m_ref[0] = momentum_ref[half]


def owned(spot, out_weight, weight_t, out_momentum_t, momentum, flows_a, flows_b, places):
    inner, model = out_weight.shape
    share, width = momentum.shape
    out_tiles, in_tiles = inner // LANES, -(-width // LANES)
    split_rows = row_split(places, share)
    rows, per_flow = share // split_rows, places // split_rows

    flows = flows_a + flows_b

    def tile_of(f, spot):
        early = jnp.minimum(f * per_flow + spot[0] // split_rows, 2 * out_tiles - 1)
        late = 2 * out_tiles + (f - flows_a) * per_flow + spot[0] // split_rows
        return jnp.where(f < flows_a, early, late)

    def out_at(f, spot):
        return jnp.clip(tile_of(f, spot), 0, out_tiles - 1)

    def in_at(f, spot):
        return jnp.clip(tile_of(f, spot) - out_tiles, 0, in_tiles - 1)

    piece = pl.BlockSpec((1, rows, LANES), lambda f, spot: (f, 0, 0))
    return pl.pallas_call(
        functools.partial(piece_kernel, (out_tiles, tile_of, split_rows)),
        grid_spec=pltpu.PrefetchScalarGridSpec(
            num_scalar_prefetch=1,
            grid=(flows,),
            in_specs=[
                pl.BlockSpec((LANES, model), lambda f, spot: (out_at(f, spot), 0)),
                pl.BlockSpec((LANES, model), lambda f, spot: (in_at(f, spot), 0)),
                pl.BlockSpec((share, LANES), lambda f, spot: (0, out_at(f, spot))),
                pl.BlockSpec((share, LANES), lambda f, spot: (0, in_at(f, spot))),
            ],
            out_specs=(piece, piece),
            scratch_shapes=[pltpu.VMEM((256, LANES), BF16)],
        ),
        out_shape=(
            jax.ShapeDtypeStruct((flows, rows, LANES), BF16),
            jax.ShapeDtypeStruct((flows, rows, LANES), F32),
        ),
        name="owned",
    )(spot, out_weight, weight_t, out_momentum_t, momentum)


def finish_kernel(
    out_steps,
    split_rows,
    gathered_a_ref,
    gathered_b_ref,
    out_momentum_ref,
    momentum_ref,
    totals_ref,
    out_weight_ref,
    weight_ref,
    new_out_momentum_ref,
    new_momentum_ref,
    conv_weight_ref,
    conv_bias_ref,
    gate_gain_ref,
    norm_gain_ref,
    skip_ref,
    dt_bias_ref,
    a_log_ref,
    output_rms_ref,
    mixer_rms_ref,
    joined,
):
    group, slots, rows, _ = gathered_a_ref.shape
    step = pl.program_id(0)

    @pl.when(step == 0)
    def _():
        heads, inner, model = skip_ref.shape[0], gate_gain_ref.shape[0], norm_gain_ref.shape[0]
        side = inner + 128
        conv_weight_ref[...] = totals_ref[0:4]
        conv_bias_ref[...] = totals_ref[4]
        gate_gain_ref[...] = totals_ref[5, :inner]
        norm_gain_ref[...] = totals_ref[7, :model]
        skip_ref[...] = totals_ref[6, :heads]
        dt_bias_ref[...] = totals_ref[5, inner : inner + heads]
        a_log_ref[...] = totals_ref[6, inner : inner + heads]
        count = jnp.maximum(totals_ref[7:8, side + 9 : side + 10], 1.0) * model
        squares = jnp.sum(totals_ref[5:7, side:], axis=1, keepdims=True)
        output_rms_ref[...] = jnp.sqrt(squares[0:1] / count)
        mixer_rms_ref[...] = jnp.sqrt(squares[1:2] / count)

    def write(gathered_ref, weights, old, new):
        for i in range(group // split_rows):
            at = slice(i * LANES, (i + 1) * LANES)
            for part in range(split_rows):
                for p in range(slots - 1):
                    to = (p * split_rows + part) * rows
                    joined[to : to + rows] = gathered_ref[i * split_rows + part, p]
                own = slice(part * rows, (part + 1) * rows)
                summed = gathered_ref[i * split_rows + part, slots - 1].astype(F32)
                new[own, at] = 0.5 * old[own, at] + summed
            weights[at] = jnp.transpose(joined[...])

    @pl.when(step < out_steps)
    def _():
        write(gathered_a_ref, out_weight_ref, out_momentum_ref, new_out_momentum_ref)

    @pl.when((step >= out_steps) & (step < 2 * out_steps))
    def _():
        write(gathered_a_ref, weight_ref, momentum_ref, new_momentum_ref)

    @pl.when(step >= 2 * out_steps)
    def _():
        write(gathered_b_ref, weight_ref, momentum_ref, new_momentum_ref)


def finish(gathered_a, gathered_b, out_momentum_t, momentum, totals, heads, split_rows, group=4):
    _, slots, rows, _ = gathered_a.shape
    share, width = momentum.shape
    inner = out_momentum_t.shape[1]
    model = (slots - 1) * share
    wide = group * LANES
    group = group * split_rows
    out_steps, in_steps = inner // wide, -(-width // wide)
    out_at = lambda j: jnp.minimum(j, out_steps - 1)
    in_at = lambda j: jnp.maximum(j - out_steps, 0)
    by_column = [
        pl.BlockSpec((share, wide), lambda j: (0, out_at(j))),
        pl.BlockSpec((share, wide), lambda j: (0, in_at(j))),
    ]
    shape = jax.ShapeDtypeStruct
    smalls = [
        shape(size, F32)
        for size in (
            (4, totals.shape[1]),
            (totals.shape[1],),
            (inner,),
            (model,),
            (heads,),
            (heads,),
            (heads,),
            (1, 1),
            (1, 1),
        )
    ]
    return pl.pallas_call(
        functools.partial(finish_kernel, out_steps, split_rows),
        grid=(out_steps + in_steps,),
        in_specs=[
            pl.BlockSpec(
                (group, slots, rows, LANES), lambda j: (jnp.minimum(j, 2 * out_steps - 1), 0, 0, 0)
            ),
            pl.BlockSpec(
                (group, slots, rows, LANES), lambda j: (jnp.maximum(j - 2 * out_steps, 0), 0, 0, 0)
            ),
        ]
        + by_column
        + [pl.BlockSpec(totals.shape, lambda j: (0, 0))],
        out_specs=[
            pl.BlockSpec((wide, model), lambda j: (out_at(j), 0)),
            pl.BlockSpec((wide, model), lambda j: (in_at(j), 0)),
        ]
        + by_column
        + [
            pl.BlockSpec(small.shape, lambda j, count=len(small.shape): (0,) * count)
            for small in smalls
        ],
        out_shape=[
            shape((inner, model), BF16),
            shape((width, model), BF16),
            shape((share, inner), F32),
            shape((share, width), F32),
        ]
        + smalls,
        scratch_shapes=[pltpu.VMEM((model, LANES), BF16)],
        name="finish",
    )(gathered_a, gathered_b, out_momentum_t, momentum, totals)


def local(
    tokens,
    cotangent,
    segment_ids,
    doc_starts,
    valid_mask,
    step_number,
    learn_rate,
    norm_gain,
    in_weight,
    conv_weight,
    conv_bias,
    dt_bias,
    a_log,
    skip_d,
    gate_gain,
    out_weight,
    in_momentum,
    out_momentum,
):
    seqs, piece, model_width = tokens.shape
    heads = dt_bias.shape[0]
    tap_count, channels = conv_weight.shape
    inner_width = gate_gain.shape[0]
    proj_width = in_weight.shape[1]
    total = seqs * piece
    sizes = (seqs, piece, inner_width, channels, heads)
    places, pieces = lax.axis_size("dp"), lax.axis_size("seq")
    turn = lax.axis_index("seq")
    seg = segment_ids.astype(F32)
    sent = jnp.concatenate(
        [
            tokens[:, piece - HALO :],
            jnp.broadcast_to(seg[:, piece - HALO :, None], (seqs, HALO, LANES)).astype(BF16),
        ],
        axis=2,
    )
    route = [(i, i + 1) for i in range(pieces - 1)]
    arrived = lax.ppermute(sent, "seq", route)
    halo = arrived[:, :, :model_width].reshape(seqs * HALO, model_width)
    early_seg = jnp.where(turn == 0, -1.0, arrived[:, :, model_width].astype(F32))
    seg_pad = jnp.concatenate([early_seg, seg], axis=1)
    seg_row = seg.reshape(1, total)
    heads_map = (
        lax.broadcasted_iota(jnp.int32, (LANES, inner_width), 0)
        == lax.broadcasted_iota(jnp.int32, (LANES, inner_width), 1) // (inner_width // heads)
    ).astype(BF16)

    def lanes(values):
        return jnp.pad(values, (0, LANES - heads)).reshape(1, LANES)

    flat_tokens = tokens.reshape(total, model_width)
    weight_t = jnp.transpose(in_weight)
    out_momentum_t = jnp.transpose(out_momentum)
    flat_cot = cotangent.reshape(total, model_width)
    bias_row, decay_row = lanes(dt_bias), lanes(a_log)
    skip_row = jnp.repeat(skip_d, inner_width // heads).reshape(1, inner_width)
    gain_row = gate_gain.reshape(1, inner_width)
    normed, masks, gate, conv, conv_halo, summed, raw, cum, fresh, keep = front(
        flat_tokens,
        halo,
        norm_gain.reshape(1, model_width),
        weight_t,
        conv_weight,
        conv_bias.reshape(1, channels),
        seg_pad,
        valid_mask,
        bias_row,
        decay_row,
        heads_map,
        sizes,
    )
    incoming = chain(fresh, keep, 1)
    output, low, out_low, gate_grad, ssm_grad, starts, dots, squares, wide, state_grad = forward(
        summed,
        gate,
        raw,
        cum,
        masks,
        seg_row,
        incoming,
        flat_tokens,
        flat_cot,
        out_weight,
        gain_row,
        skip_row,
        heads_map,
        sizes,
    )
    step_float = step_number[0].astype(F32)
    rate = (learn_rate[0] * step_float / (step_float + 16.0)).reshape(1)
    share_rows = model_width // pieces
    split_rows = row_split(places, share_rows)
    per_flow = places // split_rows
    flows_a = -(-2 * inner_width // (LANES * per_flow))
    flows_b = -(-(channels + 2 * LANES) // (LANES * per_flow))
    spot = jnp.stack([lax.axis_index("dp"), turn]).astype(jnp.int32)
    weights, momenta = owned(
        spot, out_weight, weight_t, out_momentum_t, in_momentum, flows_a, flows_b, places
    )
    input_grad, totals, gathered_a, gathered_b = tail(
        rate,
        (summed, conv, conv_halo, conv_weight, ssm_grad, starts, heads_map, skip_row),
        summed,
        (
            raw,
            cum,
            masks,
            seg_row,
            dots,
            decay_row,
            state_grad,
            keep,
            out_low,
            normed,
            low,
            gate_grad,
            weight_t,
            flat_tokens,
            norm_gain.reshape(1, model_width),
        ),
        weights,
        momenta,
        wide,
        squares,
        sizes,
        places,
        pieces,
        (flows_a, flows_b),
    )
    share = (pieces + 1, share_rows // split_rows, LANES)
    (
        new_out_weight,
        new_weight_t,
        new_out_momentum_t,
        new_in_momentum,
        conv_weight_total,
        conv_bias_total,
        gate_gain_total,
        norm_gain_total,
        skip_total,
        dt_bias_total,
        a_log_total,
        output_rms,
        mixer_rms,
    ) = finish(
        gathered_a.reshape((-1,) + share),
        gathered_b.reshape((-1,) + share),
        out_momentum_t,
        in_momentum,
        totals,
        heads,
        split_rows,
    )
    new_in_weight = jnp.transpose(new_weight_t)
    new_out_momentum = jnp.transpose(new_out_momentum_t)
    output_rms, mixer_rms = output_rms.reshape(1), mixer_rms.reshape(1)
    return (
        output.reshape(tokens.shape),
        input_grad.reshape(tokens.shape),
        new_in_weight,
        new_out_weight,
        new_in_momentum,
        new_out_momentum,
        norm_gain_total,
        conv_weight_total,
        conv_bias_total,
        dt_bias_total,
        a_log_total,
        skip_total,
        gate_gain_total,
        output_rms,
        mixer_rms,
    )


def solution(mesh):
    placed = (
        P("dp", "seq", None),
        P("dp", "seq", None),
        P("dp", "seq"),
        P("dp", "seq"),
        P("dp", "seq"),
        P(),
        P(),
        P(),
        P(),
        P(),
        P(),
        P(),
        P(),
        P(),
        P(),
        P(),
        P("seq", None),
        P(None, "seq"),
    )
    return jax.shard_map(
        local,
        mesh=mesh,
        in_specs=placed,
        out_specs=(
            P("dp", "seq", None),
            P("dp", "seq", None),
            P(),
            P(),
            P("seq", None),
            P(None, "seq"),
            P(),
            P(),
            P(),
            P(),
            P(),
            P(),
            P(),
            P(),
            P(),
        ),
        check_vma=False,
    )
```

```python
import functools

import jax
import jax.numpy as jnp
from jax import lax
from jax.experimental import pallas as pl
from jax.experimental.pallas import tpu as pltpu
from jax.sharding import PartitionSpec as P

CHUNK = 128
HALO = 16
GATE_BLOCK = 256
EPS = 1e-05
NEGATIVE = -1e30
F32, BF16 = jnp.float32, jnp.bfloat16
LANES = 128
MESH = pl.DeviceIdType.MESH


def remote(src, dst, send, recv, target):
    return pltpu.make_async_remote_copy(
        src_ref=src,
        dst_ref=dst,
        send_sem=send,
        recv_sem=recv,
        device_id=target,
        device_id_type=MESH,
    )


def greet(targets):
    barrier = pltpu.get_barrier_semaphore()
    for target in targets:
        pl.semaphore_signal(barrier, inc=1, device_id=target, device_id_type=MESH)
    pl.semaphore_wait(barrier, len(targets))


def dma_semaphores(*shape):
    return [pltpu.SemaphoreType.DMA(shape)] * 2


def part_count(pieces):
    return 2 if pieces % 2 == 0 else 1


def half_shape(bits, pieces, flows, rows, k):
    return (flows,) + (2,) * (bits - k - 1) + (pieces, rows, LANES)


def mm(a, b):
    return jnp.dot(a, b, preferred_element_type=F32)


def mm_nt(a, b):
    return lax.dot_general(a, b, (((1,), (1,)), ((), ())), preferred_element_type=F32)


def mm_tn(a, b):
    return lax.dot_general(a, b, (((0,), (0,)), ((), ())), preferred_element_type=F32)


def split(a):
    high = a.astype(BF16)
    return high, (a - high.astype(F32)).astype(BF16)


def exact_mm(a, b):
    return jnp.dot(a, b, preferred_element_type=F32, precision=lax.Precision.HIGHEST)


def spread(a, heads_ref):
    high, low = split(a)
    return mm(high, heads_ref[...]) + mm(low, heads_ref[...])


def gather_heads(a, heads_ref):
    high, low = split(a)
    return mm_nt(high, heads_ref[...]) + mm_nt(low, heads_ref[...])


def sigmoid(v):
    return 1.0 / (1.0 + jnp.exp(-v))


def gate_of(v):
    return 0.5 + 0.5 * jnp.tanh(0.5 * v)


def softplus(v):
    return jnp.maximum(v, 0.0) + jnp.log1p(jnp.exp(-jnp.abs(v)))


def triangle(size, upper):
    row = lax.broadcasted_iota(jnp.int32, (size, size), 0)
    column = lax.broadcasted_iota(jnp.int32, (size, size), 1)
    return ((row <= column) if upper else (row >= column)).astype(F32)


def front_kernel(
    sizes,
    tokens_ref,
    halo_ref,
    gain_ref,
    weight_ref,
    taps_ref,
    bias_ref,
    seg_ref,
    valid_ref,
    dt_bias_ref,
    a_log_ref,
    heads_ref,
    normed_ref,
    masks_ref,
    gate_ref,
    conv_ref,
    halo_out_ref,
    summed_ref,
    raw_ref,
    cum_ref,
    state_ref,
    keep_ref,
    padded,
    product,
    active,
):
    seqs, piece, inner, channels, heads = sizes
    gate_blocks, conv_blocks = inner // GATE_BLOCK, channels // GATE_BLOCK
    step = pl.program_id(0)
    stride = piece + HALO

    @pl.when(step == 0)
    def _():
        gain = gain_ref[...]
        for n in range(seqs):
            padded_seg = seg_ref[n : n + 1]
            seg = padded_seg[:, HALO:]

            def over_chunks(at):
                return jnp.concatenate(
                    [
                        jnp.broadcast_to(
                            padded_seg[:, c * CHUNK + at : c * CHUNK + at + 1], (1, CHUNK)
                        )
                        for c in range(piece // CHUNK)
                    ],
                    axis=1,
                )

            others = [padded_seg[:, HALO - 3 + k : HALO - 3 + k + piece] for k in range(4)] + [
                over_chunks(HALO - 1),
                over_chunks(HALO + CHUNK - 1),
                jnp.broadcast_to(padded_seg[:, HALO - 1 : HALO], (1, piece)),
                jnp.broadcast_to(padded_seg[:, HALO + piece - 1 :], (1, piece)),
            ]
            lines = [(other == seg).astype(F32) for other in others] + [
                seg,
                valid_ref[n : n + 1].astype(F32),
            ]
            lines = lines + [jnp.zeros_like(seg)] * (16 - len(lines))
            masks_ref[pl.ds(n * piece, piece)] = jnp.transpose(jnp.concatenate(lines, axis=0))
            for source, start, to, count in (
                (halo_ref, n * HALO, n * stride, HALO),
                (tokens_ref, n * piece, n * stride + HALO, piece),
            ):

                def body(i, carry):
                    values = source[pl.ds(pl.multiple_of(start + i * 16, 16), 16)].astype(F32)
                    scale = lax.rsqrt(jnp.mean(values * values, axis=-1, keepdims=True) + EPS)
                    low = (values * scale * gain).astype(BF16)
                    padded[pl.ds(pl.multiple_of(to + i * 16, 16), 16)] = low
                    return carry

                lax.fori_loop(0, count // 16, body, 0)
            normed_ref[pl.ds(n * piece, piece)] = padded[pl.ds(n * stride + HALO, piece)]

    product[...] = mm_nt(padded[...], weight_ref[...])

    @pl.when(step < gate_blocks)
    def _():
        for n in range(seqs):
            gate_ref[pl.ds(n * piece, piece)] = product[pl.ds(n * stride + HALO, piece)]

    @pl.when((step >= gate_blocks) & (step < gate_blocks + conv_blocks))
    def _():
        at = pl.multiple_of((step - gate_blocks) * GATE_BLOCK, GATE_BLOCK)
        for n in range(seqs):
            conv_ref[pl.ds(n * piece, piece)] = product[pl.ds(n * stride + HALO, piece)]
            halo_out_ref[pl.ds(n * HALO, HALO)] = product[pl.ds(n * stride, HALO)]
            for i in range(piece // 64):
                rows = pl.ds(n * piece + i * 64, 64)
                total = jnp.broadcast_to(bias_ref[...], (64, GATE_BLOCK))
                for k in range(4):
                    source = product[pl.ds(n * stride + HALO - 3 + k + i * 64, 64)]
                    total = total + source * masks_ref[rows, k : k + 1] * taps_ref[k : k + 1]
                summed_ref[rows] = total
                active[rows, pl.ds(at, GATE_BLOCK)] = (total * gate_of(total)).astype(BF16)

    @pl.when(step == gate_blocks + conv_blocks)
    def _():
        lane = lax.broadcasted_iota(jnp.int32, (piece, 128), 1)
        lower = triangle(CHUNK, False)
        for n in range(seqs):
            rows = pl.ds(n * piece, piece)
            raw = jnp.where(lane < heads, product[pl.ds(n * stride + HALO, piece), :128], 0.0)
            raw = raw + dt_bias_ref[...]
            raw_ref[rows] = raw
            steps = jnp.where(lane < heads, softplus(raw), 0.0)
            decay = -jnp.exp(a_log_ref[...]) * steps
            total = jnp.zeros((1, 128), F32)
            pieces = []
            for c in range(piece // CHUNK):
                cumulative = exact_mm(lower, decay[c * CHUNK : (c + 1) * CHUNK])
                cum_ref[pl.ds(n * piece + c * CHUNK, CHUNK)] = cumulative
                pieces.append(cumulative + total)
                total = total + cumulative[CHUNK - 1 :]
            whole = jnp.concatenate(pieces, axis=0) if len(pieces) > 1 else pieces[0]
            tails = jnp.exp(total - whole) * steps * masks_ref[rows, 7:8]
            weighted = (spread(tails, heads_ref) * active[rows, :inner].astype(F32)).astype(BF16)
            state_ref[n] = mm_tn(active[rows, inner : inner + 128], weighted)
            last = masks_ref[n * piece + piece - 1 : n * piece + piece, 6:7]
            keep = jnp.exp(total) * last
            keep_ref[n] = spread(jnp.broadcast_to(keep, (8, 128)), heads_ref)


def front(tokens, halo, gain, weight, taps, bias, segs, valid, dt_bias, a_log, heads_map, sizes):
    seqs, piece, inner, channels, heads = sizes
    total, model = tokens.shape
    stride = seqs * (piece + HALO)
    gate_blocks, conv_blocks = inner // GATE_BLOCK, channels // GATE_BLOCK
    full = lambda *shape: pl.BlockSpec(shape, lambda j: (0,) * len(shape))

    def conv_at(j):
        return (0, jnp.clip(j - gate_blocks, 0, conv_blocks - 1))

    return pl.pallas_call(
        functools.partial(front_kernel, sizes),
        grid=(gate_blocks + conv_blocks + 1,),
        in_specs=[
            full(total, model),
            full(seqs * HALO, model),
            full(1, model),
            pl.BlockSpec((GATE_BLOCK, model), lambda j: (j, 0)),
            pl.BlockSpec((4, GATE_BLOCK), conv_at),
            pl.BlockSpec((1, GATE_BLOCK), conv_at),
            full(*segs.shape),
            full(*valid.shape),
            full(1, 128),
            full(1, 128),
            full(128, inner),
        ],
        out_specs=(
            full(total, model),
            full(total, 16),
            pl.BlockSpec((total, GATE_BLOCK), lambda j: (0, jnp.minimum(j, gate_blocks - 1))),
            pl.BlockSpec((total, GATE_BLOCK), conv_at),
            pl.BlockSpec((seqs * HALO, GATE_BLOCK), conv_at),
            pl.BlockSpec((total, GATE_BLOCK), conv_at),
            full(total, 128),
            full(total, 128),
            full(seqs, 128, inner),
            full(seqs, 8, inner),
        ),
        out_shape=(
            jax.ShapeDtypeStruct((total, model), BF16),
            jax.ShapeDtypeStruct((total, 16), F32),
            jax.ShapeDtypeStruct((total, inner), F32),
            jax.ShapeDtypeStruct((total, channels), F32),
            jax.ShapeDtypeStruct((seqs * HALO, channels), F32),
            jax.ShapeDtypeStruct((total, channels), F32),
            jax.ShapeDtypeStruct((total, 128), F32),
            jax.ShapeDtypeStruct((total, 128), F32),
            jax.ShapeDtypeStruct((seqs, 128, inner), F32),
            jax.ShapeDtypeStruct((seqs, 8, inner), F32),
        ),
        scratch_shapes=[
            pltpu.VMEM((stride, model), BF16),
            pltpu.VMEM((stride, GATE_BLOCK), F32),
            pltpu.VMEM((total, channels), BF16),
        ],
        compiler_params=pltpu.CompilerParams(vmem_limit_bytes=48 * 1024 * 1024),
        name="front",
    )(tokens, halo, gain, weight, taps, bias, segs, valid, dt_bias, a_log, heads_map)


def chain_kernel(ways, blocks, own_ref, keep_ref, out_ref, sent, taken, send, recv):
    size = lax.axis_size("seq")
    turn = lax.axis_index("seq")
    first = turn == (0 if ways > 0 else size - 1)
    final = turn == (size - 1 if ways > 0 else 0)
    ahead = {"seq": lax.rem(turn + ways + size, size)}
    behind = {"seq": lax.rem(turn - ways + size, size)}
    barrier = pltpu.get_barrier_semaphore()

    @pl.when(jnp.logical_not(first))
    def _():
        pl.semaphore_signal(
            barrier, inc=1, device_id=behind, device_id_type=pl.DeviceIdType.MESH
        )

    @pl.when(jnp.logical_not(final))
    def _():
        pl.semaphore_wait(barrier, 1)

    width = own_ref.shape[2] // blocks

    def copy(c):
        return pltpu.make_async_remote_copy(
            src_ref=sent.at[c],
            dst_ref=taken.at[c],
            send_sem=send.at[c],
            recv_sem=recv.at[c],
            device_id=ahead,
            device_id_type=pl.DeviceIdType.MESH,
        )

    @pl.when(first)
    def _():
        out_ref[...] = jnp.zeros_like(out_ref)
        for c in range(blocks):
            at = slice(c * width, (c + 1) * width)
            sent[c] = own_ref[:, :, at].astype(BF16)
            copy(c).start()

    @pl.when(jnp.logical_not(first))
    def _():
        for c in range(blocks):
            at = slice(c * width, (c + 1) * width)
            copy(c).wait_recv()

            @pl.when(jnp.logical_not(final))
            def _():
                sent[c] = (
                    own_ref[:, :, at] + keep_ref[:, 0:1, at] * taken[c].astype(F32)
                ).astype(BF16)
                copy(c).start()

            out_ref[:, :, at] = taken[c].astype(F32)

    @pl.when(jnp.logical_not(final))
    def _():
        for c in range(blocks):
            copy(c).wait_send()


def chain(own, keep, ways, blocks=6):
    seqs, depth, inner = own.shape
    vmem = pl.BlockSpec(memory_space=pltpu.VMEM)
    part = (blocks, seqs, depth, inner // blocks)
    return pl.pallas_call(
        functools.partial(chain_kernel, ways, blocks),
        out_shape=jax.ShapeDtypeStruct(own.shape, F32),
        in_specs=[vmem, vmem],
        out_specs=vmem,
        scratch_shapes=[pltpu.VMEM(part, BF16)] * 2 + [pltpu.SemaphoreType.DMA((blocks,))] * 2,
        compiler_params=pltpu.CompilerParams(
            collective_id=1 if ways > 0 else 2,
            has_side_effects=True,
            vmem_limit_bytes=32 * 1024 * 1024,
        ),
        name="chain",
    )(own, keep)


def decays_of(cum, cum_t, bias, h):
    return jnp.exp(cum[:, h : h + 1] - cum_t[h : h + 1, :] + bias)


def mask_bias(seg_col, seg_row):
    row = lax.broadcasted_iota(jnp.int32, (CHUNK, CHUNK), 0)
    column = lax.broadcasted_iota(jnp.int32, (CHUNK, CHUNK), 1)
    return jnp.where((row >= column) & (seg_col == seg_row), 0.0, NEGATIVE)


def scores_of(reader, writer):
    rh, rl = split(reader)
    wh, wl = split(writer)
    return mm_nt(rh, wh) + (mm_nt(rh, wl) + mm_nt(rl, wh))


def forward_kernel(
    sizes,
    chunks,
    summed_ref,
    gate_ref,
    raw_ref,
    cum_ref,
    masks_ref,
    seg_row_ref,
    incoming_ref,
    tokens_ref,
    cot_ref,
    weight_ref,
    gain_ref,
    skip_ref,
    heads_ref,
    output_ref,
    low_ref,
    out_low_ref,
    gate_grad_ref,
    ssm_grad_ref,
    starts_ref,
    dot_ref,
    sums_ref,
    wide_ref,
    state_grad_ref,
    state,
    prefix,
    active,
    mixed_in,
    factors,
    grads,
    inv,
    totals,
):
    seqs, piece, inner, channels, heads = sizes
    c = pl.program_id(1)

    @pl.when((c == 0) & (pl.program_id(0) == 0))
    def _():
        sums_ref[...] = jnp.zeros_like(sums_ref)
        wide_ref[...] = jnp.zeros_like(wide_ref)

    @pl.when(c == 0)
    def _():
        state[...] = incoming_ref[0]
        prefix[...] = jnp.zeros_like(prefix)
        state_grad_ref[...] = jnp.zeros_like(state_grad_ref)

    def activate(i, carry):
        rows = pl.ds(pl.multiple_of(i * 16, 16), 16)
        values = summed_ref[rows]
        active[rows] = values * gate_of(values)
        return carry

    lax.fori_loop(0, CHUNK // 16, activate, 0)
    lane = lax.broadcasted_iota(jnp.int32, (CHUNK, 128), 1)
    steps = jnp.where(lane < heads, softplus(raw_ref[...]), 0.0)
    cum = cum_ref[...]
    cum_t = jnp.transpose(cum)
    final = cum[CHUNK - 1 :]
    tails = jnp.exp(final - cum) * steps * masks_ref[:, 5:6]
    before = spread(jnp.exp(prefix[...]), heads_ref)[0:1]
    prefix[...] = prefix[...] + final
    for i, block in enumerate((steps, jnp.exp(cum), tails)):
        factors[i] = spread(block, heads_ref)
    factors[3] = factors[1] * before * masks_ref[:, 6:7]
    factors[1] = factors[1] * masks_ref[:, 4:5]
    writer = active[:, inner : inner + 128]
    reader = active[:, inner + 128 : inner + 256]
    scores = scores_of(reader, writer)
    bias = mask_bias(masks_ref[:, 8:9], seg_row_ref[0:1])
    half = lax.broadcasted_iota(jnp.int32, (CHUNK, 128), 1) < 64
    state_low = state[...].astype(BF16)
    starts_ref[0] = state_low
    reader_low = reader.astype(BF16)
    for pair in range(heads // 2):
        at = slice(pair * 128, (pair + 1) * 128)
        moved = (active[:, at] * factors[0, :, at]).astype(BF16)
        zero = jnp.zeros_like(moved)
        one = (scores * decays_of(cum, cum_t, bias, 2 * pair)).astype(BF16)
        two = (scores * decays_of(cum, cum_t, bias, 2 * pair + 1)).astype(BF16)
        both = jnp.concatenate([one, two], axis=1)
        stacked = jnp.concatenate(
            [jnp.where(half, moved, zero), jnp.where(half, zero, moved)], axis=0
        )
        carried = mm(reader_low, state_low[:, at]) * factors[1, :, at]
        mixed_in[:, at] = mm(both, stacked) + carried
    weighted = (active[:, :inner] * factors[2]).astype(BF16)
    kept = jnp.exp(final) * masks_ref[CHUNK - 1 :, 4:5]
    kept = spread(jnp.broadcast_to(kept, (8, 128)), heads_ref)[0:1]
    state[...] = state[...] * kept + mm_tn(writer.astype(BF16), weighted)

    gain = gain_ref[...]
    skip = skip_ref[...]

    column_blocks = [slice(at, at + 512) for at in range(0, inner, 512)]

    def gating(i, carry):
        rows = pl.ds(pl.multiple_of(i * 16, 16), 16)
        squares = jnp.zeros((16, 512), F32)
        for at in column_blocks:
            gate = gate_ref[rows, at]
            turned = gate_of(gate)
            mixer = mixed_in[rows, at] + skip[:, at] * active[rows, at]
            product = mixer * gate * turned
            factors[0, rows, at] = product
            factors[1, rows, at] = turned
            factors[2, rows, at] = mixer
            squares = squares + product * product
        mean = jnp.sum(squares, axis=-1, keepdims=True) / inner
        scale = lax.rsqrt(mean + EPS)
        inv[rows] = jnp.broadcast_to(scale, (16, 128))
        for at in column_blocks:
            low_ref[rows, at] = (factors[0, rows, at] * scale * gain[:, at]).astype(BF16)
        return carry

    lax.fori_loop(0, CHUNK // 16, gating, 0)
    mixed = mm(low_ref[...], weight_ref[...])
    block_out = tokens_ref[...].astype(F32) + mixed
    output_ref[...] = block_out.astype(BF16)
    valid = masks_ref[:, 9:10]
    for i, block in enumerate((block_out, mixed)):
        squares = jnp.sum(valid * block * block, axis=0, keepdims=True)
        for at in range(0, squares.shape[1], 128):
            sums_ref[i : i + 1] += squares[:, at : at + 128]
    sums_ref[2:3, :16] += jnp.sum(masks_ref[...], axis=0, keepdims=True)
    out_low = (cot_ref[...].astype(F32) * valid).astype(BF16)
    out_low_ref[...] = out_low
    grads[...] = mm_nt(out_low, weight_ref[...])

    @pl.when((c == 0) & (pl.program_id(0) == 0))
    def _():
        totals[...] = jnp.zeros_like(totals)

    def backing(i, carry):
        rows = pl.ds(pl.multiple_of(i * 16, 16), 16)
        scale = inv[rows, 0:1]
        inside = jnp.zeros((16, 512), F32)
        for at in column_blocks:
            grad = grads[rows, at]
            gated = factors[0, rows, at]
            totals[0, :, at] += grad * gated * scale
            inside = inside + grad * gain[:, at] * gated
        inside = jnp.sum(inside, axis=-1, keepdims=True) / inner
        inside = scale * scale * scale * inside
        for at in column_blocks:
            gate, turned = gate_ref[rows, at], factors[1, rows, at]
            gated_grad = scale * (grads[rows, at] * gain[:, at]) - factors[0, rows, at] * inside
            ssm_grad = gated_grad * (gate * turned)
            ssm_grad_ref[rows, at] = ssm_grad
            grads[rows, at] = ssm_grad
            totals[1, :, at] += ssm_grad * active[rows, at]
            gate_grad_ref[rows, at] = (
                gated_grad * factors[2, rows, at] * turned * (1.0 + gate * (1.0 - turned))
            ).astype(BF16)
        return carry

    lax.fori_loop(0, CHUNK // 16, backing, 0)

    @pl.when((c == chunks - 1) & (pl.program_id(0) == seqs - 1))
    def _():
        wide_ref[0:1] = jnp.sum(totals[0], axis=0, keepdims=True)
        skips = jnp.sum(totals[1], axis=0, keepdims=True)
        skips = gather_heads(jnp.broadcast_to(skips, (8, inner)), heads_ref)
        wide_ref[1:2, :128] = skips[0:1]

    reader_t = jnp.transpose(reader_low)
    for pair in range(heads // 2):
        at = slice(pair * 128, (pair + 1) * 128)
        state_grad_ref[0, :, at] += mm(
            reader_t, (grads[:, at] * factors[3, :, at]).astype(BF16)
        )
        mixed_in[:, at] = mixed_in[:, at] * grads[:, at].astype(BF16).astype(F32)
    dot_ref[...] = gather_heads(mixed_in[...], heads_ref)


def forward(
    summed, gate, raw, cum, masks, seg_row, incoming, tokens, cot, weight, gain, skip, heads_map, sizes
):
    seqs, piece, inner, channels, heads = sizes
    total, model = tokens.shape
    chunks = piece // CHUNK
    full = lambda *shape: pl.BlockSpec(shape, lambda n, c: (0,) * len(shape))
    rows = lambda width: pl.BlockSpec((CHUNK, width), lambda n, c: (n * chunks + c, 0))
    each = lambda depth: pl.BlockSpec((1, depth, inner), lambda n, c: (n, 0, 0))
    shape = jax.ShapeDtypeStruct
    return pl.pallas_call(
        functools.partial(forward_kernel, sizes, chunks),
        grid=(seqs, chunks),
        in_specs=[
            rows(channels),
            rows(inner),
            rows(128),
            rows(128),
            rows(16),
            pl.BlockSpec((1, CHUNK), lambda n, c: (0, n * chunks + c)),
            each(128),
            rows(model),
            rows(model),
            full(inner, model),
            full(1, inner),
            full(1, inner),
            full(128, inner),
        ],
        out_specs=(
            rows(model),
            rows(inner),
            rows(model),
            rows(inner),
            rows(inner),
            pl.BlockSpec((1, 128, inner), lambda n, c: (n * chunks + c, 0, 0)),
            rows(128),
            full(8, 128),
            full(8, inner),
            each(128),
        ),
        out_shape=(
            shape((total, model), BF16),
            shape((total, inner), BF16),
            shape((total, model), BF16),
            shape((total, inner), BF16),
            shape((total, inner), F32),
            shape((seqs * chunks, 128, inner), BF16),
            shape((total, 128), F32),
            shape((8, 128), F32),
            shape((8, inner), F32),
            shape((seqs, 128, inner), F32),
        ),
        scratch_shapes=[
            pltpu.VMEM((128, inner), F32),
            pltpu.VMEM((8, 128), F32),
            pltpu.VMEM((CHUNK, channels), F32),
            pltpu.VMEM((CHUNK, inner), F32),
            pltpu.VMEM((4, CHUNK, inner), F32),
            pltpu.VMEM((CHUNK, inner), F32),
            pltpu.VMEM((CHUNK, 128), F32),
            pltpu.VMEM((2, 16, inner), F32),
        ],
        compiler_params=pltpu.CompilerParams(vmem_limit_bytes=48 * 1024 * 1024),
        name="forward",
    )(summed, gate, raw, cum, masks, seg_row, incoming, tokens, cot, weight, gain, skip, heads_map)


TILE = 256


class Exchange:
    def __init__(self, bits, pieces, flows):
        self.bits, self.pieces, self.flows = bits, pieces, flows
        self.parts = part_count(pieces)
        self.place, self.turn = lax.axis_index("dp"), lax.axis_index("seq")
        self.own = [(self.place // (1 << b)) % 2 for b in range(bits)]
        self.partner = [
            {"dp": self.place + (1 - 2 * self.own[b]) * (1 << b)} for b in range(bits)
        ]
        self.others = [{"seq": lax.rem(self.turn + j, pieces)} for j in range(pieces)]
        self.mine = self.index_of({b: self.own[b] for b in range(bits)})

    def index_of(self, fixed):
        return tuple(fixed.get(b, slice(None)) for b in range(self.bits - 1, -1, -1))

    def spot_of(self, d):
        return tuple((d // (1 << b)) % 2 for b in range(self.bits - 1, -1, -1))

    def order_of(self, f, h):
        rest = list(range(1, self.bits))
        shift = (f + h) % max(len(rest), 1)
        return [0] + rest[shift:] + rest[:shift]

    def share(self, h, extra=0):
        half = self.pieces // self.parts
        return pl.ds(h * half, half + (extra if h == self.parts - 1 else 0))

    def held(self, f, h, k, other):
        order = self.order_of(f, h)
        bit = order[k]
        value = 1 - self.own[bit] if other else self.own[bit]
        free = [b for b in range(self.bits - 1, -1, -1) if b not in order[:k]]
        source = self.grad if k == 0 else self.halves[k - 1]
        return source.at[
            (f,) + tuple(value if b == bit else slice(None) for b in free) + (self.share(h),)
        ]

    def landing(self, f, h, k):
        free = self.bits - k - 1
        return self.halves[k].at[(f,) + (slice(None),) * free + (self.share(h),)]

    def rs_copy(self, f, h, k):
        return remote(
            self.held(f, h, k, True),
            self.landing(f, h, k),
            self.rs_send.at[f, h, k],
            self.rs_recv.at[f, h, k],
            self.partner[self.order_of(f, h)[k]],
        )

    def rs_begin(self, f):
        for h in range(self.parts):
            self.rs_copy(f, h, 0).start()

    def rs_end(self, f, k):
        for h in range(self.parts):
            self.rs_copy(f, h, k).wait_recv()
            kept, into = self.held(f, h, k, False), self.landing(f, h, k)
            left = self.bits - k - 1
            for count in range(1 << left):
                spot = tuple((count >> (left - 1 - i)) & 1 for i in range(left))

                def body(p, carry, spot=spot, kept=kept, into=into):
                    into[spot + (p,)] = (
                        kept[spot + (p,)].astype(F32) + into[spot + (p,)].astype(F32)
                    ).astype(BF16)
                    return carry

                lax.fori_loop(0, self.pieces // self.parts, body, 0)
            if k + 1 < self.bits:
                self.rs_copy(f, h, k + 1).start()
        if k + 1 == self.bits:
            for j in range(1, self.pieces):
                self.zs_copy(f, j).start()

    def zs_copy(self, f, j):
        return remote(
            self.halves[self.bits - 1].at[f, lax.rem(self.turn + j, self.pieces)],
            self.piece_parts.at[f, j],
            self.zs_send.at[f, j],
            self.zs_recv.at[f, j],
            self.others[j],
        )

    def zs_end(self, f, rate, weight, momentum):
        for j in range(1, self.pieces):
            self.zs_copy(f, j).wait_recv()
        total = self.halves[self.bits - 1][f, self.turn].astype(F32)
        for j in range(1, self.pieces):
            total = total + self.piece_parts[f, j].astype(F32)
        summed = total.astype(BF16)
        moved = 0.5 * momentum + summed.astype(F32)
        self.gathered[(f,) + self.mine + (self.pieces,)] = summed
        self.gathered[(f,) + self.mine + (self.turn,)] = (
            weight.astype(F32) - rate * moved
        ).astype(BF16)
        for j in range(1, self.pieces):
            self.zg_copy(f, j).start()

    def zg_copy(self, f, j):
        spot = self.gathered.at[(f,) + self.mine + (self.turn,)]
        return remote(spot, spot, self.zg_send.at[f, j], self.zg_recv.at[f, j], self.others[j])

    def zg_end(self, f):
        for j in range(1, self.pieces):
            self.zg_copy(f, j).wait_recv()
        for h in range(self.parts):
            self.ag_copy(f, h, self.bits - 1).start()

    def ag_copy(self, f, h, k):
        order = self.order_of(f, h)
        fixed = {order[i]: self.own[order[i]] for i in range(k + 1)}
        spot = self.gathered.at[(f,) + self.index_of(fixed) + (self.share(h, 1),)]
        return remote(
            spot,
            spot,
            self.ag_send.at[f, h, k],
            self.ag_recv.at[f, h, k],
            self.partner[order[k]],
        )

    def ag_end(self, f, k):
        for h in range(self.parts):
            self.ag_copy(f, h, k).wait_recv()
            if k > 0:
                self.ag_copy(f, h, k - 1).start()

    def tiles_sent(self):
        for f in range(self.flows):
            for h in range(self.parts):
                self.rs_copy(f, h, 0).wait_send()

    def sent(self):
        for f in range(self.flows):
            for h in range(self.parts):
                for k in range(self.bits):
                    if k > 0:
                        self.rs_copy(f, h, k).wait_send()
                    self.ag_copy(f, h, k).wait_send()
            for j in range(1, self.pieces):
                self.zs_copy(f, j).wait_send()
                self.zg_copy(f, j).wait_send()

    def actions(self, f, rate, weights, momenta, after):
        steps = [functools.partial(self.rs_end, f, k) for k in range(self.bits)]
        steps.append(lambda: self.zs_end(f, rate, weights[f], momenta[f]))
        steps.append(functools.partial(self.zg_end, f))
        steps += [functools.partial(self.ag_end, f, k) for k in range(self.bits - 1, 0, -1)]

        def finish():
            self.ag_end(f, 0)
            after(f)

        return steps + [finish]


def exchange_scratch(bits, pieces, flows, rows, first=-1):
    parts = part_count(pieces)
    return (
        [pltpu.VMEM(half_shape(bits, pieces, flows, rows, k), BF16) for k in range(first, bits)]
        + [
            pltpu.VMEM((flows, pieces, rows, LANES), BF16),
            pltpu.VMEM((flows,) + (2,) * bits + (pieces + 1, rows, LANES), BF16),
        ]
        + dma_semaphores(flows, parts, bits)
        + dma_semaphores(flows, pieces)
        + dma_semaphores(flows, pieces)
        + dma_semaphores(flows, parts, bits)
        + [pltpu.SemaphoreType.DMA((flows,))]
    )


def give(ex, scratch, grad=None):
    if grad is None:
        grad, scratch = scratch[0], scratch[1:]
    ex.grad, ex.halves = grad, scratch[: ex.bits]
    scratch = scratch[ex.bits :]
    (ex.piece_parts, ex.gathered, ex.rs_send, ex.rs_recv, ex.zs_send, ex.zs_recv) = scratch[:6]
    (ex.zg_send, ex.zg_recv, ex.ag_send, ex.ag_recv, ex.out_sem) = scratch[6:11]
    return scratch[11:]


def tail_kernel(sizes, dims, *refs):
    seqs, piece, inner, channels, heads = sizes
    bits, pieces, flows_a, flows_b, split_rows, blocks = dims
    (
        rate_ref,
        summed_ref,
        conv_ref,
        halo_ref,
        taps_ref,
        ssm_grad_ref,
        starts_ref,
        heads_ref,
        skip_ref,
        summed_rw_ref,
        raw_ref,
        cum_ref,
        masks_ref,
        seg_row_ref,
        dot_ref,
        a_log_ref,
        own_ref,
        keep_ref,
        out_low_ref,
        normed_ref,
        low_ref,
        gate_grad_ref,
        weight_t_hbm,
        tokens_ref,
        gain_ref,
        weight_ref,
        momentum_ref,
        wide_ref,
        squares_ref,
        input_grad_ref,
        small_out_ref,
        out_a_ref,
        out_b_ref,
    ) = refs[:33]
    scratch = refs[33:]
    a, b = Exchange(bits, pieces, flows_a), Exchange(bits, pieces, flows_b)
    scratch = give(a, scratch)
    scratch = give(b, scratch, a.grad)
    (
        sent,
        taken,
        chain_send,
        chain_recv,
        later,
        out_turned,
        normed_turned,
        writer_low,
        reader_low,
        reader_turned,
        scores,
        cum_turned,
        biases,
        scores_grad,
        reader_grad,
        writer_grad,
        active,
        bent,
        step_x,
        cum_x,
        total,
        state_grad,
        ends,
        step_sum,
        move_sum,
        end_sum,
        shifted_rows,
        proj_grad,
        tails,
        rims,
        rims_in,
        rim_send,
        rim_recv,
        conv_sums,
        head_sums,
        gain_sums,
        small_acc,
        small_in,
        small_parts,
        sm_send,
        sm_recv,
        sz_send,
        sz_recv,
        weight_t_ref,
        weight_sem,
    ) = scratch
    weight_copy = pltpu.make_async_copy(weight_t_hbm, weight_t_ref, weight_sem)
    j = pl.program_id(0)
    steps = inner // TILE
    final_step = steps + 1
    places = 1 << bits
    per_flow = places // split_rows
    turn = a.turn
    chunk_count = seqs * piece // CHUNK
    rows = a.grad.shape[-2]
    chunks = piece // CHUNK
    rate = rate_ref[0]
    real = 2 * inner // LANES

    def out_copy(ex, out, f):
        return pltpu.make_async_copy(ex.gathered.at[f], out.at[f], ex.out_sem.at[f])

    a_actions = [
        a.actions(f, rate, weight_ref, momentum_ref, lambda f: out_copy(a, out_a_ref, f).start())
        for f in range(flows_a)
    ]
    late = [weight_ref.at[pl.ds(flows_a, flows_b)], momentum_ref.at[pl.ds(flows_a, flows_b)]]
    b_actions = [
        b.actions(f, rate, *late, lambda f: out_copy(b, out_b_ref, f).start())
        for f in range(flows_b)
    ]

    def store(ex, tile, values):
        for part in range(split_rows):
            d = (tile % per_flow) * split_rows + part
            spot = (tile // per_flow,) + ex.spot_of(d)
            for p in range(pieces):
                at = (p * split_rows + part) * rows
                ex.grad[spot + (p,)] = values[at : at + rows]

    def rim_copy(slot):
        return remote(
            rims.at[slot],
            rims_in.at[slot],
            rim_send.at[slot],
            rim_recv.at[slot],
            {"seq": lax.rem(turn + pieces - 1, pieces)},
        )

    def fix_rim(slot, at):
        @pl.when(turn < pieces - 1)
        def _():
            rim_copy(slot).wait_recv()
            for n in range(seqs):
                proj_grad[(n + 1) * piece - 8 : (n + 1) * piece, at] = (
                    tails[n] + rims_in[slot, n].astype(F32)
                ).astype(BF16)

    def conv_back(slot, at):
        for n in range(seqs):
            here_rows = pl.ds(n * piece, piece)
            grad = total[here_rows] * bent[here_rows]
            conv = conv_ref[here_rows]
            sums = [None] * 5
            sums[4] = jnp.sum(grad, axis=0, keepdims=True)
            sums[3] = jnp.sum(grad * conv, axis=0, keepdims=True)
            result = grad * taps_ref[3:4]
            rim = jnp.zeros((8, TILE), F32)
            shifted_rows[0:8] = jnp.zeros((8, TILE), F32)
            shifted_rows[8 + piece :] = jnp.zeros((8, TILE), F32)
            for k in range(3):
                shifted_rows[8 : 8 + piece] = grad * masks_ref[here_rows, k : k + 1]
                here = shifted_rows[11 - k : 11 - k + piece]
                result = result + here * taps_ref[k : k + 1]
                early = shifted_rows[3 - k : 11 - k]
                rim = rim + early * taps_ref[k : k + 1]
                sums[k] = jnp.sum(here * conv, axis=0, keepdims=True) + jnp.sum(
                    early * halo_ref[(n + 1) * HALO - 8 : (n + 1) * HALO], axis=0, keepdims=True
                )
            for i in range(5):
                if n == 0:
                    conv_sums[i : i + 1, at] = sums[i]
                else:
                    conv_sums[i : i + 1, at] += sums[i]
            proj_grad[here_rows, at] = result.astype(BF16)
            tails[n] = result[piece - 8 :]
            rims[slot, n] = rim.astype(BF16)

        @pl.when(turn > 0)
        def _():
            rim_copy(slot).start()

    @pl.when(j == 0)
    def _():
        greet(a.partner + a.others[1:])
        first, final = turn == pieces - 1, turn == 0
        width = inner // blocks

        def copy(c):
            ahead = {"seq": lax.rem(turn + pieces - 1, pieces)}
            return remote(sent.at[c], taken.at[c], chain_send.at[c], chain_recv.at[c], ahead)

        @pl.when(first)
        def _():
            later[...] = jnp.zeros_like(later)
            for c in range(blocks):
                sent[c] = own_ref[:, :, c * width : (c + 1) * width].astype(BF16)
                copy(c).start()

        weight_copy.start()
        out_turned[...] = jnp.transpose(out_low_ref[...])
        normed_turned[...] = jnp.transpose(normed_ref[...])
        low_tiles = inner // LANES

        def tiles(tile):
            if tile >= real:
                result = jnp.zeros((out_turned.shape[0], 2 * LANES), BF16)
            elif tile < low_tiles:
                at = tile * LANES
                result = mm(out_turned[...], low_ref[:, at : at + 2 * LANES]).astype(BF16)
            else:
                at = (tile - low_tiles) * LANES
                result = mm(normed_turned[...], gate_grad_ref[:, at : at + 2 * LANES])
                result = result.astype(BF16)
            store(a, tile, result[:, :LANES])
            store(a, tile + 1, result[:, LANES:])

        pairs = flows_a * per_flow // 2
        done = 0
        for c in range(blocks):
            until = pairs * (c + 1) // blocks
            for pair in range(done, until):
                tiles(2 * pair)
                if (2 * pair + 2) % per_flow == 0:
                    a.rs_begin(2 * pair // per_flow)
            done = until

            @pl.when(jnp.logical_not(first))
            def _():
                at = slice(c * width, (c + 1) * width)
                copy(c).wait_recv()

                @pl.when(jnp.logical_not(final))
                def _():
                    sent[c] = (
                        own_ref[:, :, at] + keep_ref[:, 0:1, at] * taken[c].astype(F32)
                    ).astype(BF16)
                    copy(c).start()

                later[:, :, at] = taken[c].astype(F32)

        for f in range(flows_a):
            a_actions[f][0]()
        a.tiles_sent()
        for ck in range(chunk_count):
            at = slice(ck * CHUNK, (ck + 1) * CHUNK)
            values = summed_rw_ref[at]
            values = values * sigmoid(values)
            writer, reader = values[:, :128], values[:, 128:]
            scores[ck] = scores_of(reader, writer)
            writer_low[at] = writer.astype(BF16)
            reader_low[at] = reader.astype(BF16)
            reader_turned[ck] = jnp.transpose(reader.astype(BF16))
            cum_turned[ck] = jnp.transpose(cum_ref[at])
            biases[ck] = mask_bias(masks_ref[at, 8:9], seg_row_ref[0:1, at])
        for ref in (
            scores_grad,
            reader_grad,
            writer_grad,
            step_sum,
            move_sum,
            end_sum,
            ends,
            gain_sums,
        ):
            ref[...] = jnp.zeros_like(ref)

        @pl.when(jnp.logical_not(final))
        def _():
            for c in range(blocks):
                copy(c).wait_send()

    agenda = {}

    def plan(step, act):
        agenda.setdefault(min(max(step, 1), steps), []).append(act)

    last_b = [((f + 1) * per_flow * LANES - 1) // TILE + 1 for f in range(flows_b)]
    a_steps = {1: 3, 2: 4} if bits == 3 else {k: 1 + k for k in range(1, bits)}
    a_done = b_ready = None
    for k in range(1, bits):
        for f in range(flows_a):
            plan(a_steps[k], a_actions[f][k])
    b_taken = []
    for f in range(flows_b):
        taken_steps = 0
        if last_b[f] + 1 <= steps:
            plan(last_b[f] + 1, functools.partial(b.rs_begin, f))
            for i in range(bits):
                if last_b[f] + 2 + i <= steps:
                    plan(last_b[f] + 2 + i, b_actions[f][i])
                    taken_steps = i + 1
            b_taken.append(taken_steps)
        else:
            b_taken.append(None)

    def weight_tiles(tile, at):
        result = mm(normed_turned[...], proj_grad[:, at]).astype(BF16)
        store(b, tile, result[:, :LANES])
        store(b, tile + 1, result[:, LANES:])

    @pl.when((j > 0) & (j < final_step))
    def _():
        at = pl.ds(pl.multiple_of((j - 1) * TILE, TILE), TILE)

        @pl.when(j > 1)
        def _():
            before = pl.ds(pl.multiple_of((j - 2) * TILE, TILE), TILE)
            fix_rim(j - 2, before)
            weight_tiles((j - 2) * (TILE // LANES), before)

        def activate(i, carry):
            rows_at = pl.ds(pl.multiple_of(i * 32, 32), 32)
            values = summed_ref[rows_at]
            turned = gate_of(values)
            active[rows_at] = values * turned
            bent[rows_at] = turned * (1.0 + values * (1.0 - turned))
            return carry

        lax.fori_loop(0, seqs * piece // 32, activate, 0)
        raw = raw_ref[...]
        lane = lax.broadcasted_iota(jnp.int32, raw.shape, 1)
        step_x[...] = spread(jnp.where(lane < heads, softplus(raw), 0.0), heads_ref)
        cum = cum_ref[...]
        high, low = split(cum)
        lowest = (cum - high.astype(F32) - low.astype(F32)).astype(BF16)
        cum_x[...] = (
            mm(high, heads_ref[...]) + mm(low, heads_ref[...]) + mm(lowest, heads_ref[...])
        )
        half = lax.broadcasted_iota(jnp.int32, (CHUNK, 128), 1) < 64
        head = (j - 1) * (TILE // 64)
        skip = skip_ref[...]
        for n in range(seqs):
            state_grad[...] = later[n, :, at]
            for c in range(chunks - 1, -1, -1):
                ck = n * chunks + c
                here = slice(ck * CHUNK, (ck + 1) * CHUNK)
                cum_here = cum_x[here]
                final_cum = cum_here[CHUNK - 1 :]
                enter_x = jnp.exp(cum_here) * masks_ref[here, 4:5]
                tail_x = jnp.exp(final_cum - cum_here) * masks_ref[here, 5:6]
                kept = jnp.exp(final_cum) * masks_ref[(ck + 1) * CHUNK - 1 : (ck + 1) * CHUNK, 4:5]
                signal = active[here]
                grad = ssm_grad_ref[here]
                moved = (signal * step_x[here]).astype(BF16)
                grad_low = grad.astype(BF16)
                later_low = state_grad[...].astype(BF16)
                from_later = mm(writer_low[here], later_low) * tail_x
                parts = []
                score = scores[ck]
                bias = biases[ck]
                grad_of_scores = scores_grad[ck]
                for pair in range(TILE // 128):
                    col = slice(pair * 128, (pair + 1) * 128)
                    ones = []
                    for i in range(2):
                        lane_at = pair * 128 + i * 64
                        ones.append(
                            jnp.exp(
                                cum_here[:, lane_at : lane_at + 1]
                                - cum_turned[ck, pl.ds(head + 2 * pair + i, 1), :]
                                + bias
                            )
                        )
                    zero = jnp.zeros((CHUNK, 128), BF16)
                    stacked = jnp.concatenate(
                        [
                            jnp.where(half, grad_low[:, col], zero),
                            jnp.where(half, zero, grad_low[:, col]),
                        ],
                        axis=0,
                    )
                    both_grad = mm_nt(stacked, moved[:, col])
                    grad_of_scores = (
                        grad_of_scores + both_grad[:CHUNK] * ones[0] + both_grad[CHUNK:] * ones[1]
                    )
                    both = jnp.concatenate([(score * one).astype(BF16) for one in ones], axis=0)
                    parts.append(mm_tn(both, stacked))
                scores_grad[ck] = grad_of_scores
                moved_grad = jnp.concatenate(parts, axis=1) + from_later
                wide_moved = moved.astype(F32)
                weighted = (wide_moved * tail_x).astype(BF16)
                entered = (grad * enter_x).astype(BF16)
                start = starts_ref[ck]
                reader_grad[here] += mm_nt(entered, start)
                writer_grad[here] += mm_nt(weighted, later_low)
                passed = jnp.sum(
                    start.astype(F32) * later_low.astype(F32), axis=0, keepdims=True
                )
                ends[ck : ck + 1] = kept * passed + jnp.sum(
                    wide_moved * from_later, axis=0, keepdims=True
                )
                state_grad[...] = state_grad[...] * kept + mm(reader_turned[ck], entered)
                step_sum[here] += gather_heads(moved_grad * signal, heads_ref)
                move_sum[here] += gather_heads(moved_grad * wide_moved, heads_ref)
                total[here] = moved_grad * step_x[here] + skip * grad
        end_sum[...] += gather_heads(ends[...], heads_ref)
        conv_back(j - 1, at)
        for step in sorted(agenda):

            @pl.when(j == step)
            def _(step=step):
                for act in agenda[step]:
                    act()

    @pl.when(j == final_step)
    def _():
        before = slice((steps - 1) * TILE, steps * TILE)
        fix_rim(steps - 1, before)
        weight_tiles((steps - 1) * (TILE // LANES), before)
        pending = []
        for f in range(flows_b):
            if last_b[f] == steps and b_taken[f] is None:
                b.rs_begin(f)
                b_taken[f] = 0
        at = slice(inner, channels)
        lane = lax.broadcasted_iota(jnp.int32, (CHUNK, 128), 1)
        row = lax.broadcasted_iota(jnp.int32, (CHUNK, 128), 0)
        upper = triangle(CHUNK, True)
        decay_rate = -jnp.exp(a_log_ref[...])
        raw_sum = jnp.zeros((1, 128), F32)
        decay_sum = jnp.zeros((1, 128), F32)
        values = summed_rw_ref[...]
        turned = sigmoid(values)
        bent[...] = turned * (1.0 + values * (1.0 - turned))
        for ck in range(chunk_count):
            here = slice(ck * CHUNK, (ck + 1) * CHUNK)
            high, low = split(scores_grad[ck])
            total[here, 128:] = (
                reader_grad[here] + mm(high, writer_low[here]) + mm(low, writer_low[here])
            )
            total[here, :128] = (
                writer_grad[here] + mm_tn(high, reader_low[here]) + mm_tn(low, reader_low[here])
            )
            raw = raw_ref[here]
            taken_steps = jnp.where(lane < heads, softplus(raw), 0.0)
            change = dot_ref[here] - move_sum[here]
            change = change + jnp.where(row == CHUNK - 1, end_sum[ck : ck + 1], 0.0)
            decay_grad = exact_mm(upper, change)
            raw_grad = jnp.where(
                lane < heads, (step_sum[here] + decay_grad * decay_rate) * sigmoid(raw), 0.0
            )
            raw_sum = raw_sum + jnp.sum(raw_grad, axis=0, keepdims=True)
            decay_sum = decay_sum + jnp.sum(
                decay_grad * taken_steps * decay_rate, axis=0, keepdims=True
            )
            proj_grad[here, channels : channels + 128] = raw_grad.astype(BF16)
            proj_grad[here, channels + 128 :] = jnp.zeros((CHUNK, 128), BF16)
        head_sums[0:1] = raw_sum
        head_sums[1:2] = decay_sum
        conv_back(steps, at)
        fix_rim(steps, at)
        for tile in range(inner // LANES, flows_b * per_flow, 2):
            if tile * LANES < channels + 256:
                weight_tiles(tile, slice(tile * LANES, (tile + 2) * LANES))
            else:
                for i in range(2):
                    store(b, tile + i, jnp.zeros((pieces * split_rows * rows, LANES), BF16))
        for f in range(flows_b):
            if b_taken[f] is None:
                b.rs_begin(f)
                b_taken[f] = 0

        rest = weight_t_ref.shape[0] - inner
        weight_copy.wait()

        def input_rows(i, carry):
            rows_at = pl.ds(pl.multiple_of(i * 128, 128), 128)
            normed_grad = mm(gate_grad_ref[rows_at], weight_t_ref[:inner]) + mm(
                proj_grad[rows_at, :rest], weight_t_ref[inner:]
            )
            values = tokens_ref[rows_at].astype(F32)
            scale = lax.rsqrt(jnp.mean(values * values, axis=-1, keepdims=True) + EPS)
            gain_sums[0:1] += jnp.sum(normed_grad * values * scale, axis=0, keepdims=True)
            pushed = normed_grad * gain_ref[...]
            inside = jnp.mean(pushed * values, axis=-1, keepdims=True)
            input_grad_ref[rows_at] = (
                out_low_ref[rows_at].astype(F32)
                + scale * pushed
                - values * (scale * scale * scale * inside)
            ).astype(BF16)
            return carry

        def sm_copy(k):
            return remote(
                small_acc.at[k], small_in.at[k], sm_send.at[k], sm_recv.at[k], a.partner[k]
            )

        def sz_copy(k):
            return remote(
                small_acc.at[bits],
                small_parts.at[turn],
                sz_send.at[k],
                sz_recv.at[k],
                a.others[k],
            )

        def small_begin():
            model = gain_sums.shape[1]
            small_acc[0, 0:5] = conv_sums[0:5]
            small_acc[0, 5:7, :inner] = wide_ref[0:2]
            small_acc[0, 5:7, inner : inner + 128] = head_sums[0:2]
            small_acc[0, 5:8, inner + 128 :] = squares_ref[0:3]
            small_acc[0, 7:8, :model] = gain_sums[0:1]
            small_acc[0, 7:8, model : inner + 128] = jnp.zeros((1, inner + 128 - model), F32)
            sm_copy(0).start()

        def small_step(k):
            sm_copy(k).wait_recv()
            small_acc[k + 1] = small_acc[k] + small_in[k]
            if k + 1 < bits:
                sm_copy(k + 1).start()
            else:
                small_parts[turn] = small_acc[bits]
                for i in range(1, pieces):
                    sz_copy(i).start()

        def small_end():
            for i in range(1, pieces):
                sz_copy(i).wait_recv()
            whole = small_parts[0]
            for i in range(1, pieces):
                whole = whole + small_parts[i]
            small_out_ref[...] = whole

        lines = [a_actions[f][bits:] for f in range(flows_a)]
        lines += [b_actions[f][b_taken[f] :] for f in range(flows_b)]
        blocks_of_rows = tokens_ref.shape[0] // 128
        extra = [
            lambda: lax.fori_loop(0, blocks_of_rows // 2, input_rows, 0),
            lambda: lax.fori_loop(blocks_of_rows // 2, blocks_of_rows, input_rows, 0),
            small_begin,
        ]
        extra += [functools.partial(small_step, k) for k in range(bits)] + [small_end]
        while any(lines) or extra:
            if extra:
                extra.pop(0)()
            for line in lines[flows_a:] + lines[:flows_a]:
                if line:
                    line.pop(0)()
        b.tiles_sent()
        a.sent()
        b.sent()
        for k in range(bits):
            sm_copy(k).wait_send()
        for i in range(1, pieces):
            sz_copy(i).wait_send()

        @pl.when(turn > 0)
        def _():
            for slot in range(steps + 1):
                rim_copy(slot).wait_send()

        for f in range(flows_a):
            out_copy(a, out_a_ref, f).wait()
        for f in range(flows_b):
            out_copy(b, out_b_ref, f).wait()


def row_split(places, rows):
    return 2 if places > 2 and rows % 32 == 0 else 1


def tail(
    rate,
    tiled,
    summed_rw_source,
    whole,
    weights,
    momenta,
    wide,
    squares,
    sizes,
    places,
    pieces,
    flows,
    blocks=6,
):
    seqs, piece, inner, channels, heads = sizes
    summed, conv, halo, taps, ssm_grad, starts, heads_map, skip = tiled
    total_rows = summed.shape[0]
    own = whole[6]
    tokens, weight_t = whole[13], whole[12]
    model = tokens.shape[1]
    flows_a, flows_b = flows
    assert flows_b <= flows_a
    bits = places.bit_length() - 1
    assert places == 1 << bits and bits >= 1 and pieces >= 2
    share = model // pieces
    split_rows = row_split(places, share)
    rows = share // split_rows
    steps = inner // TILE
    small = (8, channels)
    shape = jax.ShapeDtypeStruct
    any_space = pl.BlockSpec(memory_space=pl.ANY)
    sem = dma_semaphores

    def constant(array):
        count = array.ndim
        return pl.BlockSpec(
            array.shape, lambda j: (0,) * count, pipeline_mode=pl.Buffered(1)
        )

    def columns(height, last):
        return pl.BlockSpec((height, TILE), lambda j: (0, jnp.clip(j - 1, 0, last)))

    gathered = lambda count: (count,) + (2,) * bits + (pieces + 1, rows, LANES)
    chunk_count = total_rows // CHUNK
    square = (chunk_count, CHUNK, CHUNK)
    per_tile = (total_rows, TILE)
    per_head = (total_rows, 128)
    constants = list(whole) + [weights, momenta, wide, squares]
    return pl.pallas_call(
        functools.partial(
            tail_kernel, sizes, (bits, pieces, flows_a, flows_b, split_rows, blocks)
        ),
        grid=(steps + 2,),
        in_specs=[
            pl.BlockSpec(memory_space=pltpu.SMEM),
            columns(total_rows, steps),
            columns(total_rows, steps),
            columns(halo.shape[0], steps),
            columns(4, steps),
            columns(total_rows, steps - 1),
            pl.BlockSpec(
                (chunk_count, 128, TILE), lambda j: (0, 0, jnp.clip(j - 1, 0, steps - 1))
            ),
            columns(128, steps - 1),
            columns(1, steps - 1),
            pl.BlockSpec((total_rows, TILE), lambda j: (0, steps), pipeline_mode=pl.Buffered(1)),
        ]
        + [any_space if array is weight_t else constant(array) for array in constants],
        out_specs=(
            pl.BlockSpec((total_rows, model), lambda j: (0, 0)),
            pl.BlockSpec(small, lambda j: (0, 0)),
            any_space,
            any_space,
        ),
        out_shape=(
            shape((total_rows, model), BF16),
            shape(small, F32),
            shape(gathered(flows_a), BF16),
            shape(gathered(flows_b), BF16),
        ),
        scratch_shapes=exchange_scratch(bits, pieces, flows_a, rows)
        + exchange_scratch(bits, pieces, flows_b, rows, 0)
        + [pltpu.VMEM((blocks, seqs, 128, inner // blocks), BF16)] * 2
        + sem(blocks)
        + [
            pltpu.VMEM((seqs, 128, inner), F32),
            pltpu.VMEM((model, total_rows), BF16),
            pltpu.VMEM((model, total_rows), BF16),
            pltpu.VMEM(per_head, BF16),
            pltpu.VMEM(per_head, BF16),
            pltpu.VMEM(square, BF16),
            pltpu.VMEM(square, F32),
            pltpu.VMEM(square, F32),
            pltpu.VMEM(square, F32),
            pltpu.VMEM(square, F32),
            pltpu.VMEM(per_head, F32),
            pltpu.VMEM(per_head, F32),
            pltpu.VMEM(per_tile, F32),
            pltpu.VMEM(per_tile, F32),
            pltpu.VMEM(per_tile, F32),
            pltpu.VMEM(per_tile, F32),
            pltpu.VMEM(per_tile, F32),
            pltpu.VMEM((128, TILE), F32),
            pltpu.VMEM((max(chunk_count, 8), TILE), F32),
            pltpu.VMEM(per_head, F32),
            pltpu.VMEM(per_head, F32),
            pltpu.VMEM((max(chunk_count, 8), 128), F32),
            pltpu.VMEM((piece + 16, TILE), F32),
            pltpu.VMEM((total_rows, channels + 256), BF16),
            pltpu.VMEM((seqs, 8, TILE), F32),
            pltpu.VMEM((steps + 1, seqs, 8, TILE), BF16),
            pltpu.VMEM((steps + 1, seqs, 8, TILE), BF16),
        ]
        + sem(steps + 1)
        + [
            pltpu.VMEM(small, F32),
            pltpu.VMEM((8, 128), F32),
            pltpu.VMEM((8, model), F32),
            pltpu.VMEM((bits + 1,) + small, F32),
            pltpu.VMEM((bits,) + small, F32),
            pltpu.VMEM((pieces,) + small, F32),
        ]
        + sem(bits)
        + sem(pieces)
        + [pltpu.VMEM(weight_t.shape, BF16), pltpu.SemaphoreType.DMA],
        compiler_params=pltpu.CompilerParams(
            collective_id=2, has_side_effects=True, vmem_limit_bytes=62 * 1024 * 1024
        ),
        name="tail",
    )(rate, *tiled, summed_rw_source, *constants)


def piece_kernel(
    dims,
    out_weight_ref,
    weight_ref,
    out_momentum_ref,
    momentum_ref,
    last_momentum_ref,
    w_ref,
    m_ref,
    tiles,
    halves,
    turned,
    w_sem,
    m_sem,
):
    flows_a, flows_b, places, split_rows = dims
    place, turn = lax.axis_index("dp"), lax.axis_index("seq")
    rows, per_flow = m_ref.shape[1], places // split_rows
    inner, model = out_weight_ref.shape
    width = weight_ref.shape[0]
    out_tiles, in_tiles, rest = inner // LANES, width // LANES, width % LANES
    part = lax.rem(place, split_rows)
    first = (turn * split_rows + part) * rows
    start = jnp.minimum(lax.div(first, 128) * 128, model - 256)
    window = pl.ds(pl.multiple_of(start, 128), 256)
    mine = pl.ds(pl.multiple_of(first - start, 16), rows)
    half = pl.ds(pl.multiple_of(part * rows, 8), rows)
    within = lax.div(place, split_rows)
    flows = flows_a + flows_b

    def each(act):
        for f in range(flows):
            if f < flows_a:
                tile = f * per_flow + within
            else:
                tile = 2 * out_tiles + (f - flows_a) * per_flow + within
            act(f, tile)

    def copies(source, momentum, at, count, f):
        yield pltpu.make_async_copy(
            source.at[pl.ds(pl.multiple_of(at, 8), count), window],
            tiles.at[f, pl.ds(0, count)],
            w_sem.at[f],
        )
        if count == LANES:
            lanes = pl.ds(pl.multiple_of(at, LANES), LANES)
            yield pltpu.make_async_copy(momentum.at[half, lanes], halves.at[f], m_sem.at[f])

    def moves(f, tile, act):
        in_limit = out_tiles + in_tiles
        if f < flows_a:
            in_limit = min(in_limit, 2 * out_tiles)

        @pl.when(tile < out_tiles)
        def _():
            for copy in copies(out_weight_ref, out_momentum_ref, tile * LANES, LANES, f):
                act(copy)

        @pl.when((tile >= out_tiles) & (tile < in_limit))
        def _():
            at = (tile - out_tiles) * LANES
            for copy in copies(weight_ref, momentum_ref, at, LANES, f):
                act(copy)

        if rest and f >= flows_a:

            @pl.when(tile == in_limit)
            def _():
                for copy in copies(weight_ref, momentum_ref, in_tiles * LANES, rest, f):
                    act(copy)

    tiles[...] = jnp.zeros_like(tiles)
    halves[...] = jnp.zeros_like(halves)
    each(lambda f, tile: moves(f, tile, lambda copy: copy.start()))
    each(lambda f, tile: moves(f, tile, lambda copy: copy.wait()))

    def take(f, tile):
        turned[...] = jnp.transpose(tiles[f])
        w_ref[f] = turned[mine]
        m_ref[f] = halves[f]
        if rest and f >= flows_a:

            @pl.when(tile == out_tiles + in_tiles)
            def _():
                m_ref[f] = last_momentum_ref[half]

    each(take)


def owned(out_weight, weight_t, out_momentum_t, momentum, flows_a, flows_b, places):
    model = out_weight.shape[1]
    share, width = momentum.shape
    split_rows = row_split(places, share)
    rows, flows = share // split_rows, flows_a + flows_b
    whole = width // LANES * LANES
    last_momentum = jnp.pad(momentum[:, whole:], ((0, 0), (0, LANES - (width - whole))))
    any_space = pl.BlockSpec(memory_space=pl.ANY)
    vmem = pl.BlockSpec(memory_space=pltpu.VMEM)
    return pl.pallas_call(
        functools.partial(piece_kernel, (flows_a, flows_b, places, split_rows)),
        in_specs=[any_space] * 4 + [vmem],
        out_specs=(vmem, vmem),
        out_shape=(
            jax.ShapeDtypeStruct((flows, rows, LANES), BF16),
            jax.ShapeDtypeStruct((flows, rows, LANES), F32),
        ),
        scratch_shapes=[
            pltpu.VMEM((flows, LANES, 256), BF16),
            pltpu.VMEM((flows, rows, LANES), F32),
            pltpu.VMEM((256, LANES), BF16),
            pltpu.SemaphoreType.DMA((flows,)),
            pltpu.SemaphoreType.DMA((flows,)),
        ],
        name="owned",
    )(out_weight, weight_t, out_momentum_t, momentum, last_momentum)


def finish_kernel(
    out_steps,
    split_rows,
    gathered_a_ref,
    gathered_b_ref,
    out_momentum_ref,
    momentum_ref,
    totals_ref,
    out_weight_ref,
    weight_ref,
    new_out_momentum_ref,
    new_momentum_ref,
    conv_weight_ref,
    conv_bias_ref,
    gate_gain_ref,
    norm_gain_ref,
    skip_ref,
    dt_bias_ref,
    a_log_ref,
    output_rms_ref,
    mixer_rms_ref,
    joined,
):
    group, slots, rows, _ = gathered_a_ref.shape
    step = pl.program_id(0)

    @pl.when(step == 0)
    def _():
        heads, inner, model = skip_ref.shape[0], gate_gain_ref.shape[0], norm_gain_ref.shape[0]
        side = inner + 128
        conv_weight_ref[...] = totals_ref[0:4]
        conv_bias_ref[...] = totals_ref[4]
        gate_gain_ref[...] = totals_ref[5, :inner]
        norm_gain_ref[...] = totals_ref[7, :model]
        skip_ref[...] = totals_ref[6, :heads]
        dt_bias_ref[...] = totals_ref[5, inner : inner + heads]
        a_log_ref[...] = totals_ref[6, inner : inner + heads]
        count = jnp.maximum(totals_ref[7:8, side + 9 : side + 10], 1.0) * model
        squares = jnp.sum(totals_ref[5:7, side:], axis=1, keepdims=True)
        output_rms_ref[...] = jnp.sqrt(squares[0:1] / count)
        mixer_rms_ref[...] = jnp.sqrt(squares[1:2] / count)

    def write(gathered_ref, weights, old, new):
        for i in range(group // split_rows):
            at = slice(i * LANES, (i + 1) * LANES)
            for part in range(split_rows):
                for p in range(slots - 1):
                    to = (p * split_rows + part) * rows
                    joined[to : to + rows] = gathered_ref[i * split_rows + part, p]
                own = slice(part * rows, (part + 1) * rows)
                summed = gathered_ref[i * split_rows + part, slots - 1].astype(F32)
                new[own, at] = 0.5 * old[own, at] + summed
            weights[at] = jnp.transpose(joined[...])

    @pl.when(step < out_steps)
    def _():
        write(gathered_a_ref, out_weight_ref, out_momentum_ref, new_out_momentum_ref)

    @pl.when((step >= out_steps) & (step < 2 * out_steps))
    def _():
        write(gathered_a_ref, weight_ref, momentum_ref, new_momentum_ref)

    @pl.when(step >= 2 * out_steps)
    def _():
        write(gathered_b_ref, weight_ref, momentum_ref, new_momentum_ref)


def finish(gathered_a, gathered_b, out_momentum_t, momentum, totals, heads, split_rows, group=4):
    _, slots, rows, _ = gathered_a.shape
    share, width = momentum.shape
    inner = out_momentum_t.shape[1]
    model = (slots - 1) * share
    wide = group * LANES
    group = group * split_rows
    out_steps, in_steps = inner // wide, -(-width // wide)
    out_at = lambda j: jnp.minimum(j, out_steps - 1)
    in_at = lambda j: jnp.maximum(j - out_steps, 0)
    by_column = [
        pl.BlockSpec((share, wide), lambda j: (0, out_at(j))),
        pl.BlockSpec((share, wide), lambda j: (0, in_at(j))),
    ]
    shape = jax.ShapeDtypeStruct
    smalls = [
        shape(size, F32)
        for size in (
            (4, totals.shape[1]),
            (totals.shape[1],),
            (inner,),
            (model,),
            (heads,),
            (heads,),
            (heads,),
            (1, 1),
            (1, 1),
        )
    ]
    return pl.pallas_call(
        functools.partial(finish_kernel, out_steps, split_rows),
        grid=(out_steps + in_steps,),
        in_specs=[
            pl.BlockSpec(
                (group, slots, rows, LANES), lambda j: (jnp.minimum(j, 2 * out_steps - 1), 0, 0, 0)
            ),
            pl.BlockSpec(
                (group, slots, rows, LANES), lambda j: (jnp.maximum(j - 2 * out_steps, 0), 0, 0, 0)
            ),
        ]
        + by_column
        + [pl.BlockSpec(totals.shape, lambda j: (0, 0))],
        out_specs=[
            pl.BlockSpec((wide, model), lambda j: (out_at(j), 0)),
            pl.BlockSpec((wide, model), lambda j: (in_at(j), 0)),
        ]
        + by_column
        + [
            pl.BlockSpec(small.shape, lambda j, count=len(small.shape): (0,) * count)
            for small in smalls
        ],
        out_shape=[
            shape((inner, model), BF16),
            shape((width, model), BF16),
            shape((share, inner), F32),
            shape((share, width), F32),
        ]
        + smalls,
        scratch_shapes=[pltpu.VMEM((model, LANES), BF16)],
        name="finish",
    )(gathered_a, gathered_b, out_momentum_t, momentum, totals)


def local(
    tokens,
    cotangent,
    segment_ids,
    doc_starts,
    valid_mask,
    step_number,
    learn_rate,
    norm_gain,
    in_weight,
    conv_weight,
    conv_bias,
    dt_bias,
    a_log,
    skip_d,
    gate_gain,
    out_weight,
    in_momentum,
    out_momentum,
):
    seqs, piece, model_width = tokens.shape
    heads = dt_bias.shape[0]
    tap_count, channels = conv_weight.shape
    inner_width = gate_gain.shape[0]
    proj_width = in_weight.shape[1]
    total = seqs * piece
    sizes = (seqs, piece, inner_width, channels, heads)
    places, pieces = lax.axis_size("dp"), lax.axis_size("seq")
    turn = lax.axis_index("seq")
    seg = segment_ids.astype(F32)
    sent = jnp.concatenate(
        [
            tokens[:, piece - HALO :],
            jnp.broadcast_to(seg[:, piece - HALO :, None], (seqs, HALO, LANES)).astype(BF16),
        ],
        axis=2,
    )
    route = [(i, i + 1) for i in range(pieces - 1)]
    arrived = lax.ppermute(sent, "seq", route)
    halo = arrived[:, :, :model_width].reshape(seqs * HALO, model_width)
    early_seg = jnp.where(turn == 0, -1.0, arrived[:, :, model_width].astype(F32))
    seg_pad = jnp.concatenate([early_seg, seg], axis=1)
    seg_row = seg.reshape(1, total)
    heads_map = (
        lax.broadcasted_iota(jnp.int32, (LANES, inner_width), 0)
        == lax.broadcasted_iota(jnp.int32, (LANES, inner_width), 1) // (inner_width // heads)
    ).astype(BF16)

    def lanes(values):
        return jnp.pad(values, (0, LANES - heads)).reshape(1, LANES)

    flat_tokens = tokens.reshape(total, model_width)
    weight_t = jnp.transpose(in_weight)
    out_momentum_t = jnp.transpose(out_momentum)
    flat_cot = cotangent.reshape(total, model_width)
    bias_row, decay_row = lanes(dt_bias), lanes(a_log)
    skip_row = jnp.repeat(skip_d, inner_width // heads).reshape(1, inner_width)
    gain_row = gate_gain.reshape(1, inner_width)
    normed, masks, gate, conv, conv_halo, summed, raw, cum, fresh, keep = front(
        flat_tokens,
        halo,
        norm_gain.reshape(1, model_width),
        weight_t,
        conv_weight,
        conv_bias.reshape(1, channels),
        seg_pad,
        valid_mask,
        bias_row,
        decay_row,
        heads_map,
        sizes,
    )
    incoming = chain(fresh, keep, 1)
    output, low, out_low, gate_grad, ssm_grad, starts, dots, squares, wide, state_grad = forward(
        summed,
        gate,
        raw,
        cum,
        masks,
        seg_row,
        incoming,
        flat_tokens,
        flat_cot,
        out_weight,
        gain_row,
        skip_row,
        heads_map,
        sizes,
    )
    step_float = step_number[0].astype(F32)
    rate = (learn_rate[0] * step_float / (step_float + 16.0)).reshape(1)
    share_rows = model_width // pieces
    split_rows = row_split(places, share_rows)
    per_flow = places // split_rows
    flows_a = -(-2 * inner_width // (LANES * per_flow))
    flows_b = -(-(channels + 2 * LANES) // (LANES * per_flow))
    weights, momenta = owned(
        out_weight, weight_t, out_momentum_t, in_momentum, flows_a, flows_b, places
    )
    input_grad, totals, gathered_a, gathered_b = tail(
        rate,
        (summed, conv, conv_halo, conv_weight, ssm_grad, starts, heads_map, skip_row),
        summed,
        (
            raw,
            cum,
            masks,
            seg_row,
            dots,
            decay_row,
            state_grad,
            keep,
            out_low,
            normed,
            low,
            gate_grad,
            weight_t,
            flat_tokens,
            norm_gain.reshape(1, model_width),
        ),
        weights,
        momenta,
        wide,
        squares,
        sizes,
        places,
        pieces,
        (flows_a, flows_b),
    )
    share = (pieces + 1, share_rows // split_rows, LANES)
    (
        new_out_weight,
        new_weight_t,
        new_out_momentum_t,
        new_in_momentum,
        conv_weight_total,
        conv_bias_total,
        gate_gain_total,
        norm_gain_total,
        skip_total,
        dt_bias_total,
        a_log_total,
        output_rms,
        mixer_rms,
    ) = finish(
        gathered_a.reshape((-1,) + share),
        gathered_b.reshape((-1,) + share),
        out_momentum_t,
        in_momentum,
        totals,
        heads,
        split_rows,
    )
    new_in_weight = jnp.transpose(new_weight_t)
    new_out_momentum = jnp.transpose(new_out_momentum_t)
    output_rms, mixer_rms = output_rms.reshape(1), mixer_rms.reshape(1)
    return (
        output.reshape(tokens.shape),
        input_grad.reshape(tokens.shape),
        new_in_weight,
        new_out_weight,
        new_in_momentum,
        new_out_momentum,
        norm_gain_total,
        conv_weight_total,
        conv_bias_total,
        dt_bias_total,
        a_log_total,
        skip_total,
        gate_gain_total,
        output_rms,
        mixer_rms,
    )


def solution(mesh):
    placed = (
        P("dp", "seq", None),
        P("dp", "seq", None),
        P("dp", "seq"),
        P("dp", "seq"),
        P("dp", "seq"),
        P(),
        P(),
        P(),
        P(),
        P(),
        P(),
        P(),
        P(),
        P(),
        P(),
        P(),
        P("seq", None),
        P(None, "seq"),
    )
    return jax.shard_map(
        local,
        mesh=mesh,
        in_specs=placed,
        out_specs=(
            P("dp", "seq", None),
            P("dp", "seq", None),
            P(),
            P(),
            P("seq", None),
            P(None, "seq"),
            P(),
            P(),
            P(),
            P(),
            P(),
            P(),
            P(),
            P(),
            P(),
        ),
        check_vma=False,
    )
```

```python
import functools

import jax
import jax.numpy as jnp
from jax import lax
from jax.experimental import pallas as pl
from jax.experimental.pallas import tpu as pltpu
from jax.sharding import PartitionSpec as P

CHUNK = 128
HALO = 16
GATE_BLOCK = 256
EPS = 1e-05
NEGATIVE = -1e30
F32, BF16 = jnp.float32, jnp.bfloat16
LANES = 128
MESH = pl.DeviceIdType.MESH


def remote(src, dst, send, recv, target):
    return pltpu.make_async_remote_copy(
        src_ref=src,
        dst_ref=dst,
        send_sem=send,
        recv_sem=recv,
        device_id=target,
        device_id_type=MESH,
    )


def greet(targets):
    barrier = pltpu.get_barrier_semaphore()
    for target in targets:
        pl.semaphore_signal(barrier, inc=1, device_id=target, device_id_type=MESH)
    pl.semaphore_wait(barrier, len(targets))


def dma_semaphores(*shape):
    return [pltpu.SemaphoreType.DMA(shape)] * 2


def part_count(pieces):
    return 2 if pieces % 2 == 0 else 1


def half_shape(bits, pieces, flows, rows, k):
    return (flows,) + (2,) * (bits - k - 1) + (pieces, rows, LANES)


def mm(a, b):
    return jnp.dot(a, b, preferred_element_type=F32)


def mm_nt(a, b):
    return lax.dot_general(a, b, (((1,), (1,)), ((), ())), preferred_element_type=F32)


def mm_tn(a, b):
    return lax.dot_general(a, b, (((0,), (0,)), ((), ())), preferred_element_type=F32)


def split(a):
    high = a.astype(BF16)
    return high, (a - high.astype(F32)).astype(BF16)


def exact_mm(a, b):
    return jnp.dot(a, b, preferred_element_type=F32, precision=lax.Precision.HIGHEST)


def spread(a, heads_ref):
    high, low = split(a)
    return mm(high, heads_ref[...]) + mm(low, heads_ref[...])


def gather_heads(a, heads_ref):
    high, low = split(a)
    return mm_nt(high, heads_ref[...]) + mm_nt(low, heads_ref[...])


def sigmoid(v):
    return 1.0 / (1.0 + jnp.exp(-v))


def gate_of(v):
    return 0.5 + 0.5 * jnp.tanh(0.5 * v)


def softplus(v):
    return jnp.maximum(v, 0.0) + jnp.log1p(jnp.exp(-jnp.abs(v)))


def triangle(size, upper):
    row = lax.broadcasted_iota(jnp.int32, (size, size), 0)
    column = lax.broadcasted_iota(jnp.int32, (size, size), 1)
    return ((row <= column) if upper else (row >= column)).astype(F32)


def front_kernel(
    sizes,
    tokens_ref,
    halo_ref,
    gain_ref,
    weight_ref,
    taps_ref,
    bias_ref,
    seg_ref,
    valid_ref,
    dt_bias_ref,
    a_log_ref,
    heads_ref,
    normed_ref,
    masks_ref,
    gate_ref,
    conv_ref,
    halo_out_ref,
    summed_ref,
    raw_ref,
    cum_ref,
    state_ref,
    keep_ref,
    padded,
    product,
    active,
):
    seqs, piece, inner, channels, heads = sizes
    gate_blocks, conv_blocks = inner // GATE_BLOCK, channels // GATE_BLOCK
    step = pl.program_id(0)
    stride = piece + HALO

    @pl.when(step == 0)
    def _():
        gain = gain_ref[...]
        for n in range(seqs):
            padded_seg = seg_ref[n : n + 1]
            seg = padded_seg[:, HALO:]

            def over_chunks(at):
                return jnp.concatenate(
                    [
                        jnp.broadcast_to(
                            padded_seg[:, c * CHUNK + at : c * CHUNK + at + 1], (1, CHUNK)
                        )
                        for c in range(piece // CHUNK)
                    ],
                    axis=1,
                )

            others = [padded_seg[:, HALO - 3 + k : HALO - 3 + k + piece] for k in range(4)] + [
                over_chunks(HALO - 1),
                over_chunks(HALO + CHUNK - 1),
                jnp.broadcast_to(padded_seg[:, HALO - 1 : HALO], (1, piece)),
                jnp.broadcast_to(padded_seg[:, HALO + piece - 1 :], (1, piece)),
            ]
            lines = [(other == seg).astype(F32) for other in others] + [
                seg,
                valid_ref[n : n + 1].astype(F32),
            ]
            lines = lines + [jnp.zeros_like(seg)] * (16 - len(lines))
            masks_ref[pl.ds(n * piece, piece)] = jnp.transpose(jnp.concatenate(lines, axis=0))
            for source, start, to, count in (
                (halo_ref, n * HALO, n * stride, HALO),
                (tokens_ref, n * piece, n * stride + HALO, piece),
            ):

                def body(i, carry):
                    values = source[pl.ds(pl.multiple_of(start + i * 16, 16), 16)].astype(F32)
                    scale = lax.rsqrt(jnp.mean(values * values, axis=-1, keepdims=True) + EPS)
                    low = (values * scale * gain).astype(BF16)
                    padded[pl.ds(pl.multiple_of(to + i * 16, 16), 16)] = low
                    return carry

                lax.fori_loop(0, count // 16, body, 0)
            normed_ref[pl.ds(n * piece, piece)] = padded[pl.ds(n * stride + HALO, piece)]

    product[...] = mm_nt(padded[...], weight_ref[...])

    @pl.when(step < gate_blocks)
    def _():
        for n in range(seqs):
            gate_ref[pl.ds(n * piece, piece)] = product[pl.ds(n * stride + HALO, piece)]

    @pl.when((step >= gate_blocks) & (step < gate_blocks + conv_blocks))
    def _():
        at = pl.multiple_of((step - gate_blocks) * GATE_BLOCK, GATE_BLOCK)
        for n in range(seqs):
            conv_ref[pl.ds(n * piece, piece)] = product[pl.ds(n * stride + HALO, piece)]
            halo_out_ref[pl.ds(n * HALO, HALO)] = product[pl.ds(n * stride, HALO)]
            for i in range(piece // 64):
                rows = pl.ds(n * piece + i * 64, 64)
                total = jnp.broadcast_to(bias_ref[...], (64, GATE_BLOCK))
                for k in range(4):
                    source = product[pl.ds(n * stride + HALO - 3 + k + i * 64, 64)]
                    total = total + source * masks_ref[rows, k : k + 1] * taps_ref[k : k + 1]
                summed_ref[rows] = total
                active[rows, pl.ds(at, GATE_BLOCK)] = (total * gate_of(total)).astype(BF16)

    @pl.when(step == gate_blocks + conv_blocks)
    def _():
        lane = lax.broadcasted_iota(jnp.int32, (piece, 128), 1)
        lower = triangle(CHUNK, False)
        for n in range(seqs):
            rows = pl.ds(n * piece, piece)
            raw = jnp.where(lane < heads, product[pl.ds(n * stride + HALO, piece), :128], 0.0)
            raw = raw + dt_bias_ref[...]
            raw_ref[rows] = raw
            steps = jnp.where(lane < heads, softplus(raw), 0.0)
            decay = -jnp.exp(a_log_ref[...]) * steps
            total = jnp.zeros((1, 128), F32)
            pieces = []
            for c in range(piece // CHUNK):
                cumulative = exact_mm(lower, decay[c * CHUNK : (c + 1) * CHUNK])
                cum_ref[pl.ds(n * piece + c * CHUNK, CHUNK)] = cumulative
                pieces.append(cumulative + total)
                total = total + cumulative[CHUNK - 1 :]
            whole = jnp.concatenate(pieces, axis=0) if len(pieces) > 1 else pieces[0]
            tails = jnp.exp(total - whole) * steps * masks_ref[rows, 7:8]
            weighted = (spread(tails, heads_ref) * active[rows, :inner].astype(F32)).astype(BF16)
            state_ref[n] = mm_tn(active[rows, inner : inner + 128], weighted)
            last = masks_ref[n * piece + piece - 1 : n * piece + piece, 6:7]
            keep = jnp.exp(total) * last
            keep_ref[n] = spread(jnp.broadcast_to(keep, (8, 128)), heads_ref)


def front(tokens, halo, gain, weight, taps, bias, segs, valid, dt_bias, a_log, heads_map, sizes):
    seqs, piece, inner, channels, heads = sizes
    total, model = tokens.shape
    stride = seqs * (piece + HALO)
    gate_blocks, conv_blocks = inner // GATE_BLOCK, channels // GATE_BLOCK
    full = lambda *shape: pl.BlockSpec(shape, lambda j: (0,) * len(shape))

    def conv_at(j):
        return (0, jnp.clip(j - gate_blocks, 0, conv_blocks - 1))

    return pl.pallas_call(
        functools.partial(front_kernel, sizes),
        grid=(gate_blocks + conv_blocks + 1,),
        in_specs=[
            full(total, model),
            full(seqs * HALO, model),
            full(1, model),
            pl.BlockSpec((GATE_BLOCK, model), lambda j: (j, 0)),
            pl.BlockSpec((4, GATE_BLOCK), conv_at),
            pl.BlockSpec((1, GATE_BLOCK), conv_at),
            full(*segs.shape),
            full(*valid.shape),
            full(1, 128),
            full(1, 128),
            full(128, inner),
        ],
        out_specs=(
            full(total, model),
            full(total, 16),
            pl.BlockSpec((total, GATE_BLOCK), lambda j: (0, jnp.minimum(j, gate_blocks - 1))),
            pl.BlockSpec((total, GATE_BLOCK), conv_at),
            pl.BlockSpec((seqs * HALO, GATE_BLOCK), conv_at),
            pl.BlockSpec((total, GATE_BLOCK), conv_at),
            full(total, 128),
            full(total, 128),
            full(seqs, 128, inner),
            full(seqs, 8, inner),
        ),
        out_shape=(
            jax.ShapeDtypeStruct((total, model), BF16),
            jax.ShapeDtypeStruct((total, 16), F32),
            jax.ShapeDtypeStruct((total, inner), F32),
            jax.ShapeDtypeStruct((total, channels), F32),
            jax.ShapeDtypeStruct((seqs * HALO, channels), F32),
            jax.ShapeDtypeStruct((total, channels), F32),
            jax.ShapeDtypeStruct((total, 128), F32),
            jax.ShapeDtypeStruct((total, 128), F32),
            jax.ShapeDtypeStruct((seqs, 128, inner), F32),
            jax.ShapeDtypeStruct((seqs, 8, inner), F32),
        ),
        scratch_shapes=[
            pltpu.VMEM((stride, model), BF16),
            pltpu.VMEM((stride, GATE_BLOCK), F32),
            pltpu.VMEM((total, channels), BF16),
        ],
        compiler_params=pltpu.CompilerParams(vmem_limit_bytes=48 * 1024 * 1024),
        name="front",
    )(tokens, halo, gain, weight, taps, bias, segs, valid, dt_bias, a_log, heads_map)


def chain_kernel(ways, blocks, own_ref, keep_ref, out_ref, sent, taken, send, recv):
    size = lax.axis_size("seq")
    turn = lax.axis_index("seq")
    first = turn == (0 if ways > 0 else size - 1)
    final = turn == (size - 1 if ways > 0 else 0)
    ahead = {"seq": lax.rem(turn + ways + size, size)}
    behind = {"seq": lax.rem(turn - ways + size, size)}
    barrier = pltpu.get_barrier_semaphore()

    @pl.when(jnp.logical_not(first))
    def _():
        pl.semaphore_signal(
            barrier, inc=1, device_id=behind, device_id_type=pl.DeviceIdType.MESH
        )

    @pl.when(jnp.logical_not(final))
    def _():
        pl.semaphore_wait(barrier, 1)

    width = own_ref.shape[2] // blocks

    def copy(c):
        return pltpu.make_async_remote_copy(
            src_ref=sent.at[c],
            dst_ref=taken.at[c],
            send_sem=send.at[c],
            recv_sem=recv.at[c],
            device_id=ahead,
            device_id_type=pl.DeviceIdType.MESH,
        )

    @pl.when(first)
    def _():
        out_ref[...] = jnp.zeros_like(out_ref)
        for c in range(blocks):
            at = slice(c * width, (c + 1) * width)
            sent[c] = own_ref[:, :, at].astype(BF16)
            copy(c).start()

    @pl.when(jnp.logical_not(first))
    def _():
        for c in range(blocks):
            at = slice(c * width, (c + 1) * width)
            copy(c).wait_recv()

            @pl.when(jnp.logical_not(final))
            def _():
                sent[c] = (
                    own_ref[:, :, at] + keep_ref[:, 0:1, at] * taken[c].astype(F32)
                ).astype(BF16)
                copy(c).start()

            out_ref[:, :, at] = taken[c].astype(F32)

    @pl.when(jnp.logical_not(final))
    def _():
        for c in range(blocks):
            copy(c).wait_send()


def chain(own, keep, ways, blocks=12):
    seqs, depth, inner = own.shape
    vmem = pl.BlockSpec(memory_space=pltpu.VMEM)
    part = (blocks, seqs, depth, inner // blocks)
    return pl.pallas_call(
        functools.partial(chain_kernel, ways, blocks),
        out_shape=jax.ShapeDtypeStruct(own.shape, F32),
        in_specs=[vmem, vmem],
        out_specs=vmem,
        scratch_shapes=[pltpu.VMEM(part, BF16)] * 2 + [pltpu.SemaphoreType.DMA((blocks,))] * 2,
        compiler_params=pltpu.CompilerParams(
            collective_id=1 if ways > 0 else 2,
            has_side_effects=True,
            vmem_limit_bytes=32 * 1024 * 1024,
        ),
        name="chain",
    )(own, keep)


def decays_of(cum, cum_t, bias, h):
    return jnp.exp(cum[:, h : h + 1] - cum_t[h : h + 1, :] + bias)


def mask_bias(seg_col, seg_row):
    row = lax.broadcasted_iota(jnp.int32, (CHUNK, CHUNK), 0)
    column = lax.broadcasted_iota(jnp.int32, (CHUNK, CHUNK), 1)
    return jnp.where((row >= column) & (seg_col == seg_row), 0.0, NEGATIVE)


def scores_of(reader, writer):
    rh, rl = split(reader)
    wh, wl = split(writer)
    return mm_nt(rh, wh) + (mm_nt(rh, wl) + mm_nt(rl, wh))


def forward_kernel(
    sizes,
    chunks,
    summed_ref,
    gate_ref,
    raw_ref,
    cum_ref,
    masks_ref,
    seg_row_ref,
    incoming_ref,
    tokens_ref,
    cot_ref,
    weight_ref,
    gain_ref,
    skip_ref,
    heads_ref,
    output_ref,
    low_ref,
    out_low_ref,
    gate_grad_ref,
    ssm_grad_ref,
    starts_ref,
    dot_ref,
    sums_ref,
    wide_ref,
    state_grad_ref,
    state,
    prefix,
    active,
    mixed_in,
    factors,
    grads,
    inv,
    totals,
):
    seqs, piece, inner, channels, heads = sizes
    c = pl.program_id(1)

    @pl.when((c == 0) & (pl.program_id(0) == 0))
    def _():
        sums_ref[...] = jnp.zeros_like(sums_ref)
        wide_ref[...] = jnp.zeros_like(wide_ref)

    @pl.when(c == 0)
    def _():
        state[...] = incoming_ref[0]
        prefix[...] = jnp.zeros_like(prefix)
        state_grad_ref[...] = jnp.zeros_like(state_grad_ref)

    def activate(i, carry):
        rows = pl.ds(pl.multiple_of(i * 16, 16), 16)
        values = summed_ref[rows]
        active[rows] = values * gate_of(values)
        return carry

    lax.fori_loop(0, CHUNK // 16, activate, 0)
    lane = lax.broadcasted_iota(jnp.int32, (CHUNK, 128), 1)
    steps = jnp.where(lane < heads, softplus(raw_ref[...]), 0.0)
    cum = cum_ref[...]
    cum_t = jnp.transpose(cum)
    final = cum[CHUNK - 1 :]
    tails = jnp.exp(final - cum) * steps * masks_ref[:, 5:6]
    before = spread(jnp.exp(prefix[...]), heads_ref)[0:1]
    prefix[...] = prefix[...] + final
    for i, block in enumerate((steps, jnp.exp(cum), tails)):
        factors[i] = spread(block, heads_ref)
    factors[3] = factors[1] * before * masks_ref[:, 6:7]
    factors[1] = factors[1] * masks_ref[:, 4:5]
    writer = active[:, inner : inner + 128]
    reader = active[:, inner + 128 : inner + 256]
    scores = scores_of(reader, writer)
    bias = mask_bias(masks_ref[:, 8:9], seg_row_ref[0:1])
    half = lax.broadcasted_iota(jnp.int32, (CHUNK, 128), 1) < 64
    state_low = state[...].astype(BF16)
    starts_ref[0] = state_low
    reader_low = reader.astype(BF16)
    for pair in range(heads // 2):
        at = slice(pair * 128, (pair + 1) * 128)
        moved = (active[:, at] * factors[0, :, at]).astype(BF16)
        zero = jnp.zeros_like(moved)
        one = (scores * decays_of(cum, cum_t, bias, 2 * pair)).astype(BF16)
        two = (scores * decays_of(cum, cum_t, bias, 2 * pair + 1)).astype(BF16)
        both = jnp.concatenate([one, two], axis=1)
        stacked = jnp.concatenate(
            [jnp.where(half, moved, zero), jnp.where(half, zero, moved)], axis=0
        )
        carried = mm(reader_low, state_low[:, at]) * factors[1, :, at]
        mixed_in[:, at] = mm(both, stacked) + carried
    weighted = (active[:, :inner] * factors[2]).astype(BF16)
    kept = jnp.exp(final) * masks_ref[CHUNK - 1 :, 4:5]
    kept = spread(jnp.broadcast_to(kept, (8, 128)), heads_ref)[0:1]
    state[...] = state[...] * kept + mm_tn(writer.astype(BF16), weighted)

    gain = gain_ref[...]
    skip = skip_ref[...]

    column_blocks = [slice(at, at + 512) for at in range(0, inner, 512)]

    def gating(i, carry):
        rows = pl.ds(pl.multiple_of(i * 16, 16), 16)
        squares = jnp.zeros((16, 512), F32)
        for at in column_blocks:
            gate = gate_ref[rows, at]
            turned = gate_of(gate)
            mixer = mixed_in[rows, at] + skip[:, at] * active[rows, at]
            product = mixer * gate * turned
            factors[0, rows, at] = product
            factors[1, rows, at] = turned
            factors[2, rows, at] = mixer
            squares = squares + product * product
        mean = jnp.sum(squares, axis=-1, keepdims=True) / inner
        scale = lax.rsqrt(mean + EPS)
        inv[rows] = jnp.broadcast_to(scale, (16, 128))
        for at in column_blocks:
            low_ref[rows, at] = (factors[0, rows, at] * scale * gain[:, at]).astype(BF16)
        return carry

    lax.fori_loop(0, CHUNK // 16, gating, 0)
    mixed = mm(low_ref[...], weight_ref[...])
    block_out = tokens_ref[...].astype(F32) + mixed
    output_ref[...] = block_out.astype(BF16)
    valid = masks_ref[:, 9:10]
    for i, block in enumerate((block_out, mixed)):
        squares = jnp.sum(valid * block * block, axis=0, keepdims=True)
        for at in range(0, squares.shape[1], 128):
            sums_ref[i : i + 1] += squares[:, at : at + 128]
    sums_ref[2:3, :16] += jnp.sum(masks_ref[...], axis=0, keepdims=True)
    out_low = (cot_ref[...].astype(F32) * valid).astype(BF16)
    out_low_ref[...] = out_low
    grads[...] = mm_nt(out_low, weight_ref[...])

    @pl.when((c == 0) & (pl.program_id(0) == 0))
    def _():
        totals[...] = jnp.zeros_like(totals)

    def backing(i, carry):
        rows = pl.ds(pl.multiple_of(i * 16, 16), 16)
        scale = inv[rows, 0:1]
        inside = jnp.zeros((16, 512), F32)
        for at in column_blocks:
            grad = grads[rows, at]
            gated = factors[0, rows, at]
            totals[0, :, at] += grad * gated * scale
            inside = inside + grad * gain[:, at] * gated
        inside = jnp.sum(inside, axis=-1, keepdims=True) / inner
        inside = scale * scale * scale * inside
        for at in column_blocks:
            gate, turned = gate_ref[rows, at], factors[1, rows, at]
            gated_grad = scale * (grads[rows, at] * gain[:, at]) - factors[0, rows, at] * inside
            ssm_grad = gated_grad * (gate * turned)
            ssm_grad_ref[rows, at] = ssm_grad
            grads[rows, at] = ssm_grad
            totals[1, :, at] += ssm_grad * active[rows, at]
            gate_grad_ref[rows, at] = (
                gated_grad * factors[2, rows, at] * turned * (1.0 + gate * (1.0 - turned))
            ).astype(BF16)
        return carry

    lax.fori_loop(0, CHUNK // 16, backing, 0)

    @pl.when((c == chunks - 1) & (pl.program_id(0) == seqs - 1))
    def _():
        wide_ref[0:1] = jnp.sum(totals[0], axis=0, keepdims=True)
        skips = jnp.sum(totals[1], axis=0, keepdims=True)
        skips = gather_heads(jnp.broadcast_to(skips, (8, inner)), heads_ref)
        wide_ref[1:2, :128] = skips[0:1]

    reader_t = jnp.transpose(reader_low)
    for pair in range(heads // 2):
        at = slice(pair * 128, (pair + 1) * 128)
        state_grad_ref[0, :, at] += mm(
            reader_t, (grads[:, at] * factors[3, :, at]).astype(BF16)
        )
        mixed_in[:, at] = mixed_in[:, at] * grads[:, at].astype(BF16).astype(F32)
    dot_ref[...] = gather_heads(mixed_in[...], heads_ref)


def forward(
    summed, gate, raw, cum, masks, seg_row, incoming, tokens, cot, weight, gain, skip, heads_map, sizes
):
    seqs, piece, inner, channels, heads = sizes
    total, model = tokens.shape
    chunks = piece // CHUNK
    full = lambda *shape: pl.BlockSpec(shape, lambda n, c: (0,) * len(shape))
    rows = lambda width: pl.BlockSpec((CHUNK, width), lambda n, c: (n * chunks + c, 0))
    each = lambda depth: pl.BlockSpec((1, depth, inner), lambda n, c: (n, 0, 0))
    shape = jax.ShapeDtypeStruct
    return pl.pallas_call(
        functools.partial(forward_kernel, sizes, chunks),
        grid=(seqs, chunks),
        in_specs=[
            rows(channels),
            rows(inner),
            rows(128),
            rows(128),
            rows(16),
            pl.BlockSpec((1, CHUNK), lambda n, c: (0, n * chunks + c)),
            each(128),
            rows(model),
            rows(model),
            full(inner, model),
            full(1, inner),
            full(1, inner),
            full(128, inner),
        ],
        out_specs=(
            rows(model),
            rows(inner),
            rows(model),
            rows(inner),
            rows(inner),
            pl.BlockSpec((1, 128, inner), lambda n, c: (n * chunks + c, 0, 0)),
            rows(128),
            full(8, 128),
            full(8, inner),
            each(128),
        ),
        out_shape=(
            shape((total, model), BF16),
            shape((total, inner), BF16),
            shape((total, model), BF16),
            shape((total, inner), BF16),
            shape((total, inner), F32),
            shape((seqs * chunks, 128, inner), BF16),
            shape((total, 128), F32),
            shape((8, 128), F32),
            shape((8, inner), F32),
            shape((seqs, 128, inner), F32),
        ),
        scratch_shapes=[
            pltpu.VMEM((128, inner), F32),
            pltpu.VMEM((8, 128), F32),
            pltpu.VMEM((CHUNK, channels), F32),
            pltpu.VMEM((CHUNK, inner), F32),
            pltpu.VMEM((4, CHUNK, inner), F32),
            pltpu.VMEM((CHUNK, inner), F32),
            pltpu.VMEM((CHUNK, 128), F32),
            pltpu.VMEM((2, 16, inner), F32),
        ],
        compiler_params=pltpu.CompilerParams(vmem_limit_bytes=48 * 1024 * 1024),
        name="forward",
    )(summed, gate, raw, cum, masks, seg_row, incoming, tokens, cot, weight, gain, skip, heads_map)


TILE = 256


class Exchange:
    def __init__(self, bits, pieces, flows):
        self.bits, self.pieces, self.flows = bits, pieces, flows
        self.parts = part_count(pieces)
        self.place, self.turn = lax.axis_index("dp"), lax.axis_index("seq")
        self.own = [(self.place // (1 << b)) % 2 for b in range(bits)]
        self.partner = [
            {"dp": self.place + (1 - 2 * self.own[b]) * (1 << b)} for b in range(bits)
        ]
        self.others = [{"seq": lax.rem(self.turn + j, pieces)} for j in range(pieces)]
        self.mine = self.index_of({b: self.own[b] for b in range(bits)})

    def index_of(self, fixed):
        return tuple(fixed.get(b, slice(None)) for b in range(self.bits - 1, -1, -1))

    def spot_of(self, d):
        return tuple((d // (1 << b)) % 2 for b in range(self.bits - 1, -1, -1))

    def order_of(self, f, h):
        rest = list(range(1, self.bits))
        shift = (f + h) % max(len(rest), 1)
        return [0] + rest[shift:] + rest[:shift]

    def share(self, h, extra=0):
        half = self.pieces // self.parts
        return pl.ds(h * half, half + (extra if h == self.parts - 1 else 0))

    def held(self, f, h, k, other):
        order = self.order_of(f, h)
        bit = order[k]
        value = 1 - self.own[bit] if other else self.own[bit]
        free = [b for b in range(self.bits - 1, -1, -1) if b not in order[:k]]
        source = self.grad if k == 0 else self.halves[k - 1]
        return source.at[
            (f,) + tuple(value if b == bit else slice(None) for b in free) + (self.share(h),)
        ]

    def landing(self, f, h, k):
        free = self.bits - k - 1
        return self.halves[k].at[(f,) + (slice(None),) * free + (self.share(h),)]

    def rs_copy(self, f, h, k):
        return remote(
            self.held(f, h, k, True),
            self.landing(f, h, k),
            self.rs_send.at[f, h, k],
            self.rs_recv.at[f, h, k],
            self.partner[self.order_of(f, h)[k]],
        )

    def rs_begin(self, f):
        for h in range(self.parts):
            self.rs_copy(f, h, 0).start()

    def rs_end(self, f, k):
        for h in range(self.parts):
            self.rs_copy(f, h, k).wait_recv()
            kept, into = self.held(f, h, k, False), self.landing(f, h, k)
            left = self.bits - k - 1
            for count in range(1 << left):
                spot = tuple((count >> (left - 1 - i)) & 1 for i in range(left))

                def body(p, carry, spot=spot, kept=kept, into=into):
                    into[spot + (p,)] = (
                        kept[spot + (p,)].astype(F32) + into[spot + (p,)].astype(F32)
                    ).astype(BF16)
                    return carry

                lax.fori_loop(0, self.pieces // self.parts, body, 0)
            if k + 1 < self.bits:
                self.rs_copy(f, h, k + 1).start()
        if k + 1 == self.bits:
            for j in range(1, self.pieces):
                self.zs_copy(f, j).start()

    def zs_copy(self, f, j):
        return remote(
            self.halves[self.bits - 1].at[f, lax.rem(self.turn + j, self.pieces)],
            self.piece_parts.at[f, j],
            self.zs_send.at[f, j],
            self.zs_recv.at[f, j],
            self.others[j],
        )

    def zs_end(self, f, rate, weight, momentum):
        for j in range(1, self.pieces):
            self.zs_copy(f, j).wait_recv()
        total = self.halves[self.bits - 1][f, self.turn].astype(F32)
        for j in range(1, self.pieces):
            total = total + self.piece_parts[f, j].astype(F32)
        summed = total.astype(BF16)
        moved = 0.5 * momentum + summed.astype(F32)
        self.gathered[(f,) + self.mine + (self.pieces,)] = summed
        self.gathered[(f,) + self.mine + (self.turn,)] = (
            weight.astype(F32) - rate * moved
        ).astype(BF16)
        for j in range(1, self.pieces):
            self.zg_copy(f, j).start()

    def zg_copy(self, f, j):
        spot = self.gathered.at[(f,) + self.mine + (self.turn,)]
        return remote(spot, spot, self.zg_send.at[f, j], self.zg_recv.at[f, j], self.others[j])

    def zg_end(self, f):
        for j in range(1, self.pieces):
            self.zg_copy(f, j).wait_recv()
        for h in range(self.parts):
            self.ag_copy(f, h, self.bits - 1).start()

    def ag_copy(self, f, h, k):
        order = self.order_of(f, h)
        fixed = {order[i]: self.own[order[i]] for i in range(k + 1)}
        spot = self.gathered.at[(f,) + self.index_of(fixed) + (self.share(h, 1),)]
        return remote(
            spot,
            spot,
            self.ag_send.at[f, h, k],
            self.ag_recv.at[f, h, k],
            self.partner[order[k]],
        )

    def ag_end(self, f, k):
        for h in range(self.parts):
            self.ag_copy(f, h, k).wait_recv()
            if k > 0:
                self.ag_copy(f, h, k - 1).start()

    def tiles_sent(self):
        for f in range(self.flows):
            for h in range(self.parts):
                self.rs_copy(f, h, 0).wait_send()

    def sent(self):
        for f in range(self.flows):
            for h in range(self.parts):
                for k in range(self.bits):
                    if k > 0:
                        self.rs_copy(f, h, k).wait_send()
                    self.ag_copy(f, h, k).wait_send()
            for j in range(1, self.pieces):
                self.zs_copy(f, j).wait_send()
                self.zg_copy(f, j).wait_send()

    def actions(self, f, rate, weights, momenta, after):
        steps = [functools.partial(self.rs_end, f, k) for k in range(self.bits)]
        steps.append(lambda: self.zs_end(f, rate, weights[f], momenta[f]))
        steps.append(functools.partial(self.zg_end, f))
        steps += [functools.partial(self.ag_end, f, k) for k in range(self.bits - 1, 0, -1)]

        def finish():
            self.ag_end(f, 0)
            after(f)

        return steps + [finish]


def exchange_scratch(bits, pieces, flows, rows, first=-1):
    parts = part_count(pieces)
    return (
        [pltpu.VMEM(half_shape(bits, pieces, flows, rows, k), BF16) for k in range(first, bits)]
        + [
            pltpu.VMEM((flows, pieces, rows, LANES), BF16),
            pltpu.VMEM((flows,) + (2,) * bits + (pieces + 1, rows, LANES), BF16),
        ]
        + dma_semaphores(flows, parts, bits)
        + dma_semaphores(flows, pieces)
        + dma_semaphores(flows, pieces)
        + dma_semaphores(flows, parts, bits)
        + [pltpu.SemaphoreType.DMA((flows,))]
    )


def give(ex, scratch, grad=None):
    if grad is None:
        grad, scratch = scratch[0], scratch[1:]
    ex.grad, ex.halves = grad, scratch[: ex.bits]
    scratch = scratch[ex.bits :]
    (ex.piece_parts, ex.gathered, ex.rs_send, ex.rs_recv, ex.zs_send, ex.zs_recv) = scratch[:6]
    (ex.zg_send, ex.zg_recv, ex.ag_send, ex.ag_recv, ex.out_sem) = scratch[6:11]
    return scratch[11:]


def tail_kernel(sizes, dims, *refs):
    seqs, piece, inner, channels, heads = sizes
    bits, pieces, flows_a, flows_b, split_rows, blocks = dims
    (
        rate_ref,
        summed_ref,
        conv_ref,
        halo_ref,
        taps_ref,
        ssm_grad_ref,
        starts_ref,
        heads_ref,
        skip_ref,
        summed_rw_ref,
        raw_ref,
        cum_ref,
        masks_ref,
        seg_row_ref,
        dot_ref,
        a_log_ref,
        own_ref,
        keep_ref,
        out_low_ref,
        normed_ref,
        low_ref,
        gate_grad_ref,
        weight_t_hbm,
        tokens_ref,
        gain_ref,
        weight_ref,
        momentum_ref,
        wide_ref,
        squares_ref,
        input_grad_ref,
        small_out_ref,
        out_a_ref,
        out_b_ref,
    ) = refs[:33]
    scratch = refs[33:]
    a, b = Exchange(bits, pieces, flows_a), Exchange(bits, pieces, flows_b)
    scratch = give(a, scratch)
    scratch = give(b, scratch, a.grad)
    (
        sent,
        taken,
        chain_send,
        chain_recv,
        later,
        out_turned,
        normed_turned,
        writer_low,
        reader_low,
        reader_turned,
        scores,
        cum_turned,
        biases,
        scores_grad,
        reader_grad,
        writer_grad,
        active,
        bent,
        step_x,
        cum_x,
        total,
        state_grad,
        ends,
        step_sum,
        move_sum,
        end_sum,
        shifted_rows,
        proj_grad,
        tails,
        rims,
        rims_in,
        rim_send,
        rim_recv,
        conv_sums,
        head_sums,
        gain_sums,
        small_acc,
        small_in,
        small_parts,
        sm_send,
        sm_recv,
        sz_send,
        sz_recv,
        weight_t_ref,
        weight_sem,
    ) = scratch
    weight_copy = pltpu.make_async_copy(weight_t_hbm, weight_t_ref, weight_sem)
    j = pl.program_id(0)
    steps = inner // TILE
    final_step = steps + 1
    places = 1 << bits
    per_flow = places // split_rows
    turn = a.turn
    chunk_count = seqs * piece // CHUNK
    rows = a.grad.shape[-2]
    chunks = piece // CHUNK
    rate = rate_ref[0]
    real = 2 * inner // LANES

    def out_copy(ex, out, f):
        return pltpu.make_async_copy(ex.gathered.at[f], out.at[f], ex.out_sem.at[f])

    a_actions = [
        a.actions(f, rate, weight_ref, momentum_ref, lambda f: out_copy(a, out_a_ref, f).start())
        for f in range(flows_a)
    ]
    late = [weight_ref.at[pl.ds(flows_a, flows_b)], momentum_ref.at[pl.ds(flows_a, flows_b)]]
    b_actions = [
        b.actions(f, rate, *late, lambda f: out_copy(b, out_b_ref, f).start())
        for f in range(flows_b)
    ]

    def store(ex, tile, values):
        for part in range(split_rows):
            d = (tile % per_flow) * split_rows + part
            spot = (tile // per_flow,) + ex.spot_of(d)
            for p in range(pieces):
                at = (p * split_rows + part) * rows
                ex.grad[spot + (p,)] = values[at : at + rows]

    def rim_copy(slot):
        return remote(
            rims.at[slot],
            rims_in.at[slot],
            rim_send.at[slot],
            rim_recv.at[slot],
            {"seq": lax.rem(turn + pieces - 1, pieces)},
        )

    def fix_rim(slot, at):
        @pl.when(turn < pieces - 1)
        def _():
            rim_copy(slot).wait_recv()
            for n in range(seqs):
                proj_grad[(n + 1) * piece - 8 : (n + 1) * piece, at] = (
                    tails[n] + rims_in[slot, n].astype(F32)
                ).astype(BF16)

    def conv_back(slot, at):
        for n in range(seqs):
            here_rows = pl.ds(n * piece, piece)
            grad = total[here_rows] * bent[here_rows]
            conv = conv_ref[here_rows]
            sums = [None] * 5
            sums[4] = jnp.sum(grad, axis=0, keepdims=True)
            sums[3] = jnp.sum(grad * conv, axis=0, keepdims=True)
            result = grad * taps_ref[3:4]
            rim = jnp.zeros((8, TILE), F32)
            shifted_rows[0:8] = jnp.zeros((8, TILE), F32)
            shifted_rows[8 + piece :] = jnp.zeros((8, TILE), F32)
            for k in range(3):
                shifted_rows[8 : 8 + piece] = grad * masks_ref[here_rows, k : k + 1]
                here = shifted_rows[11 - k : 11 - k + piece]
                result = result + here * taps_ref[k : k + 1]
                early = shifted_rows[3 - k : 11 - k]
                rim = rim + early * taps_ref[k : k + 1]
                sums[k] = jnp.sum(here * conv, axis=0, keepdims=True) + jnp.sum(
                    early * halo_ref[(n + 1) * HALO - 8 : (n + 1) * HALO], axis=0, keepdims=True
                )
            for i in range(5):
                if n == 0:
                    conv_sums[i : i + 1, at] = sums[i]
                else:
                    conv_sums[i : i + 1, at] += sums[i]
            proj_grad[here_rows, at] = result.astype(BF16)
            tails[n] = result[piece - 8 :]
            rims[slot, n] = rim.astype(BF16)

        @pl.when(turn > 0)
        def _():
            rim_copy(slot).start()

    @pl.when(j == 0)
    def _():
        greet(a.partner + a.others[1:])
        first, final = turn == pieces - 1, turn == 0
        width = inner // blocks

        def copy(c):
            ahead = {"seq": lax.rem(turn + pieces - 1, pieces)}
            return remote(sent.at[c], taken.at[c], chain_send.at[c], chain_recv.at[c], ahead)

        @pl.when(first)
        def _():
            later[...] = jnp.zeros_like(later)
            for c in range(blocks):
                sent[c] = own_ref[:, :, c * width : (c + 1) * width].astype(BF16)
                copy(c).start()

        weight_copy.start()
        out_turned[...] = jnp.transpose(out_low_ref[...])
        normed_turned[...] = jnp.transpose(normed_ref[...])
        low_tiles = inner // LANES

        def tiles(tile):
            if tile >= real:
                result = jnp.zeros((out_turned.shape[0], 2 * LANES), BF16)
            elif tile < low_tiles:
                at = tile * LANES
                result = mm(out_turned[...], low_ref[:, at : at + 2 * LANES]).astype(BF16)
            else:
                at = (tile - low_tiles) * LANES
                result = mm(normed_turned[...], gate_grad_ref[:, at : at + 2 * LANES])
                result = result.astype(BF16)
            store(a, tile, result[:, :LANES])
            store(a, tile + 1, result[:, LANES:])

        pairs = flows_a * per_flow // 2
        done = 0
        for c in range(blocks):
            until = pairs * (c + 1) // blocks
            for pair in range(done, until):
                tiles(2 * pair)
                if (2 * pair + 2) % per_flow == 0:
                    a.rs_begin(2 * pair // per_flow)
            done = until

            @pl.when(jnp.logical_not(first))
            def _():
                at = slice(c * width, (c + 1) * width)
                copy(c).wait_recv()

                @pl.when(jnp.logical_not(final))
                def _():
                    sent[c] = (
                        own_ref[:, :, at] + keep_ref[:, 0:1, at] * taken[c].astype(F32)
                    ).astype(BF16)
                    copy(c).start()

                later[:, :, at] = taken[c].astype(F32)

        for f in range(flows_a):
            a_actions[f][0]()
        a.tiles_sent()
        for ck in range(chunk_count):
            at = slice(ck * CHUNK, (ck + 1) * CHUNK)
            values = summed_rw_ref[at]
            values = values * sigmoid(values)
            writer, reader = values[:, :128], values[:, 128:]
            scores[ck] = scores_of(reader, writer)
            writer_low[at] = writer.astype(BF16)
            reader_low[at] = reader.astype(BF16)
            reader_turned[ck] = jnp.transpose(reader.astype(BF16))
            cum_turned[ck] = jnp.transpose(cum_ref[at])
            biases[ck] = mask_bias(masks_ref[at, 8:9], seg_row_ref[0:1, at])
        for ref in (
            scores_grad,
            reader_grad,
            writer_grad,
            step_sum,
            move_sum,
            end_sum,
            ends,
            gain_sums,
        ):
            ref[...] = jnp.zeros_like(ref)

        @pl.when(jnp.logical_not(final))
        def _():
            for c in range(blocks):
                copy(c).wait_send()

    agenda = {}

    def plan(step, act):
        agenda.setdefault(min(max(step, 1), steps), []).append(act)

    last_b = [((f + 1) * per_flow * LANES - 1) // TILE + 1 for f in range(flows_b)]
    a_steps = {1: 3, 2: 4} if bits == 3 else {k: 1 + k for k in range(1, bits)}
    a_done = b_ready = None
    for k in range(1, bits):
        for f in range(flows_a):
            plan(a_steps[k], a_actions[f][k])
    b_taken = []
    for f in range(flows_b):
        taken_steps = 0
        if last_b[f] + 1 <= steps:
            plan(last_b[f] + 1, functools.partial(b.rs_begin, f))
            for i in range(bits):
                if last_b[f] + 2 + i <= steps:
                    plan(last_b[f] + 2 + i, b_actions[f][i])
                    taken_steps = i + 1
            b_taken.append(taken_steps)
        else:
            b_taken.append(None)

    def weight_tiles(tile, at):
        result = mm(normed_turned[...], proj_grad[:, at]).astype(BF16)
        store(b, tile, result[:, :LANES])
        store(b, tile + 1, result[:, LANES:])

    @pl.when((j > 0) & (j < final_step))
    def _():
        at = pl.ds(pl.multiple_of((j - 1) * TILE, TILE), TILE)

        @pl.when(j > 1)
        def _():
            before = pl.ds(pl.multiple_of((j - 2) * TILE, TILE), TILE)
            fix_rim(j - 2, before)
            weight_tiles((j - 2) * (TILE // LANES), before)

        def activate(i, carry):
            rows_at = pl.ds(pl.multiple_of(i * 32, 32), 32)
            values = summed_ref[rows_at]
            turned = gate_of(values)
            active[rows_at] = values * turned
            bent[rows_at] = turned * (1.0 + values * (1.0 - turned))
            return carry

        lax.fori_loop(0, seqs * piece // 32, activate, 0)
        raw = raw_ref[...]
        lane = lax.broadcasted_iota(jnp.int32, raw.shape, 1)
        step_x[...] = spread(jnp.where(lane < heads, softplus(raw), 0.0), heads_ref)
        cum = cum_ref[...]
        high, low = split(cum)
        lowest = (cum - high.astype(F32) - low.astype(F32)).astype(BF16)
        cum_x[...] = (
            mm(high, heads_ref[...]) + mm(low, heads_ref[...]) + mm(lowest, heads_ref[...])
        )
        half = lax.broadcasted_iota(jnp.int32, (CHUNK, 128), 1) < 64
        head = (j - 1) * (TILE // 64)
        skip = skip_ref[...]
        for n in range(seqs):
            state_grad[...] = later[n, :, at]
            for c in range(chunks - 1, -1, -1):
                ck = n * chunks + c
                here = slice(ck * CHUNK, (ck + 1) * CHUNK)
                cum_here = cum_x[here]
                final_cum = cum_here[CHUNK - 1 :]
                enter_x = jnp.exp(cum_here) * masks_ref[here, 4:5]
                tail_x = jnp.exp(final_cum - cum_here) * masks_ref[here, 5:6]
                kept = jnp.exp(final_cum) * masks_ref[(ck + 1) * CHUNK - 1 : (ck + 1) * CHUNK, 4:5]
                signal = active[here]
                grad = ssm_grad_ref[here]
                moved = (signal * step_x[here]).astype(BF16)
                grad_low = grad.astype(BF16)
                later_low = state_grad[...].astype(BF16)
                from_later = mm(writer_low[here], later_low) * tail_x
                parts = []
                score = scores[ck]
                bias = biases[ck]
                grad_of_scores = scores_grad[ck]
                for pair in range(TILE // 128):
                    col = slice(pair * 128, (pair + 1) * 128)
                    ones = []
                    for i in range(2):
                        lane_at = pair * 128 + i * 64
                        ones.append(
                            jnp.exp(
                                cum_here[:, lane_at : lane_at + 1]
                                - cum_turned[ck, pl.ds(head + 2 * pair + i, 1), :]
                                + bias
                            )
                        )
                    zero = jnp.zeros((CHUNK, 128), BF16)
                    stacked = jnp.concatenate(
                        [
                            jnp.where(half, grad_low[:, col], zero),
                            jnp.where(half, zero, grad_low[:, col]),
                        ],
                        axis=0,
                    )
                    both_grad = mm_nt(stacked, moved[:, col])
                    grad_of_scores = (
                        grad_of_scores + both_grad[:CHUNK] * ones[0] + both_grad[CHUNK:] * ones[1]
                    )
                    both = jnp.concatenate([(score * one).astype(BF16) for one in ones], axis=0)
                    parts.append(mm_tn(both, stacked))
                scores_grad[ck] = grad_of_scores
                moved_grad = jnp.concatenate(parts, axis=1) + from_later
                wide_moved = moved.astype(F32)
                weighted = (wide_moved * tail_x).astype(BF16)
                entered = (grad * enter_x).astype(BF16)
                start = starts_ref[ck]
                reader_grad[here] += mm_nt(entered, start)
                writer_grad[here] += mm_nt(weighted, later_low)
                passed = jnp.sum(
                    start.astype(F32) * later_low.astype(F32), axis=0, keepdims=True
                )
                ends[ck : ck + 1] = kept * passed + jnp.sum(
                    wide_moved * from_later, axis=0, keepdims=True
                )
                state_grad[...] = state_grad[...] * kept + mm(reader_turned[ck], entered)
                step_sum[here] += gather_heads(moved_grad * signal, heads_ref)
                move_sum[here] += gather_heads(moved_grad * wide_moved, heads_ref)
                total[here] = moved_grad * step_x[here] + skip * grad
        end_sum[...] += gather_heads(ends[...], heads_ref)
        conv_back(j - 1, at)
        for step in sorted(agenda):

            @pl.when(j == step)
            def _(step=step):
                for act in agenda[step]:
                    act()

    @pl.when(j == final_step)
    def _():
        before = slice((steps - 1) * TILE, steps * TILE)
        fix_rim(steps - 1, before)
        weight_tiles((steps - 1) * (TILE // LANES), before)
        pending = []
        for f in range(flows_b):
            if last_b[f] == steps and b_taken[f] is None:
                b.rs_begin(f)
                b_taken[f] = 0
        at = slice(inner, channels)
        lane = lax.broadcasted_iota(jnp.int32, (CHUNK, 128), 1)
        row = lax.broadcasted_iota(jnp.int32, (CHUNK, 128), 0)
        upper = triangle(CHUNK, True)
        decay_rate = -jnp.exp(a_log_ref[...])
        raw_sum = jnp.zeros((1, 128), F32)
        decay_sum = jnp.zeros((1, 128), F32)
        values = summed_rw_ref[...]
        turned = sigmoid(values)
        bent[...] = turned * (1.0 + values * (1.0 - turned))
        for ck in range(chunk_count):
            here = slice(ck * CHUNK, (ck + 1) * CHUNK)
            high, low = split(scores_grad[ck])
            total[here, 128:] = (
                reader_grad[here] + mm(high, writer_low[here]) + mm(low, writer_low[here])
            )
            total[here, :128] = (
                writer_grad[here] + mm_tn(high, reader_low[here]) + mm_tn(low, reader_low[here])
            )
            raw = raw_ref[here]
            taken_steps = jnp.where(lane < heads, softplus(raw), 0.0)
            change = dot_ref[here] - move_sum[here]
            change = change + jnp.where(row == CHUNK - 1, end_sum[ck : ck + 1], 0.0)
            decay_grad = exact_mm(upper, change)
            raw_grad = jnp.where(
                lane < heads, (step_sum[here] + decay_grad * decay_rate) * sigmoid(raw), 0.0
            )
            raw_sum = raw_sum + jnp.sum(raw_grad, axis=0, keepdims=True)
            decay_sum = decay_sum + jnp.sum(
                decay_grad * taken_steps * decay_rate, axis=0, keepdims=True
            )
            proj_grad[here, channels : channels + 128] = raw_grad.astype(BF16)
            proj_grad[here, channels + 128 :] = jnp.zeros((CHUNK, 128), BF16)
        head_sums[0:1] = raw_sum
        head_sums[1:2] = decay_sum
        conv_back(steps, at)
        fix_rim(steps, at)
        for tile in range(inner // LANES, flows_b * per_flow, 2):
            if tile * LANES < channels + 256:
                weight_tiles(tile, slice(tile * LANES, (tile + 2) * LANES))
            else:
                for i in range(2):
                    store(b, tile + i, jnp.zeros((pieces * split_rows * rows, LANES), BF16))
        for f in range(flows_b):
            if b_taken[f] is None:
                b.rs_begin(f)
                b_taken[f] = 0

        rest = weight_t_ref.shape[0] - inner
        weight_copy.wait()

        def input_rows(i, carry):
            rows_at = pl.ds(pl.multiple_of(i * 128, 128), 128)
            normed_grad = mm(gate_grad_ref[rows_at], weight_t_ref[:inner]) + mm(
                proj_grad[rows_at, :rest], weight_t_ref[inner:]
            )
            values = tokens_ref[rows_at].astype(F32)
            scale = lax.rsqrt(jnp.mean(values * values, axis=-1, keepdims=True) + EPS)
            gain_sums[0:1] += jnp.sum(normed_grad * values * scale, axis=0, keepdims=True)
            pushed = normed_grad * gain_ref[...]
            inside = jnp.mean(pushed * values, axis=-1, keepdims=True)
            input_grad_ref[rows_at] = (
                out_low_ref[rows_at].astype(F32)
                + scale * pushed
                - values * (scale * scale * scale * inside)
            ).astype(BF16)
            return carry

        def sm_copy(k):
            return remote(
                small_acc.at[k], small_in.at[k], sm_send.at[k], sm_recv.at[k], a.partner[k]
            )

        def sz_copy(k):
            return remote(
                small_acc.at[bits],
                small_parts.at[turn],
                sz_send.at[k],
                sz_recv.at[k],
                a.others[k],
            )

        def small_begin():
            model = gain_sums.shape[1]
            small_acc[0, 0:5] = conv_sums[0:5]
            small_acc[0, 5:7, :inner] = wide_ref[0:2]
            small_acc[0, 5:7, inner : inner + 128] = head_sums[0:2]
            small_acc[0, 5:8, inner + 128 :] = squares_ref[0:3]
            small_acc[0, 7:8, :model] = gain_sums[0:1]
            small_acc[0, 7:8, model : inner + 128] = jnp.zeros((1, inner + 128 - model), F32)
            sm_copy(0).start()

        def small_step(k):
            sm_copy(k).wait_recv()
            small_acc[k + 1] = small_acc[k] + small_in[k]
            if k + 1 < bits:
                sm_copy(k + 1).start()
            else:
                small_parts[turn] = small_acc[bits]
                for i in range(1, pieces):
                    sz_copy(i).start()

        def small_end():
            for i in range(1, pieces):
                sz_copy(i).wait_recv()
            whole = small_parts[0]
            for i in range(1, pieces):
                whole = whole + small_parts[i]
            small_out_ref[...] = whole

        lines = [a_actions[f][bits:] for f in range(flows_a)]
        lines += [b_actions[f][b_taken[f] :] for f in range(flows_b)]
        blocks_of_rows = tokens_ref.shape[0] // 128
        extra = [
            lambda: lax.fori_loop(0, blocks_of_rows // 2, input_rows, 0),
            lambda: lax.fori_loop(blocks_of_rows // 2, blocks_of_rows, input_rows, 0),
            small_begin,
        ]
        extra += [functools.partial(small_step, k) for k in range(bits)] + [small_end]
        while any(lines) or extra:
            if extra:
                extra.pop(0)()
            for line in lines[flows_a:] + lines[:flows_a]:
                if line:
                    line.pop(0)()
        b.tiles_sent()
        a.sent()
        b.sent()
        for k in range(bits):
            sm_copy(k).wait_send()
        for i in range(1, pieces):
            sz_copy(i).wait_send()

        @pl.when(turn > 0)
        def _():
            for slot in range(steps + 1):
                rim_copy(slot).wait_send()

        for f in range(flows_a):
            out_copy(a, out_a_ref, f).wait()
        for f in range(flows_b):
            out_copy(b, out_b_ref, f).wait()


def row_split(places, rows):
    return 2 if places > 2 and rows % 32 == 0 else 1


def tail(
    rate,
    tiled,
    summed_rw_source,
    whole,
    weights,
    momenta,
    wide,
    squares,
    sizes,
    places,
    pieces,
    flows,
    blocks=6,
):
    seqs, piece, inner, channels, heads = sizes
    summed, conv, halo, taps, ssm_grad, starts, heads_map, skip = tiled
    total_rows = summed.shape[0]
    own = whole[6]
    tokens, weight_t = whole[13], whole[12]
    model = tokens.shape[1]
    flows_a, flows_b = flows
    assert flows_b <= flows_a
    bits = places.bit_length() - 1
    assert places == 1 << bits and bits >= 1 and pieces >= 2
    share = model // pieces
    split_rows = row_split(places, share)
    rows = share // split_rows
    steps = inner // TILE
    small = (8, channels)
    shape = jax.ShapeDtypeStruct
    any_space = pl.BlockSpec(memory_space=pl.ANY)
    sem = dma_semaphores

    def constant(array):
        count = array.ndim
        return pl.BlockSpec(
            array.shape, lambda j: (0,) * count, pipeline_mode=pl.Buffered(1)
        )

    def columns(height, last):
        return pl.BlockSpec((height, TILE), lambda j: (0, jnp.clip(j - 1, 0, last)))

    gathered = lambda count: (count,) + (2,) * bits + (pieces + 1, rows, LANES)
    chunk_count = total_rows // CHUNK
    square = (chunk_count, CHUNK, CHUNK)
    per_tile = (total_rows, TILE)
    per_head = (total_rows, 128)
    constants = list(whole) + [weights, momenta, wide, squares]
    return pl.pallas_call(
        functools.partial(
            tail_kernel, sizes, (bits, pieces, flows_a, flows_b, split_rows, blocks)
        ),
        grid=(steps + 2,),
        in_specs=[
            pl.BlockSpec(memory_space=pltpu.SMEM),
            columns(total_rows, steps),
            columns(total_rows, steps),
            columns(halo.shape[0], steps),
            columns(4, steps),
            columns(total_rows, steps - 1),
            pl.BlockSpec(
                (chunk_count, 128, TILE), lambda j: (0, 0, jnp.clip(j - 1, 0, steps - 1))
            ),
            columns(128, steps - 1),
            columns(1, steps - 1),
            pl.BlockSpec((total_rows, TILE), lambda j: (0, steps), pipeline_mode=pl.Buffered(1)),
        ]
        + [any_space if array is weight_t else constant(array) for array in constants],
        out_specs=(
            pl.BlockSpec((total_rows, model), lambda j: (0, 0)),
            pl.BlockSpec(small, lambda j: (0, 0)),
            any_space,
            any_space,
        ),
        out_shape=(
            shape((total_rows, model), BF16),
            shape(small, F32),
            shape(gathered(flows_a), BF16),
            shape(gathered(flows_b), BF16),
        ),
        scratch_shapes=exchange_scratch(bits, pieces, flows_a, rows)
        + exchange_scratch(bits, pieces, flows_b, rows, 0)
        + [pltpu.VMEM((blocks, seqs, 128, inner // blocks), BF16)] * 2
        + sem(blocks)
        + [
            pltpu.VMEM((seqs, 128, inner), F32),
            pltpu.VMEM((model, total_rows), BF16),
            pltpu.VMEM((model, total_rows), BF16),
            pltpu.VMEM(per_head, BF16),
            pltpu.VMEM(per_head, BF16),
            pltpu.VMEM(square, BF16),
            pltpu.VMEM(square, F32),
            pltpu.VMEM(square, F32),
            pltpu.VMEM(square, F32),
            pltpu.VMEM(square, F32),
            pltpu.VMEM(per_head, F32),
            pltpu.VMEM(per_head, F32),
            pltpu.VMEM(per_tile, F32),
            pltpu.VMEM(per_tile, F32),
            pltpu.VMEM(per_tile, F32),
            pltpu.VMEM(per_tile, F32),
            pltpu.VMEM(per_tile, F32),
            pltpu.VMEM((128, TILE), F32),
            pltpu.VMEM((max(chunk_count, 8), TILE), F32),
            pltpu.VMEM(per_head, F32),
            pltpu.VMEM(per_head, F32),
            pltpu.VMEM((max(chunk_count, 8), 128), F32),
            pltpu.VMEM((piece + 16, TILE), F32),
            pltpu.VMEM((total_rows, channels + 256), BF16),
            pltpu.VMEM((seqs, 8, TILE), F32),
            pltpu.VMEM((steps + 1, seqs, 8, TILE), BF16),
            pltpu.VMEM((steps + 1, seqs, 8, TILE), BF16),
        ]
        + sem(steps + 1)
        + [
            pltpu.VMEM(small, F32),
            pltpu.VMEM((8, 128), F32),
            pltpu.VMEM((8, model), F32),
            pltpu.VMEM((bits + 1,) + small, F32),
            pltpu.VMEM((bits,) + small, F32),
            pltpu.VMEM((pieces,) + small, F32),
        ]
        + sem(bits)
        + sem(pieces)
        + [pltpu.VMEM(weight_t.shape, BF16), pltpu.SemaphoreType.DMA],
        compiler_params=pltpu.CompilerParams(
            collective_id=2, has_side_effects=True, vmem_limit_bytes=62 * 1024 * 1024
        ),
        name="tail",
    )(rate, *tiled, summed_rw_source, *constants)


def piece_kernel(
    dims,
    out_weight_ref,
    weight_ref,
    out_momentum_ref,
    momentum_ref,
    last_momentum_ref,
    w_ref,
    m_ref,
    tiles,
    halves,
    turned,
    w_sem,
    m_sem,
):
    flows_a, flows_b, places, split_rows = dims
    place, turn = lax.axis_index("dp"), lax.axis_index("seq")
    rows, per_flow = m_ref.shape[1], places // split_rows
    inner, model = out_weight_ref.shape
    width = weight_ref.shape[0]
    out_tiles, in_tiles, rest = inner // LANES, width // LANES, width % LANES
    part = lax.rem(place, split_rows)
    first = (turn * split_rows + part) * rows
    start = jnp.minimum(lax.div(first, 128) * 128, model - 256)
    window = pl.ds(pl.multiple_of(start, 128), 256)
    mine = pl.ds(pl.multiple_of(first - start, 16), rows)
    half = pl.ds(pl.multiple_of(part * rows, 8), rows)
    within = lax.div(place, split_rows)
    flows = flows_a + flows_b

    def each(act):
        for f in range(flows):
            if f < flows_a:
                tile = f * per_flow + within
            else:
                tile = 2 * out_tiles + (f - flows_a) * per_flow + within
            act(f, tile)

    def copies(source, momentum, at, count, f):
        yield pltpu.make_async_copy(
            source.at[pl.ds(pl.multiple_of(at, 8), count), window],
            tiles.at[f, pl.ds(0, count)],
            w_sem.at[f],
        )
        if count == LANES:
            lanes = pl.ds(pl.multiple_of(at, LANES), LANES)
            yield pltpu.make_async_copy(momentum.at[half, lanes], halves.at[f], m_sem.at[f])

    def moves(f, tile, act):
        in_limit = out_tiles + in_tiles
        if f < flows_a:
            in_limit = min(in_limit, 2 * out_tiles)

        @pl.when(tile < out_tiles)
        def _():
            for copy in copies(out_weight_ref, out_momentum_ref, tile * LANES, LANES, f):
                act(copy)

        @pl.when((tile >= out_tiles) & (tile < in_limit))
        def _():
            at = (tile - out_tiles) * LANES
            for copy in copies(weight_ref, momentum_ref, at, LANES, f):
                act(copy)

        if rest and f >= flows_a:

            @pl.when(tile == in_limit)
            def _():
                for copy in copies(weight_ref, momentum_ref, in_tiles * LANES, rest, f):
                    act(copy)

    tiles[...] = jnp.zeros_like(tiles)
    halves[...] = jnp.zeros_like(halves)
    each(lambda f, tile: moves(f, tile, lambda copy: copy.start()))
    each(lambda f, tile: moves(f, tile, lambda copy: copy.wait()))

    def take(f, tile):
        turned[...] = jnp.transpose(tiles[f])
        w_ref[f] = turned[mine]
        m_ref[f] = halves[f]
        if rest and f >= flows_a:

            @pl.when(tile == out_tiles + in_tiles)
            def _():
                m_ref[f] = last_momentum_ref[half]

    each(take)


def owned(out_weight, weight_t, out_momentum_t, momentum, flows_a, flows_b, places):
    model = out_weight.shape[1]
    share, width = momentum.shape
    split_rows = row_split(places, share)
    rows, flows = share // split_rows, flows_a + flows_b
    whole = width // LANES * LANES
    last_momentum = jnp.pad(momentum[:, whole:], ((0, 0), (0, LANES - (width - whole))))
    any_space = pl.BlockSpec(memory_space=pl.ANY)
    vmem = pl.BlockSpec(memory_space=pltpu.VMEM)
    return pl.pallas_call(
        functools.partial(piece_kernel, (flows_a, flows_b, places, split_rows)),
        in_specs=[any_space] * 4 + [vmem],
        out_specs=(vmem, vmem),
        out_shape=(
            jax.ShapeDtypeStruct((flows, rows, LANES), BF16),
            jax.ShapeDtypeStruct((flows, rows, LANES), F32),
        ),
        scratch_shapes=[
            pltpu.VMEM((flows, LANES, 256), BF16),
            pltpu.VMEM((flows, rows, LANES), F32),
            pltpu.VMEM((256, LANES), BF16),
            pltpu.SemaphoreType.DMA((flows,)),
            pltpu.SemaphoreType.DMA((flows,)),
        ],
        name="owned",
    )(out_weight, weight_t, out_momentum_t, momentum, last_momentum)


def finish_kernel(
    out_steps,
    split_rows,
    gathered_a_ref,
    gathered_b_ref,
    out_momentum_ref,
    momentum_ref,
    totals_ref,
    out_weight_ref,
    weight_ref,
    new_out_momentum_ref,
    new_momentum_ref,
    conv_weight_ref,
    conv_bias_ref,
    gate_gain_ref,
    norm_gain_ref,
    skip_ref,
    dt_bias_ref,
    a_log_ref,
    output_rms_ref,
    mixer_rms_ref,
    joined,
):
    group, slots, rows, _ = gathered_a_ref.shape
    step = pl.program_id(0)

    @pl.when(step == 0)
    def _():
        heads, inner, model = skip_ref.shape[0], gate_gain_ref.shape[0], norm_gain_ref.shape[0]
        side = inner + 128
        conv_weight_ref[...] = totals_ref[0:4]
        conv_bias_ref[...] = totals_ref[4]
        gate_gain_ref[...] = totals_ref[5, :inner]
        norm_gain_ref[...] = totals_ref[7, :model]
        skip_ref[...] = totals_ref[6, :heads]
        dt_bias_ref[...] = totals_ref[5, inner : inner + heads]
        a_log_ref[...] = totals_ref[6, inner : inner + heads]
        count = jnp.maximum(totals_ref[7:8, side + 9 : side + 10], 1.0) * model
        squares = jnp.sum(totals_ref[5:7, side:], axis=1, keepdims=True)
        output_rms_ref[...] = jnp.sqrt(squares[0:1] / count)
        mixer_rms_ref[...] = jnp.sqrt(squares[1:2] / count)

    def write(gathered_ref, weights, old, new):
        for i in range(group // split_rows):
            at = slice(i * LANES, (i + 1) * LANES)
            for part in range(split_rows):
                for p in range(slots - 1):
                    to = (p * split_rows + part) * rows
                    joined[i, to : to + rows] = gathered_ref[i * split_rows + part, p]
                own = slice(part * rows, (part + 1) * rows)
                summed = gathered_ref[i * split_rows + part, slots - 1].astype(F32)
                new[own, at] = 0.5 * old[own, at] + summed
            weights[at] = jnp.transpose(joined[i])

    @pl.when(step < out_steps)
    def _():
        write(gathered_a_ref, out_weight_ref, out_momentum_ref, new_out_momentum_ref)

    @pl.when((step >= out_steps) & (step < 2 * out_steps))
    def _():
        write(gathered_a_ref, weight_ref, momentum_ref, new_momentum_ref)

    @pl.when(step >= 2 * out_steps)
    def _():
        write(gathered_b_ref, weight_ref, momentum_ref, new_momentum_ref)


def finish(gathered_a, gathered_b, out_momentum_t, momentum, totals, heads, split_rows, group=4):
    _, slots, rows, _ = gathered_a.shape
    share, width = momentum.shape
    inner = out_momentum_t.shape[1]
    model = (slots - 1) * share
    wide = group * LANES
    group = group * split_rows
    out_steps, in_steps = inner // wide, -(-width // wide)
    out_at = lambda j: jnp.minimum(j, out_steps - 1)
    in_at = lambda j: jnp.maximum(j - out_steps, 0)
    by_column = [
        pl.BlockSpec((share, wide), lambda j: (0, out_at(j))),
        pl.BlockSpec((share, wide), lambda j: (0, in_at(j))),
    ]
    shape = jax.ShapeDtypeStruct
    smalls = [
        shape(size, F32)
        for size in (
            (4, totals.shape[1]),
            (totals.shape[1],),
            (inner,),
            (model,),
            (heads,),
            (heads,),
            (heads,),
            (1, 1),
            (1, 1),
        )
    ]
    return pl.pallas_call(
        functools.partial(finish_kernel, out_steps, split_rows),
        grid=(out_steps + in_steps,),
        in_specs=[
            pl.BlockSpec(
                (group, slots, rows, LANES), lambda j: (jnp.minimum(j, 2 * out_steps - 1), 0, 0, 0)
            ),
            pl.BlockSpec(
                (group, slots, rows, LANES), lambda j: (jnp.maximum(j - 2 * out_steps, 0), 0, 0, 0)
            ),
        ]
        + by_column
        + [pl.BlockSpec(totals.shape, lambda j: (0, 0))],
        out_specs=[
            pl.BlockSpec((wide, model), lambda j: (out_at(j), 0)),
            pl.BlockSpec((wide, model), lambda j: (in_at(j), 0)),
        ]
        + by_column
        + [
            pl.BlockSpec(small.shape, lambda j, count=len(small.shape): (0,) * count)
            for small in smalls
        ],
        out_shape=[
            shape((inner, model), BF16),
            shape((width, model), BF16),
            shape((share, inner), F32),
            shape((share, width), F32),
        ]
        + smalls,
        scratch_shapes=[pltpu.VMEM((group // split_rows, model, LANES), BF16)],
        name="finish",
    )(gathered_a, gathered_b, out_momentum_t, momentum, totals)


def local(
    tokens,
    cotangent,
    segment_ids,
    doc_starts,
    valid_mask,
    step_number,
    learn_rate,
    norm_gain,
    in_weight,
    conv_weight,
    conv_bias,
    dt_bias,
    a_log,
    skip_d,
    gate_gain,
    out_weight,
    in_momentum,
    out_momentum,
):
    seqs, piece, model_width = tokens.shape
    heads = dt_bias.shape[0]
    tap_count, channels = conv_weight.shape
    inner_width = gate_gain.shape[0]
    proj_width = in_weight.shape[1]
    total = seqs * piece
    sizes = (seqs, piece, inner_width, channels, heads)
    places, pieces = lax.axis_size("dp"), lax.axis_size("seq")
    turn = lax.axis_index("seq")
    seg = segment_ids.astype(F32)
    sent = jnp.concatenate(
        [
            tokens[:, piece - HALO :],
            jnp.broadcast_to(seg[:, piece - HALO :, None], (seqs, HALO, LANES)).astype(BF16),
        ],
        axis=2,
    )
    route = [(i, i + 1) for i in range(pieces - 1)]
    arrived = lax.ppermute(sent, "seq", route)
    halo = arrived[:, :, :model_width].reshape(seqs * HALO, model_width)
    early_seg = jnp.where(turn == 0, -1.0, arrived[:, :, model_width].astype(F32))
    seg_pad = jnp.concatenate([early_seg, seg], axis=1)
    seg_row = seg.reshape(1, total)
    heads_map = (
        lax.broadcasted_iota(jnp.int32, (LANES, inner_width), 0)
        == lax.broadcasted_iota(jnp.int32, (LANES, inner_width), 1) // (inner_width // heads)
    ).astype(BF16)

    def lanes(values):
        return jnp.pad(values, (0, LANES - heads)).reshape(1, LANES)

    flat_tokens = tokens.reshape(total, model_width)
    weight_t = jnp.transpose(in_weight)
    out_momentum_t = jnp.transpose(out_momentum)
    flat_cot = cotangent.reshape(total, model_width)
    bias_row, decay_row = lanes(dt_bias), lanes(a_log)
    skip_row = jnp.repeat(skip_d, inner_width // heads).reshape(1, inner_width)
    gain_row = gate_gain.reshape(1, inner_width)
    normed, masks, gate, conv, conv_halo, summed, raw, cum, fresh, keep = front(
        flat_tokens,
        halo,
        norm_gain.reshape(1, model_width),
        weight_t,
        conv_weight,
        conv_bias.reshape(1, channels),
        seg_pad,
        valid_mask,
        bias_row,
        decay_row,
        heads_map,
        sizes,
    )
    incoming = chain(fresh, keep, 1)
    output, low, out_low, gate_grad, ssm_grad, starts, dots, squares, wide, state_grad = forward(
        summed,
        gate,
        raw,
        cum,
        masks,
        seg_row,
        incoming,
        flat_tokens,
        flat_cot,
        out_weight,
        gain_row,
        skip_row,
        heads_map,
        sizes,
    )
    step_float = step_number[0].astype(F32)
    rate = (learn_rate[0] * step_float / (step_float + 16.0)).reshape(1)
    share_rows = model_width // pieces
    split_rows = row_split(places, share_rows)
    per_flow = places // split_rows
    flows_a = -(-2 * inner_width // (LANES * per_flow))
    flows_b = -(-(channels + 2 * LANES) // (LANES * per_flow))
    weights, momenta = owned(
        out_weight, weight_t, out_momentum_t, in_momentum, flows_a, flows_b, places
    )
    input_grad, totals, gathered_a, gathered_b = tail(
        rate,
        (summed, conv, conv_halo, conv_weight, ssm_grad, starts, heads_map, skip_row),
        summed,
        (
            raw,
            cum,
            masks,
            seg_row,
            dots,
            decay_row,
            state_grad,
            keep,
            out_low,
            normed,
            low,
            gate_grad,
            weight_t,
            flat_tokens,
            norm_gain.reshape(1, model_width),
        ),
        weights,
        momenta,
        wide,
        squares,
        sizes,
        places,
        pieces,
        (flows_a, flows_b),
    )
    share = (pieces + 1, share_rows // split_rows, LANES)
    (
        new_out_weight,
        new_weight_t,
        new_out_momentum_t,
        new_in_momentum,
        conv_weight_total,
        conv_bias_total,
        gate_gain_total,
        norm_gain_total,
        skip_total,
        dt_bias_total,
        a_log_total,
        output_rms,
        mixer_rms,
    ) = finish(
        gathered_a.reshape((-1,) + share),
        gathered_b.reshape((-1,) + share),
        out_momentum_t,
        in_momentum,
        totals,
        heads,
        split_rows,
    )
    new_in_weight = jnp.transpose(new_weight_t)
    new_out_momentum = jnp.transpose(new_out_momentum_t)
    output_rms, mixer_rms = output_rms.reshape(1), mixer_rms.reshape(1)
    return (
        output.reshape(tokens.shape),
        input_grad.reshape(tokens.shape),
        new_in_weight,
        new_out_weight,
        new_in_momentum,
        new_out_momentum,
        norm_gain_total,
        conv_weight_total,
        conv_bias_total,
        dt_bias_total,
        a_log_total,
        skip_total,
        gate_gain_total,
        output_rms,
        mixer_rms,
    )


def solution(mesh):
    placed = (
        P("dp", "seq", None),
        P("dp", "seq", None),
        P("dp", "seq"),
        P("dp", "seq"),
        P("dp", "seq"),
        P(),
        P(),
        P(),
        P(),
        P(),
        P(),
        P(),
        P(),
        P(),
        P(),
        P(),
        P("seq", None),
        P(None, "seq"),
    )
    return jax.shard_map(
        local,
        mesh=mesh,
        in_specs=placed,
        out_specs=(
            P("dp", "seq", None),
            P("dp", "seq", None),
            P(),
            P(),
            P("seq", None),
            P(None, "seq"),
            P(),
            P(),
            P(),
            P(),
            P(),
            P(),
            P(),
            P(),
            P(),
        ),
        check_vma=False,
    )
```
